32 devices in a mesh: dp: 8 (over z, x), tensor: 4 (over y, core).
Axes of the slice: x: 2, y: 2, z: 4, core: 2. Of those that a mesh axis runs over, the one named last changes fastest.
Arguments:
- tokens: bfloat16 [8192, 1152], P('dp'), may hold values from -6 to 6
- segment_ids: int32 [8192], P('dp'), may hold values from 0 to 1, as said below
- cotangent: bfloat16 [8192, 1152], P('dp'), may hold values from -6 to 6
- w_query: bfloat16 [1152, 1024], P(None, 'tensor'), may hold values from -0.1875 to 0.1875
- w_key: bfloat16 [1152, 256], replicated, may hold values from -0.1875 to 0.1875
- w_value: bfloat16 [1152, 256], replicated, may hold values from -0.1875 to 0.1875
- w_out: bfloat16 [1024, 1152], P('tensor'), may hold values from -0.1875 to 0.1875
- w_gate: bfloat16 [1152, 6912], P(None, 'tensor'), may hold values from -0.1875 to 0.1875
- w_up: bfloat16 [1152, 6912], P(None, 'tensor'), may hold values from -0.1875 to 0.1875
- w_down: bfloat16 [6912, 1152], P('tensor'), may hold values from -0.078125 to 0.078125
- gain_attn_in: float32 [1152], replicated, may hold values from -0.4 to 0.4
- gain_attn_out: float32 [1152], replicated, may hold values from -0.4 to 0.4
- gain_ffn_in: float32 [1152], replicated, may hold values from -0.4 to 0.4
- gain_ffn_out: float32 [1152], replicated, may hold values from -0.4 to 0.4
- gain_query: float32 [256], replicated, may hold values from -0.4 to 0.4
- gain_key: float32 [256], replicated, may hold values from -0.4 to 0.4
Outputs:
- layer_out: bfloat16 [8192, 1152], P('dp')
- input_grad: bfloat16 [8192, 1152], P('dp')
- grad_query_w: float32 [1152, 1024], P('dp', 'tensor')
- grad_key_w: float32 [1152, 256], P('dp')
- grad_value_w: float32 [1152, 256], P('dp')
- grad_out_w: float32 [1024, 1152], P('tensor', 'dp')
- grad_gate_w: float32 [1152, 6912], P('dp', 'tensor')
- grad_up_w: float32 [1152, 6912], P('dp', 'tensor')
- grad_down_w: float32 [6912, 1152], P('tensor', 'dp')
- grad_attn_in: float32 [1152], P('dp')
- grad_attn_out: float32 [1152], P('dp')
- grad_ffn_in: float32 [1152], P('dp')
- grad_ffn_out: float32 [1152], P('dp')
- grad_query_gain: float32 [256], P('dp')
- grad_key_gain: float32 [256], P('dp')
The draws below stay inside these ranges and needn't reach their ends.
Inputs may be any that keep to these rules, and one draw needn't show every extreme that they name: `segment_ids`: within each group of 1024 tokens the ids are all 0 (one sequence) or 0 for the first 640 tokens and 1 for the rest (two sequences); at least one group holds two.
All inputs are finite; a program needn't handle non-finite values.
Results may differ from the reference program's by a relative error of at most 0.02.
Values sent between devices are 32-bit elements; how exact they have to be, the bound alone decides.
A program may use at most 192 MiB of HBM per device.

```python
import jax
import jax.numpy as jnp
from jax import lax

D = 1152
HEADS = 4
HD = 256
FF = 6912
GROUP = 1024
SPLIT = 640
TOKENS = 8192


def draw_segment_ids(key, part):
    count = TOKENS // GROUP
    pairs = jax.random.randint(jax.random.fold_in(key, 11), (count,), 0, 2).astype(jnp.int32)
    chosen = jax.random.randint(jax.random.fold_in(key, 12), (), 0, count).astype(jnp.int32)
    pairs = jnp.where(jnp.arange(count, dtype=jnp.int32) == chosen, 1, pairs).astype(jnp.int32)
    places = jnp.arange(GROUP, dtype=jnp.int32)
    later = (places >= SPLIT).astype(jnp.int32)
    return (pairs[:, None] * later[None, :]).reshape(TOKENS).astype(jnp.int32)


def block_scale(key, dims, pieces, low, high):
    level, own = 1.0, jax.random.fold_in(key, 6)
    for axis_at, blocks in pieces:
        heights = jnp.exp(jax.random.uniform(jax.random.fold_in(own, axis_at), (blocks,), jnp.float32, low / len(pieces), high / len(pieces)))
        level = level * jnp.repeat(heights, dims[axis_at] // blocks).reshape([-1 if axis == axis_at else 1 for axis in range(len(dims))])
    return level


def centred(stream_key, shape, scale, limit, pieces=(), held_as=jnp.bfloat16):
    factor_of = block_scale(stream_key, shape, pieces, -0.22, 0.18) if pieces else 1.0
    values = jax.random.normal(stream_key, shape, jnp.float32) * scale * factor_of
    return jnp.minimum(jnp.maximum(values, -limit), limit).astype(held_as)


def setup_inputs(seed: int = 0) -> dict:
    key_list = jax.random.split(jax.random.key(seed), 17)
    return {
        "tokens": centred(key_list[0], (TOKENS, D), 1.0, 6.0, ((0, 8),)),
        "segment_ids": draw_segment_ids(jax.random.fold_in(key_list[16], 71), 0),
        "cotangent": centred(key_list[2], (TOKENS, D), 1.0, 6.0, ((0, 8),)),
        "w_query": centred(key_list[3], (D, HEADS * HD), D ** -0.5, 0.1875, ((1, 4),)),
        "w_key": centred(key_list[4], (D, HD), D ** -0.5, 0.1875),
        "w_value": centred(key_list[5], (D, HD), D ** -0.5, 0.1875),
        "w_out": centred(key_list[6], (HEADS * HD, D), (HEADS * HD) ** -0.5, 0.1875, ((0, 4),)),
        "w_gate": centred(key_list[7], (D, FF), D ** -0.5, 0.1875, ((1, 4),)),
        "w_up": centred(key_list[8], (D, FF), D ** -0.5, 0.1875, ((1, 4),)),
        "w_down": centred(key_list[9], (FF, D), FF ** -0.5, 0.078125, ((0, 4),)),
        "gain_attn_in": jnp.clip(jax.random.uniform(key_list[10], (D,), jnp.float32, -0.4, 0.4), -0.4, 0.4),
        "gain_attn_out": jnp.clip(jax.random.uniform(key_list[11], (D,), jnp.float32, -0.4, 0.4), -0.4, 0.4),
        "gain_ffn_in": jnp.clip(jax.random.uniform(key_list[12], (D,), jnp.float32, -0.4, 0.4), -0.4, 0.4),
        "gain_ffn_out": jnp.clip(jax.random.uniform(key_list[13], (D,), jnp.float32, -0.4, 0.4), -0.4, 0.4),
        "gain_query": jnp.clip(jax.random.uniform(key_list[14], (HD,), jnp.float32, -0.4, 0.4), -0.4, 0.4),
        "gain_key": jnp.clip(jax.random.uniform(key_list[15], (HD,), jnp.float32, -0.4, 0.4), -0.4, 0.4),
    }


epsilon = 1e-06
score_scale = 0.0625
highest = lax.Precision.HIGHEST

@jax.custom_vjp
def low(v):
    return lax.optimization_barrier(v.astype(jnp.bfloat16)).astype(jnp.float32)

@jax.custom_vjp
def low_back(v):
    return v

def low_keep(v):
    return (low(v), None)

def low_pass(kept, grad):
    return (grad,)

def back_keep(v):
    return (v, None)

def back_low(kept, grad):
    return (low(grad),)
low.defvjp(low_keep, low_pass)
low_back.defvjp(back_keep, back_low)

def rms_norm(values, gain):
    inverse = lax.rsqrt(lax.optimization_barrier(jnp.mean(values * values, axis=-1, keepdims=True)) + epsilon)
    return values * inverse * (1.0 + gain)

def matmul(left, right):
    return jnp.dot(left, right, precision=highest, preferred_element_type=jnp.float32)

def layer(hidden_in, segments, w_query, w_key, w_value, w_out, w_gate, w_up, w_down, gain_attn_in, gain_attn_out, gain_ffn_in, gain_ffn_out, gain_query, gain_key):
    length = hidden_in.shape[0]
    normed = low(rms_norm(hidden_in, gain_attn_in))
    query = low_back(matmul(normed, w_query).reshape(length, HEADS, HD))
    query = low(rms_norm(query, gain_query))
    keys = jnp.broadcast_to(matmul(normed, w_key)[:, None, :], (length, HEADS, HD))
    keys = low(rms_norm(low_back(keys), gain_key))
    values = jnp.broadcast_to(matmul(normed, w_value)[:, None, :], (length, HEADS, HD))
    values = low(low_back(values))
    scores = low_back(jnp.einsum('thd,shd->hts', query, keys, precision=highest) * score_scale)
    places = jnp.arange(length)
    allowed = (places[:, None] >= places[None, :]) & (segments[:, None] == segments[None, :])
    scores = jnp.where(allowed[None], scores, -1e+30)
    attn_prob = jax.nn.softmax(scores, axis=-1)
    context = jnp.einsum('hts,shd->thd', low(attn_prob), values, precision=highest)
    context = low(low_back(context)).reshape(length, HEADS * HD)
    branch = low_back(matmul(context, w_out))
    middle = hidden_in + rms_norm(branch, gain_attn_out)
    normed_two = low(rms_norm(middle, gain_ffn_in))
    gate = low_back(matmul(normed_two, w_gate))
    upward = low_back(matmul(normed_two, w_up))
    inner = low(jax.nn.gelu(gate, approximate=True) * upward)
    output = low_back(matmul(inner, w_down))
    return middle + rms_norm(output, gain_ffn_out)

def reference(tokens, segment_ids, cotangent, w_query, w_key, w_value, w_out, w_gate, w_up, w_down, gain_attn_in, gain_attn_out, gain_ffn_in, gain_ffn_out, gain_query, gain_key):
    weights = tuple((item.astype(jnp.float32) for item in (w_query, w_key, w_value, w_out, w_gate, w_up, w_down, gain_attn_in, gain_attn_out, gain_ffn_in, gain_ffn_out, gain_query, gain_key)))
    count = TOKENS // GROUP
    inputs = tokens.astype(jnp.float32).reshape(count, GROUP, D)
    segments_all = segment_ids.reshape(count, GROUP)
    incoming_all = cotangent.astype(jnp.float32).reshape(count, GROUP, D)

    def step(totals, batch):
        hidden_in, segments, incoming = batch
        result, pull = jax.vjp(lambda first, *others: layer(first, segments, *others), hidden_in, *weights)
        grads = pull(incoming)
        summed = tuple((total + grad_item for total, grad_item in zip(totals, grads[1:])))
        return (summed, (result.astype(jnp.bfloat16), grads[0].astype(jnp.bfloat16)))
    zeros = tuple((jnp.zeros_like(item) for item in weights))
    totals, (outputs, input_grads) = lax.scan(step, zeros, (inputs, segments_all, incoming_all))
    return (outputs.reshape(TOKENS, D), input_grads.reshape(TOKENS, D), totals[0], totals[1], totals[2], totals[3], totals[4], totals[5], totals[6], totals[7], totals[8], totals[9], totals[10], totals[11], totals[12])
```

```python
import functools

import jax
import jax.numpy as jnp
from jax import lax
from jax.sharding import PartitionSpec as P

epsilon = 1e-06
score_scale = 0.0625
NZ = 4

f32 = jnp.float32
bf16 = jnp.bfloat16


def rms_norm(values, gain):
    inverse = lax.rsqrt(jnp.mean(values * values, axis=-1, keepdims=True) + epsilon)
    return values * inverse * (1.0 + gain)


def rms_back(values, gain, grad):
    inverse = lax.rsqrt(jnp.mean(values * values, axis=-1, keepdims=True) + epsilon)
    hat = values * inverse
    scaled = grad * (1.0 + gain)
    back = inverse * (scaled - hat * jnp.mean(scaled * hat, axis=-1, keepdims=True))
    return back, jnp.sum(grad * hat, axis=0)


def product(left, right):
    return jnp.dot(left, right, preferred_element_type=f32)


def product_t(left, right):
    return lax.dot_general(left, right, (((1,), (1,)), ((), ())), preferred_element_type=f32)


def t_product(left, right):
    return lax.dot_general(left, right, (((0,), (0,)), ((), ())), preferred_element_type=f32)


def activate(gate, upward):
    return jax.nn.gelu(gate, approximate=True) * upward


class Links:
    def __init__(self, mesh):
        self.dp_size = mesh.shape["dp"]
        self.nx = self.dp_size // NZ
        tensor = mesh.shape["tensor"]
        self.perm_core = [(t, t ^ 1) for t in range(tensor)]
        self.perm_y = [(t, t ^ 2) for t in range(tensor)]
        nx = self.nx
        self.perm_z1 = [(z * nx + x, (z ^ 1) * nx + x) for z in range(NZ) for x in range(nx)]
        self.perm_z2 = [(z * nx + x, (z ^ 2) * nx + x) for z in range(NZ) for x in range(nx)]

    def core(self, a):
        return lax.ppermute(a, "tensor", self.perm_core)

    def y(self, a):
        return lax.ppermute(a, "tensor", self.perm_y)

    def z1(self, a):
        return lax.ppermute(a, "dp", self.perm_z1)

    def z2(self, a):
        return lax.ppermute(a, "dp", self.perm_z2)

    def x(self, a, step):
        nx = self.nx
        return lax.ppermute(a, "dp", [(z * nx + x, z * nx + (x + step) % nx) for z in range(NZ) for x in range(nx)])


def low(a):
    return a.astype(bf16)


def body(
    links,
    tokens,
    segment_ids,
    cotangent,
    w_query,
    w_key,
    w_value,
    w_out,
    w_gate,
    w_up,
    w_down,
    gain_attn_in,
    gain_attn_out,
    gain_ffn_in,
    gain_ffn_out,
    gain_query,
    gain_key,
):
    length, width = tokens.shape
    head = w_query.shape[1]
    quarter = length // 4
    half_ff = w_gate.shape[1] // 2
    nx = links.nx
    blk = width // links.dp_size
    dp, t = lax.axis_index("dp"), lax.axis_index("tensor")
    z, x = dp // nx, dp % nx
    y, c = t // 2, t % 2
    parity = z % 2
    one = jnp.where(segment_ids[0] < length, 1.0, 0.5).astype(f32)

    def keep_low(a):
        return (a * one).astype(bf16)

    def place(dc, dy):
        return ((c ^ dc) * 2 + (y ^ dy)) * quarter

    def rows(a, dc, dy):
        return lax.dynamic_slice_in_dim(a, place(dc, dy), quarter, 0)

    def to_absolute(pieces):
        stack = jnp.stack([pieces[0][0], pieces[0][1], pieces[1][0], pieces[1][1]])
        mine = c * 2 + y
        return jnp.concatenate([lax.dynamic_index_in_dim(stack, mine ^ b, 0, keepdims=False) for b in range(4)], axis=0)

    out_own = w_out.astype(f32)
    out_y = links.y(out_own)
    out_c = links.core(out_own)
    out_yc = links.core(out_y)
    w_out_all = jnp.concatenate([w_out, keep_low(out_c), keep_low(out_y), keep_low(out_yc)], axis=0)

    wg_h = jnp.where(parity == 0, w_gate[:, :half_ff], w_gate[:, half_ff:])
    wu_h = jnp.where(parity == 0, w_up[:, :half_ff], w_up[:, half_ff:])
    wd_h = jnp.where(parity == 0, w_down[:half_ff], w_down[half_ff:])

    hidden_in = tokens.astype(f32)
    normed_low = low(rms_norm(hidden_in, gain_attn_in))
    query_raw = product(normed_low, w_query)
    keys_raw = product(normed_low, w_key)
    query_low = low(rms_norm(query_raw, gain_query))
    keys_low = low(rms_norm(keys_raw, gain_key))
    values_low = low(product(normed_low, w_value))
    places = jnp.arange(length)
    allowed = (places[:, None] >= places[None, :]) & (segment_ids[:, None] == segment_ids[None, :])

    def scores_of():
        raw = product_t(query_low, keys_low) * score_scale
        return jnp.where(allowed, raw, -1e30)

    scores = scores_of()
    largest = jnp.max(scores, axis=-1, keepdims=True)
    exponent = jnp.exp(scores - largest)
    total = jnp.sum(exponent, axis=-1, keepdims=True)
    log_total = largest + jnp.log(total)
    context_low = low(product(low(exponent / total), values_low))

    context = context_low.astype(f32)
    mine = jnp.concatenate([rows(context, 0, 1), rows(context, 0, 0)], axis=0)
    of_core = links.core(jnp.concatenate([rows(context, 1, 1), rows(context, 1, 0)], axis=0))
    of_y = links.y(jnp.concatenate([rows(context, 0, 0), rows(context, 0, 1)], axis=0))
    of_yc = links.y(jnp.concatenate([of_core[quarter:], of_core[:quarter]], axis=0))
    context_all = jnp.concatenate([low(mine), keep_low(of_core), keep_low(of_y), keep_low(of_yc)], axis=1)
    branch = product(context_all, w_out_all)
    hidden_rows = jnp.concatenate([rows(tokens, 0, 1), rows(tokens, 0, 0)], axis=0).astype(f32)
    middle_own = hidden_rows + rms_norm(branch, gain_attn_out)
    middle_core = links.core(middle_own)

    middles, normed_two, inners, parts = [], [], [], []
    saved = []
    for k in range(2):
        at = slice(k * quarter, (k + 1) * quarter)
        middle = jnp.concatenate([middle_own[at], middle_core[at]], axis=0)
        normed_k = low(rms_norm(middle, gain_ffn_in))
        gate, upward = product(normed_k, w_gate), product(normed_k, w_up)
        inner = low(activate(gate, upward))
        part = product(inner, w_down)
        middles.append(middle)
        normed_two.append(normed_k)
        saved.append((gate, upward))
        parts.append(part)
    normed_own = low(rms_norm(middle_own, gain_ffn_in)).astype(f32)
    other_own = links.z1(normed_own)
    other_core = links.core(other_own)
    normed_other = jnp.concatenate([keep_low(other_own), keep_low(other_core)], axis=0)

    def gather_quarters(parts):
        sums = [part[:quarter] + links.core(part[quarter:]) for part in parts]
        return sums[1] + links.y(sums[0])

    output_q = gather_quarters(parts)
    output_y = links.y(output_q)
    output_c = links.core(output_q)
    output_yc = links.core(output_y)
    outputs = [jnp.concatenate([output_y, output_yc], axis=0), jnp.concatenate([output_q, output_c], axis=0)]
    grad_out = cotangent.astype(f32)
    d_outputs, layer_pieces, grad_ffn_out = [], [], 0.0
    for k in range(2):
        dy_k = jnp.concatenate([rows(cotangent, 0, 1 - k), rows(cotangent, 1, 1 - k)], axis=0).astype(f32)
        layer_k = low(middles[k] + rms_norm(outputs[k], gain_ffn_out))
        d_k, gain_k = rms_back(outputs[k], gain_ffn_out, dy_k)
        grad_ffn_out = grad_ffn_out + gain_k
        d_outputs.append(low(d_k))
        layer_pieces.append(layer_k)
    layer_out = to_absolute(
        [
            [layer_pieces[1][:quarter], layer_pieces[0][:quarter]],
            [layer_pieces[1][quarter:], layer_pieces[0][quarter:]],
        ]
    )

    d_own_rows = [d[:quarter].astype(f32) for d in d_outputs]
    got_own = [links.z1(d_own_rows[1]), links.z1(d_own_rows[0])]
    got_core = [links.core(g) for g in got_own]
    d_other = jnp.concatenate(
        [keep_low(got_own[1]), keep_low(got_own[0]), keep_low(got_core[1]), keep_low(got_core[0])], axis=0
    )

    back_parts = []
    for k in range(2):
        gate, upward = saved[k]
        d_inner = product_t(d_outputs[k], w_down)
        _, pull = jax.vjp(activate, gate, upward)
        d_gate, d_up = pull(d_inner)
        back_parts.append(product_t(low(d_gate), w_gate) + product_t(low(d_up), w_up))
    d_normed_q = gather_quarters(back_parts)
    middle_q = middle_own[quarter:]
    branch_q = branch[quarter:]
    dy_q = rows(cotangent, 0, 0).astype(f32)
    d_mid, grad_ffn_in = rms_back(middle_q, gain_ffn_in, d_normed_q)
    d_middle = dy_q + d_mid
    d_branch, grad_attn_out = rms_back(branch_q, gain_attn_out, d_middle)
    d_branch_low = low(d_branch)
    d_context = low(product_t(d_branch_low, w_out_all)).astype(f32)
    heads = [d_context[:, i * head : (i + 1) * head] for i in range(4)]
    c_got = links.core(jnp.concatenate([heads[1], heads[3]], axis=1))
    y_got = links.y(jnp.concatenate([heads[2], c_got[:, head:]], axis=1))
    grad_context = keep_low(
        to_absolute([[heads[0], y_got[:, :head]], [c_got[:, :head], y_got[:, head:]]])
    )
    d_branch_own = d_branch_low.astype(f32)
    d_branch_y = links.y(d_branch_own)
    d_branch_c = links.core(d_branch_own)
    d_branch_yc = links.core(d_branch_y)
    d_branch_all = jnp.concatenate(
        [d_branch_low, keep_low(d_branch_y), keep_low(d_branch_c), keep_low(d_branch_yc)], axis=0
    )
    context_rel = jnp.concatenate(
        [rows(context_low, 0, 0), rows(context_low, 0, 1), rows(context_low, 1, 0), rows(context_low, 1, 1)], axis=0
    )
    grad_w_out_t = t_product(d_branch_all, context_rel)

    attn_prob = jnp.exp(scores_of() - log_total)
    prob_low = low(attn_prob)
    grad_prob = product_t(grad_context, values_low)
    grad_values = low(t_product(prob_low, grad_context))
    balance = jnp.sum(grad_prob * attn_prob, axis=-1, keepdims=True)
    grad_scores = low(attn_prob * (grad_prob - balance))
    grad_query_n = product(grad_scores, keys_low) * score_scale
    grad_keys_n = t_product(grad_scores, query_low) * score_scale
    d_query, grad_gain_query = rms_back(query_raw, gain_query, grad_query_n)
    d_keys, grad_gain_key = rms_back(keys_raw, gain_key, grad_keys_n)
    d_query, d_keys = low(d_query), low(d_keys)
    d_qkv = jnp.concatenate([d_query, d_keys, grad_values], axis=1)
    w_qkv = jnp.concatenate([w_query, w_key, w_value], axis=1)
    in_parts = []
    for k in range(2):
        rows_k = jnp.concatenate([rows(d_qkv, 0, 1 - k), rows(d_qkv, 1, 1 - k)], axis=0)
        in_parts.append(product_t(rows_k, w_qkv))
    d_normed_in = gather_quarters(in_parts)
    hidden_q = rows(tokens, 0, 0).astype(f32)
    d_in, grad_attn_in = rms_back(hidden_q, gain_attn_in, d_normed_in)
    input_q = low(d_middle + d_in)
    input_own = input_q.astype(f32)
    input_y = links.y(input_own)
    input_c = links.core(input_own)
    input_yc = links.core(input_y)
    input_grad = keep_low(to_absolute([[input_own, input_y], [input_c, input_yc]]))

    grad_qkv = t_product(normed_low, d_qkv)
    grad_w_query, grad_kv = grad_qkv[:, :head], grad_qkv[:, head:]
    kv_keep = jnp.where(c == 0, grad_kv[:, :head], grad_kv[:, head:])
    kv_send = jnp.where(c == 0, grad_kv[:, head:], grad_kv[:, :head])
    kv = kv_keep + links.core(kv_send)
    kv_half = head // 2
    kv_keep = jnp.where(y == 0, kv[:, :kv_half], kv[:, kv_half:])
    kv_send = jnp.where(y == 0, kv[:, kv_half:], kv[:, :kv_half])
    kv = kv_keep + links.y(kv_send)
    attn_grads = jnp.concatenate([grad_w_query, grad_w_out_t, kv], axis=1)

    normed_all = jnp.concatenate(
        [normed_two[0][:quarter], normed_two[1][:quarter], normed_two[0][quarter:], normed_two[1][quarter:], normed_other],
        axis=0,
    )
    d_all = jnp.concatenate(
        [d_outputs[0][:quarter], d_outputs[1][:quarter], d_outputs[0][quarter:], d_outputs[1][quarter:], d_other], axis=0
    )
    gate, upward = product(normed_all, wg_h), product(normed_all, wu_h)
    inner, pull = jax.vjp(activate, gate, upward)
    inner = low(inner)
    d_inner = product_t(d_all, wd_h)
    d_gate, d_up = pull(d_inner)
    ff_grads = [t_product(d_all, inner), t_product(normed_all, low(d_gate)), t_product(normed_all, low(d_up))]

    zh, zl = z // 2, z % 2

    def sum_x(grads, z_half):
        mine = lax.dynamic_index_in_dim(grads, z_half, 0, keepdims=False)
        acc = lax.dynamic_index_in_dim(mine, x, 1, keepdims=False)
        for step in range(1, nx):
            to = lax.dynamic_index_in_dim(mine, (x + step) % nx, 1, keepdims=False)
            acc = acc + links.x(to, step)
        return acc

    def scatter(grads):
        grads = grads.reshape(2, 2, nx, blk, grads.shape[1])
        far = sum_x(grads, 1 - zh)
        near = sum_x(grads, zh)
        return near + links.z2(far)

    ff_sums = []
    for grads in ff_grads:
        got = scatter(grads)
        own = lax.dynamic_index_in_dim(got, zl, 0, keepdims=False)
        other = links.z1(lax.dynamic_index_in_dim(got, 1 - zl, 0, keepdims=False))
        ff_sums.append(
            jnp.where(
                parity == 0, jnp.concatenate([own, other], axis=1), jnp.concatenate([other, own], axis=1)
            )
        )
    grad_w_down, grad_w_gate, grad_w_up = ff_sums[0].T, ff_sums[1], ff_sums[2]

    got = scatter(attn_grads)
    attn_sum = lax.dynamic_index_in_dim(got, zl, 0, keepdims=False) + links.z1(
        lax.dynamic_index_in_dim(got, 1 - zl, 0, keepdims=False)
    )
    grad_w_query = attn_sum[:, :head]
    grad_w_out = attn_sum[:, head : 2 * head].T
    kv_own = attn_sum[:, 2 * head :]
    kv_y = links.y(kv_own)
    kv_wide = jnp.where(y == 0, jnp.concatenate([kv_own, kv_y], axis=1), jnp.concatenate([kv_y, kv_own], axis=1))
    kv_c = links.core(kv_wide)
    grad_w_key = jnp.where(c == 0, kv_wide, kv_c)
    grad_w_value = jnp.where(c == 0, kv_c, kv_wide)

    small = jnp.concatenate(
        [
            grad_attn_in.reshape(links.dp_size, -1),
            grad_attn_out.reshape(links.dp_size, -1),
            grad_ffn_in.reshape(links.dp_size, -1),
            (grad_ffn_out * 0.25).reshape(links.dp_size, -1),
            grad_gain_query.reshape(links.dp_size, -1),
            grad_gain_key.reshape(links.dp_size, -1),
        ],
        axis=1,
    )
    small = small + links.core(small)
    small = small + links.y(small)
    small = small.reshape(2, 2, nx, 1, small.shape[1])
    acc = lax.dynamic_index_in_dim(small, x, 2, keepdims=False)
    for step in range(1, nx):
        acc = acc + links.x(lax.dynamic_index_in_dim(small, (x + step) % nx, 2, keepdims=False), step)
    acc = lax.dynamic_index_in_dim(acc, zh, 0, keepdims=False) + links.z2(
        lax.dynamic_index_in_dim(acc, 1 - zh, 0, keepdims=False)
    )
    acc = lax.dynamic_index_in_dim(acc, zl, 0, keepdims=False) + links.z1(
        lax.dynamic_index_in_dim(acc, 1 - zl, 0, keepdims=False)
    )
    acc = acc.reshape(-1)
    hb = head // links.dp_size
    return (
        layer_out,
        input_grad,
        grad_w_query,
        grad_w_key,
        grad_w_value,
        grad_w_out,
        grad_w_gate,
        grad_w_up,
        grad_w_down,
        acc[:blk],
        acc[blk : 2 * blk],
        acc[2 * blk : 3 * blk],
        acc[3 * blk : 4 * blk],
        acc[4 * blk : 4 * blk + hb],
        acc[4 * blk + hb :],
    )


def solution(mesh):
    return jax.shard_map(
        functools.partial(body, Links(mesh)),
        mesh=mesh,
        in_specs=(
            P("dp", None),
            P("dp"),
            P("dp", None),
            P(None, "tensor"),
            P(),
            P(),
            P("tensor", None),
            P(None, "tensor"),
            P(None, "tensor"),
            P("tensor", None),
            P(),
            P(),
            P(),
            P(),
            P(),
            P(),
        ),
        out_specs=(
            P("dp", None),
            P("dp", None),
            P("dp", "tensor"),
            P("dp", None),
            P("dp", None),
            P("tensor", "dp"),
            P("dp", "tensor"),
            P("dp", "tensor"),
            P("tensor", "dp"),
            P("dp"),
            P("dp"),
            P("dp"),
            P("dp"),
            P("dp"),
            P("dp"),
        ),
        check_vma=False,
    )
```

```python
import functools

import jax
import jax.numpy as jnp
from jax import lax
from jax.experimental import pallas as pl
from jax.experimental.pallas import tpu as pltpu
from jax.sharding import PartitionSpec as P

epsilon = 1e-06
score_scale = 0.0625
NZ = 4

f32 = jnp.float32
bf16 = jnp.bfloat16


def rms_norm(values, gain):
    inverse = lax.rsqrt(jnp.mean(values * values, axis=-1, keepdims=True) + epsilon)
    return values * inverse * (1.0 + gain)


def rms_back(values, gain, grad):
    inverse = lax.rsqrt(jnp.mean(values * values, axis=-1, keepdims=True) + epsilon)
    hat = values * inverse
    scaled = grad * (1.0 + gain)
    back = inverse * (scaled - hat * jnp.mean(scaled * hat, axis=-1, keepdims=True))
    return back, jnp.sum(grad * hat, axis=0)


def product(left, right):
    return jnp.dot(left, right, preferred_element_type=f32)


def product_t(left, right):
    return lax.dot_general(left, right, (((1,), (1,)), ((), ())), preferred_element_type=f32)


def t_product(left, right):
    return lax.dot_general(left, right, (((0,), (0,)), ((), ())), preferred_element_type=f32)


def activate(gate, upward):
    return jax.nn.gelu(gate, approximate=True) * upward


class Links:
    def __init__(self, mesh):
        self.dp_size = mesh.shape["dp"]
        self.nx = self.dp_size // NZ
        tensor = mesh.shape["tensor"]
        self.perm_core = [(t, t ^ 1) for t in range(tensor)]
        self.perm_y = [(t, t ^ 2) for t in range(tensor)]
        nx = self.nx
        self.perm_z1 = [(z * nx + x, (z ^ 1) * nx + x) for z in range(NZ) for x in range(nx)]
        self.perm_z2 = [(z * nx + x, (z ^ 2) * nx + x) for z in range(NZ) for x in range(nx)]

    def core(self, a):
        return lax.ppermute(a, "tensor", self.perm_core)

    def y(self, a):
        return lax.ppermute(a, "tensor", self.perm_y)

    def z1(self, a):
        return lax.ppermute(a, "dp", self.perm_z1)

    def z2(self, a):
        return lax.ppermute(a, "dp", self.perm_z2)

    def x(self, a, step):
        nx = self.nx
        return lax.ppermute(a, "dp", [(z * nx + x, z * nx + (x + step) % nx) for z in range(NZ) for x in range(nx)])


def low(a):
    return a.astype(bf16)


def remote(src, dst, send, recv, index, to):
    return pltpu.make_async_remote_copy(
        src_ref=src,
        dst_ref=dst,
        send_sem=send.at[index],
        recv_sem=recv.at[index],
        device_id={"tensor": to},
        device_id_type=pl.DeviceIdType.MESH,
    )


def greet(*others):
    barrier = pltpu.get_barrier_semaphore()
    for other in others:
        pl.semaphore_signal(barrier, inc=1, device_id={"tensor": other}, device_id_type=pl.DeviceIdType.MESH)
    pl.semaphore_wait(barrier, len(others))


def gelu_tanh(u):
    return 0.5 * u * (1.0 + jnp.tanh(0.7978845608028654 * (u + 0.044715 * (u * u * u))))


def forward_kernel(
    middle, gain, w_gate, w_up, w_down, out, normed, inner, part, from_core, from_y, core_send, core_recv, y_send, y_recv
):
    t = lax.axis_index("tensor")
    core, across = t ^ 1, t ^ 2
    greet(core, across)
    tile, half = 256, 128
    columns = w_gate.shape[1]
    cut = 7 * (columns // 14) // 128 * 128 if columns % 14 == 0 else columns // 2 // 128 * 128
    pieces = [(0, cut), (cut, columns)]

    def step(i, carry):
        at = pl.ds(pl.multiple_of(i * tile, tile), tile)
        m = middle[at, :]
        inverse = lax.rsqrt(jnp.mean(m * m, axis=-1, keepdims=True) + epsilon)
        n = (m * inverse * (1.0 + gain[...])).astype(bf16)
        normed[at, :] = n
        for lo, hi in pieces:
            g = product(n, w_gate[:, lo:hi])
            u = product(n, w_up[:, lo:hi])
            inner[:, lo:hi] = (gelu_tanh(g) * u).astype(bf16)
        part[i] = product(inner[...], w_down[...])
        copy = remote(part.at[i, pl.ds(half, half)], from_core.at[i], core_send, core_recv, i, core)
        copy.start()
        copy.wait_recv()
        part[i, :half] = part[i, :half] + from_core[i]

        @pl.when(i < 2)
        def _():
            remote(part.at[i, pl.ds(0, half)], from_y.at[i], y_send, y_recv, i, across).start()

        return carry

    lax.fori_loop(0, 4, step, 0)
    spread = []
    for h in range(2):
        remote(part.at[h, pl.ds(0, half)], from_y.at[h], y_send, y_recv, h, across).wait_recv()
        lo = (2 + h) * tile
        out[lo : lo + half, :] = part[2 + h, :half] + from_y[h]
        mine = out.at[pl.ds(lo, half)]
        to_y = remote(mine, out.at[pl.ds(h * tile, half)], y_send, y_recv, 2 + h, across)
        to_y.start()
        to_core = remote(mine, out.at[pl.ds(lo + half, half)], core_send, core_recv, 4 + h, core)
        to_core.start()
        spread.append((to_y, to_core))
    last = []
    for h in range(2):
        to_y, to_core = spread[h]
        to_y.wait_recv()
        lo = h * tile
        copy = remote(out.at[pl.ds(lo, half)], out.at[pl.ds(lo + half, half)], core_send, core_recv, 6 + h, core)
        copy.start()
        last.append(copy)
    for h in range(2):
        spread[h][1].wait_recv()
        last[h].wait_recv()
    for i in range(4):
        remote(part.at[i, pl.ds(half, half)], from_core.at[i], core_send, core_recv, i, core).wait_send()
    for h in range(2):
        remote(part.at[h, pl.ds(0, half)], from_y.at[h], y_send, y_recv, h, across).wait_send()
        spread[h][0].wait_send()
        spread[h][1].wait_send()
        last[h].wait_send()


def feed_forward(middle, gain, w_gate, w_up, w_down):
    length, width = middle.shape
    columns = w_gate.shape[1]
    vmem = pl.BlockSpec(memory_space=pltpu.VMEM)
    return pl.pallas_call(
        forward_kernel,
        out_shape=(jax.ShapeDtypeStruct((length, width), f32), jax.ShapeDtypeStruct((length, width), bf16)),
        in_specs=[vmem] * 5,
        out_specs=(vmem, vmem),
        scratch_shapes=[
            pltpu.VMEM((256, columns), bf16),
            pltpu.VMEM((4, 256, width), f32),
            pltpu.VMEM((4, 128, width), f32),
            pltpu.VMEM((2, 128, width), f32),
            pltpu.SemaphoreType.DMA((8,)),
            pltpu.SemaphoreType.DMA((8,)),
            pltpu.SemaphoreType.DMA((4,)),
            pltpu.SemaphoreType.DMA((4,)),
        ],
        compiler_params=pltpu.CompilerParams(collective_id=0, has_side_effects=True, vmem_limit_bytes=58 << 20),
        name="feed_forward",
    )(middle, gain.reshape(1, -1), w_gate, w_up, w_down)


def body(
    links,
    tokens,
    segment_ids,
    cotangent,
    w_query,
    w_key,
    w_value,
    w_out,
    w_gate,
    w_up,
    w_down,
    gain_attn_in,
    gain_attn_out,
    gain_ffn_in,
    gain_ffn_out,
    gain_query,
    gain_key,
):
    length, width = tokens.shape
    head = w_query.shape[1]
    quarter = length // 4
    half_ff = w_gate.shape[1] // 2
    nx = links.nx
    blk = width // links.dp_size
    dp, t = lax.axis_index("dp"), lax.axis_index("tensor")
    z, x = dp // nx, dp % nx
    y, c = t // 2, t % 2
    parity = z % 2
    one = jnp.where(segment_ids[0] < length, 1.0, 0.5).astype(f32)

    def keep_low(a):
        return (a * one).astype(bf16)

    def place(dc, dy):
        return ((c ^ dc) * 2 + (y ^ dy)) * quarter

    def rows(a, dc, dy):
        return lax.dynamic_slice_in_dim(a, place(dc, dy), quarter, 0)

    def to_absolute(pieces):
        stack = jnp.stack([pieces[0][0], pieces[0][1], pieces[1][0], pieces[1][1]])
        mine = c * 2 + y
        return jnp.concatenate([lax.dynamic_index_in_dim(stack, mine ^ b, 0, keepdims=False) for b in range(4)], axis=0)

    out_own = w_out.astype(f32)
    out_y = links.y(out_own)
    out_c = links.core(out_own)
    out_yc = links.core(out_y)
    w_out_all = jnp.concatenate([w_out, keep_low(out_c), keep_low(out_y), keep_low(out_yc)], axis=0)

    wg_h = jnp.where(parity == 0, w_gate[:, :half_ff], w_gate[:, half_ff:])
    wu_h = jnp.where(parity == 0, w_up[:, :half_ff], w_up[:, half_ff:])
    wd_h = jnp.where(parity == 0, w_down[:half_ff], w_down[half_ff:])

    hidden_in = tokens.astype(f32)
    normed_low = low(rms_norm(hidden_in, gain_attn_in))
    query_raw = product(normed_low, w_query)
    keys_raw = product(normed_low, w_key)
    query_low = low(rms_norm(query_raw, gain_query))
    keys_low = low(rms_norm(keys_raw, gain_key))
    values_low = low(product(normed_low, w_value))
    places = jnp.arange(length)
    allowed = (places[:, None] >= places[None, :]) & (segment_ids[:, None] == segment_ids[None, :])

    def scores_of():
        raw = product_t(query_low, keys_low) * score_scale
        return jnp.where(allowed, raw, -1e30)

    scores = scores_of()
    largest = jnp.max(scores, axis=-1, keepdims=True)
    exponent = jnp.exp(scores - largest)
    total = jnp.sum(exponent, axis=-1, keepdims=True)
    log_total = largest + jnp.log(total)
    context_low = low(product(low(exponent / total), values_low))

    context = context_low.astype(f32)
    mine = jnp.concatenate([rows(context, 0, 1), rows(context, 0, 0)], axis=0)
    of_core = links.core(jnp.concatenate([rows(context, 1, 1), rows(context, 1, 0)], axis=0))
    of_y = links.y(jnp.concatenate([rows(context, 0, 0), rows(context, 0, 1)], axis=0))
    of_yc = links.y(jnp.concatenate([of_core[quarter:], of_core[:quarter]], axis=0))
    context_all = jnp.concatenate([low(mine), keep_low(of_core), keep_low(of_y), keep_low(of_yc)], axis=1)
    branch = product(context_all, w_out_all)
    hidden_rows = jnp.concatenate([rows(tokens, 0, 1), rows(tokens, 0, 0)], axis=0).astype(f32)
    middle_own = hidden_rows + rms_norm(branch, gain_attn_out)
    middle_core = links.core(middle_own)

    eighth = length // 8
    tiles = []
    for k in range(4):
        at = slice(k * eighth, (k + 1) * eighth)
        tiles += [middle_own[at], middle_core[at]]
    out_tiles, normed_tiles = feed_forward(jnp.concatenate(tiles, axis=0), gain_ffn_in, w_gate, w_up, w_down)

    def untile(a, k):
        a = a.reshape(2, 2, 2, eighth, a.shape[1])[k]
        return a.transpose(1, 0, 2, 3).reshape(2 * quarter, a.shape[3])

    middles = [
        jnp.concatenate([middle_own[k * quarter : (k + 1) * quarter], middle_core[k * quarter : (k + 1) * quarter]], axis=0)
        for k in range(2)
    ]
    normed_two = [untile(normed_tiles, k) for k in range(2)]
    saved = [(product(normed_two[k], w_gate), product(normed_two[k], w_up)) for k in range(2)]
    normed_own = low(rms_norm(middle_own, gain_ffn_in)).astype(f32)
    other_own = links.z1(normed_own)
    other_core = links.core(other_own)
    normed_other = jnp.concatenate([keep_low(other_own), keep_low(other_core)], axis=0)

    def gather_quarters(parts):
        sums = [part[:quarter] + links.core(part[quarter:]) for part in parts]
        return sums[1] + links.y(sums[0])

    outputs = [untile(out_tiles, k) for k in range(2)]
    grad_out = cotangent.astype(f32)
    d_outputs, layer_pieces, grad_ffn_out = [], [], 0.0
    for k in range(2):
        dy_k = jnp.concatenate([rows(cotangent, 0, 1 - k), rows(cotangent, 1, 1 - k)], axis=0).astype(f32)
        layer_k = low(middles[k] + rms_norm(outputs[k], gain_ffn_out))
        d_k, gain_k = rms_back(outputs[k], gain_ffn_out, dy_k)
        grad_ffn_out = grad_ffn_out + gain_k
        d_outputs.append(low(d_k))
        layer_pieces.append(layer_k)
    layer_out = to_absolute(
        [
            [layer_pieces[1][:quarter], layer_pieces[0][:quarter]],
            [layer_pieces[1][quarter:], layer_pieces[0][quarter:]],
        ]
    )

    d_own_rows = [d[:quarter].astype(f32) for d in d_outputs]
    got_own = [links.z1(d_own_rows[1]), links.z1(d_own_rows[0])]
    got_core = [links.core(g) for g in got_own]
    d_other = jnp.concatenate(
        [keep_low(got_own[1]), keep_low(got_own[0]), keep_low(got_core[1]), keep_low(got_core[0])], axis=0
    )

    back_parts = []
    for k in range(2):
        gate, upward = saved[k]
        d_inner = product_t(d_outputs[k], w_down)
        _, pull = jax.vjp(activate, gate, upward)
        d_gate, d_up = pull(d_inner)
        back_parts.append(product_t(low(d_gate), w_gate) + product_t(low(d_up), w_up))
    d_normed_q = gather_quarters(back_parts)
    middle_q = middle_own[quarter:]
    branch_q = branch[quarter:]
    dy_q = rows(cotangent, 0, 0).astype(f32)
    d_mid, grad_ffn_in = rms_back(middle_q, gain_ffn_in, d_normed_q)
    d_middle = dy_q + d_mid
    d_branch, grad_attn_out = rms_back(branch_q, gain_attn_out, d_middle)
    d_branch_low = low(d_branch)
    d_context = low(product_t(d_branch_low, w_out_all)).astype(f32)
    heads = [d_context[:, i * head : (i + 1) * head] for i in range(4)]
    c_got = links.core(jnp.concatenate([heads[1], heads[3]], axis=1))
    y_got = links.y(jnp.concatenate([heads[2], c_got[:, head:]], axis=1))
    grad_context = keep_low(
        to_absolute([[heads[0], y_got[:, :head]], [c_got[:, :head], y_got[:, head:]]])
    )
    d_branch_own = d_branch_low.astype(f32)
    d_branch_y = links.y(d_branch_own)
    d_branch_c = links.core(d_branch_own)
    d_branch_yc = links.core(d_branch_y)
    d_branch_all = jnp.concatenate(
        [d_branch_low, keep_low(d_branch_y), keep_low(d_branch_c), keep_low(d_branch_yc)], axis=0
    )
    context_rel = jnp.concatenate(
        [rows(context_low, 0, 0), rows(context_low, 0, 1), rows(context_low, 1, 0), rows(context_low, 1, 1)], axis=0
    )
    grad_w_out_t = t_product(d_branch_all, context_rel)

    attn_prob = jnp.exp(scores_of() - log_total)
    prob_low = low(attn_prob)
    grad_prob = product_t(grad_context, values_low)
    grad_values = low(t_product(prob_low, grad_context))
    balance = jnp.sum(grad_prob * attn_prob, axis=-1, keepdims=True)
    grad_scores = low(attn_prob * (grad_prob - balance))
    grad_query_n = product(grad_scores, keys_low) * score_scale
    grad_keys_n = t_product(grad_scores, query_low) * score_scale
    d_query, grad_gain_query = rms_back(query_raw, gain_query, grad_query_n)
    d_keys, grad_gain_key = rms_back(keys_raw, gain_key, grad_keys_n)
    d_query, d_keys = low(d_query), low(d_keys)
    d_qkv = jnp.concatenate([d_query, d_keys, grad_values], axis=1)
    w_qkv = jnp.concatenate([w_query, w_key, w_value], axis=1)
    in_parts = []
    for k in range(2):
        rows_k = jnp.concatenate([rows(d_qkv, 0, 1 - k), rows(d_qkv, 1, 1 - k)], axis=0)
        in_parts.append(product_t(rows_k, w_qkv))
    d_normed_in = gather_quarters(in_parts)
    hidden_q = rows(tokens, 0, 0).astype(f32)
    d_in, grad_attn_in = rms_back(hidden_q, gain_attn_in, d_normed_in)
    input_q = low(d_middle + d_in)
    input_own = input_q.astype(f32)
    input_y = links.y(input_own)
    input_c = links.core(input_own)
    input_yc = links.core(input_y)
    input_grad = keep_low(to_absolute([[input_own, input_y], [input_c, input_yc]]))

    grad_qkv = t_product(normed_low, d_qkv)
    grad_w_query, grad_kv = grad_qkv[:, :head], grad_qkv[:, head:]
    kv_keep = jnp.where(c == 0, grad_kv[:, :head], grad_kv[:, head:])
    kv_send = jnp.where(c == 0, grad_kv[:, head:], grad_kv[:, :head])
    kv = kv_keep + links.core(kv_send)
    kv_half = head // 2
    kv_keep = jnp.where(y == 0, kv[:, :kv_half], kv[:, kv_half:])
    kv_send = jnp.where(y == 0, kv[:, kv_half:], kv[:, :kv_half])
    kv = kv_keep + links.y(kv_send)
    attn_grads = jnp.concatenate([grad_w_query, grad_w_out_t, kv], axis=1)

    normed_all = jnp.concatenate(
        [normed_two[0][:quarter], normed_two[1][:quarter], normed_two[0][quarter:], normed_two[1][quarter:], normed_other],
        axis=0,
    )
    d_all = jnp.concatenate(
        [d_outputs[0][:quarter], d_outputs[1][:quarter], d_outputs[0][quarter:], d_outputs[1][quarter:], d_other], axis=0
    )
    gate, upward = product(normed_all, wg_h), product(normed_all, wu_h)
    inner, pull = jax.vjp(activate, gate, upward)
    inner = low(inner)
    d_inner = product_t(d_all, wd_h)
    d_gate, d_up = pull(d_inner)
    ff_grads = [t_product(d_all, inner), t_product(normed_all, low(d_gate)), t_product(normed_all, low(d_up))]

    zh, zl = z // 2, z % 2

    def sum_x(grads, z_half):
        mine = lax.dynamic_index_in_dim(grads, z_half, 0, keepdims=False)
        acc = lax.dynamic_index_in_dim(mine, x, 1, keepdims=False)
        for step in range(1, nx):
            to = lax.dynamic_index_in_dim(mine, (x + step) % nx, 1, keepdims=False)
            acc = acc + links.x(to, step)
        return acc

    def scatter(grads):
        grads = grads.reshape(2, 2, nx, blk, grads.shape[1])
        far = sum_x(grads, 1 - zh)
        near = sum_x(grads, zh)
        return near + links.z2(far)

    ff_sums = []
    for grads in ff_grads:
        got = scatter(grads)
        own = lax.dynamic_index_in_dim(got, zl, 0, keepdims=False)
        other = links.z1(lax.dynamic_index_in_dim(got, 1 - zl, 0, keepdims=False))
        ff_sums.append(
            jnp.where(
                parity == 0, jnp.concatenate([own, other], axis=1), jnp.concatenate([other, own], axis=1)
            )
        )
    grad_w_down, grad_w_gate, grad_w_up = ff_sums[0].T, ff_sums[1], ff_sums[2]

    got = scatter(attn_grads)
    attn_sum = lax.dynamic_index_in_dim(got, zl, 0, keepdims=False) + links.z1(
        lax.dynamic_index_in_dim(got, 1 - zl, 0, keepdims=False)
    )
    grad_w_query = attn_sum[:, :head]
    grad_w_out = attn_sum[:, head : 2 * head].T
    kv_own = attn_sum[:, 2 * head :]
    kv_y = links.y(kv_own)
    kv_wide = jnp.where(y == 0, jnp.concatenate([kv_own, kv_y], axis=1), jnp.concatenate([kv_y, kv_own], axis=1))
    kv_c = links.core(kv_wide)
    grad_w_key = jnp.where(c == 0, kv_wide, kv_c)
    grad_w_value = jnp.where(c == 0, kv_c, kv_wide)

    small = jnp.concatenate(
        [
            grad_attn_in.reshape(links.dp_size, -1),
            grad_attn_out.reshape(links.dp_size, -1),
            grad_ffn_in.reshape(links.dp_size, -1),
            (grad_ffn_out * 0.25).reshape(links.dp_size, -1),
            grad_gain_query.reshape(links.dp_size, -1),
            grad_gain_key.reshape(links.dp_size, -1),
        ],
        axis=1,
    )
    small = small + links.core(small)
    small = small + links.y(small)
    small = small.reshape(2, 2, nx, 1, small.shape[1])
    acc = lax.dynamic_index_in_dim(small, x, 2, keepdims=False)
    for step in range(1, nx):
        acc = acc + links.x(lax.dynamic_index_in_dim(small, (x + step) % nx, 2, keepdims=False), step)
    acc = lax.dynamic_index_in_dim(acc, zh, 0, keepdims=False) + links.z2(
        lax.dynamic_index_in_dim(acc, 1 - zh, 0, keepdims=False)
    )
    acc = lax.dynamic_index_in_dim(acc, zl, 0, keepdims=False) + links.z1(
        lax.dynamic_index_in_dim(acc, 1 - zl, 0, keepdims=False)
    )
    acc = acc.reshape(-1)
    hb = head // links.dp_size
    return (
        layer_out,
        input_grad,
        grad_w_query,
        grad_w_key,
        grad_w_value,
        grad_w_out,
        grad_w_gate,
        grad_w_up,
        grad_w_down,
        acc[:blk],
        acc[blk : 2 * blk],
        acc[2 * blk : 3 * blk],
        acc[3 * blk : 4 * blk],
        acc[4 * blk : 4 * blk + hb],
        acc[4 * blk + hb :],
    )


def solution(mesh):
    return jax.shard_map(
        functools.partial(body, Links(mesh)),
        mesh=mesh,
        in_specs=(
            P("dp", None),
            P("dp"),
            P("dp", None),
            P(None, "tensor"),
            P(),
            P(),
            P("tensor", None),
            P(None, "tensor"),
            P(None, "tensor"),
            P("tensor", None),
            P(),
            P(),
            P(),
            P(),
            P(),
            P(),
        ),
        out_specs=(
            P("dp", None),
            P("dp", None),
            P("dp", "tensor"),
            P("dp", None),
            P("dp", None),
            P("tensor", "dp"),
            P("dp", "tensor"),
            P("dp", "tensor"),
            P("tensor", "dp"),
            P("dp"),
            P("dp"),
            P("dp"),
            P("dp"),
            P("dp"),
            P("dp"),
        ),
        check_vma=False,
    )
```

```python
import functools

import jax
import jax.numpy as jnp
from jax import lax
from jax.experimental import pallas as pl
from jax.experimental.pallas import tpu as pltpu
from jax.sharding import PartitionSpec as P

epsilon = 1e-06
score_scale = 0.0625
NZ = 4

f32 = jnp.float32
bf16 = jnp.bfloat16


def rms_norm(values, gain):
    inverse = lax.rsqrt(jnp.mean(values * values, axis=-1, keepdims=True) + epsilon)
    return values * inverse * (1.0 + gain)


def rms_back(values, gain, grad):
    inverse = lax.rsqrt(jnp.mean(values * values, axis=-1, keepdims=True) + epsilon)
    hat = values * inverse
    scaled = grad * (1.0 + gain)
    back = inverse * (scaled - hat * jnp.mean(scaled * hat, axis=-1, keepdims=True))
    return back, jnp.sum(grad * hat, axis=0)


def product(left, right):
    return jnp.dot(left, right, preferred_element_type=f32)


def product_t(left, right):
    return lax.dot_general(left, right, (((1,), (1,)), ((), ())), preferred_element_type=f32)


def t_product(left, right):
    return lax.dot_general(left, right, (((0,), (0,)), ((), ())), preferred_element_type=f32)


def activate(gate, upward):
    return jax.nn.gelu(gate, approximate=True) * upward


class Links:
    def __init__(self, mesh):
        self.dp_size = mesh.shape["dp"]
        self.nx = self.dp_size // NZ
        tensor = mesh.shape["tensor"]
        self.perm_core = [(t, t ^ 1) for t in range(tensor)]
        self.perm_y = [(t, t ^ 2) for t in range(tensor)]
        nx = self.nx
        self.perm_z1 = [(z * nx + x, (z ^ 1) * nx + x) for z in range(NZ) for x in range(nx)]
        self.perm_z2 = [(z * nx + x, (z ^ 2) * nx + x) for z in range(NZ) for x in range(nx)]

    def core(self, a):
        return lax.ppermute(a, "tensor", self.perm_core)

    def y(self, a):
        return lax.ppermute(a, "tensor", self.perm_y)

    def z1(self, a):
        return lax.ppermute(a, "dp", self.perm_z1)

    def z2(self, a):
        return lax.ppermute(a, "dp", self.perm_z2)

    def x(self, a, step):
        nx = self.nx
        return lax.ppermute(a, "dp", [(z * nx + x, z * nx + (x + step) % nx) for z in range(NZ) for x in range(nx)])


def low(a):
    return a.astype(bf16)


MESH = pl.DeviceIdType.MESH
ANY = pl.BlockSpec(memory_space=pl.ANY)
VMEM = pl.BlockSpec(memory_space=pltpu.VMEM)
TILE, HALF, QUARTER = 256, 128, 256


def spots(nx):
    dp, t = lax.axis_index("dp"), lax.axis_index("tensor")
    z, x = dp // nx, dp % nx
    near = {
        "c": {"tensor": t ^ 1},
        "y": {"tensor": t ^ 2},
        "z1": {"dp": (z ^ 1) * nx + x},
        "z2": {"dp": (z ^ 2) * nx + x},
        "x": {"dp": z * nx + (x ^ 1)},
    }
    return z, x, t // 2, t % 2, near


def remote(src, dst, sems, index, to):
    return pltpu.make_async_remote_copy(
        src_ref=src, dst_ref=dst, send_sem=sems[0].at[index], recv_sem=sems[1].at[index], device_id=to, device_id_type=MESH
    )


def greet(others):
    barrier = pltpu.get_barrier_semaphore()
    for other in others:
        pl.semaphore_signal(barrier, inc=1, device_id=other, device_id_type=MESH)
    pl.semaphore_wait(barrier, len(others))


def tile_row(c, y, i, dc):
    dy = 1 - i // 2
    return pl.multiple_of(((c ^ dc) * 2 + (y ^ dy)) * QUARTER + (i % 2) * HALF, HALF)


def gelu_parts(u):
    k = 0.7978845608028654
    square = u * u
    th = jnp.tanh(k * u * (1.0 + 0.044715 * square))
    side = 0.5 * (1.0 + th)
    return u * side, side + 0.5 * u * (1.0 - th * th) * (k * (1.0 + 3.0 * 0.044715 * square))


def gelu_tanh(u):
    return 0.5 * u * (1.0 + jnp.tanh(0.7978845608028654 * u * (1.0 + 0.044715 * (u * u))))


def forward_kernel(
    nx,
    middle,
    cotangent,
    gain_in,
    gain_out,
    w_gate,
    w_up,
    w_down,
    normed,
    normed_other,
    d_out,
    d_own,
    layer_out,
    gain_grad,
    out,
    dy,
    inner,
    part,
    from_core,
    from_y,
    z_stage,
    z_land,
    c_land,
    local,
    c_send,
    c_recv,
    y_send,
    y_recv,
    z_send,
    z_recv,
):
    z, x, y, c, near = spots(nx)
    core, across, pair = near["c"], near["y"], near["z1"]
    cs, ys, zs = (c_send, c_recv), (y_send, y_recv), (z_send, z_recv)
    loads = []
    for i in range(4):
        for dc in range(2):
            copy = pltpu.make_async_copy(
                cotangent.at[pl.ds(tile_row(c, y, i, dc), HALF)],
                dy.at[pl.ds(i * TILE + dc * HALF, HALF)],
                local.at[i * 2 + dc],
            )
            copy.start()
            loads.append(copy)
    greet([core, across, pair])
    columns = w_gate.shape[1]
    cut = columns // 2

    def core_copy(i):
        return remote(part.at[i, pl.ds(HALF, HALF)], from_core.at[i], cs, i, core)

    def y_copy(h):
        return remote(part.at[h, pl.ds(0, HALF)], from_y.at[h], ys, h, across)

    def z_copy(i):
        return remote(z_stage.at[i], z_land.at[i], zs, i, pair)

    def z_forward(i):
        return remote(z_land.at[i], c_land.at[i], cs, 8 + i, core)

    def step(i, carry):
        at = pl.ds(pl.multiple_of(i * TILE, TILE), TILE)
        m = middle[at, :]
        inverse = lax.rsqrt(jnp.mean(m * m, axis=-1, keepdims=True) + epsilon)
        n = (m * inverse * (1.0 + gain_in[...])).astype(bf16)
        normed[at, :] = n
        z_stage[i] = n[:HALF].astype(f32)
        z_copy(i).start()
        for lo in (0, cut):
            g = product(n, w_gate[:, lo : lo + cut])
            u = product(n, w_up[:, lo : lo + cut])
            inner[:, lo : lo + cut] = (gelu_tanh(g) * u).astype(bf16)
        part[i] = product(inner[...], w_down[...])
        core_copy(i).start()
        core_copy(i).wait_recv()
        part[i, :HALF] = part[i, :HALF] + from_core[i]

        @pl.when(i < 2)
        def _():
            y_copy(i).start()

        return carry

    lax.fori_loop(0, 4, step, 0)
    for copy in loads:
        copy.wait()
    gain_grad[...] = jnp.zeros_like(gain_grad)
    gain = 1.0 + gain_out[...]

    def finish(i, dc):
        lo = i * TILE + dc * HALF
        o, g = out[lo : lo + HALF, :], dy[lo : lo + HALF, :].astype(f32)
        inverse = lax.rsqrt(jnp.mean(o * o, axis=-1, keepdims=True) + epsilon)
        hat = o * inverse
        scaled = g * gain
        d = (inverse * (scaled - hat * jnp.mean(scaled * hat, axis=-1, keepdims=True))).astype(bf16)
        d_out[lo : lo + HALF, :] = d
        if dc == 0:
            d_own[i] = d.astype(f32)
        gain_grad[...] = gain_grad[...] + jnp.sum((g * hat).reshape(HALF // 8, 8, g.shape[1]), axis=0)
        layer_out[pl.ds(tile_row(c, y, i, dc), HALF), :] = (middle[lo : lo + HALF, :] + hat * gain).astype(bf16)

    def spread_y(h):
        return remote(out.at[pl.ds((2 + h) * TILE, HALF)], out.at[pl.ds(h * TILE, HALF)], ys, 2 + h, across)

    def spread_core(i):
        return remote(out.at[pl.ds(i * TILE, HALF)], out.at[pl.ds(i * TILE + HALF, HALF)], cs, 4 + i, core)

    for h in range(2):
        y_copy(h).wait_recv()
        lo = (2 + h) * TILE
        out[lo : lo + HALF, :] = part[2 + h, :HALF] + from_y[h]
        spread_y(h).start()
        spread_core(2 + h).start()
        finish(2 + h, 0)
        z_copy(h).wait_recv()
        z_forward(h).start()
    for h in range(2):
        spread_core(2 + h).wait_recv()
        finish(2 + h, 1)
    for h in range(2):
        spread_y(h).wait_recv()
        spread_core(h).start()
        finish(h, 0)
        z_copy(2 + h).wait_recv()
        z_forward(2 + h).start()
        spread_core(h).wait_recv()
        finish(h, 1)
    for i in range(4):
        z_forward(i).wait_recv()
        normed_other[i * TILE : i * TILE + HALF, :] = z_land[i].astype(bf16)
        normed_other[i * TILE + HALF : (i + 1) * TILE, :] = c_land[i].astype(bf16)
    for i in range(4):
        core_copy(i).wait_send()
        z_copy(i).wait_send()
        z_forward(i).wait_send()
        spread_core(i).wait_send()
    for h in range(2):
        y_copy(h).wait_send()
        spread_y(h).wait_send()


def dma(*counts):
    return [pltpu.SemaphoreType.DMA((n,)) for n in counts]


def feed_forward(nx, middle, cotangent, gain_in, gain_out, w_gate, w_up, w_down):
    length, width = middle.shape
    columns = w_gate.shape[1]
    rows_low = jax.ShapeDtypeStruct((length, width), bf16)
    return pl.pallas_call(
        functools.partial(forward_kernel, nx),
        out_shape=(
            rows_low,
            rows_low,
            rows_low,
            jax.ShapeDtypeStruct((4, HALF, width), f32),
            rows_low,
            jax.ShapeDtypeStruct((8, width), f32),
        ),
        in_specs=[VMEM, ANY] + [VMEM] * 5,
        out_specs=(VMEM,) * 6,
        scratch_shapes=[
            pltpu.VMEM((length, width), f32),
            pltpu.VMEM((length, width), bf16),
            pltpu.VMEM((TILE, columns), bf16),
            pltpu.VMEM((4, TILE, width), f32),
            pltpu.VMEM((4, HALF, width), f32),
            pltpu.VMEM((2, HALF, width), f32),
            pltpu.VMEM((4, HALF, width), f32),
            pltpu.VMEM((4, HALF, width), f32),
            pltpu.VMEM((4, HALF, width), f32),
        ]
        + dma(8, 12, 12, 4, 4, 4, 4),
        compiler_params=pltpu.CompilerParams(collective_id=0, has_side_effects=True, vmem_limit_bytes=62 << 20),
        name="feed_forward",
    )(middle, cotangent, gain_in.reshape(1, -1), gain_out.reshape(1, -1), w_gate, w_up, w_down)


def back_kernel(
    nx,
    d_out_hbm,
    d_own_hbm,
    normed_hbm,
    other_hbm,
    w_gate_hbm,
    w_up_hbm,
    w_down_hbm,
    w_out_hbm,
    middle_hbm,
    branch_hbm,
    dy_hbm,
    gain_in,
    gain_branch,
    d_other,
    pair_in,
    pair_gates,
    grad_context,
    d_branch_out,
    d_middle_out,
    gain_grads,
    d_out,
    normed,
    other,
    w_gate,
    w_up,
    w_down,
    w_out,
    middle,
    branch,
    dy,
    gates,
    ups,
    inner,
    part,
    from_core,
    from_y,
    z_land,
    c_land,
    heads_c,
    heads_y,
    got_c,
    got_y,
    loads_sem,
    stores_sem,
    c_send,
    c_recv,
    y_send,
    y_recv,
    z_send,
    z_recv,
):
    z, x, y, c, near = spots(nx)
    core, across, pair = near["c"], near["y"], near["z1"]
    cs, ys, zs = (c_send, c_recv), (y_send, y_recv), (z_send, z_recv)
    parity = z % 2
    columns = w_gate.shape[1]
    half = columns // 2
    head = heads_c.shape[2]
    own_row = pl.multiple_of((c * 2 + y) * QUARTER, QUARTER)
    sources = [
        (d_out_hbm, d_out),
        (normed_hbm, normed),
        (w_gate_hbm, w_gate),
        (w_up_hbm, w_up),
        (w_down_hbm, w_down),
        (other_hbm, other),
        (w_out_hbm, w_out),
        (middle_hbm, middle),
        (branch_hbm, branch),
        (dy_hbm.at[pl.ds(own_row, QUARTER)], dy),
    ]
    loads = [pltpu.make_async_copy(src, dst, loads_sem.at[k]) for k, (src, dst) in enumerate(sources)]
    for copy in loads:
        copy.start()
    greet([core, across, pair])

    def core_copy(i):
        return remote(part.at[i, pl.ds(HALF, HALF)], from_core.at[i], cs, i, core)

    def y_copy(h):
        return remote(part.at[h, pl.ds(0, HALF)], from_y.at[h], ys, h, across)

    def z_copy(i):
        return remote(d_own_hbm.at[i], z_land.at[i], zs, i, pair)

    def z_forward(i):
        return remote(z_land.at[i], c_land.at[i], cs, 4 + i, core)

    for i in range(4):
        z_copy(i).start()
    for copy in loads[:5]:
        copy.wait()

    mine = pl.multiple_of(parity * half, HALF)

    def stores(i, base):
        slot = i % 2
        at = pl.ds(pl.multiple_of(base + i * TILE, TILE), TILE)
        pick = pl.ds(mine, half)
        return [
            pltpu.make_async_copy(inner.at[slot, :, pick], pair_in.at[at], stores_sem.at[slot, 0]),
            pltpu.make_async_copy(gates.at[slot, :, pick], pair_gates.at[at, pl.ds(0, half)], stores_sem.at[slot, 1]),
            pltpu.make_async_copy(ups.at[slot, :, pick], pair_gates.at[at, pl.ds(half, half)], stores_sem.at[slot, 2]),
        ]

    def piece(n, d, slot, at):
        g = product(n, w_gate[:, at])
        u = product(n, w_up[:, at])
        di = product_t(d, w_down[at, :])
        act, slope = gelu_parts(g)
        inner[slot, :, at] = (act * u).astype(bf16)
        gates[slot, :, at] = (di * u * slope).astype(bf16)
        ups[slot, :, at] = (di * act).astype(bf16)

    def own_tile(i, carry):
        at = pl.ds(pl.multiple_of(i * TILE, TILE), TILE)
        slot = i % 2

        @pl.when(i >= 2)
        def _():
            for copy in stores(i - 2, 0):
                copy.wait()

        n, d = normed[at, :], d_out[at, :]
        for lo in range(0, columns, TILE):
            piece(n, d, slot, pl.ds(lo, TILE))
        for copy in stores(i, 0):
            copy.start()
        part[i] = product_t(gates[slot], w_gate[...]) + product_t(ups[slot], w_up[...])
        core_copy(i).start()
        core_copy(i).wait_recv()
        part[i, :HALF] = part[i, :HALF] + from_core[i]

        @pl.when(i < 2)
        def _():
            y_copy(i).start()

        return carry

    lax.fori_loop(0, 4, own_tile, 0)
    for copy in loads[5:]:
        copy.wait()

    def other_tile(i, carry):
        slot = i % 2
        z_copy(i).wait_recv()
        z_forward(i).start()

        @pl.when(i < 2)
        def _():
            for copy in stores(i + 2, 0):
                copy.wait()

        @pl.when(i >= 2)
        def _():
            for copy in stores(i - 2, d_out.shape[0]):
                copy.wait()

        z_forward(i).wait_recv()
        lo = pl.multiple_of(i * TILE, TILE)
        d_other[pl.ds(lo, HALF), :] = z_land[i].astype(bf16)
        d_other[pl.ds(lo + HALF, HALF), :] = c_land[i].astype(bf16)
        n, d = other[pl.ds(lo, TILE), :], d_other[pl.ds(lo, TILE), :]
        for off in range(0, half, TILE):
            size = min(TILE, half - off)
            piece(n, d, slot, pl.ds(pl.multiple_of(mine + off, HALF), size))
        for copy in stores(i, d_out.shape[0]):
            copy.start()
        return carry

    lax.fori_loop(0, 2, other_tile, 0)

    gain_grads[...] = jnp.zeros_like(gain_grads)

    def fold(a):
        return jnp.sum(a.reshape(a.shape[0] // 8, 8, a.shape[1]), axis=0)

    for h in range(2):
        y_copy(h).wait_recv()
        at = slice(h * HALF, (h + 1) * HALF)
        grad = part[2 + h, :HALF] + from_y[h]
        m = middle[at, :]
        inverse = lax.rsqrt(jnp.mean(m * m, axis=-1, keepdims=True) + epsilon)
        hat = m * inverse
        scaled = grad * (1.0 + gain_in[...])
        d_middle = dy[at, :].astype(f32) + inverse * (scaled - hat * jnp.mean(scaled * hat, axis=-1, keepdims=True))
        gain_grads[0] = gain_grads[0] + fold(grad * hat)
        d_middle_out[at, :] = d_middle
        b = branch[at, :]
        inverse = lax.rsqrt(jnp.mean(b * b, axis=-1, keepdims=True) + epsilon)
        hat = b * inverse
        scaled = d_middle * (1.0 + gain_branch[...])
        d_low = (inverse * (scaled - hat * jnp.mean(scaled * hat, axis=-1, keepdims=True))).astype(bf16)
        gain_grads[1] = gain_grads[1] + fold(d_middle * hat)
        d_branch_out[at, :] = d_low.astype(f32)
        for k, (ref, slot) in enumerate([(None, 0), (heads_y, 0), (heads_c, 0), (heads_c, 1)]):
            piece_of = product_t(d_low, w_out[k * head : (k + 1) * head, :]).astype(bf16)
            if ref is None:
                grad_context[pl.ds(own_row + h * HALF, HALF), :] = piece_of
            else:
                ref[slot, at, :] = piece_of.astype(f32)
    to_core = remote(heads_c, got_c, cs, 8, core)
    to_core.start()
    to_core.wait_recv()
    heads_y[1] = got_c[1]
    to_y = remote(heads_y, got_y, ys, 2, across)
    to_y.start()
    grad_context[pl.ds(pl.multiple_of(((c ^ 1) * 2 + y) * QUARTER, QUARTER), QUARTER), :] = got_c[0].astype(bf16)

    lax.fori_loop(2, 4, other_tile, 0)
    to_y.wait_recv()
    grad_context[pl.ds(pl.multiple_of((c * 2 + (y ^ 1)) * QUARTER, QUARTER), QUARTER), :] = got_y[0].astype(bf16)
    grad_context[pl.ds(pl.multiple_of(((c ^ 1) * 2 + (y ^ 1)) * QUARTER, QUARTER), QUARTER), :] = got_y[1].astype(bf16)
    for i in (2, 3):
        for copy in stores(i, d_out.shape[0]):
            copy.wait()
    for i in range(4):
        core_copy(i).wait_send()
        z_copy(i).wait_send()
        z_forward(i).wait_send()
    for h in range(2):
        y_copy(h).wait_send()
    to_core.wait_send()
    to_y.wait_send()


def feed_back(nx, d_out, d_own, normed, other, w_gate, w_up, w_down, w_out, middle, branch, dy, gain_in, gain_branch):
    length, width = d_out.shape
    columns = w_gate.shape[1]
    head = w_out.shape[0] // 4
    return pl.pallas_call(
        functools.partial(back_kernel, nx),
        out_shape=(
            jax.ShapeDtypeStruct((length, width), bf16),
            jax.ShapeDtypeStruct((2 * length, columns // 2), bf16),
            jax.ShapeDtypeStruct((2 * length, columns), bf16),
            jax.ShapeDtypeStruct((length, head), bf16),
            jax.ShapeDtypeStruct((QUARTER, width), f32),
            jax.ShapeDtypeStruct((QUARTER, width), f32),
            jax.ShapeDtypeStruct((2, 8, width), f32),
        ),
        in_specs=[ANY] * 11 + [VMEM] * 2,
        out_specs=(VMEM, ANY, ANY) + (VMEM,) * 4,
        scratch_shapes=[
            pltpu.VMEM((length, width), bf16),
            pltpu.VMEM((length, width), bf16),
            pltpu.VMEM((length, width), bf16),
            pltpu.VMEM((width, columns), bf16),
            pltpu.VMEM((width, columns), bf16),
            pltpu.VMEM((columns, width), bf16),
            pltpu.VMEM((4 * head, width), bf16),
            pltpu.VMEM((QUARTER, width), f32),
            pltpu.VMEM((QUARTER, width), f32),
            pltpu.VMEM((QUARTER, width), bf16),
            pltpu.VMEM((2, TILE, columns), bf16),
            pltpu.VMEM((2, TILE, columns), bf16),
            pltpu.VMEM((2, TILE, columns), bf16),
            pltpu.VMEM((4, TILE, width), f32),
            pltpu.VMEM((4, HALF, width), f32),
            pltpu.VMEM((2, HALF, width), f32),
            pltpu.VMEM((4, HALF, width), f32),
            pltpu.VMEM((4, HALF, width), f32),
            pltpu.VMEM((2, QUARTER, head), f32),
            pltpu.VMEM((2, QUARTER, head), f32),
            pltpu.VMEM((2, QUARTER, head), f32),
            pltpu.VMEM((2, QUARTER, head), f32),
            pltpu.SemaphoreType.DMA((10,)),
            pltpu.SemaphoreType.DMA((2, 3)),
        ]
        + dma(9, 9, 3, 3, 4, 4),
        compiler_params=pltpu.CompilerParams(collective_id=1, has_side_effects=True, vmem_limit_bytes=62 << 20),
        name="feed_back",
    )(
        d_out,
        d_own,
        normed,
        other,
        w_gate,
        w_up,
        w_down,
        w_out,
        middle,
        branch,
        dy,
        gain_in.reshape(1, -1),
        gain_branch.reshape(1, -1),
    )


def body(
    links,
    tokens,
    segment_ids,
    cotangent,
    w_query,
    w_key,
    w_value,
    w_out,
    w_gate,
    w_up,
    w_down,
    gain_attn_in,
    gain_attn_out,
    gain_ffn_in,
    gain_ffn_out,
    gain_query,
    gain_key,
):
    length, width = tokens.shape
    head = w_query.shape[1]
    quarter = length // 4
    half_ff = w_gate.shape[1] // 2
    nx = links.nx
    blk = width // links.dp_size
    dp, t = lax.axis_index("dp"), lax.axis_index("tensor")
    z, x = dp // nx, dp % nx
    y, c = t // 2, t % 2
    parity = z % 2
    one = jnp.where(segment_ids[0] < length, 1.0, 0.5).astype(f32)

    def keep_low(a):
        return (a * one).astype(bf16)

    def place(dc, dy):
        return ((c ^ dc) * 2 + (y ^ dy)) * quarter

    def rows(a, dc, dy):
        return lax.dynamic_slice_in_dim(a, place(dc, dy), quarter, 0)

    def to_absolute(pieces):
        stack = jnp.stack([pieces[0][0], pieces[0][1], pieces[1][0], pieces[1][1]])
        mine = c * 2 + y
        return jnp.concatenate([lax.dynamic_index_in_dim(stack, mine ^ b, 0, keepdims=False) for b in range(4)], axis=0)

    out_own = w_out.astype(f32)
    out_y = links.y(out_own)
    out_c = links.core(out_own)
    out_yc = links.core(out_y)
    w_out_all = jnp.concatenate([w_out, keep_low(out_y), keep_low(out_c), keep_low(out_yc)], axis=0)

    columns = w_gate.shape[1]
    padded = -columns % (2 * HALF)
    wg, wu = jnp.pad(w_gate, ((0, 0), (0, padded))), jnp.pad(w_up, ((0, 0), (0, padded)))
    wd = jnp.pad(w_down, ((0, padded), (0, 0)))
    half_ff = (columns + padded) // 2

    hidden_in = tokens.astype(f32)
    normed_low = low(rms_norm(hidden_in, gain_attn_in))
    query_raw = product(normed_low, w_query)
    keys_raw = product(normed_low, w_key)
    query_low = low(rms_norm(query_raw, gain_query))
    keys_low = low(rms_norm(keys_raw, gain_key))
    values_low = low(product(normed_low, w_value))
    places = jnp.arange(length)
    allowed = (places[:, None] >= places[None, :]) & (segment_ids[:, None] == segment_ids[None, :])

    def scores_of():
        raw = product_t(query_low, keys_low) * score_scale
        return jnp.where(allowed, raw, -1e30)

    scores = scores_of()
    largest = jnp.max(scores, axis=-1, keepdims=True)
    exponent = jnp.exp(scores - largest)
    total = jnp.sum(exponent, axis=-1, keepdims=True)
    log_total = largest + jnp.log(total)
    context_low = low(product(low(exponent / total), values_low))

    context = context_low.astype(f32)
    mine = jnp.concatenate([rows(context, 0, 1), rows(context, 0, 0)], axis=0)
    of_core = links.core(jnp.concatenate([rows(context, 1, 1), rows(context, 1, 0)], axis=0))
    of_y = links.y(jnp.concatenate([rows(context, 0, 0), rows(context, 0, 1)], axis=0))
    of_yc = links.y(jnp.concatenate([of_core[quarter:], of_core[:quarter]], axis=0))
    context_all = jnp.concatenate([low(mine), keep_low(of_y), keep_low(of_core), keep_low(of_yc)], axis=1)
    branch = product(context_all, w_out_all)
    hidden_rows = jnp.concatenate([rows(tokens, 0, 1), rows(tokens, 0, 0)], axis=0).astype(f32)
    middle_own = hidden_rows + rms_norm(branch, gain_attn_out)
    middle_core = links.core(middle_own)

    eighth = length // 8
    tiles = []
    for k in range(4):
        at = slice(k * eighth, (k + 1) * eighth)
        tiles += [middle_own[at], middle_core[at]]
    normed_two, normed_other, d_out, d_own, layer_out, ffn_out_rows = feed_forward(
        nx, jnp.concatenate(tiles, axis=0), cotangent, gain_ffn_in, gain_ffn_out, wg, wu, wd
    )
    grad_ffn_out = jnp.sum(ffn_out_rows, axis=0)
    d_other, pair_in, pair_gates, grad_context, d_branch_own, d_middle, gain_rows = feed_back(
        nx,
        d_out,
        d_own,
        normed_two,
        normed_other,
        wg,
        wu,
        wd,
        w_out_all,
        middle_own[quarter:],
        branch[quarter:],
        cotangent,
        gain_ffn_in,
        gain_attn_out,
    )
    gain_rows = jnp.sum(gain_rows, axis=1)
    grad_ffn_in, grad_attn_out = gain_rows[0], gain_rows[1]

    d_branch_low = low(d_branch_own)
    def gather_quarters(parts):
        sums = [part[:quarter] + links.core(part[quarter:]) for part in parts]
        return sums[1] + links.y(sums[0])

    d_branch_y = links.y(d_branch_own)
    d_branch_c = links.core(d_branch_own)
    d_branch_yc = links.core(d_branch_y)
    d_branch_all = jnp.concatenate(
        [d_branch_low, keep_low(d_branch_y), keep_low(d_branch_c), keep_low(d_branch_yc)], axis=0
    )
    context_rel = jnp.concatenate(
        [rows(context_low, 0, 0), rows(context_low, 0, 1), rows(context_low, 1, 0), rows(context_low, 1, 1)], axis=0
    )
    grad_w_out_t = t_product(d_branch_all, context_rel)

    attn_prob = jnp.exp(scores_of() - log_total)
    prob_low = low(attn_prob)
    grad_prob = product_t(grad_context, values_low)
    grad_values = low(t_product(prob_low, grad_context))
    balance = jnp.sum(grad_prob * attn_prob, axis=-1, keepdims=True)
    grad_scores = low(attn_prob * (grad_prob - balance))
    grad_query_n = product(grad_scores, keys_low) * score_scale
    grad_keys_n = t_product(grad_scores, query_low) * score_scale
    d_query, grad_gain_query = rms_back(query_raw, gain_query, grad_query_n)
    d_keys, grad_gain_key = rms_back(keys_raw, gain_key, grad_keys_n)
    d_query, d_keys = low(d_query), low(d_keys)
    d_qkv = jnp.concatenate([d_query, d_keys, grad_values], axis=1)
    w_qkv = jnp.concatenate([w_query, w_key, w_value], axis=1)
    in_parts = []
    for k in range(2):
        rows_k = jnp.concatenate([rows(d_qkv, 0, 1 - k), rows(d_qkv, 1, 1 - k)], axis=0)
        in_parts.append(product_t(rows_k, w_qkv))
    d_normed_in = gather_quarters(in_parts)
    hidden_q = rows(tokens, 0, 0).astype(f32)
    d_in, grad_attn_in = rms_back(hidden_q, gain_attn_in, d_normed_in)
    input_q = low(d_middle + d_in)
    input_own = input_q.astype(f32)
    input_y = links.y(input_own)
    input_c = links.core(input_own)
    input_yc = links.core(input_y)
    input_grad = keep_low(to_absolute([[input_own, input_y], [input_c, input_yc]]))

    grad_qkv = t_product(normed_low, d_qkv)
    grad_w_query, grad_kv = grad_qkv[:, :head], grad_qkv[:, head:]
    kv_keep = jnp.where(c == 0, grad_kv[:, :head], grad_kv[:, head:])
    kv_send = jnp.where(c == 0, grad_kv[:, head:], grad_kv[:, :head])
    kv = kv_keep + links.core(kv_send)
    kv_half = head // 2
    kv_keep = jnp.where(y == 0, kv[:, :kv_half], kv[:, kv_half:])
    kv_send = jnp.where(y == 0, kv[:, kv_half:], kv[:, :kv_half])
    kv = kv_keep + links.y(kv_send)
    attn_grads = jnp.concatenate([grad_w_query, grad_w_out_t, kv], axis=1)

    d_all = jnp.concatenate([d_out, d_other], axis=0)
    normed_all = jnp.concatenate([normed_two, normed_other], axis=0)
    gates = t_product(normed_all, pair_gates)
    ff_grads = [t_product(d_all, pair_in), gates[:, :half_ff], gates[:, half_ff:]]

    zh, zl = z // 2, z % 2

    def sum_x(grads, z_half):
        mine = lax.dynamic_index_in_dim(grads, z_half, 0, keepdims=False)
        acc = lax.dynamic_index_in_dim(mine, x, 1, keepdims=False)
        for step in range(1, nx):
            to = lax.dynamic_index_in_dim(mine, (x + step) % nx, 1, keepdims=False)
            acc = acc + links.x(to, step)
        return acc

    def scatter(grads):
        grads = grads.reshape(2, 2, nx, blk, grads.shape[1])
        far = sum_x(grads, 1 - zh)
        near = sum_x(grads, zh)
        return near + links.z2(far)

    ff_sums = []
    for grads in ff_grads:
        got = scatter(grads)
        own = lax.dynamic_index_in_dim(got, zl, 0, keepdims=False)
        other = links.z1(lax.dynamic_index_in_dim(got, 1 - zl, 0, keepdims=False))
        ff_sums.append(
            jnp.where(
                parity == 0, jnp.concatenate([own, other], axis=1), jnp.concatenate([other, own], axis=1)
            )
        )
    ff_sums = [a[:, :columns] for a in ff_sums]
    grad_w_down, grad_w_gate, grad_w_up = ff_sums[0].T, ff_sums[1], ff_sums[2]

    got = scatter(attn_grads)
    attn_sum = lax.dynamic_index_in_dim(got, zl, 0, keepdims=False) + links.z1(
        lax.dynamic_index_in_dim(got, 1 - zl, 0, keepdims=False)
    )
    grad_w_query = attn_sum[:, :head]
    grad_w_out = attn_sum[:, head : 2 * head].T
    kv_own = attn_sum[:, 2 * head :]
    kv_y = links.y(kv_own)
    kv_wide = jnp.where(y == 0, jnp.concatenate([kv_own, kv_y], axis=1), jnp.concatenate([kv_y, kv_own], axis=1))
    kv_c = links.core(kv_wide)
    grad_w_key = jnp.where(c == 0, kv_wide, kv_c)
    grad_w_value = jnp.where(c == 0, kv_c, kv_wide)

    small = jnp.concatenate(
        [
            grad_attn_in.reshape(links.dp_size, -1),
            grad_attn_out.reshape(links.dp_size, -1),
            grad_ffn_in.reshape(links.dp_size, -1),
            (grad_ffn_out * 0.25).reshape(links.dp_size, -1),
            grad_gain_query.reshape(links.dp_size, -1),
            grad_gain_key.reshape(links.dp_size, -1),
        ],
        axis=1,
    )
    small = small + links.core(small)
    small = small + links.y(small)
    small = small.reshape(2, 2, nx, 1, small.shape[1])
    acc = lax.dynamic_index_in_dim(small, x, 2, keepdims=False)
    for step in range(1, nx):
        acc = acc + links.x(lax.dynamic_index_in_dim(small, (x + step) % nx, 2, keepdims=False), step)
    acc = lax.dynamic_index_in_dim(acc, zh, 0, keepdims=False) + links.z2(
        lax.dynamic_index_in_dim(acc, 1 - zh, 0, keepdims=False)
    )
    acc = lax.dynamic_index_in_dim(acc, zl, 0, keepdims=False) + links.z1(
        lax.dynamic_index_in_dim(acc, 1 - zl, 0, keepdims=False)
    )
    acc = acc.reshape(-1)
    hb = head // links.dp_size
    return (
        layer_out,
        input_grad,
        grad_w_query,
        grad_w_key,
        grad_w_value,
        grad_w_out,
        grad_w_gate,
        grad_w_up,
        grad_w_down,
        acc[:blk],
        acc[blk : 2 * blk],
        acc[2 * blk : 3 * blk],
        acc[3 * blk : 4 * blk],
        acc[4 * blk : 4 * blk + hb],
        acc[4 * blk + hb :],
    )


def body_any(
    links,
    tokens,
    segment_ids,
    cotangent,
    w_query,
    w_key,
    w_value,
    w_out,
    w_gate,
    w_up,
    w_down,
    gain_attn_in,
    gain_attn_out,
    gain_ffn_in,
    gain_ffn_out,
    gain_query,
    gain_key,
):
    length, width = tokens.shape
    head = w_query.shape[1]
    quarter = length // 4
    half_ff = w_gate.shape[1] // 2
    nx = links.nx
    blk = width // links.dp_size
    dp, t = lax.axis_index("dp"), lax.axis_index("tensor")
    z, x = dp // nx, dp % nx
    y, c = t // 2, t % 2
    parity = z % 2
    one = jnp.where(segment_ids[0] < length, 1.0, 0.5).astype(f32)

    def keep_low(a):
        return (a * one).astype(bf16)

    def place(dc, dy):
        return ((c ^ dc) * 2 + (y ^ dy)) * quarter

    def rows(a, dc, dy):
        return lax.dynamic_slice_in_dim(a, place(dc, dy), quarter, 0)

    def to_absolute(pieces):
        stack = jnp.stack([pieces[0][0], pieces[0][1], pieces[1][0], pieces[1][1]])
        mine = c * 2 + y
        return jnp.concatenate([lax.dynamic_index_in_dim(stack, mine ^ b, 0, keepdims=False) for b in range(4)], axis=0)

    out_own = w_out.astype(f32)
    out_y = links.y(out_own)
    out_c = links.core(out_own)
    out_yc = links.core(out_y)
    w_out_all = jnp.concatenate([w_out, keep_low(out_c), keep_low(out_y), keep_low(out_yc)], axis=0)

    wg_h = jnp.where(parity == 0, w_gate[:, :half_ff], w_gate[:, half_ff:])
    wu_h = jnp.where(parity == 0, w_up[:, :half_ff], w_up[:, half_ff:])
    wd_h = jnp.where(parity == 0, w_down[:half_ff], w_down[half_ff:])

    hidden_in = tokens.astype(f32)
    normed_low = low(rms_norm(hidden_in, gain_attn_in))
    query_raw = product(normed_low, w_query)
    keys_raw = product(normed_low, w_key)
    query_low = low(rms_norm(query_raw, gain_query))
    keys_low = low(rms_norm(keys_raw, gain_key))
    values_low = low(product(normed_low, w_value))
    places = jnp.arange(length)
    allowed = (places[:, None] >= places[None, :]) & (segment_ids[:, None] == segment_ids[None, :])

    def scores_of():
        raw = product_t(query_low, keys_low) * score_scale
        return jnp.where(allowed, raw, -1e30)

    scores = scores_of()
    largest = jnp.max(scores, axis=-1, keepdims=True)
    exponent = jnp.exp(scores - largest)
    total = jnp.sum(exponent, axis=-1, keepdims=True)
    log_total = largest + jnp.log(total)
    context_low = low(product(low(exponent / total), values_low))

    context = context_low.astype(f32)
    mine = jnp.concatenate([rows(context, 0, 1), rows(context, 0, 0)], axis=0)
    of_core = links.core(jnp.concatenate([rows(context, 1, 1), rows(context, 1, 0)], axis=0))
    of_y = links.y(jnp.concatenate([rows(context, 0, 0), rows(context, 0, 1)], axis=0))
    of_yc = links.y(jnp.concatenate([of_core[quarter:], of_core[:quarter]], axis=0))
    context_all = jnp.concatenate([low(mine), keep_low(of_core), keep_low(of_y), keep_low(of_yc)], axis=1)
    branch = product(context_all, w_out_all)
    hidden_rows = jnp.concatenate([rows(tokens, 0, 1), rows(tokens, 0, 0)], axis=0).astype(f32)
    middle_own = hidden_rows + rms_norm(branch, gain_attn_out)
    middle_core = links.core(middle_own)

    middles, normed_two, inners, parts = [], [], [], []
    saved = []
    for k in range(2):
        at = slice(k * quarter, (k + 1) * quarter)
        middle = jnp.concatenate([middle_own[at], middle_core[at]], axis=0)
        normed_k = low(rms_norm(middle, gain_ffn_in))
        gate, upward = product(normed_k, w_gate), product(normed_k, w_up)
        inner = low(activate(gate, upward))
        part = product(inner, w_down)
        middles.append(middle)
        normed_two.append(normed_k)
        saved.append((gate, upward))
        parts.append(part)
    normed_own = low(rms_norm(middle_own, gain_ffn_in)).astype(f32)
    other_own = links.z1(normed_own)
    other_core = links.core(other_own)
    normed_other = jnp.concatenate([keep_low(other_own), keep_low(other_core)], axis=0)

    def gather_quarters(parts):
        sums = [part[:quarter] + links.core(part[quarter:]) for part in parts]
        return sums[1] + links.y(sums[0])

    output_q = gather_quarters(parts)
    output_y = links.y(output_q)
    output_c = links.core(output_q)
    output_yc = links.core(output_y)
    outputs = [jnp.concatenate([output_y, output_yc], axis=0), jnp.concatenate([output_q, output_c], axis=0)]
    grad_out = cotangent.astype(f32)
    d_outputs, layer_pieces, grad_ffn_out = [], [], 0.0
    for k in range(2):
        dy_k = jnp.concatenate([rows(cotangent, 0, 1 - k), rows(cotangent, 1, 1 - k)], axis=0).astype(f32)
        layer_k = low(middles[k] + rms_norm(outputs[k], gain_ffn_out))
        d_k, gain_k = rms_back(outputs[k], gain_ffn_out, dy_k)
        grad_ffn_out = grad_ffn_out + gain_k
        d_outputs.append(low(d_k))
        layer_pieces.append(layer_k)
    layer_out = to_absolute(
        [
            [layer_pieces[1][:quarter], layer_pieces[0][:quarter]],
            [layer_pieces[1][quarter:], layer_pieces[0][quarter:]],
        ]
    )

    d_own_rows = [d[:quarter].astype(f32) for d in d_outputs]
    got_own = [links.z1(d_own_rows[1]), links.z1(d_own_rows[0])]
    got_core = [links.core(g) for g in got_own]
    d_other = jnp.concatenate(
        [keep_low(got_own[1]), keep_low(got_own[0]), keep_low(got_core[1]), keep_low(got_core[0])], axis=0
    )

    back_parts = []
    for k in range(2):
        gate, upward = saved[k]
        d_inner = product_t(d_outputs[k], w_down)
        _, pull = jax.vjp(activate, gate, upward)
        d_gate, d_up = pull(d_inner)
        back_parts.append(product_t(low(d_gate), w_gate) + product_t(low(d_up), w_up))
    d_normed_q = gather_quarters(back_parts)
    middle_q = middle_own[quarter:]
    branch_q = branch[quarter:]
    dy_q = rows(cotangent, 0, 0).astype(f32)
    d_mid, grad_ffn_in = rms_back(middle_q, gain_ffn_in, d_normed_q)
    d_middle = dy_q + d_mid
    d_branch, grad_attn_out = rms_back(branch_q, gain_attn_out, d_middle)
    d_branch_low = low(d_branch)
    d_context = low(product_t(d_branch_low, w_out_all)).astype(f32)
    heads = [d_context[:, i * head : (i + 1) * head] for i in range(4)]
    c_got = links.core(jnp.concatenate([heads[1], heads[3]], axis=1))
    y_got = links.y(jnp.concatenate([heads[2], c_got[:, head:]], axis=1))
    grad_context = keep_low(
        to_absolute([[heads[0], y_got[:, :head]], [c_got[:, :head], y_got[:, head:]]])
    )
    d_branch_own = d_branch_low.astype(f32)
    d_branch_y = links.y(d_branch_own)
    d_branch_c = links.core(d_branch_own)
    d_branch_yc = links.core(d_branch_y)
    d_branch_all = jnp.concatenate(
        [d_branch_low, keep_low(d_branch_y), keep_low(d_branch_c), keep_low(d_branch_yc)], axis=0
    )
    context_rel = jnp.concatenate(
        [rows(context_low, 0, 0), rows(context_low, 0, 1), rows(context_low, 1, 0), rows(context_low, 1, 1)], axis=0
    )
    grad_w_out_t = t_product(d_branch_all, context_rel)

    attn_prob = jnp.exp(scores_of() - log_total)
    prob_low = low(attn_prob)
    grad_prob = product_t(grad_context, values_low)
    grad_values = low(t_product(prob_low, grad_context))
    balance = jnp.sum(grad_prob * attn_prob, axis=-1, keepdims=True)
    grad_scores = low(attn_prob * (grad_prob - balance))
    grad_query_n = product(grad_scores, keys_low) * score_scale
    grad_keys_n = t_product(grad_scores, query_low) * score_scale
    d_query, grad_gain_query = rms_back(query_raw, gain_query, grad_query_n)
    d_keys, grad_gain_key = rms_back(keys_raw, gain_key, grad_keys_n)
    d_query, d_keys = low(d_query), low(d_keys)
    d_qkv = jnp.concatenate([d_query, d_keys, grad_values], axis=1)
    w_qkv = jnp.concatenate([w_query, w_key, w_value], axis=1)
    in_parts = []
    for k in range(2):
        rows_k = jnp.concatenate([rows(d_qkv, 0, 1 - k), rows(d_qkv, 1, 1 - k)], axis=0)
        in_parts.append(product_t(rows_k, w_qkv))
    d_normed_in = gather_quarters(in_parts)
    hidden_q = rows(tokens, 0, 0).astype(f32)
    d_in, grad_attn_in = rms_back(hidden_q, gain_attn_in, d_normed_in)
    input_q = low(d_middle + d_in)
    input_own = input_q.astype(f32)
    input_y = links.y(input_own)
    input_c = links.core(input_own)
    input_yc = links.core(input_y)
    input_grad = keep_low(to_absolute([[input_own, input_y], [input_c, input_yc]]))

    grad_qkv = t_product(normed_low, d_qkv)
    grad_w_query, grad_kv = grad_qkv[:, :head], grad_qkv[:, head:]
    kv_keep = jnp.where(c == 0, grad_kv[:, :head], grad_kv[:, head:])
    kv_send = jnp.where(c == 0, grad_kv[:, head:], grad_kv[:, :head])
    kv = kv_keep + links.core(kv_send)
    kv_half = head // 2
    kv_keep = jnp.where(y == 0, kv[:, :kv_half], kv[:, kv_half:])
    kv_send = jnp.where(y == 0, kv[:, kv_half:], kv[:, :kv_half])
    kv = kv_keep + links.y(kv_send)
    attn_grads = jnp.concatenate([grad_w_query, grad_w_out_t, kv], axis=1)

    normed_all = jnp.concatenate(
        [normed_two[0][:quarter], normed_two[1][:quarter], normed_two[0][quarter:], normed_two[1][quarter:], normed_other],
        axis=0,
    )
    d_all = jnp.concatenate(
        [d_outputs[0][:quarter], d_outputs[1][:quarter], d_outputs[0][quarter:], d_outputs[1][quarter:], d_other], axis=0
    )
    gate, upward = product(normed_all, wg_h), product(normed_all, wu_h)
    inner, pull = jax.vjp(activate, gate, upward)
    inner = low(inner)
    d_inner = product_t(d_all, wd_h)
    d_gate, d_up = pull(d_inner)
    ff_grads = [t_product(d_all, inner), t_product(normed_all, low(d_gate)), t_product(normed_all, low(d_up))]

    zh, zl = z // 2, z % 2

    def sum_x(grads, z_half):
        mine = lax.dynamic_index_in_dim(grads, z_half, 0, keepdims=False)
        acc = lax.dynamic_index_in_dim(mine, x, 1, keepdims=False)
        for step in range(1, nx):
            to = lax.dynamic_index_in_dim(mine, (x + step) % nx, 1, keepdims=False)
            acc = acc + links.x(to, step)
        return acc

    def scatter(grads):
        grads = grads.reshape(2, 2, nx, blk, grads.shape[1])
        far = sum_x(grads, 1 - zh)
        near = sum_x(grads, zh)
        return near + links.z2(far)

    ff_sums = []
    for grads in ff_grads:
        got = scatter(grads)
        own = lax.dynamic_index_in_dim(got, zl, 0, keepdims=False)
        other = links.z1(lax.dynamic_index_in_dim(got, 1 - zl, 0, keepdims=False))
        ff_sums.append(
            jnp.where(
                parity == 0, jnp.concatenate([own, other], axis=1), jnp.concatenate([other, own], axis=1)
            )
        )
    grad_w_down, grad_w_gate, grad_w_up = ff_sums[0].T, ff_sums[1], ff_sums[2]

    got = scatter(attn_grads)
    attn_sum = lax.dynamic_index_in_dim(got, zl, 0, keepdims=False) + links.z1(
        lax.dynamic_index_in_dim(got, 1 - zl, 0, keepdims=False)
    )
    grad_w_query = attn_sum[:, :head]
    grad_w_out = attn_sum[:, head : 2 * head].T
    kv_own = attn_sum[:, 2 * head :]
    kv_y = links.y(kv_own)
    kv_wide = jnp.where(y == 0, jnp.concatenate([kv_own, kv_y], axis=1), jnp.concatenate([kv_y, kv_own], axis=1))
    kv_c = links.core(kv_wide)
    grad_w_key = jnp.where(c == 0, kv_wide, kv_c)
    grad_w_value = jnp.where(c == 0, kv_c, kv_wide)

    small = jnp.concatenate(
        [
            grad_attn_in.reshape(links.dp_size, -1),
            grad_attn_out.reshape(links.dp_size, -1),
            grad_ffn_in.reshape(links.dp_size, -1),
            (grad_ffn_out * 0.25).reshape(links.dp_size, -1),
            grad_gain_query.reshape(links.dp_size, -1),
            grad_gain_key.reshape(links.dp_size, -1),
        ],
        axis=1,
    )
    small = small + links.core(small)
    small = small + links.y(small)
    small = small.reshape(2, 2, nx, 1, small.shape[1])
    acc = lax.dynamic_index_in_dim(small, x, 2, keepdims=False)
    for step in range(1, nx):
        acc = acc + links.x(lax.dynamic_index_in_dim(small, (x + step) % nx, 2, keepdims=False), step)
    acc = lax.dynamic_index_in_dim(acc, zh, 0, keepdims=False) + links.z2(
        lax.dynamic_index_in_dim(acc, 1 - zh, 0, keepdims=False)
    )
    acc = lax.dynamic_index_in_dim(acc, zl, 0, keepdims=False) + links.z1(
        lax.dynamic_index_in_dim(acc, 1 - zl, 0, keepdims=False)
    )
    acc = acc.reshape(-1)
    hb = head // links.dp_size
    return (
        layer_out,
        input_grad,
        grad_w_query,
        grad_w_key,
        grad_w_value,
        grad_w_out,
        grad_w_gate,
        grad_w_up,
        grad_w_down,
        acc[:blk],
        acc[blk : 2 * blk],
        acc[2 * blk : 3 * blk],
        acc[3 * blk : 4 * blk],
        acc[4 * blk : 4 * blk + hb],
        acc[4 * blk + hb :],
    )


def solution(mesh):
    links = Links(mesh)
    return jax.shard_map(
        functools.partial(body if links.nx == 2 else body_any, links),
        mesh=mesh,
        in_specs=(
            P("dp", None),
            P("dp"),
            P("dp", None),
            P(None, "tensor"),
            P(),
            P(),
            P("tensor", None),
            P(None, "tensor"),
            P(None, "tensor"),
            P("tensor", None),
            P(),
            P(),
            P(),
            P(),
            P(),
            P(),
        ),
        out_specs=(
            P("dp", None),
            P("dp", None),
            P("dp", "tensor"),
            P("dp", None),
            P("dp", None),
            P("tensor", "dp"),
            P("dp", "tensor"),
            P("dp", "tensor"),
            P("tensor", "dp"),
            P("dp"),
            P("dp"),
            P("dp"),
            P("dp"),
            P("dp"),
            P("dp"),
        ),
        check_vma=False,
    )
```

```python
import functools

import jax
import jax.numpy as jnp
from jax import lax
from jax.experimental import pallas as pl
from jax.experimental.pallas import tpu as pltpu
from jax.sharding import PartitionSpec as P

epsilon = 1e-06
score_scale = 0.0625
NZ = 4

f32 = jnp.float32
bf16 = jnp.bfloat16


def rms_norm(values, gain):
    inverse = lax.rsqrt(jnp.mean(values * values, axis=-1, keepdims=True) + epsilon)
    return values * inverse * (1.0 + gain)


def rms_back(values, gain, grad):
    inverse = lax.rsqrt(jnp.mean(values * values, axis=-1, keepdims=True) + epsilon)
    hat = values * inverse
    scaled = grad * (1.0 + gain)
    back = inverse * (scaled - hat * jnp.mean(scaled * hat, axis=-1, keepdims=True))
    return back, jnp.sum(grad * hat, axis=0)


def product(left, right):
    return jnp.dot(left, right, preferred_element_type=f32)


def product_t(left, right):
    return lax.dot_general(left, right, (((1,), (1,)), ((), ())), preferred_element_type=f32)


def t_product(left, right):
    return lax.dot_general(left, right, (((0,), (0,)), ((), ())), preferred_element_type=f32)


def activate(gate, upward):
    return jax.nn.gelu(gate, approximate=True) * upward


class Links:
    def __init__(self, mesh):
        self.dp_size = mesh.shape["dp"]
        self.nx = self.dp_size // NZ
        tensor = mesh.shape["tensor"]
        self.perm_core = [(t, t ^ 1) for t in range(tensor)]
        self.perm_y = [(t, t ^ 2) for t in range(tensor)]
        nx = self.nx
        self.perm_z1 = [(z * nx + x, (z ^ 1) * nx + x) for z in range(NZ) for x in range(nx)]
        self.perm_z2 = [(z * nx + x, (z ^ 2) * nx + x) for z in range(NZ) for x in range(nx)]

    def core(self, a):
        return lax.ppermute(a, "tensor", self.perm_core)

    def y(self, a):
        return lax.ppermute(a, "tensor", self.perm_y)

    def z1(self, a):
        return lax.ppermute(a, "dp", self.perm_z1)

    def z2(self, a):
        return lax.ppermute(a, "dp", self.perm_z2)

    def x(self, a, step):
        nx = self.nx
        return lax.ppermute(a, "dp", [(z * nx + x, z * nx + (x + step) % nx) for z in range(NZ) for x in range(nx)])


def low(a):
    return a.astype(bf16)


MESH = pl.DeviceIdType.MESH
ANY = pl.BlockSpec(memory_space=pl.ANY)
VMEM = pl.BlockSpec(memory_space=pltpu.VMEM)
TILE, HALF, QUARTER = 256, 128, 256


def spots(nx):
    dp, t = lax.axis_index("dp"), lax.axis_index("tensor")
    z, x = dp // nx, dp % nx
    near = {
        "c": {"tensor": t ^ 1},
        "y": {"tensor": t ^ 2},
        "z1": {"dp": (z ^ 1) * nx + x},
        "z2": {"dp": (z ^ 2) * nx + x},
        "x": {"dp": z * nx + (x ^ 1)},
    }
    return z, x, t // 2, t % 2, near


def remote(src, dst, sems, index, to):
    return pltpu.make_async_remote_copy(
        src_ref=src, dst_ref=dst, send_sem=sems[0].at[index], recv_sem=sems[1].at[index], device_id=to, device_id_type=MESH
    )


def greet(others):
    barrier = pltpu.get_barrier_semaphore()
    for other in others:
        pl.semaphore_signal(barrier, inc=1, device_id=other, device_id_type=MESH)
    pl.semaphore_wait(barrier, len(others))


def tile_row(c, y, i, dc):
    dy = 1 - i // 2
    return pl.multiple_of(((c ^ dc) * 2 + (y ^ dy)) * QUARTER + (i % 2) * HALF, HALF)


def gelu_parts(u):
    k = 0.7978845608028654
    square = u * u
    th = jnp.tanh(k * u * (1.0 + 0.044715 * square))
    side = 0.5 * (1.0 + th)
    return u * side, side + 0.5 * u * (1.0 - th * th) * (k * (1.0 + 3.0 * 0.044715 * square))


def gelu_tanh(u):
    return 0.5 * u * (1.0 + jnp.tanh(0.7978845608028654 * u * (1.0 + 0.044715 * (u * u))))


def forward_kernel(
    nx,
    middle,
    cotangent,
    gain_in,
    gain_out,
    w_gate,
    w_up,
    w_down,
    normed,
    normed_other,
    d_out,
    d_own,
    layer_out,
    gain_grad,
    out,
    dy,
    inner,
    part,
    from_core,
    from_y,
    z_stage,
    z_land,
    c_land,
    local,
    c_send,
    c_recv,
    y_send,
    y_recv,
    z_send,
    z_recv,
):
    z, x, y, c, near = spots(nx)
    core, across, pair = near["c"], near["y"], near["z1"]
    cs, ys, zs = (c_send, c_recv), (y_send, y_recv), (z_send, z_recv)
    loads = []
    for i in range(4):
        for dc in range(2):
            copy = pltpu.make_async_copy(
                cotangent.at[pl.ds(tile_row(c, y, i, dc), HALF)],
                dy.at[pl.ds(i * TILE + dc * HALF, HALF)],
                local.at[i * 2 + dc],
            )
            copy.start()
            loads.append(copy)
    greet([core, across, pair])
    columns = w_gate.shape[1]
    cut = columns // 2

    def core_copy(i):
        return remote(part.at[i, pl.ds(HALF, HALF)], from_core.at[i], cs, i, core)

    def y_copy(h):
        return remote(part.at[h, pl.ds(0, HALF)], from_y.at[h], ys, h, across)

    def z_copy(i):
        return remote(z_stage.at[i], z_land.at[i], zs, i, pair)

    def z_forward(i):
        return remote(z_land.at[i], c_land.at[i], cs, 8 + i, core)

    def step(i, carry):
        at = pl.ds(pl.multiple_of(i * TILE, TILE), TILE)
        m = middle[at, :]
        inverse = lax.rsqrt(jnp.mean(m * m, axis=-1, keepdims=True) + epsilon)
        n = (m * inverse * (1.0 + gain_in[...])).astype(bf16)
        normed[at, :] = n
        z_stage[i] = n[:HALF].astype(f32)
        z_copy(i).start()
        for lo in (0, cut):
            g = product(n, w_gate[:, lo : lo + cut])
            u = product(n, w_up[:, lo : lo + cut])
            inner[:, lo : lo + cut] = (gelu_tanh(g) * u).astype(bf16)
        part[i] = product(inner[...], w_down[...])
        core_copy(i).start()
        core_copy(i).wait_recv()
        part[i, :HALF] = part[i, :HALF] + from_core[i]

        @pl.when(i < 2)
        def _():
            y_copy(i).start()

        return carry

    lax.fori_loop(0, 4, step, 0)
    for copy in loads:
        copy.wait()
    gain_grad[...] = jnp.zeros_like(gain_grad)
    gain = 1.0 + gain_out[...]

    def finish(i, dc):
        lo = i * TILE + dc * HALF
        o, g = out[lo : lo + HALF, :], dy[lo : lo + HALF, :].astype(f32)
        inverse = lax.rsqrt(jnp.mean(o * o, axis=-1, keepdims=True) + epsilon)
        hat = o * inverse
        scaled = g * gain
        d = (inverse * (scaled - hat * jnp.mean(scaled * hat, axis=-1, keepdims=True))).astype(bf16)
        d_out[lo : lo + HALF, :] = d
        if dc == 0:
            d_own[i] = d.astype(f32)
        gain_grad[...] = gain_grad[...] + jnp.sum((g * hat).reshape(HALF // 8, 8, g.shape[1]), axis=0)
        layer_out[pl.ds(tile_row(c, y, i, dc), HALF), :] = (middle[lo : lo + HALF, :] + hat * gain).astype(bf16)

    def spread_y(h):
        return remote(out.at[pl.ds((2 + h) * TILE, HALF)], out.at[pl.ds(h * TILE, HALF)], ys, 2 + h, across)

    def spread_core(i):
        return remote(out.at[pl.ds(i * TILE, HALF)], out.at[pl.ds(i * TILE + HALF, HALF)], cs, 4 + i, core)

    for h in range(2):
        y_copy(h).wait_recv()
        lo = (2 + h) * TILE
        out[lo : lo + HALF, :] = part[2 + h, :HALF] + from_y[h]
        spread_y(h).start()
        spread_core(2 + h).start()
        finish(2 + h, 0)
        z_copy(h).wait_recv()
        z_forward(h).start()
    for h in range(2):
        spread_core(2 + h).wait_recv()
        finish(2 + h, 1)
    for h in range(2):
        spread_y(h).wait_recv()
        spread_core(h).start()
        finish(h, 0)
        z_copy(2 + h).wait_recv()
        z_forward(2 + h).start()
        spread_core(h).wait_recv()
        finish(h, 1)
    for i in range(4):
        z_forward(i).wait_recv()
        normed_other[i * TILE : i * TILE + HALF, :] = z_land[i].astype(bf16)
        normed_other[i * TILE + HALF : (i + 1) * TILE, :] = c_land[i].astype(bf16)
    for i in range(4):
        core_copy(i).wait_send()
        z_copy(i).wait_send()
        z_forward(i).wait_send()
        spread_core(i).wait_send()
    for h in range(2):
        y_copy(h).wait_send()
        spread_y(h).wait_send()


def dma(*counts):
    return [pltpu.SemaphoreType.DMA((n,)) for n in counts]


def feed_forward(nx, middle, cotangent, gain_in, gain_out, w_gate, w_up, w_down):
    length, width = middle.shape
    columns = w_gate.shape[1]
    rows_low = jax.ShapeDtypeStruct((length, width), bf16)
    return pl.pallas_call(
        functools.partial(forward_kernel, nx),
        out_shape=(
            rows_low,
            rows_low,
            rows_low,
            jax.ShapeDtypeStruct((4, HALF, width), f32),
            rows_low,
            jax.ShapeDtypeStruct((8, width), f32),
        ),
        in_specs=[VMEM, ANY] + [VMEM] * 5,
        out_specs=(VMEM,) * 6,
        scratch_shapes=[
            pltpu.VMEM((length, width), f32),
            pltpu.VMEM((length, width), bf16),
            pltpu.VMEM((TILE, columns), bf16),
            pltpu.VMEM((4, TILE, width), f32),
            pltpu.VMEM((4, HALF, width), f32),
            pltpu.VMEM((2, HALF, width), f32),
            pltpu.VMEM((4, HALF, width), f32),
            pltpu.VMEM((4, HALF, width), f32),
            pltpu.VMEM((4, HALF, width), f32),
        ]
        + dma(8, 12, 12, 4, 4, 4, 4),
        compiler_params=pltpu.CompilerParams(collective_id=0, has_side_effects=True, vmem_limit_bytes=62 << 20),
        name="feed_forward",
    )(middle, cotangent, gain_in.reshape(1, -1), gain_out.reshape(1, -1), w_gate, w_up, w_down)


def back_kernel(
    nx,
    d_out_hbm,
    d_own_hbm,
    normed_hbm,
    other_hbm,
    w_gate_hbm,
    w_up_hbm,
    w_down_hbm,
    w_out_hbm,
    middle_hbm,
    branch_hbm,
    dy_hbm,
    gain_in,
    gain_branch,
    d_other,
    pair_in,
    pair_gates,
    grad_context,
    d_branch_out,
    d_middle_out,
    gain_grads,
    d_out,
    normed,
    other,
    w_gate,
    w_up,
    w_down,
    w_out,
    middle,
    branch,
    dy,
    gates,
    ups,
    inner,
    part,
    from_core,
    from_y,
    z_land,
    c_land,
    heads_c,
    heads_y,
    got_c,
    got_y,
    loads_sem,
    stores_sem,
    c_send,
    c_recv,
    y_send,
    y_recv,
    z_send,
    z_recv,
):
    z, x, y, c, near = spots(nx)
    core, across, pair = near["c"], near["y"], near["z1"]
    cs, ys, zs = (c_send, c_recv), (y_send, y_recv), (z_send, z_recv)
    parity = z % 2
    columns = w_gate.shape[1]
    half = columns // 2
    head = heads_c.shape[2]
    own_row = pl.multiple_of((c * 2 + y) * QUARTER, QUARTER)
    sources = [
        (d_out_hbm, d_out),
        (normed_hbm, normed),
        (w_gate_hbm, w_gate),
        (w_up_hbm, w_up),
        (w_down_hbm, w_down),
        (other_hbm, other),
        (w_out_hbm, w_out),
        (middle_hbm, middle),
        (branch_hbm, branch),
        (dy_hbm.at[pl.ds(own_row, QUARTER)], dy),
    ]
    loads = [pltpu.make_async_copy(src, dst, loads_sem.at[k]) for k, (src, dst) in enumerate(sources)]
    for copy in loads:
        copy.start()
    greet([core, across, pair])

    def core_copy(i):
        return remote(part.at[i, pl.ds(HALF, HALF)], from_core.at[i], cs, i, core)

    def y_copy(h):
        return remote(part.at[h, pl.ds(0, HALF)], from_y.at[h], ys, h, across)

    def z_copy(i):
        return remote(d_own_hbm.at[i], z_land.at[i], zs, i, pair)

    def z_forward(i):
        return remote(z_land.at[i], c_land.at[i], cs, 4 + i, core)

    for i in range(4):
        z_copy(i).start()
    for copy in loads[:5]:
        copy.wait()

    mine = pl.multiple_of(parity * half, HALF)

    def stores(i, base):
        slot = i % 2
        at = pl.ds(pl.multiple_of(base + i * TILE, TILE), TILE)
        pick = pl.ds(mine, half)
        return [
            pltpu.make_async_copy(inner.at[slot, :, pick], pair_in.at[at], stores_sem.at[slot, 0]),
            pltpu.make_async_copy(gates.at[slot, :, pick], pair_gates.at[at, pl.ds(0, half)], stores_sem.at[slot, 1]),
            pltpu.make_async_copy(ups.at[slot, :, pick], pair_gates.at[at, pl.ds(half, half)], stores_sem.at[slot, 2]),
        ]

    def piece(n, d, slot, at):
        g = product(n, w_gate[:, at])
        u = product(n, w_up[:, at])
        di = product_t(d, w_down[at, :])
        act, slope = gelu_parts(g)
        inner[slot, :, at] = (act * u).astype(bf16)
        gates[slot, :, at] = (di * u * slope).astype(bf16)
        ups[slot, :, at] = (di * act).astype(bf16)

    def own_tile(i, carry):
        at = pl.ds(pl.multiple_of(i * TILE, TILE), TILE)
        slot = i % 2

        @pl.when(i >= 2)
        def _():
            for copy in stores(i - 2, 0):
                copy.wait()

        n, d = normed[at, :], d_out[at, :]
        for lo in range(0, columns, TILE):
            piece(n, d, slot, pl.ds(lo, TILE))
        for copy in stores(i, 0):
            copy.start()
        part[i] = product_t(gates[slot], w_gate[...]) + product_t(ups[slot], w_up[...])
        core_copy(i).start()
        core_copy(i).wait_recv()
        part[i, :HALF] = part[i, :HALF] + from_core[i]

        @pl.when(i < 2)
        def _():
            y_copy(i).start()

        return carry

    lax.fori_loop(0, 4, own_tile, 0)
    for copy in loads[5:]:
        copy.wait()

    def other_tile(i, carry):
        slot = i % 2
        z_copy(i).wait_recv()
        z_forward(i).start()

        @pl.when(i < 2)
        def _():
            for copy in stores(i + 2, 0):
                copy.wait()

        @pl.when(i >= 2)
        def _():
            for copy in stores(i - 2, d_out.shape[0]):
                copy.wait()

        z_forward(i).wait_recv()
        lo = pl.multiple_of(i * TILE, TILE)
        d_other[pl.ds(lo, HALF), :] = z_land[i].astype(bf16)
        d_other[pl.ds(lo + HALF, HALF), :] = c_land[i].astype(bf16)
        n, d = other[pl.ds(lo, TILE), :], d_other[pl.ds(lo, TILE), :]
        for off in range(0, half, TILE):
            size = min(TILE, half - off)
            piece(n, d, slot, pl.ds(pl.multiple_of(mine + off, HALF), size))
        for copy in stores(i, d_out.shape[0]):
            copy.start()
        return carry

    lax.fori_loop(0, 2, other_tile, 0)

    gain_grads[...] = jnp.zeros_like(gain_grads)

    def fold(a):
        return jnp.sum(a.reshape(a.shape[0] // 8, 8, a.shape[1]), axis=0)

    for h in range(2):
        y_copy(h).wait_recv()
        at = slice(h * HALF, (h + 1) * HALF)
        grad = part[2 + h, :HALF] + from_y[h]
        m = middle[at, :]
        inverse = lax.rsqrt(jnp.mean(m * m, axis=-1, keepdims=True) + epsilon)
        hat = m * inverse
        scaled = grad * (1.0 + gain_in[...])
        d_middle = dy[at, :].astype(f32) + inverse * (scaled - hat * jnp.mean(scaled * hat, axis=-1, keepdims=True))
        gain_grads[0] = gain_grads[0] + fold(grad * hat)
        d_middle_out[at, :] = d_middle
        b = branch[at, :]
        inverse = lax.rsqrt(jnp.mean(b * b, axis=-1, keepdims=True) + epsilon)
        hat = b * inverse
        scaled = d_middle * (1.0 + gain_branch[...])
        d_low = (inverse * (scaled - hat * jnp.mean(scaled * hat, axis=-1, keepdims=True))).astype(bf16)
        gain_grads[1] = gain_grads[1] + fold(d_middle * hat)
        d_branch_out[at, :] = d_low.astype(f32)
        for k, (ref, slot) in enumerate([(None, 0), (heads_y, 0), (heads_c, 0), (heads_c, 1)]):
            piece_of = product_t(d_low, w_out[k * head : (k + 1) * head, :]).astype(bf16)
            if ref is None:
                grad_context[pl.ds(own_row + h * HALF, HALF), :] = piece_of
            else:
                ref[slot, at, :] = piece_of.astype(f32)
    to_core = remote(heads_c, got_c, cs, 8, core)
    to_core.start()
    to_core.wait_recv()
    heads_y[1] = got_c[1]
    to_y = remote(heads_y, got_y, ys, 2, across)
    to_y.start()
    grad_context[pl.ds(pl.multiple_of(((c ^ 1) * 2 + y) * QUARTER, QUARTER), QUARTER), :] = got_c[0].astype(bf16)

    lax.fori_loop(2, 4, other_tile, 0)
    to_y.wait_recv()
    grad_context[pl.ds(pl.multiple_of((c * 2 + (y ^ 1)) * QUARTER, QUARTER), QUARTER), :] = got_y[0].astype(bf16)
    grad_context[pl.ds(pl.multiple_of(((c ^ 1) * 2 + (y ^ 1)) * QUARTER, QUARTER), QUARTER), :] = got_y[1].astype(bf16)
    for i in (2, 3):
        for copy in stores(i, d_out.shape[0]):
            copy.wait()
    for i in range(4):
        core_copy(i).wait_send()
        z_copy(i).wait_send()
        z_forward(i).wait_send()
    for h in range(2):
        y_copy(h).wait_send()
    to_core.wait_send()
    to_y.wait_send()


def feed_back(nx, d_out, d_own, normed, other, w_gate, w_up, w_down, w_out, middle, branch, dy, gain_in, gain_branch):
    length, width = d_out.shape
    columns = w_gate.shape[1]
    head = w_out.shape[0] // 4
    return pl.pallas_call(
        functools.partial(back_kernel, nx),
        out_shape=(
            jax.ShapeDtypeStruct((length, width), bf16),
            jax.ShapeDtypeStruct((2 * length, columns // 2), bf16),
            jax.ShapeDtypeStruct((2 * length, columns), bf16),
            jax.ShapeDtypeStruct((length, head), bf16),
            jax.ShapeDtypeStruct((QUARTER, width), f32),
            jax.ShapeDtypeStruct((QUARTER, width), f32),
            jax.ShapeDtypeStruct((2, 8, width), f32),
        ),
        in_specs=[ANY] * 11 + [VMEM] * 2,
        out_specs=(VMEM, ANY, ANY) + (VMEM,) * 4,
        scratch_shapes=[
            pltpu.VMEM((length, width), bf16),
            pltpu.VMEM((length, width), bf16),
            pltpu.VMEM((length, width), bf16),
            pltpu.VMEM((width, columns), bf16),
            pltpu.VMEM((width, columns), bf16),
            pltpu.VMEM((columns, width), bf16),
            pltpu.VMEM((4 * head, width), bf16),
            pltpu.VMEM((QUARTER, width), f32),
            pltpu.VMEM((QUARTER, width), f32),
            pltpu.VMEM((QUARTER, width), bf16),
            pltpu.VMEM((2, TILE, columns), bf16),
            pltpu.VMEM((2, TILE, columns), bf16),
            pltpu.VMEM((2, TILE, columns), bf16),
            pltpu.VMEM((4, TILE, width), f32),
            pltpu.VMEM((4, HALF, width), f32),
            pltpu.VMEM((2, HALF, width), f32),
            pltpu.VMEM((4, HALF, width), f32),
            pltpu.VMEM((4, HALF, width), f32),
            pltpu.VMEM((2, QUARTER, head), f32),
            pltpu.VMEM((2, QUARTER, head), f32),
            pltpu.VMEM((2, QUARTER, head), f32),
            pltpu.VMEM((2, QUARTER, head), f32),
            pltpu.SemaphoreType.DMA((10,)),
            pltpu.SemaphoreType.DMA((2, 3)),
        ]
        + dma(9, 9, 3, 3, 4, 4),
        compiler_params=pltpu.CompilerParams(collective_id=1, has_side_effects=True, vmem_limit_bytes=62 << 20),
        name="feed_back",
    )(
        d_out,
        d_own,
        normed,
        other,
        w_gate,
        w_up,
        w_down,
        w_out,
        middle,
        branch,
        dy,
        gain_in.reshape(1, -1),
        gain_branch.reshape(1, -1),
    )


def reduce_kernel(
    nx,
    d_out_hbm,
    d_other_hbm,
    normed_hbm,
    other_hbm,
    pair_in_hbm,
    pair_gates_hbm,
    d_branch_hbm,
    d_middle_hbm,
    tokens_hbm,
    normed_in_hbm,
    query_hbm,
    keys_hbm,
    values_hbm,
    query_raw_hbm,
    keys_raw_hbm,
    context_hbm,
    grad_context_hbm,
    w_qkv_hbm,
    log_total,
    segment_col,
    segment_row,
    gain_in,
    gain_query,
    gain_key,
    gains_so_far,
    ff_out,
    attn_out,
    kv_out,
    input_grad,
    gains,
    dw,
    x_land,
    z2_land,
    z1_land,
    from_core,
    from_y,
    branch_land,
    input_own,
    input_land,
    d_qkv,
    attn,
    attn_z1,
    attn_x,
    attn_z2,
    kv_core,
    kv_across,
    kv_own,
    kv_y,
    kv_wide,
    kv_wide_core,
    gains_land,
    loads,
    c_send,
    c_recv,
    y_send,
    y_recv,
    x_send,
    x_recv,
    z2_send,
    z2_recv,
    z1_send,
    z1_recv,
):
    z, x, y, c, near = spots(nx)
    zh, zl = z // 2, z % 2
    cs, ys, xs = (c_send, c_recv), (y_send, y_recv), (x_send, x_recv)
    z2s, z1s = (z2_send, z2_recv), (z1_send, z1_recv)
    length, width = d_out_hbm.shape
    half = pair_in_hbm.shape[1]
    head = query_hbm.shape[1]
    blk = x_land.shape[1]
    own_row = pl.multiple_of((c * 2 + y) * QUARTER, QUARTER)

    def block(a, b):
        return pl.ds(pl.multiple_of(b * blk, 8), blk)

    def quarter_rows(dc, dy):
        return pl.ds(pl.multiple_of(((c ^ dc) * 2 + (y ^ dy)) * QUARTER, QUARTER), QUARTER)

    greet([near[k] for k in ("c", "y", "x", "z2", "z1")])

    branch_y = remote(d_branch_hbm, branch_land.at[0], ys, 0, near["y"])
    branch_c = remote(d_branch_hbm, branch_land.at[1], cs, 0, near["c"])
    branch_fwd = remote(branch_land.at[0], branch_land.at[2], cs, 1, near["c"])
    branch_y.start()
    branch_c.start()

    def owner(j):
        return 2 * jnp.where(j < 2, 1 - zh, zh) + j % 2

    def x_copy(m, j):
        return remote(dw.at[m, block(dw, owner(j) * 2 + (1 - x))], x_land.at[m * 4 + j], xs, m * 4 + j, near["x"])

    def z2_copy(m, k):
        return remote(dw.at[m, block(dw, owner(k) * 2 + x)], z2_land.at[m * 2 + k], z2s, m * 2 + k, near["z2"])

    def z1_copy(m):
        return remote(dw.at[m, block(dw, (2 * zh + 1 - zl) * 2 + x)], z1_land.at[m], z1s, m, near["z1"])

    def far(m):
        for k in range(2):
            x_copy(m, k).wait_recv()
            rows = block(dw, owner(k) * 2 + x)
            dw[m, rows, :] = dw[m, rows, :] + x_land[m * 4 + k]
            z2_copy(m, k).start()

    def close(m):
        for k in range(2):
            x_copy(m, 2 + k).wait_recv()
            z2_copy(m, k).wait_recv()
            rows = block(dw, owner(2 + k) * 2 + x)
            dw[m, rows, :] = dw[m, rows, :] + x_land[m * 4 + 2 + k] + z2_land[m * 2 + k]
        z1_copy(m).start()
        ff_out[m, zl] = dw[m, block(dw, (2 * zh + zl) * 2 + x), :]

    def copies(pairs):
        started = [pltpu.make_async_copy(src, dst, loads.at[k]) for k, (src, dst) in enumerate(pairs)]
        for copy in started:
            copy.start()
        return started

    def weights(left, right):
        step = 3 * HALF

        def form(m, lo):
            def one(r, carry):
                cols = pl.ds(pl.multiple_of(r * step, HALF), step)
                dw[m, cols, :] = t_product(left[:, cols], right[:, lo : lo + half])
                return carry

            lax.fori_loop(0, width // step, one, 0)
            for k in range(2):
                x_copy(m, k).start()

        for copy in copies(
            [
                (d_out_hbm, left.at[pl.ds(0, length)]),
                (d_other_hbm, left.at[pl.ds(length, length)]),
                (pair_in_hbm, right.at[:, pl.ds(0, half)]),
            ]
        ):
            copy.wait()
        form(0, 0)
        for copy in copies(
            [
                (normed_hbm, left.at[pl.ds(0, length)]),
                (other_hbm, left.at[pl.ds(length, length)]),
                (pair_gates_hbm, right),
            ]
        ):
            copy.wait()
        form(1, 0)
        form(2, half)
        for m in range(2):
            for k in range(2):
                x_copy(m, 2 + k).start()

    pl.run_scoped(weights, pltpu.VMEM((2 * length, width), bf16), pltpu.VMEM((2 * length, 2 * half), bf16))

    gains[...] = gains_so_far[...]

    def back_norm(raw, gain, grad):
        inverse = lax.rsqrt(jnp.mean(raw * raw, axis=-1, keepdims=True) + epsilon)
        hat = raw * inverse
        scaled = grad * (1.0 + gain)
        return inverse * (scaled - hat * jnp.mean(scaled * hat, axis=-1, keepdims=True)), grad * hat

    def attention(query, keys, values, query_raw, keys_raw, grad_context, d_keys, d_values):
        for copy in copies(
            [
                (query_hbm, query),
                (keys_hbm, keys),
                (values_hbm, values),
                (query_raw_hbm, query_raw),
                (keys_raw_hbm, keys_raw),
                (grad_context_hbm, grad_context),
            ]
        ):
            copy.wait()
        d_keys[...] = jnp.zeros_like(d_keys)
        d_values[...] = jnp.zeros_like(d_values)
        for i in range(length // TILE):
            at, seen = slice(i * TILE, (i + 1) * TILE), (i + 1) * TILE
            q, k = query[at, :], keys[:seen, :]
            s = product_t(q, k) * score_scale
            row = lax.broadcasted_iota(jnp.int32, s.shape, 0) + i * TILE
            col = lax.broadcasted_iota(jnp.int32, s.shape, 1)
            visible = (row >= col) & (segment_col[at, :] == segment_row[:, :seen])
            p = jnp.exp(jnp.where(visible, s, -1e30) - log_total[at, :])
            g = grad_context[at, :]
            dp = product_t(g, values[:seen, :])
            balance = jnp.sum(dp * p, axis=-1, keepdims=True)
            ds = (p * (dp - balance)).astype(bf16)
            dq, of_gain = back_norm(query_raw[at, :], gain_query[...], product(ds, k) * score_scale)
            d_qkv[at, :head] = dq.astype(bf16)
            gains[4:5, :head] = gains[4:5, :head] + jnp.sum(of_gain, axis=0, keepdims=True)
            d_keys[:seen, :] = d_keys[:seen, :] + t_product(ds, q)
            d_values[:seen, :] = d_values[:seen, :] + t_product(p.astype(bf16), g)
        for i in range(length // TILE):
            at = slice(i * TILE, (i + 1) * TILE)
            dk, of_gain = back_norm(keys_raw[at, :], gain_key[...], d_keys[at, :] * score_scale)
            d_qkv[at, head : 2 * head] = dk.astype(bf16)
            gains[5:6, :head] = gains[5:6, :head] + jnp.sum(of_gain, axis=0, keepdims=True)
            d_qkv[at, 2 * head :] = d_values[at, :].astype(bf16)

    pl.run_scoped(
        attention,
        pltpu.VMEM((length, head), bf16),
        pltpu.VMEM((length, head), bf16),
        pltpu.VMEM((length, head), bf16),
        pltpu.VMEM((length, head), f32),
        pltpu.VMEM((length, head), f32),
        pltpu.VMEM((length, head), bf16),
        pltpu.VMEM((length, head), f32),
        pltpu.VMEM((length, head), f32),
    )
    far(0)

    def attn_z1_copy(i):
        b = (2 * (i // 2) + 1 - zl) * 2 + i % 2
        return remote(attn.at[block(attn, b)], attn_z1.at[i], z1s, 3 + i, near["z1"])

    def attn_x_copy(j):
        b = (2 * (zh ^ j) + zl) * 2 + 1 - x
        return remote(attn.at[block(attn, b)], attn_x.at[j], xs, 12 + j, near["x"])

    attn_z2_copy = remote(attn.at[block(attn, (2 * (1 - zh) + zl) * 2 + x)], attn_z2, z2s, 6, near["z2"])

    input_y = remote(input_own, input_land.at[0], ys, 4, near["y"])
    input_c = remote(input_own, input_land.at[1], cs, 7, near["c"])
    input_fwd = remote(input_land.at[0], input_land.at[2], cs, 8, near["c"])

    def rest(w_qkv, part, kv_halves):
        for copy in copies([(w_qkv_hbm, w_qkv)]):
            copy.wait()

        def core_copy(i):
            return remote(part.at[i, pl.ds(HALF, HALF)], from_core.at[i], cs, 2 + i, near["c"])

        def y_copy(h):
            return remote(part.at[h, pl.ds(0, HALF)], from_y.at[h], ys, 1 + h, near["y"])

        def tile(i, carry):
            for dc in range(2):
                rows = d_qkv[pl.ds(tile_row(c, y, i, dc), HALF), :]
                part[i, dc * HALF : (dc + 1) * HALF] = product_t(rows, w_qkv[...])
            core_copy(i).start()
            core_copy(i).wait_recv()
            part[i, :HALF] = part[i, :HALF] + from_core[i]

            @pl.when(i < 2)
            def _():
                y_copy(i).start()

            return carry

        lax.fori_loop(0, 4, tile, 0)

        def of_inputs(normed_in, kv):
            for copy in copies([(normed_in_hbm, normed_in)]):
                copy.wait()
            for k in range(2):
                kv[k] = t_product(normed_in[...], d_qkv[:, (1 + k) * head : (2 + k) * head])
            to_core = remote(kv.at[1 - c], kv_core, cs, 6, near["c"])
            to_core.start()
            attn[:, :head] = t_product(normed_in[...], d_qkv[:, :head])
            to_core.wait_recv()
            for k in range(2):
                lanes = slice(k * (head // 2), (k + 1) * (head // 2))
                kv_halves[k] = kv[c, :, lanes] + kv_core[:, lanes]
            to_core.wait_send()

        pl.run_scoped(of_inputs, pltpu.VMEM((length, width), bf16), pltpu.VMEM((2, width, head), f32))
        to_y = remote(kv_halves.at[1 - y], kv_across, ys, 3, near["y"])
        to_y.start()

        def of_branch(context, d_branch, d_middle, tokens):
            waits = copies(
                [
                    (context_hbm, context),
                    (d_branch_hbm, d_branch),
                    (d_middle_hbm, d_middle),
                    (tokens_hbm.at[pl.ds(own_row, QUARTER)], tokens),
                ]
            )
            branch_y.wait_recv()
            branch_fwd.start()
            for copy in waits:
                copy.wait()
            acc = t_product(d_branch[...].astype(bf16), context[quarter_rows(0, 0), :])
            branch_c.wait_recv()
            branch_fwd.wait_recv()
            for k, (dc, dy) in enumerate([(0, 1), (1, 0), (1, 1)]):
                acc = acc + t_product(branch_land[k].astype(bf16), context[quarter_rows(dc, dy), :])
            attn[:, head : 2 * head] = acc
            far(1)
            for h in range(2):
                y_copy(h).wait_recv()
                at = slice(h * HALF, (h + 1) * HALF)
                grad = part[2 + h, :HALF] + from_y[h]
                d_in, of_gain = back_norm(tokens[at, :].astype(f32), gain_in[...], grad)
                gains[0:1, :] = gains[0:1, :] + jnp.sum(of_gain, axis=0, keepdims=True)
                d = (d_middle[at, :] + d_in).astype(bf16)
                input_grad[pl.ds(pl.multiple_of(own_row + h * HALF, HALF), HALF), :] = d
                input_own[at, :] = d.astype(f32)

        pl.run_scoped(
            of_branch,
            pltpu.VMEM((length, head), bf16),
            pltpu.VMEM((QUARTER, width), f32),
            pltpu.VMEM((QUARTER, width), f32),
            pltpu.VMEM((QUARTER, width), bf16),
        )
        input_y.start()
        input_c.start()
        far(2)
        to_y.wait_recv()
        attn[:, 2 * head :] = kv_halves[y] + kv_across[...]
        for i in range(4):
            attn_z1_copy(i).start()
        for i in range(4):
            core_copy(i).wait_send()
        for h in range(2):
            y_copy(h).wait_send()
        to_y.wait_send()

    pl.run_scoped(
        rest,
        pltpu.VMEM((width, 3 * head), bf16),
        pltpu.VMEM((4, TILE, width), f32),
        pltpu.VMEM((2, width, head // 2), f32),
    )

    for k, (sems, index, to) in enumerate([(cs, 10, "c"), (ys, 6, "y"), (xs, 14, "x"), (z2s, 7, "z2"), (z1s, 7, "z1")]):
        hop = remote(gains, gains_land.at[k], sems, index, near[to])
        hop.start()
        hop.wait()
        gains[...] = gains[...] + gains_land[k]

    close(0)
    for i in range(4):
        attn_z1_copy(i).wait_recv()
        rows = block(attn, (2 * (i // 2) + zl) * 2 + i % 2)
        attn[rows, :] = attn[rows, :] + attn_z1[i]
    for j in (1, 0):
        attn_x_copy(j).start()
    for k in range(2):
        x_copy(2, 2 + k).start()
    input_y.wait_recv()
    input_fwd.start()
    input_grad[quarter_rows(0, 1), :] = input_land[0].astype(bf16)
    input_c.wait_recv()
    input_grad[quarter_rows(1, 0), :] = input_land[1].astype(bf16)
    input_fwd.wait_recv()
    input_grad[quarter_rows(1, 1), :] = input_land[2].astype(bf16)
    close(1)
    for j in (1, 0):
        attn_x_copy(j).wait_recv()
        rows = block(attn, (2 * (zh ^ j) + zl) * 2 + x)
        attn[rows, :] = attn[rows, :] + attn_x[j]
        if j == 1:
            attn_z2_copy.start()
    attn_z2_copy.wait_recv()
    total = attn[block(attn, (2 * zh + zl) * 2 + x), :] + attn_z2[...]
    attn_out[...] = total[:, : 2 * head]
    kv_own[...] = total[:, 2 * head :]
    wide_y = remote(kv_own, kv_y, ys, 5, near["y"])
    wide_y.start()
    wide_y.wait_recv()
    kv_wide[:, : head // 2] = jnp.where(y == 0, kv_own[...], kv_y[...])
    kv_wide[:, head // 2 :] = jnp.where(y == 0, kv_y[...], kv_own[...])
    wide_c = remote(kv_wide, kv_wide_core, cs, 9, near["c"])
    wide_c.start()
    wide_c.wait_recv()
    kv_out[c] = kv_wide[...]
    kv_out[1 - c] = kv_wide_core[...]
    close(2)
    for m in range(3):
        z1_copy(m).wait_recv()
        ff_out[m, 1 - zl] = z1_land[m]
    for m in range(3):
        for j in range(4):
            x_copy(m, j).wait_send()
        for k in range(2):
            z2_copy(m, k).wait_send()
        z1_copy(m).wait_send()
    for i in range(4):
        attn_z1_copy(i).wait_send()
    for j in range(2):
        attn_x_copy(j).wait_send()
    for copy in (attn_z2_copy, branch_y, branch_c, branch_fwd, input_y, input_c, input_fwd, wide_y, wide_c):
        copy.wait_send()


def reduce_all(nx, dp_size, whole, small):
    length, width = whole[0].shape
    half = whole[4].shape[1]
    head = whole[10].shape[1]
    blk = width // dp_size
    return pl.pallas_call(
        functools.partial(reduce_kernel, nx),
        out_shape=(
            jax.ShapeDtypeStruct((3, 2, blk, half), f32),
            jax.ShapeDtypeStruct((blk, 2 * head), f32),
            jax.ShapeDtypeStruct((2, blk, head), f32),
            jax.ShapeDtypeStruct((length, width), bf16),
            jax.ShapeDtypeStruct((8, width), f32),
        ),
        in_specs=[ANY] * len(whole) + [VMEM] * len(small),
        out_specs=(VMEM,) * 5,
        scratch_shapes=[
            pltpu.VMEM((3, width, half), f32),
            pltpu.VMEM((12, blk, half), f32),
            pltpu.VMEM((6, blk, half), f32),
            pltpu.VMEM((3, blk, half), f32),
            pltpu.VMEM((4, HALF, width), f32),
            pltpu.VMEM((2, HALF, width), f32),
            pltpu.VMEM((3, QUARTER, width), f32),
            pltpu.VMEM((QUARTER, width), f32),
            pltpu.VMEM((3, QUARTER, width), f32),
            pltpu.VMEM((length, 3 * head), bf16),
            pltpu.VMEM((width, 2 * head + head // 2), f32),
            pltpu.VMEM((4, blk, 2 * head + head // 2), f32),
            pltpu.VMEM((2, blk, 2 * head + head // 2), f32),
            pltpu.VMEM((blk, 2 * head + head // 2), f32),
            pltpu.VMEM((width, head), f32),
            pltpu.VMEM((width, head // 2), f32),
            pltpu.VMEM((blk, head // 2), f32),
            pltpu.VMEM((blk, head // 2), f32),
            pltpu.VMEM((blk, head), f32),
            pltpu.VMEM((blk, head), f32),
            pltpu.VMEM((5, 8, width), f32),
        ]
        + dma(6, 11, 11, 7, 7, 15, 15, 8, 8, 8, 8),
        compiler_params=pltpu.CompilerParams(collective_id=2, has_side_effects=True, vmem_limit_bytes=int(63.5 * 2**20)),
        name="reduce_all",
    )(*whole, *small)


def body(
    links,
    tokens,
    segment_ids,
    cotangent,
    w_query,
    w_key,
    w_value,
    w_out,
    w_gate,
    w_up,
    w_down,
    gain_attn_in,
    gain_attn_out,
    gain_ffn_in,
    gain_ffn_out,
    gain_query,
    gain_key,
):
    length, width = tokens.shape
    head = w_query.shape[1]
    quarter = length // 4
    half_ff = w_gate.shape[1] // 2
    nx = links.nx
    blk = width // links.dp_size
    dp, t = lax.axis_index("dp"), lax.axis_index("tensor")
    z, x = dp // nx, dp % nx
    y, c = t // 2, t % 2
    parity = z % 2
    one = jnp.where(segment_ids[0] < length, 1.0, 0.5).astype(f32)

    def keep_low(a):
        return (a * one).astype(bf16)

    def place(dc, dy):
        return ((c ^ dc) * 2 + (y ^ dy)) * quarter

    def rows(a, dc, dy):
        return lax.dynamic_slice_in_dim(a, place(dc, dy), quarter, 0)

    def to_absolute(pieces):
        stack = jnp.stack([pieces[0][0], pieces[0][1], pieces[1][0], pieces[1][1]])
        mine = c * 2 + y
        return jnp.concatenate([lax.dynamic_index_in_dim(stack, mine ^ b, 0, keepdims=False) for b in range(4)], axis=0)

    out_own = w_out.astype(f32)
    out_y = links.y(out_own)
    out_c = links.core(out_own)
    out_yc = links.core(out_y)
    w_out_all = jnp.concatenate([w_out, keep_low(out_y), keep_low(out_c), keep_low(out_yc)], axis=0)

    columns = w_gate.shape[1]
    padded = -columns % (2 * HALF)
    wg, wu = jnp.pad(w_gate, ((0, 0), (0, padded))), jnp.pad(w_up, ((0, 0), (0, padded)))
    wd = jnp.pad(w_down, ((0, padded), (0, 0)))
    half_ff = (columns + padded) // 2

    hidden_in = tokens.astype(f32)
    normed_low = low(rms_norm(hidden_in, gain_attn_in))
    query_raw = product(normed_low, w_query)
    keys_raw = product(normed_low, w_key)
    query_low = low(rms_norm(query_raw, gain_query))
    keys_low = low(rms_norm(keys_raw, gain_key))
    values_low = low(product(normed_low, w_value))
    places = jnp.arange(length)
    allowed = (places[:, None] >= places[None, :]) & (segment_ids[:, None] == segment_ids[None, :])

    def scores_of():
        raw = product_t(query_low, keys_low) * score_scale
        return jnp.where(allowed, raw, -1e30)

    scores = scores_of()
    largest = jnp.max(scores, axis=-1, keepdims=True)
    exponent = jnp.exp(scores - largest)
    total = jnp.sum(exponent, axis=-1, keepdims=True)
    log_total = largest + jnp.log(total)
    context_low = low(product(low(exponent / total), values_low))

    context = context_low.astype(f32)
    mine = jnp.concatenate([rows(context, 0, 1), rows(context, 0, 0)], axis=0)
    of_core = links.core(jnp.concatenate([rows(context, 1, 1), rows(context, 1, 0)], axis=0))
    of_y = links.y(jnp.concatenate([rows(context, 0, 0), rows(context, 0, 1)], axis=0))
    of_yc = links.y(jnp.concatenate([of_core[quarter:], of_core[:quarter]], axis=0))
    context_all = jnp.concatenate([low(mine), keep_low(of_y), keep_low(of_core), keep_low(of_yc)], axis=1)
    branch = product(context_all, w_out_all)
    hidden_rows = jnp.concatenate([rows(tokens, 0, 1), rows(tokens, 0, 0)], axis=0).astype(f32)
    middle_own = hidden_rows + rms_norm(branch, gain_attn_out)
    middle_core = links.core(middle_own)

    eighth = length // 8
    tiles = []
    for k in range(4):
        at = slice(k * eighth, (k + 1) * eighth)
        tiles += [middle_own[at], middle_core[at]]
    normed_two, normed_other, d_out, d_own, layer_out, ffn_out_rows = feed_forward(
        nx, jnp.concatenate(tiles, axis=0), cotangent, gain_ffn_in, gain_ffn_out, wg, wu, wd
    )
    grad_ffn_out = jnp.sum(ffn_out_rows, axis=0)
    d_other, pair_in, pair_gates, grad_context, d_branch_own, d_middle, gain_rows = feed_back(
        nx,
        d_out,
        d_own,
        normed_two,
        normed_other,
        wg,
        wu,
        wd,
        w_out_all,
        middle_own[quarter:],
        branch[quarter:],
        cotangent,
        gain_ffn_in,
        gain_attn_out,
    )
    gain_rows = jnp.sum(gain_rows, axis=1)
    grad_ffn_in, grad_attn_out = gain_rows[0], gain_rows[1]

    row = jnp.zeros((1, width), f32)
    so_far = jnp.concatenate(
        [row, grad_attn_out[None], grad_ffn_in[None], 0.25 * grad_ffn_out[None]] + [row] * 4, axis=0
    )
    ff, attn_sum, kv_sum, input_grad, gains = reduce_all(
        nx,
        links.dp_size,
        [
            d_out,
            d_other,
            normed_two,
            normed_other,
            pair_in,
            pair_gates,
            d_branch_own,
            d_middle,
            tokens,
            normed_low,
            query_low,
            keys_low,
            values_low,
            query_raw,
            keys_raw,
            context_low,
            grad_context,
            jnp.concatenate([w_query, w_key, w_value], axis=1),
        ],
        [
            log_total,
            segment_ids.reshape(length, 1),
            segment_ids.reshape(1, length),
            gain_attn_in.reshape(1, width),
            gain_query.reshape(1, head),
            gain_key.reshape(1, head),
            so_far,
        ],
    )
    ff = jnp.concatenate([ff[:, 0], ff[:, 1, :, : columns - half_ff]], axis=2)
    part = lax.dynamic_slice_in_dim(gains, dp * blk, blk, 1)
    hb = head // links.dp_size
    head_part = lax.dynamic_slice_in_dim(gains, dp * hb, hb, 1)
    return (
        layer_out,
        input_grad,
        attn_sum[:, :head],
        kv_sum[0],
        kv_sum[1],
        attn_sum[:, head:].T,
        ff[1],
        ff[2],
        ff[0].T,
        part[0],
        part[1],
        part[2],
        part[3],
        head_part[4],
        head_part[5],
    )


def body_any(
    links,
    tokens,
    segment_ids,
    cotangent,
    w_query,
    w_key,
    w_value,
    w_out,
    w_gate,
    w_up,
    w_down,
    gain_attn_in,
    gain_attn_out,
    gain_ffn_in,
    gain_ffn_out,
    gain_query,
    gain_key,
):
    length, width = tokens.shape
    head = w_query.shape[1]
    quarter = length // 4
    half_ff = w_gate.shape[1] // 2
    nx = links.nx
    blk = width // links.dp_size
    dp, t = lax.axis_index("dp"), lax.axis_index("tensor")
    z, x = dp // nx, dp % nx
    y, c = t // 2, t % 2
    parity = z % 2
    one = jnp.where(segment_ids[0] < length, 1.0, 0.5).astype(f32)

    def keep_low(a):
        return (a * one).astype(bf16)

    def place(dc, dy):
        return ((c ^ dc) * 2 + (y ^ dy)) * quarter

    def rows(a, dc, dy):
        return lax.dynamic_slice_in_dim(a, place(dc, dy), quarter, 0)

    def to_absolute(pieces):
        stack = jnp.stack([pieces[0][0], pieces[0][1], pieces[1][0], pieces[1][1]])
        mine = c * 2 + y
        return jnp.concatenate([lax.dynamic_index_in_dim(stack, mine ^ b, 0, keepdims=False) for b in range(4)], axis=0)

    out_own = w_out.astype(f32)
    out_y = links.y(out_own)
    out_c = links.core(out_own)
    out_yc = links.core(out_y)
    w_out_all = jnp.concatenate([w_out, keep_low(out_c), keep_low(out_y), keep_low(out_yc)], axis=0)

    wg_h = jnp.where(parity == 0, w_gate[:, :half_ff], w_gate[:, half_ff:])
    wu_h = jnp.where(parity == 0, w_up[:, :half_ff], w_up[:, half_ff:])
    wd_h = jnp.where(parity == 0, w_down[:half_ff], w_down[half_ff:])

    hidden_in = tokens.astype(f32)
    normed_low = low(rms_norm(hidden_in, gain_attn_in))
    query_raw = product(normed_low, w_query)
    keys_raw = product(normed_low, w_key)
    query_low = low(rms_norm(query_raw, gain_query))
    keys_low = low(rms_norm(keys_raw, gain_key))
    values_low = low(product(normed_low, w_value))
    places = jnp.arange(length)
    allowed = (places[:, None] >= places[None, :]) & (segment_ids[:, None] == segment_ids[None, :])

    def scores_of():
        raw = product_t(query_low, keys_low) * score_scale
        return jnp.where(allowed, raw, -1e30)

    scores = scores_of()
    largest = jnp.max(scores, axis=-1, keepdims=True)
    exponent = jnp.exp(scores - largest)
    total = jnp.sum(exponent, axis=-1, keepdims=True)
    log_total = largest + jnp.log(total)
    context_low = low(product(low(exponent / total), values_low))

    context = context_low.astype(f32)
    mine = jnp.concatenate([rows(context, 0, 1), rows(context, 0, 0)], axis=0)
    of_core = links.core(jnp.concatenate([rows(context, 1, 1), rows(context, 1, 0)], axis=0))
    of_y = links.y(jnp.concatenate([rows(context, 0, 0), rows(context, 0, 1)], axis=0))
    of_yc = links.y(jnp.concatenate([of_core[quarter:], of_core[:quarter]], axis=0))
    context_all = jnp.concatenate([low(mine), keep_low(of_core), keep_low(of_y), keep_low(of_yc)], axis=1)
    branch = product(context_all, w_out_all)
    hidden_rows = jnp.concatenate([rows(tokens, 0, 1), rows(tokens, 0, 0)], axis=0).astype(f32)
    middle_own = hidden_rows + rms_norm(branch, gain_attn_out)
    middle_core = links.core(middle_own)

    middles, normed_two, inners, parts = [], [], [], []
    saved = []
    for k in range(2):
        at = slice(k * quarter, (k + 1) * quarter)
        middle = jnp.concatenate([middle_own[at], middle_core[at]], axis=0)
        normed_k = low(rms_norm(middle, gain_ffn_in))
        gate, upward = product(normed_k, w_gate), product(normed_k, w_up)
        inner = low(activate(gate, upward))
        part = product(inner, w_down)
        middles.append(middle)
        normed_two.append(normed_k)
        saved.append((gate, upward))
        parts.append(part)
    normed_own = low(rms_norm(middle_own, gain_ffn_in)).astype(f32)
    other_own = links.z1(normed_own)
    other_core = links.core(other_own)
    normed_other = jnp.concatenate([keep_low(other_own), keep_low(other_core)], axis=0)

    def gather_quarters(parts):
        sums = [part[:quarter] + links.core(part[quarter:]) for part in parts]
        return sums[1] + links.y(sums[0])

    output_q = gather_quarters(parts)
    output_y = links.y(output_q)
    output_c = links.core(output_q)
    output_yc = links.core(output_y)
    outputs = [jnp.concatenate([output_y, output_yc], axis=0), jnp.concatenate([output_q, output_c], axis=0)]
    grad_out = cotangent.astype(f32)
    d_outputs, layer_pieces, grad_ffn_out = [], [], 0.0
    for k in range(2):
        dy_k = jnp.concatenate([rows(cotangent, 0, 1 - k), rows(cotangent, 1, 1 - k)], axis=0).astype(f32)
        layer_k = low(middles[k] + rms_norm(outputs[k], gain_ffn_out))
        d_k, gain_k = rms_back(outputs[k], gain_ffn_out, dy_k)
        grad_ffn_out = grad_ffn_out + gain_k
        d_outputs.append(low(d_k))
        layer_pieces.append(layer_k)
    layer_out = to_absolute(
        [
            [layer_pieces[1][:quarter], layer_pieces[0][:quarter]],
            [layer_pieces[1][quarter:], layer_pieces[0][quarter:]],
        ]
    )

    d_own_rows = [d[:quarter].astype(f32) for d in d_outputs]
    got_own = [links.z1(d_own_rows[1]), links.z1(d_own_rows[0])]
    got_core = [links.core(g) for g in got_own]
    d_other = jnp.concatenate(
        [keep_low(got_own[1]), keep_low(got_own[0]), keep_low(got_core[1]), keep_low(got_core[0])], axis=0
    )

    back_parts = []
    for k in range(2):
        gate, upward = saved[k]
        d_inner = product_t(d_outputs[k], w_down)
        _, pull = jax.vjp(activate, gate, upward)
        d_gate, d_up = pull(d_inner)
        back_parts.append(product_t(low(d_gate), w_gate) + product_t(low(d_up), w_up))
    d_normed_q = gather_quarters(back_parts)
    middle_q = middle_own[quarter:]
    branch_q = branch[quarter:]
    dy_q = rows(cotangent, 0, 0).astype(f32)
    d_mid, grad_ffn_in = rms_back(middle_q, gain_ffn_in, d_normed_q)
    d_middle = dy_q + d_mid
    d_branch, grad_attn_out = rms_back(branch_q, gain_attn_out, d_middle)
    d_branch_low = low(d_branch)
    d_context = low(product_t(d_branch_low, w_out_all)).astype(f32)
    heads = [d_context[:, i * head : (i + 1) * head] for i in range(4)]
    c_got = links.core(jnp.concatenate([heads[1], heads[3]], axis=1))
    y_got = links.y(jnp.concatenate([heads[2], c_got[:, head:]], axis=1))
    grad_context = keep_low(
        to_absolute([[heads[0], y_got[:, :head]], [c_got[:, :head], y_got[:, head:]]])
    )
    d_branch_own = d_branch_low.astype(f32)
    d_branch_y = links.y(d_branch_own)
    d_branch_c = links.core(d_branch_own)
    d_branch_yc = links.core(d_branch_y)
    d_branch_all = jnp.concatenate(
        [d_branch_low, keep_low(d_branch_y), keep_low(d_branch_c), keep_low(d_branch_yc)], axis=0
    )
    context_rel = jnp.concatenate(
        [rows(context_low, 0, 0), rows(context_low, 0, 1), rows(context_low, 1, 0), rows(context_low, 1, 1)], axis=0
    )
    grad_w_out_t = t_product(d_branch_all, context_rel)

    attn_prob = jnp.exp(scores_of() - log_total)
    prob_low = low(attn_prob)
    grad_prob = product_t(grad_context, values_low)
    grad_values = low(t_product(prob_low, grad_context))
    balance = jnp.sum(grad_prob * attn_prob, axis=-1, keepdims=True)
    grad_scores = low(attn_prob * (grad_prob - balance))
    grad_query_n = product(grad_scores, keys_low) * score_scale
    grad_keys_n = t_product(grad_scores, query_low) * score_scale
    d_query, grad_gain_query = rms_back(query_raw, gain_query, grad_query_n)
    d_keys, grad_gain_key = rms_back(keys_raw, gain_key, grad_keys_n)
    d_query, d_keys = low(d_query), low(d_keys)
    d_qkv = jnp.concatenate([d_query, d_keys, grad_values], axis=1)
    w_qkv = jnp.concatenate([w_query, w_key, w_value], axis=1)
    in_parts = []
    for k in range(2):
        rows_k = jnp.concatenate([rows(d_qkv, 0, 1 - k), rows(d_qkv, 1, 1 - k)], axis=0)
        in_parts.append(product_t(rows_k, w_qkv))
    d_normed_in = gather_quarters(in_parts)
    hidden_q = rows(tokens, 0, 0).astype(f32)
    d_in, grad_attn_in = rms_back(hidden_q, gain_attn_in, d_normed_in)
    input_q = low(d_middle + d_in)
    input_own = input_q.astype(f32)
    input_y = links.y(input_own)
    input_c = links.core(input_own)
    input_yc = links.core(input_y)
    input_grad = keep_low(to_absolute([[input_own, input_y], [input_c, input_yc]]))

    grad_qkv = t_product(normed_low, d_qkv)
    grad_w_query, grad_kv = grad_qkv[:, :head], grad_qkv[:, head:]
    kv_keep = jnp.where(c == 0, grad_kv[:, :head], grad_kv[:, head:])
    kv_send = jnp.where(c == 0, grad_kv[:, head:], grad_kv[:, :head])
    kv = kv_keep + links.core(kv_send)
    kv_half = head // 2
    kv_keep = jnp.where(y == 0, kv[:, :kv_half], kv[:, kv_half:])
    kv_send = jnp.where(y == 0, kv[:, kv_half:], kv[:, :kv_half])
    kv = kv_keep + links.y(kv_send)
    attn_grads = jnp.concatenate([grad_w_query, grad_w_out_t, kv], axis=1)

    normed_all = jnp.concatenate(
        [normed_two[0][:quarter], normed_two[1][:quarter], normed_two[0][quarter:], normed_two[1][quarter:], normed_other],
        axis=0,
    )
    d_all = jnp.concatenate(
        [d_outputs[0][:quarter], d_outputs[1][:quarter], d_outputs[0][quarter:], d_outputs[1][quarter:], d_other], axis=0
    )
    gate, upward = product(normed_all, wg_h), product(normed_all, wu_h)
    inner, pull = jax.vjp(activate, gate, upward)
    inner = low(inner)
    d_inner = product_t(d_all, wd_h)
    d_gate, d_up = pull(d_inner)
    ff_grads = [t_product(d_all, inner), t_product(normed_all, low(d_gate)), t_product(normed_all, low(d_up))]

    zh, zl = z // 2, z % 2

    def sum_x(grads, z_half):
        mine = lax.dynamic_index_in_dim(grads, z_half, 0, keepdims=False)
        acc = lax.dynamic_index_in_dim(mine, x, 1, keepdims=False)
        for step in range(1, nx):
            to = lax.dynamic_index_in_dim(mine, (x + step) % nx, 1, keepdims=False)
            acc = acc + links.x(to, step)
        return acc

    def scatter(grads):
        grads = grads.reshape(2, 2, nx, blk, grads.shape[1])
        far = sum_x(grads, 1 - zh)
        near = sum_x(grads, zh)
        return near + links.z2(far)

    ff_sums = []
    for grads in ff_grads:
        got = scatter(grads)
        own = lax.dynamic_index_in_dim(got, zl, 0, keepdims=False)
        other = links.z1(lax.dynamic_index_in_dim(got, 1 - zl, 0, keepdims=False))
        ff_sums.append(
            jnp.where(
                parity == 0, jnp.concatenate([own, other], axis=1), jnp.concatenate([other, own], axis=1)
            )
        )
    grad_w_down, grad_w_gate, grad_w_up = ff_sums[0].T, ff_sums[1], ff_sums[2]

    got = scatter(attn_grads)
    attn_sum = lax.dynamic_index_in_dim(got, zl, 0, keepdims=False) + links.z1(
        lax.dynamic_index_in_dim(got, 1 - zl, 0, keepdims=False)
    )
    grad_w_query = attn_sum[:, :head]
    grad_w_out = attn_sum[:, head : 2 * head].T
    kv_own = attn_sum[:, 2 * head :]
    kv_y = links.y(kv_own)
    kv_wide = jnp.where(y == 0, jnp.concatenate([kv_own, kv_y], axis=1), jnp.concatenate([kv_y, kv_own], axis=1))
    kv_c = links.core(kv_wide)
    grad_w_key = jnp.where(c == 0, kv_wide, kv_c)
    grad_w_value = jnp.where(c == 0, kv_c, kv_wide)

    small = jnp.concatenate(
        [
            grad_attn_in.reshape(links.dp_size, -1),
            grad_attn_out.reshape(links.dp_size, -1),
            grad_ffn_in.reshape(links.dp_size, -1),
            (grad_ffn_out * 0.25).reshape(links.dp_size, -1),
            grad_gain_query.reshape(links.dp_size, -1),
            grad_gain_key.reshape(links.dp_size, -1),
        ],
        axis=1,
    )
    small = small + links.core(small)
    small = small + links.y(small)
    small = small.reshape(2, 2, nx, 1, small.shape[1])
    acc = lax.dynamic_index_in_dim(small, x, 2, keepdims=False)
    for step in range(1, nx):
        acc = acc + links.x(lax.dynamic_index_in_dim(small, (x + step) % nx, 2, keepdims=False), step)
    acc = lax.dynamic_index_in_dim(acc, zh, 0, keepdims=False) + links.z2(
        lax.dynamic_index_in_dim(acc, 1 - zh, 0, keepdims=False)
    )
    acc = lax.dynamic_index_in_dim(acc, zl, 0, keepdims=False) + links.z1(
        lax.dynamic_index_in_dim(acc, 1 - zl, 0, keepdims=False)
    )
    acc = acc.reshape(-1)
    hb = head // links.dp_size
    return (
        layer_out,
        input_grad,
        grad_w_query,
        grad_w_key,
        grad_w_value,
        grad_w_out,
        grad_w_gate,
        grad_w_up,
        grad_w_down,
        acc[:blk],
        acc[blk : 2 * blk],
        acc[2 * blk : 3 * blk],
        acc[3 * blk : 4 * blk],
        acc[4 * blk : 4 * blk + hb],
        acc[4 * blk + hb :],
    )


def solution(mesh):
    links = Links(mesh)
    return jax.shard_map(
        functools.partial(body if links.nx == 2 else body_any, links),
        mesh=mesh,
        in_specs=(
            P("dp", None),
            P("dp"),
            P("dp", None),
            P(None, "tensor"),
            P(),
            P(),
            P("tensor", None),
            P(None, "tensor"),
            P(None, "tensor"),
            P("tensor", None),
            P(),
            P(),
            P(),
            P(),
            P(),
            P(),
        ),
        out_specs=(
            P("dp", None),
            P("dp", None),
            P("dp", "tensor"),
            P("dp", None),
            P("dp", None),
            P("tensor", "dp"),
            P("dp", "tensor"),
            P("dp", "tensor"),
            P("tensor", "dp"),
            P("dp"),
            P("dp"),
            P("dp"),
            P("dp"),
            P("dp"),
            P("dp"),
        ),
        check_vma=False,
    )
```

```python
import functools

import jax
import jax.numpy as jnp
from jax import lax
from jax.experimental import pallas as pl
from jax.experimental.pallas import tpu as pltpu
from jax.sharding import PartitionSpec as P

epsilon = 1e-06
score_scale = 0.0625
NZ = 4

f32 = jnp.float32
bf16 = jnp.bfloat16


def rms_norm(values, gain):
    inverse = lax.rsqrt(jnp.mean(values * values, axis=-1, keepdims=True) + epsilon)
    return values * inverse * (1.0 + gain)


def rms_back(values, gain, grad):
    inverse = lax.rsqrt(jnp.mean(values * values, axis=-1, keepdims=True) + epsilon)
    hat = values * inverse
    scaled = grad * (1.0 + gain)
    back = inverse * (scaled - hat * jnp.mean(scaled * hat, axis=-1, keepdims=True))
    return back, jnp.sum(grad * hat, axis=0)


def product(left, right):
    return jnp.dot(left, right, preferred_element_type=f32)


def product_t(left, right):
    return lax.dot_general(left, right, (((1,), (1,)), ((), ())), preferred_element_type=f32)


def t_product(left, right):
    return lax.dot_general(left, right, (((0,), (0,)), ((), ())), preferred_element_type=f32)


def activate(gate, upward):
    return jax.nn.gelu(gate, approximate=True) * upward


class Links:
    def __init__(self, mesh):
        self.dp_size = mesh.shape["dp"]
        self.nx = self.dp_size // NZ
        tensor = mesh.shape["tensor"]
        self.perm_core = [(t, t ^ 1) for t in range(tensor)]
        self.perm_y = [(t, t ^ 2) for t in range(tensor)]
        nx = self.nx
        self.perm_z1 = [(z * nx + x, (z ^ 1) * nx + x) for z in range(NZ) for x in range(nx)]
        self.perm_z2 = [(z * nx + x, (z ^ 2) * nx + x) for z in range(NZ) for x in range(nx)]

    def core(self, a):
        return lax.ppermute(a, "tensor", self.perm_core)

    def y(self, a):
        return lax.ppermute(a, "tensor", self.perm_y)

    def z1(self, a):
        return lax.ppermute(a, "dp", self.perm_z1)

    def z2(self, a):
        return lax.ppermute(a, "dp", self.perm_z2)

    def x(self, a, step):
        nx = self.nx
        return lax.ppermute(a, "dp", [(z * nx + x, z * nx + (x + step) % nx) for z in range(NZ) for x in range(nx)])


def low(a):
    return a.astype(bf16)


MESH = pl.DeviceIdType.MESH
ANY = pl.BlockSpec(memory_space=pl.ANY)
VMEM = pl.BlockSpec(memory_space=pltpu.VMEM)
TILE, HALF, QUARTER = 256, 128, 256


def spots(nx):
    dp, t = lax.axis_index("dp"), lax.axis_index("tensor")
    z, x = dp // nx, dp % nx
    near = {
        "c": {"tensor": t ^ 1},
        "y": {"tensor": t ^ 2},
        "z1": {"dp": (z ^ 1) * nx + x},
        "z2": {"dp": (z ^ 2) * nx + x},
        "x": {"dp": z * nx + (x ^ 1)},
    }
    return z, x, t // 2, t % 2, near


def remote(src, dst, sems, index, to):
    return pltpu.make_async_remote_copy(
        src_ref=src, dst_ref=dst, send_sem=sems[0].at[index], recv_sem=sems[1].at[index], device_id=to, device_id_type=MESH
    )


def greet(others):
    barrier = pltpu.get_barrier_semaphore()
    for other in others:
        pl.semaphore_signal(barrier, inc=1, device_id=other, device_id_type=MESH)
    pl.semaphore_wait(barrier, len(others))


def tile_row(c, y, i, dc):
    dy = 1 - i // 2
    return pl.multiple_of(((c ^ dc) * 2 + (y ^ dy)) * QUARTER + (i % 2) * HALF, HALF)


def gelu_parts(u):
    k = 0.7978845608028654
    square = u * u
    th = jnp.tanh(k * u * (1.0 + 0.044715 * square))
    side = 0.5 * (1.0 + th)
    return u * side, side + 0.5 * u * (1.0 - th * th) * (k * (1.0 + 3.0 * 0.044715 * square))


def gelu_tanh(u):
    return 0.5 * u * (1.0 + jnp.tanh(0.7978845608028654 * u * (1.0 + 0.044715 * (u * u))))


def forward_kernel(
    nx,
    middle,
    cotangent,
    gain_in,
    gain_out,
    w_gate,
    w_up,
    w_down,
    normed,
    normed_other,
    d_out,
    d_own,
    layer_out,
    gain_grad,
    out,
    dy,
    inner,
    part,
    from_core,
    from_y,
    z_stage,
    z_land,
    c_land,
    local,
    c_send,
    c_recv,
    y_send,
    y_recv,
    z_send,
    z_recv,
):
    z, x, y, c, near = spots(nx)
    core, across, pair = near["c"], near["y"], near["z1"]
    cs, ys, zs = (c_send, c_recv), (y_send, y_recv), (z_send, z_recv)
    loads = []
    for i in range(4):
        for dc in range(2):
            copy = pltpu.make_async_copy(
                cotangent.at[pl.ds(tile_row(c, y, i, dc), HALF)],
                dy.at[pl.ds(i * TILE + dc * HALF, HALF)],
                local.at[i * 2 + dc],
            )
            copy.start()
            loads.append(copy)
    greet([core, across, pair])
    columns = w_gate.shape[0]
    cut = pl.cdiv(columns, TILE) * HALF

    def core_copy(i):
        return remote(part.at[i, pl.ds(HALF, HALF)], from_core.at[i], cs, i, core)

    def y_copy(h):
        return remote(part.at[h, pl.ds(0, HALF)], from_y.at[h], ys, h, across)

    def z_copy(i):
        return remote(z_stage.at[i], z_land.at[i], zs, i, pair)

    def z_forward(i):
        return remote(z_land.at[i], c_land.at[i], cs, 8 + i, core)

    def step(i, carry):
        at = pl.ds(pl.multiple_of(i * TILE, TILE), TILE)
        m = middle[at, :]
        inverse = lax.rsqrt(jnp.mean(m * m, axis=-1, keepdims=True) + epsilon)
        n = (m * inverse * (1.0 + gain_in[...])).astype(bf16)
        normed[at, :] = n
        z_stage[i] = n[:HALF].astype(f32)
        z_copy(i).start()
        for lo, hi in ((0, cut), (cut, columns)):
            g = product_t(n, w_gate[lo:hi, :])
            u = product_t(n, w_up[lo:hi, :])
            inner[:, lo:hi] = (gelu_tanh(g) * u).astype(bf16)
        part[i] = product(inner[...], w_down[...])
        core_copy(i).start()
        core_copy(i).wait_recv()
        part[i, :HALF] = part[i, :HALF] + from_core[i]

        @pl.when(i < 2)
        def _():
            y_copy(i).start()

        return carry

    lax.fori_loop(0, 4, step, 0)
    for copy in loads:
        copy.wait()
    gain_grad[...] = jnp.zeros_like(gain_grad)
    gain = 1.0 + gain_out[...]

    def finish(i, dc):
        lo = i * TILE + dc * HALF
        o, g = out[lo : lo + HALF, :], dy[lo : lo + HALF, :].astype(f32)
        inverse = lax.rsqrt(jnp.mean(o * o, axis=-1, keepdims=True) + epsilon)
        hat = o * inverse
        scaled = g * gain
        d = (inverse * (scaled - hat * jnp.mean(scaled * hat, axis=-1, keepdims=True))).astype(bf16)
        d_out[lo : lo + HALF, :] = d
        if dc == 0:
            d_own[i] = d.astype(f32)
        gain_grad[...] = gain_grad[...] + jnp.sum((g * hat).reshape(HALF // 8, 8, g.shape[1]), axis=0)
        layer_out[pl.ds(tile_row(c, y, i, dc), HALF), :] = (middle[lo : lo + HALF, :] + hat * gain).astype(bf16)

    def spread_y(h):
        return remote(out.at[pl.ds((2 + h) * TILE, HALF)], out.at[pl.ds(h * TILE, HALF)], ys, 2 + h, across)

    def spread_core(i):
        return remote(out.at[pl.ds(i * TILE, HALF)], out.at[pl.ds(i * TILE + HALF, HALF)], cs, 4 + i, core)

    for h in range(2):
        y_copy(h).wait_recv()
        lo = (2 + h) * TILE
        out[lo : lo + HALF, :] = part[2 + h, :HALF] + from_y[h]
        spread_y(h).start()
        spread_core(2 + h).start()
        finish(2 + h, 0)
        z_copy(h).wait_recv()
        z_forward(h).start()
    for h in range(2):
        spread_core(2 + h).wait_recv()
        finish(2 + h, 1)
    for h in range(2):
        spread_y(h).wait_recv()
        spread_core(h).start()
        finish(h, 0)
        z_copy(2 + h).wait_recv()
        z_forward(2 + h).start()
        spread_core(h).wait_recv()
        finish(h, 1)
    for i in range(4):
        z_forward(i).wait_recv()
        normed_other[i * TILE : i * TILE + HALF, :] = z_land[i].astype(bf16)
        normed_other[i * TILE + HALF : (i + 1) * TILE, :] = c_land[i].astype(bf16)
    for i in range(4):
        core_copy(i).wait_send()
        z_copy(i).wait_send()
        z_forward(i).wait_send()
        spread_core(i).wait_send()
    for h in range(2):
        y_copy(h).wait_send()
        spread_y(h).wait_send()


def dma(*counts):
    return [pltpu.SemaphoreType.DMA((n,)) for n in counts]


def feed_forward(nx, middle, cotangent, gain_in, gain_out, w_gate, w_up, w_down):
    length, width = middle.shape
    columns = w_gate.shape[0]
    rows_low = jax.ShapeDtypeStruct((length, width), bf16)
    return pl.pallas_call(
        functools.partial(forward_kernel, nx),
        out_shape=(
            rows_low,
            rows_low,
            rows_low,
            jax.ShapeDtypeStruct((4, HALF, width), f32),
            rows_low,
            jax.ShapeDtypeStruct((8, width), f32),
        ),
        in_specs=[VMEM, ANY] + [VMEM] * 5,
        out_specs=(VMEM,) * 6,
        scratch_shapes=[
            pltpu.VMEM((length, width), f32),
            pltpu.VMEM((length, width), bf16),
            pltpu.VMEM((TILE, columns), bf16),
            pltpu.VMEM((4, TILE, width), f32),
            pltpu.VMEM((4, HALF, width), f32),
            pltpu.VMEM((2, HALF, width), f32),
            pltpu.VMEM((4, HALF, width), f32),
            pltpu.VMEM((4, HALF, width), f32),
            pltpu.VMEM((4, HALF, width), f32),
        ]
        + dma(8, 12, 12, 4, 4, 4, 4),
        compiler_params=pltpu.CompilerParams(collective_id=0, has_side_effects=True, vmem_limit_bytes=62 << 20),
        name="feed_forward",
    )(middle, cotangent, gain_in.reshape(1, -1), gain_out.reshape(1, -1), w_gate, w_up, w_down)


def back_kernel(
    nx,
    d_out_hbm,
    d_own_hbm,
    normed_hbm,
    other_hbm,
    w_gate_hbm,
    w_up_hbm,
    w_down_hbm,
    w_out_hbm,
    middle_hbm,
    branch_hbm,
    dy_hbm,
    gain_in,
    gain_branch,
    d_other,
    pair_in,
    pair_gates,
    grad_context,
    d_branch_out,
    d_middle_out,
    gain_grads,
    d_out,
    normed,
    other,
    w_gate,
    w_up,
    w_down,
    w_out,
    middle,
    branch,
    dy,
    gates,
    ups,
    inner,
    part,
    from_core,
    from_y,
    z_land,
    c_land,
    heads_c,
    heads_y,
    got_c,
    got_y,
    loads_sem,
    stores_sem,
    c_send,
    c_recv,
    y_send,
    y_recv,
    z_send,
    z_recv,
):
    z, x, y, c, near = spots(nx)
    core, across, pair = near["c"], near["y"], near["z1"]
    cs, ys, zs = (c_send, c_recv), (y_send, y_recv), (z_send, z_recv)
    parity = z % 2
    real, columns = w_gate_hbm.shape[0], w_gate.shape[0]
    half = columns // 2
    head = heads_c.shape[2]
    own_row = pl.multiple_of((c * 2 + y) * QUARTER, QUARTER)
    sources = [
        (d_out_hbm, d_out),
        (normed_hbm, normed),
        (w_gate_hbm, w_gate.at[pl.ds(0, real)]),
        (w_up_hbm, w_up.at[pl.ds(0, real)]),
        (w_down_hbm, w_down.at[pl.ds(0, real)]),
        (other_hbm, other),
        (w_out_hbm, w_out),
        (middle_hbm.at[pl.ds(2 * TILE, HALF)], middle.at[pl.ds(0, HALF)]),
        (middle_hbm.at[pl.ds(3 * TILE, HALF)], middle.at[pl.ds(HALF, HALF)]),
        (branch_hbm, branch),
        (dy_hbm.at[pl.ds(own_row, QUARTER)], dy),
    ]
    loads = [pltpu.make_async_copy(src, dst, loads_sem.at[k]) for k, (src, dst) in enumerate(sources)]
    for copy in loads:
        copy.start()
    if real < columns:
        for ref in (w_gate, w_up, w_down):
            ref[real:, :] = jnp.zeros((columns - real, ref.shape[1]), bf16)
    greet([core, across, pair])

    def core_copy(i):
        return remote(part.at[i, pl.ds(HALF, HALF)], from_core.at[i], cs, i, core)

    def y_copy(h):
        return remote(part.at[h, pl.ds(0, HALF)], from_y.at[h], ys, h, across)

    def z_copy(i):
        return remote(d_own_hbm.at[i], z_land.at[i], zs, i, pair)

    def z_forward(i):
        return remote(z_land.at[i], c_land.at[i], cs, 4 + i, core)

    for i in range(4):
        z_copy(i).start()
    for copy in loads[:5]:
        copy.wait()

    mine = pl.multiple_of(parity * half, HALF)

    def stores(i, base):
        slot = i % 2
        at = pl.ds(pl.multiple_of(base + i * TILE, TILE), TILE)
        pick = pl.ds(mine, half)
        return [
            pltpu.make_async_copy(inner.at[slot, :, pick], pair_in.at[at], stores_sem.at[slot, 0]),
            pltpu.make_async_copy(gates.at[slot, :, pick], pair_gates.at[at, pl.ds(0, half)], stores_sem.at[slot, 1]),
            pltpu.make_async_copy(ups.at[slot, :, pick], pair_gates.at[at, pl.ds(half, half)], stores_sem.at[slot, 2]),
        ]

    def piece(n, d, slot, at):
        g = product_t(n, w_gate[at, :])
        u = product_t(n, w_up[at, :])
        di = product_t(d, w_down[at, :])
        act, slope = gelu_parts(g)
        inner[slot, :, at] = (act * u).astype(bf16)
        gates[slot, :, at] = (di * u * slope).astype(bf16)
        ups[slot, :, at] = (di * act).astype(bf16)

    def own_tile(i, carry):
        at = pl.ds(pl.multiple_of(i * TILE, TILE), TILE)
        slot = i % 2

        @pl.when(i >= 2)
        def _():
            for copy in stores(i - 2, 0):
                copy.wait()

        n, d = normed[at, :], d_out[at, :]
        for lo in range(0, columns, TILE):
            piece(n, d, slot, pl.ds(lo, TILE))
        for copy in stores(i, 0):
            copy.start()
        part[i] = product(gates[slot], w_gate[...]) + product(ups[slot], w_up[...])
        core_copy(i).start()
        core_copy(i).wait_recv()
        part[i, :HALF] = part[i, :HALF] + from_core[i]

        @pl.when(i < 2)
        def _():
            y_copy(i).start()

        return carry

    lax.fori_loop(0, 4, own_tile, 0)
    for copy in loads[5:]:
        copy.wait()

    def other_tile(i, carry):
        slot = i % 2
        z_copy(i).wait_recv()
        z_forward(i).start()

        @pl.when(i < 2)
        def _():
            for copy in stores(i + 2, 0):
                copy.wait()

        @pl.when(i >= 2)
        def _():
            for copy in stores(i - 2, d_out.shape[0]):
                copy.wait()

        z_forward(i).wait_recv()
        lo = pl.multiple_of(i * TILE, TILE)
        d_other[pl.ds(lo, HALF), :] = z_land[i].astype(bf16)
        d_other[pl.ds(lo + HALF, HALF), :] = c_land[i].astype(bf16)
        n, d = other[pl.ds(lo, TILE), :], d_other[pl.ds(lo, TILE), :]
        for off in range(0, half, TILE):
            size = min(TILE, half - off)
            piece(n, d, slot, pl.ds(pl.multiple_of(mine + off, HALF), size))
        for copy in stores(i, d_out.shape[0]):
            copy.start()
        return carry

    lax.fori_loop(0, 2, other_tile, 0)

    gain_grads[...] = jnp.zeros_like(gain_grads)

    def fold(a):
        return jnp.sum(a.reshape(a.shape[0] // 8, 8, a.shape[1]), axis=0)

    for h in range(2):
        y_copy(h).wait_recv()
        at = slice(h * HALF, (h + 1) * HALF)
        grad = part[2 + h, :HALF] + from_y[h]
        m = middle[at, :]
        inverse = lax.rsqrt(jnp.mean(m * m, axis=-1, keepdims=True) + epsilon)
        hat = m * inverse
        scaled = grad * (1.0 + gain_in[...])
        d_middle = dy[at, :].astype(f32) + inverse * (scaled - hat * jnp.mean(scaled * hat, axis=-1, keepdims=True))
        gain_grads[0] = gain_grads[0] + fold(grad * hat)
        d_middle_out[at, :] = d_middle
        b = branch[at, :]
        inverse = lax.rsqrt(jnp.mean(b * b, axis=-1, keepdims=True) + epsilon)
        hat = b * inverse
        scaled = d_middle * (1.0 + gain_branch[...])
        d_low = (inverse * (scaled - hat * jnp.mean(scaled * hat, axis=-1, keepdims=True))).astype(bf16)
        gain_grads[1] = gain_grads[1] + fold(d_middle * hat)
        d_branch_out[at, :] = d_low.astype(f32)
        for k, (ref, slot) in enumerate([(None, 0), (heads_y, 0), (heads_c, 0), (heads_c, 1)]):
            piece_of = product_t(d_low, w_out[k * head : (k + 1) * head, :]).astype(bf16)
            if ref is None:
                grad_context[pl.ds(own_row + h * HALF, HALF), :] = piece_of
            else:
                ref[slot, at, :] = piece_of.astype(f32)
    to_core = remote(heads_c, got_c, cs, 8, core)
    to_core.start()
    to_core.wait_recv()
    heads_y[1] = got_c[1]
    to_y = remote(heads_y, got_y, ys, 2, across)
    to_y.start()
    grad_context[pl.ds(pl.multiple_of(((c ^ 1) * 2 + y) * QUARTER, QUARTER), QUARTER), :] = got_c[0].astype(bf16)

    lax.fori_loop(2, 4, other_tile, 0)
    to_y.wait_recv()
    grad_context[pl.ds(pl.multiple_of((c * 2 + (y ^ 1)) * QUARTER, QUARTER), QUARTER), :] = got_y[0].astype(bf16)
    grad_context[pl.ds(pl.multiple_of(((c ^ 1) * 2 + (y ^ 1)) * QUARTER, QUARTER), QUARTER), :] = got_y[1].astype(bf16)
    for i in (2, 3):
        for copy in stores(i, d_out.shape[0]):
            copy.wait()
    for i in range(4):
        core_copy(i).wait_send()
        z_copy(i).wait_send()
        z_forward(i).wait_send()
    for h in range(2):
        y_copy(h).wait_send()
    to_core.wait_send()
    to_y.wait_send()


def feed_back(nx, d_out, d_own, normed, other, w_gate, w_up, w_down, w_out, middle, branch, dy, gain_in, gain_branch):
    length, width = d_out.shape
    columns = pl.cdiv(w_gate.shape[0], TILE) * TILE
    head = w_out.shape[0] // 4
    return pl.pallas_call(
        functools.partial(back_kernel, nx),
        out_shape=(
            jax.ShapeDtypeStruct((length, width), bf16),
            jax.ShapeDtypeStruct((2 * length, columns // 2), bf16),
            jax.ShapeDtypeStruct((2 * length, columns), bf16),
            jax.ShapeDtypeStruct((length, head), bf16),
            jax.ShapeDtypeStruct((QUARTER, width), f32),
            jax.ShapeDtypeStruct((QUARTER, width), f32),
            jax.ShapeDtypeStruct((2, 8, width), f32),
        ),
        in_specs=[ANY] * 11 + [VMEM] * 2,
        out_specs=(VMEM, ANY, ANY) + (VMEM,) * 4,
        scratch_shapes=[
            pltpu.VMEM((length, width), bf16),
            pltpu.VMEM((length, width), bf16),
            pltpu.VMEM((length, width), bf16),
            pltpu.VMEM((columns, width), bf16),
            pltpu.VMEM((columns, width), bf16),
            pltpu.VMEM((columns, width), bf16),
            pltpu.VMEM((4 * head, width), bf16),
            pltpu.VMEM((QUARTER, width), f32),
            pltpu.VMEM((QUARTER, width), f32),
            pltpu.VMEM((QUARTER, width), bf16),
            pltpu.VMEM((2, TILE, columns), bf16),
            pltpu.VMEM((2, TILE, columns), bf16),
            pltpu.VMEM((2, TILE, columns), bf16),
            pltpu.VMEM((4, TILE, width), f32),
            pltpu.VMEM((4, HALF, width), f32),
            pltpu.VMEM((2, HALF, width), f32),
            pltpu.VMEM((4, HALF, width), f32),
            pltpu.VMEM((4, HALF, width), f32),
            pltpu.VMEM((2, QUARTER, head), f32),
            pltpu.VMEM((2, QUARTER, head), f32),
            pltpu.VMEM((2, QUARTER, head), f32),
            pltpu.VMEM((2, QUARTER, head), f32),
            pltpu.SemaphoreType.DMA((11,)),
            pltpu.SemaphoreType.DMA((2, 3)),
        ]
        + dma(9, 9, 3, 3, 4, 4),
        compiler_params=pltpu.CompilerParams(collective_id=1, has_side_effects=True, vmem_limit_bytes=62 << 20),
        name="feed_back",
    )(
        d_out,
        d_own,
        normed,
        other,
        w_gate,
        w_up,
        w_down,
        w_out,
        middle,
        branch,
        dy,
        gain_in.reshape(1, -1),
        gain_branch.reshape(1, -1),
    )


def attention_kernel(
    nx,
    tokens,
    w_query,
    w_key,
    w_value,
    w_out,
    segment_col,
    segment_row,
    gain_in,
    gain_query,
    gain_key,
    gain_out,
    normed,
    query,
    keys,
    values,
    query_raw,
    keys_raw,
    log_total,
    context,
    w_out_all,
    middle,
    branch,
    out_own,
    out_land,
    context_own,
    context_core,
    context_land,
    context_all,
    c_send,
    c_recv,
    y_send,
    y_recv,
    x_send,
    x_recv,
):
    z, x, y, c, near = spots(nx)
    cs, ys, xs = (c_send, c_recv), (y_send, y_recv), (x_send, x_recv)
    length, width = tokens.shape
    head = w_query.shape[1]
    out_own[...] = w_out[...].astype(f32)
    greet([near[k] for k in ("c", "y", "x")])
    mine = pl.ds(pl.multiple_of(x * (head // 2), 8), head // 2)
    out_y = remote(out_own.at[mine], out_land.at[0, mine], ys, 0, near["y"])
    out_x = remote(out_land.at[0, mine], out_land.at[0, mine], xs, 0, near["x"])
    out_c = remote(out_own, out_land.at[1], cs, 0, near["c"])
    out_yc = remote(out_land.at[0], out_land.at[2], cs, 1, near["c"])
    out_y.start()
    out_c.start()
    w_out_all[:head, :] = w_out[...]

    def norm(v, gain):
        return v * lax.rsqrt(jnp.mean(v * v, axis=-1, keepdims=True) + epsilon) * (1.0 + gain)

    def inputs(i, carry):
        at = pl.ds(pl.multiple_of(i * TILE, TILE), TILE)
        n = norm(tokens[at, :].astype(f32), gain_in[...]).astype(bf16)
        normed[at, :] = n
        raw = product(n, w_query[...])
        query_raw[at, :] = raw
        query[at, :] = norm(raw, gain_query[...]).astype(bf16)
        raw = product(n, w_key[...])
        keys_raw[at, :] = raw
        keys[at, :] = norm(raw, gain_key[...]).astype(bf16)
        values[at, :] = product(n, w_value[...]).astype(bf16)
        return carry

    lax.fori_loop(0, length // TILE, inputs, 0)
    for i in range(length // TILE):
        at, seen = slice(i * TILE, (i + 1) * TILE), (i + 1) * TILE
        s = product_t(query[at, :], keys[:seen, :]) * score_scale
        row = lax.broadcasted_iota(jnp.int32, s.shape, 0) + i * TILE
        col = lax.broadcasted_iota(jnp.int32, s.shape, 1)
        visible = (row >= col) & (segment_col[at, :] == segment_row[:, :seen])
        s = jnp.where(visible, s, -1e30)
        largest = jnp.max(s, axis=-1, keepdims=True)
        e = jnp.exp(s - largest)
        total = jnp.sum(e, axis=-1, keepdims=True)
        log_total[at, :] = largest + jnp.log(total)
        low_context = product((e / total).astype(bf16), values[:seen, :]).astype(bf16)
        context[at, :] = low_context
        context_own[at, :] = low_context.astype(f32)

    span = length // 2
    to_core = remote(context_own.at[pl.ds(pl.multiple_of((1 - c) * span, span), span)], context_core, cs, 2, near["c"])
    to_core.start()

    def local(i, other):
        dy = 1 - i // 2
        return pl.multiple_of(((y ^ other) ^ dy) * QUARTER + (i % 2) * HALF, HALF)

    def context_copy(i, k):
        if k == 0:
            src = context_own.at[pl.ds(pl.multiple_of(c * span + local(i, 1), HALF), HALF)]
        else:
            src = context_core.at[pl.ds(local(i, 1), HALF)]
        return remote(src, context_land.at[k, i], ys, 1 + 2 * i + k, near["y"])

    context_copy(0, 0).start()
    out_y.wait_recv()
    out_x.start()
    to_core.wait_recv()
    for i in range(4):
        for k in range(2):
            if i + k > 0:
                context_copy(i, k).start()
    out_c.wait_recv()
    w_out_all[2 * head : 3 * head, :] = out_land[1].astype(bf16)
    for i in range(4):
        rows = pl.ds(i * HALF, HALF)
        context_all[rows, :head] = context[pl.ds(pl.multiple_of(c * span + local(i, 0), HALF), HALF), :]
        context_all[rows, 2 * head : 3 * head] = context_core[pl.ds(local(i, 0), HALF), :].astype(bf16)
    out_x.wait_recv()
    out_yc.start()
    w_out_all[head : 2 * head, :] = out_land[0].astype(bf16)
    out_yc.wait_recv()
    w_out_all[3 * head :, :] = out_land[2].astype(bf16)

    def middle_copy(i):
        at = pl.multiple_of(i * TILE, TILE)
        return remote(middle.at[pl.ds(at, HALF)], middle.at[pl.ds(at + HALF, HALF)], cs, 3 + i, near["c"])

    for i in range(4):
        rows = pl.ds(i * HALF, HALF)
        context_copy(i, 0).wait_recv()
        context_all[rows, head : 2 * head] = context_land[0, i].astype(bf16)
        context_copy(i, 1).wait_recv()
        context_all[rows, 3 * head :] = context_land[1, i].astype(bf16)
        b = product(context_all[rows, :], w_out_all[...])
        if i >= 2:
            branch[(i - 2) * HALF : (i - 1) * HALF, :] = b
        hidden = tokens[pl.ds(pl.multiple_of(c * span + local(i, 0), HALF), HALF), :].astype(f32)
        middle[i * TILE : i * TILE + HALF, :] = hidden + norm(b, gain_out[...])
        middle_copy(i).start()
    for i in range(4):
        middle_copy(i).wait()
        for k in range(2):
            context_copy(i, k).wait_send()
    for copy in (out_y, out_x, out_c, out_yc, to_core):
        copy.wait_send()


def attend(nx, tokens, w_query, w_key, w_value, w_out, segment_ids, gain_in, gain_query, gain_key, gain_out):
    length, width = tokens.shape
    head = w_query.shape[1]
    of_head = jax.ShapeDtypeStruct((length, head), bf16)
    raw = jax.ShapeDtypeStruct((length, head), f32)
    return pl.pallas_call(
        functools.partial(attention_kernel, nx),
        out_shape=(
            jax.ShapeDtypeStruct((length, width), bf16),
            of_head,
            of_head,
            of_head,
            raw,
            raw,
            jax.ShapeDtypeStruct((length, 1), f32),
            of_head,
            jax.ShapeDtypeStruct((4 * head, width), bf16),
            jax.ShapeDtypeStruct((length, width), f32),
            jax.ShapeDtypeStruct((QUARTER, width), f32),
        ),
        in_specs=[VMEM] * 11,
        out_specs=(VMEM,) * 11,
        scratch_shapes=[
            pltpu.VMEM((head, width), f32),
            pltpu.VMEM((3, head, width), f32),
            pltpu.VMEM((length, head), f32),
            pltpu.VMEM((length // 2, head), f32),
            pltpu.VMEM((2, 4, HALF, head), f32),
            pltpu.VMEM((length // 2, 4 * head), bf16),
        ]
        + dma(7, 7, 9, 9, 1, 1),
        compiler_params=pltpu.CompilerParams(collective_id=3, has_side_effects=True, vmem_limit_bytes=48 << 20),
        name="attend",
    )(
        tokens,
        w_query,
        w_key,
        w_value,
        w_out,
        segment_ids.reshape(length, 1),
        segment_ids.reshape(1, length),
        gain_in.reshape(1, width),
        gain_query.reshape(1, head),
        gain_key.reshape(1, head),
        gain_out.reshape(1, width),
    )


def reduce_kernel(
    nx,
    d_out_hbm,
    d_other_hbm,
    normed_hbm,
    other_hbm,
    pair_in_hbm,
    pair_gates_hbm,
    d_branch_hbm,
    d_middle_hbm,
    tokens_hbm,
    normed_in_hbm,
    query_hbm,
    keys_hbm,
    values_hbm,
    query_raw_hbm,
    keys_raw_hbm,
    context_hbm,
    grad_context_hbm,
    w_qkv_hbm,
    log_total,
    segment_col,
    segment_row,
    gain_in,
    gain_query,
    gain_key,
    gains_so_far,
    ff_out,
    attn_out,
    kv_out,
    input_grad,
    gains,
    dw,
    x_land,
    z2_land,
    z1_land,
    from_core,
    from_y,
    branch_land,
    input_own,
    input_land,
    d_qkv,
    attn,
    attn_z1,
    attn_x,
    attn_z2,
    kv_core,
    kv_across,
    kv_own,
    kv_y,
    kv_wide,
    kv_wide_core,
    gains_land,
    loads,
    c_send,
    c_recv,
    y_send,
    y_recv,
    x_send,
    x_recv,
    z2_send,
    z2_recv,
    z1_send,
    z1_recv,
):
    z, x, y, c, near = spots(nx)
    zh, zl = z // 2, z % 2
    cs, ys, xs = (c_send, c_recv), (y_send, y_recv), (x_send, x_recv)
    z2s, z1s = (z2_send, z2_recv), (z1_send, z1_recv)
    length, width = d_out_hbm.shape
    half = pair_in_hbm.shape[1]
    head = query_hbm.shape[1]
    blk = x_land.shape[1]
    own_row = pl.multiple_of((c * 2 + y) * QUARTER, QUARTER)

    def block(a, b):
        return pl.ds(pl.multiple_of(b * blk, 8), blk)

    def quarter_rows(dc, dy):
        return pl.ds(pl.multiple_of(((c ^ dc) * 2 + (y ^ dy)) * QUARTER, QUARTER), QUARTER)

    greet([near[k] for k in ("c", "y", "x", "z2", "z1")])

    branch_y = remote(d_branch_hbm, branch_land.at[0], ys, 0, near["y"])
    branch_c = remote(d_branch_hbm, branch_land.at[1], cs, 0, near["c"])
    branch_fwd = remote(branch_land.at[0], branch_land.at[2], cs, 1, near["c"])
    branch_y.start()
    branch_c.start()

    def owner(j):
        return 2 * jnp.where(j < 2, 1 - zh, zh) + j % 2

    def x_copy(m, j):
        return remote(dw.at[m, block(dw, owner(j) * 2 + (1 - x))], x_land.at[m * 4 + j], xs, m * 4 + j, near["x"])

    def z2_copy(m, k):
        return remote(dw.at[m, block(dw, owner(k) * 2 + x)], z2_land.at[m * 2 + k], z2s, m * 2 + k, near["z2"])

    def z1_copy(m):
        return remote(dw.at[m, block(dw, (2 * zh + 1 - zl) * 2 + x)], z1_land.at[m], z1s, m, near["z1"])

    def far(m):
        for k in range(2):
            x_copy(m, k).wait_recv()
            rows = block(dw, owner(k) * 2 + x)
            dw[m, rows, :] = dw[m, rows, :] + x_land[m * 4 + k]
            z2_copy(m, k).start()

    def close(m):
        for k in range(2):
            x_copy(m, 2 + k).wait_recv()
            z2_copy(m, k).wait_recv()
            rows = block(dw, owner(2 + k) * 2 + x)
            dw[m, rows, :] = dw[m, rows, :] + x_land[m * 4 + 2 + k] + z2_land[m * 2 + k]
        z1_copy(m).start()
        ff_out[m, zl] = dw[m, block(dw, (2 * zh + zl) * 2 + x), :]

    def copies(pairs):
        started = [pltpu.make_async_copy(src, dst, loads.at[k]) for k, (src, dst) in enumerate(pairs)]
        for copy in started:
            copy.start()
        return started

    def weights(left, right):
        step = 3 * HALF

        def form(m, lo):
            def one(r, carry):
                cols = pl.ds(pl.multiple_of(r * step, HALF), step)
                dw[m, cols, :] = t_product(left[:, cols], right[:, lo : lo + half])
                return carry

            lax.fori_loop(0, width // step, one, 0)
            for k in range(2):
                x_copy(m, k).start()

        for copy in copies(
            [
                (d_out_hbm, left.at[pl.ds(0, length)]),
                (d_other_hbm, left.at[pl.ds(length, length)]),
                (pair_in_hbm, right.at[:, pl.ds(0, half)]),
            ]
        ):
            copy.wait()
        form(0, 0)
        for copy in copies(
            [
                (normed_hbm, left.at[pl.ds(0, length)]),
                (other_hbm, left.at[pl.ds(length, length)]),
                (pair_gates_hbm, right),
            ]
        ):
            copy.wait()
        form(1, 0)
        form(2, half)
        for m in range(2):
            for k in range(2):
                x_copy(m, 2 + k).start()

    pl.run_scoped(weights, pltpu.VMEM((2 * length, width), bf16), pltpu.VMEM((2 * length, 2 * half), bf16))

    gains[...] = gains_so_far[...]

    def back_norm(raw, gain, grad):
        inverse = lax.rsqrt(jnp.mean(raw * raw, axis=-1, keepdims=True) + epsilon)
        hat = raw * inverse
        scaled = grad * (1.0 + gain)
        return inverse * (scaled - hat * jnp.mean(scaled * hat, axis=-1, keepdims=True)), grad * hat

    def attention(query, keys, values, query_raw, keys_raw, grad_context, d_keys, d_values):
        for copy in copies(
            [
                (query_hbm, query),
                (keys_hbm, keys),
                (values_hbm, values),
                (query_raw_hbm, query_raw),
                (keys_raw_hbm, keys_raw),
                (grad_context_hbm, grad_context),
            ]
        ):
            copy.wait()
        d_keys[...] = jnp.zeros_like(d_keys)
        d_values[...] = jnp.zeros_like(d_values)
        for i in range(length // TILE):
            at, seen = slice(i * TILE, (i + 1) * TILE), (i + 1) * TILE
            q, k = query[at, :], keys[:seen, :]
            s = product_t(q, k) * score_scale
            row = lax.broadcasted_iota(jnp.int32, s.shape, 0) + i * TILE
            col = lax.broadcasted_iota(jnp.int32, s.shape, 1)
            visible = (row >= col) & (segment_col[at, :] == segment_row[:, :seen])
            p = jnp.exp(jnp.where(visible, s, -1e30) - log_total[at, :])
            g = grad_context[at, :]
            dp = product_t(g, values[:seen, :])
            balance = jnp.sum(dp * p, axis=-1, keepdims=True)
            ds = (p * (dp - balance)).astype(bf16)
            dq, of_gain = back_norm(query_raw[at, :], gain_query[...], product(ds, k) * score_scale)
            d_qkv[at, :head] = dq.astype(bf16)
            gains[4:5, :head] = gains[4:5, :head] + jnp.sum(of_gain, axis=0, keepdims=True)
            d_keys[:seen, :] = d_keys[:seen, :] + t_product(ds, q)
            d_values[:seen, :] = d_values[:seen, :] + t_product(p.astype(bf16), g)
        for i in range(length // TILE):
            at = slice(i * TILE, (i + 1) * TILE)
            dk, of_gain = back_norm(keys_raw[at, :], gain_key[...], d_keys[at, :] * score_scale)
            d_qkv[at, head : 2 * head] = dk.astype(bf16)
            gains[5:6, :head] = gains[5:6, :head] + jnp.sum(of_gain, axis=0, keepdims=True)
            d_qkv[at, 2 * head :] = d_values[at, :].astype(bf16)

    pl.run_scoped(
        attention,
        pltpu.VMEM((length, head), bf16),
        pltpu.VMEM((length, head), bf16),
        pltpu.VMEM((length, head), bf16),
        pltpu.VMEM((length, head), f32),
        pltpu.VMEM((length, head), f32),
        pltpu.VMEM((length, head), bf16),
        pltpu.VMEM((length, head), f32),
        pltpu.VMEM((length, head), f32),
    )
    far(0)

    def attn_z1_copy(i):
        b = (2 * (i // 2) + 1 - zl) * 2 + i % 2
        return remote(attn.at[block(attn, b)], attn_z1.at[i], z1s, 3 + i, near["z1"])

    def attn_x_copy(j):
        b = (2 * (zh ^ j) + zl) * 2 + 1 - x
        return remote(attn.at[block(attn, b)], attn_x.at[j], xs, 12 + j, near["x"])

    attn_z2_copy = remote(attn.at[block(attn, (2 * (1 - zh) + zl) * 2 + x)], attn_z2, z2s, 6, near["z2"])

    input_y = remote(input_own, input_land.at[0], ys, 4, near["y"])
    input_c = remote(input_own, input_land.at[1], cs, 7, near["c"])
    input_fwd = remote(input_land.at[0], input_land.at[2], cs, 8, near["c"])

    def rest(w_qkv, part, kv_halves):
        for copy in copies([(w_qkv_hbm, w_qkv)]):
            copy.wait()

        def core_copy(i):
            return remote(part.at[i, pl.ds(HALF, HALF)], from_core.at[i], cs, 2 + i, near["c"])

        def y_copy(h):
            return remote(part.at[h, pl.ds(0, HALF)], from_y.at[h], ys, 1 + h, near["y"])

        def tile(i, carry):
            for dc in range(2):
                rows = d_qkv[pl.ds(tile_row(c, y, i, dc), HALF), :]
                part[i, dc * HALF : (dc + 1) * HALF] = product_t(rows, w_qkv[...])
            core_copy(i).start()
            core_copy(i).wait_recv()
            part[i, :HALF] = part[i, :HALF] + from_core[i]

            @pl.when(i < 2)
            def _():
                y_copy(i).start()

            return carry

        lax.fori_loop(0, 4, tile, 0)

        def of_inputs(normed_in, kv):
            for copy in copies([(normed_in_hbm, normed_in)]):
                copy.wait()
            for k in range(2):
                kv[k] = t_product(normed_in[...], d_qkv[:, (1 + k) * head : (2 + k) * head])
            to_core = remote(kv.at[1 - c], kv_core, cs, 6, near["c"])
            to_core.start()
            attn[:, :head] = t_product(normed_in[...], d_qkv[:, :head])
            to_core.wait_recv()
            for k in range(2):
                lanes = slice(k * (head // 2), (k + 1) * (head // 2))
                kv_halves[k] = kv[c, :, lanes] + kv_core[:, lanes]
            to_core.wait_send()

        pl.run_scoped(of_inputs, pltpu.VMEM((length, width), bf16), pltpu.VMEM((2, width, head), f32))
        to_y = remote(kv_halves.at[1 - y], kv_across, ys, 3, near["y"])
        to_y.start()

        def of_branch(context, d_branch, d_middle, tokens):
            waits = copies(
                [
                    (context_hbm, context),
                    (d_branch_hbm, d_branch),
                    (d_middle_hbm, d_middle),
                    (tokens_hbm.at[pl.ds(own_row, QUARTER)], tokens),
                ]
            )
            branch_y.wait_recv()
            branch_fwd.start()
            for copy in waits:
                copy.wait()
            acc = t_product(d_branch[...].astype(bf16), context[quarter_rows(0, 0), :])
            branch_c.wait_recv()
            branch_fwd.wait_recv()
            for k, (dc, dy) in enumerate([(0, 1), (1, 0), (1, 1)]):
                acc = acc + t_product(branch_land[k].astype(bf16), context[quarter_rows(dc, dy), :])
            attn[:, head : 2 * head] = acc
            far(1)
            for h in range(2):
                y_copy(h).wait_recv()
                at = slice(h * HALF, (h + 1) * HALF)
                grad = part[2 + h, :HALF] + from_y[h]
                d_in, of_gain = back_norm(tokens[at, :].astype(f32), gain_in[...], grad)
                gains[0:1, :] = gains[0:1, :] + jnp.sum(of_gain, axis=0, keepdims=True)
                d = (d_middle[at, :] + d_in).astype(bf16)
                input_grad[pl.ds(pl.multiple_of(own_row + h * HALF, HALF), HALF), :] = d
                input_own[at, :] = d.astype(f32)

        pl.run_scoped(
            of_branch,
            pltpu.VMEM((length, head), bf16),
            pltpu.VMEM((QUARTER, width), f32),
            pltpu.VMEM((QUARTER, width), f32),
            pltpu.VMEM((QUARTER, width), bf16),
        )
        input_y.start()
        input_c.start()
        far(2)
        to_y.wait_recv()
        attn[:, 2 * head :] = kv_halves[y] + kv_across[...]
        for i in range(4):
            attn_z1_copy(i).start()
        for i in range(4):
            core_copy(i).wait_send()
        for h in range(2):
            y_copy(h).wait_send()
        to_y.wait_send()

    pl.run_scoped(
        rest,
        pltpu.VMEM((width, 3 * head), bf16),
        pltpu.VMEM((4, TILE, width), f32),
        pltpu.VMEM((2, width, head // 2), f32),
    )

    for k, (sems, index, to) in enumerate([(cs, 10, "c"), (ys, 6, "y"), (xs, 14, "x"), (z2s, 7, "z2"), (z1s, 7, "z1")]):
        hop = remote(gains, gains_land.at[k], sems, index, near[to])
        hop.start()
        hop.wait()
        gains[...] = gains[...] + gains_land[k]

    close(0)
    for i in range(4):
        attn_z1_copy(i).wait_recv()
        rows = block(attn, (2 * (i // 2) + zl) * 2 + i % 2)
        attn[rows, :] = attn[rows, :] + attn_z1[i]
    for j in (1, 0):
        attn_x_copy(j).start()
    for k in range(2):
        x_copy(2, 2 + k).start()
    input_y.wait_recv()
    input_fwd.start()
    input_grad[quarter_rows(0, 1), :] = input_land[0].astype(bf16)
    input_c.wait_recv()
    input_grad[quarter_rows(1, 0), :] = input_land[1].astype(bf16)
    input_fwd.wait_recv()
    input_grad[quarter_rows(1, 1), :] = input_land[2].astype(bf16)
    close(1)
    for j in (1, 0):
        attn_x_copy(j).wait_recv()
        rows = block(attn, (2 * (zh ^ j) + zl) * 2 + x)
        attn[rows, :] = attn[rows, :] + attn_x[j]
        if j == 1:
            attn_z2_copy.start()
    attn_z2_copy.wait_recv()
    total = attn[block(attn, (2 * zh + zl) * 2 + x), :] + attn_z2[...]
    attn_out[...] = total[:, : 2 * head]
    kv_own[...] = total[:, 2 * head :]
    wide_y = remote(kv_own, kv_y, ys, 5, near["y"])
    wide_y.start()
    wide_y.wait_recv()
    kv_wide[:, : head // 2] = jnp.where(y == 0, kv_own[...], kv_y[...])
    kv_wide[:, head // 2 :] = jnp.where(y == 0, kv_y[...], kv_own[...])
    wide_c = remote(kv_wide, kv_wide_core, cs, 9, near["c"])
    wide_c.start()
    wide_c.wait_recv()
    kv_out[c] = kv_wide[...]
    kv_out[1 - c] = kv_wide_core[...]
    close(2)
    for m in range(3):
        z1_copy(m).wait_recv()
        ff_out[m, 1 - zl] = z1_land[m]
    for m in range(3):
        for j in range(4):
            x_copy(m, j).wait_send()
        for k in range(2):
            z2_copy(m, k).wait_send()
        z1_copy(m).wait_send()
    for i in range(4):
        attn_z1_copy(i).wait_send()
    for j in range(2):
        attn_x_copy(j).wait_send()
    for copy in (attn_z2_copy, branch_y, branch_c, branch_fwd, input_y, input_c, input_fwd, wide_y, wide_c):
        copy.wait_send()


def reduce_all(nx, dp_size, whole, small):
    length, width = whole[0].shape
    half = whole[4].shape[1]
    head = whole[10].shape[1]
    blk = width // dp_size
    return pl.pallas_call(
        functools.partial(reduce_kernel, nx),
        out_shape=(
            jax.ShapeDtypeStruct((3, 2, blk, half), f32),
            jax.ShapeDtypeStruct((blk, 2 * head), f32),
            jax.ShapeDtypeStruct((2, blk, head), f32),
            jax.ShapeDtypeStruct((length, width), bf16),
            jax.ShapeDtypeStruct((8, width), f32),
        ),
        in_specs=[ANY] * len(whole) + [VMEM] * len(small),
        out_specs=(VMEM,) * 5,
        scratch_shapes=[
            pltpu.VMEM((3, width, half), f32),
            pltpu.VMEM((12, blk, half), f32),
            pltpu.VMEM((6, blk, half), f32),
            pltpu.VMEM((3, blk, half), f32),
            pltpu.VMEM((4, HALF, width), f32),
            pltpu.VMEM((2, HALF, width), f32),
            pltpu.VMEM((3, QUARTER, width), f32),
            pltpu.VMEM((QUARTER, width), f32),
            pltpu.VMEM((3, QUARTER, width), f32),
            pltpu.VMEM((length, 3 * head), bf16),
            pltpu.VMEM((width, 2 * head + head // 2), f32),
            pltpu.VMEM((4, blk, 2 * head + head // 2), f32),
            pltpu.VMEM((2, blk, 2 * head + head // 2), f32),
            pltpu.VMEM((blk, 2 * head + head // 2), f32),
            pltpu.VMEM((width, head), f32),
            pltpu.VMEM((width, head // 2), f32),
            pltpu.VMEM((blk, head // 2), f32),
            pltpu.VMEM((blk, head // 2), f32),
            pltpu.VMEM((blk, head), f32),
            pltpu.VMEM((blk, head), f32),
            pltpu.VMEM((5, 8, width), f32),
        ]
        + dma(6, 11, 11, 7, 7, 15, 15, 8, 8, 8, 8),
        compiler_params=pltpu.CompilerParams(collective_id=2, has_side_effects=True, vmem_limit_bytes=int(63.5 * 2**20)),
        name="reduce_all",
    )(*whole, *small)


def body(
    links,
    tokens,
    segment_ids,
    cotangent,
    w_query,
    w_key,
    w_value,
    w_out,
    w_gate,
    w_up,
    w_down,
    gain_attn_in,
    gain_attn_out,
    gain_ffn_in,
    gain_ffn_out,
    gain_query,
    gain_key,
):
    length, width = tokens.shape
    head = w_query.shape[1]
    columns = w_gate.shape[1]
    nx = links.nx
    blk = width // links.dp_size
    dp = lax.axis_index("dp")
    wg, wu = w_gate.T, w_up.T
    (
        normed_low,
        query_low,
        keys_low,
        values_low,
        query_raw,
        keys_raw,
        log_total,
        context_low,
        w_out_all,
        middle,
        branch,
    ) = attend(
        nx, tokens, w_query, w_key, w_value, w_out, segment_ids, gain_attn_in, gain_query, gain_key, gain_attn_out
    )
    normed_two, normed_other, d_out, d_own, layer_out, ffn_out_rows = feed_forward(
        nx, middle, cotangent, gain_ffn_in, gain_ffn_out, wg, wu, w_down
    )
    grad_ffn_out = jnp.sum(ffn_out_rows, axis=0)
    d_other, pair_in, pair_gates, grad_context, d_branch_own, d_middle, gain_rows = feed_back(
        nx,
        d_out,
        d_own,
        normed_two,
        normed_other,
        wg,
        wu,
        w_down,
        w_out_all,
        middle,
        branch,
        cotangent,
        gain_ffn_in,
        gain_attn_out,
    )
    gain_rows = jnp.sum(gain_rows, axis=1)
    grad_ffn_in, grad_attn_out = gain_rows[0], gain_rows[1]

    row = jnp.zeros((1, width), f32)
    so_far = jnp.concatenate(
        [row, grad_attn_out[None], grad_ffn_in[None], 0.25 * grad_ffn_out[None]] + [row] * 4, axis=0
    )
    ff, attn_sum, kv_sum, input_grad, gains = reduce_all(
        nx,
        links.dp_size,
        [
            d_out,
            d_other,
            normed_two,
            normed_other,
            pair_in,
            pair_gates,
            d_branch_own,
            d_middle,
            tokens,
            normed_low,
            query_low,
            keys_low,
            values_low,
            query_raw,
            keys_raw,
            context_low,
            grad_context,
            jnp.concatenate([w_query, w_key, w_value], axis=1),
        ],
        [
            log_total,
            segment_ids.reshape(length, 1),
            segment_ids.reshape(1, length),
            gain_attn_in.reshape(1, width),
            gain_query.reshape(1, head),
            gain_key.reshape(1, head),
            so_far,
        ],
    )
    ff = jnp.concatenate([ff[:, 0], ff[:, 1, :, : columns - ff.shape[3]]], axis=2)
    part = lax.dynamic_slice_in_dim(gains, dp * blk, blk, 1)
    hb = head // links.dp_size
    head_part = lax.dynamic_slice_in_dim(gains, dp * hb, hb, 1)
    return (
        layer_out,
        input_grad,
        attn_sum[:, :head],
        kv_sum[0],
        kv_sum[1],
        attn_sum[:, head:].T,
        ff[1],
        ff[2],
        ff[0].T,
        part[0],
        part[1],
        part[2],
        part[3],
        head_part[4],
        head_part[5],
    )


def body_any(
    links,
    tokens,
    segment_ids,
    cotangent,
    w_query,
    w_key,
    w_value,
    w_out,
    w_gate,
    w_up,
    w_down,
    gain_attn_in,
    gain_attn_out,
    gain_ffn_in,
    gain_ffn_out,
    gain_query,
    gain_key,
):
    length, width = tokens.shape
    head = w_query.shape[1]
    quarter = length // 4
    half_ff = w_gate.shape[1] // 2
    nx = links.nx
    blk = width // links.dp_size
    dp, t = lax.axis_index("dp"), lax.axis_index("tensor")
    z, x = dp // nx, dp % nx
    y, c = t // 2, t % 2
    parity = z % 2
    one = jnp.where(segment_ids[0] < length, 1.0, 0.5).astype(f32)

    def keep_low(a):
        return (a * one).astype(bf16)

    def place(dc, dy):
        return ((c ^ dc) * 2 + (y ^ dy)) * quarter

    def rows(a, dc, dy):
        return lax.dynamic_slice_in_dim(a, place(dc, dy), quarter, 0)

    def to_absolute(pieces):
        stack = jnp.stack([pieces[0][0], pieces[0][1], pieces[1][0], pieces[1][1]])
        mine = c * 2 + y
        return jnp.concatenate([lax.dynamic_index_in_dim(stack, mine ^ b, 0, keepdims=False) for b in range(4)], axis=0)

    out_own = w_out.astype(f32)
    out_y = links.y(out_own)
    out_c = links.core(out_own)
    out_yc = links.core(out_y)
    w_out_all = jnp.concatenate([w_out, keep_low(out_c), keep_low(out_y), keep_low(out_yc)], axis=0)

    wg_h = jnp.where(parity == 0, w_gate[:, :half_ff], w_gate[:, half_ff:])
    wu_h = jnp.where(parity == 0, w_up[:, :half_ff], w_up[:, half_ff:])
    wd_h = jnp.where(parity == 0, w_down[:half_ff], w_down[half_ff:])

    hidden_in = tokens.astype(f32)
    normed_low = low(rms_norm(hidden_in, gain_attn_in))
    query_raw = product(normed_low, w_query)
    keys_raw = product(normed_low, w_key)
    query_low = low(rms_norm(query_raw, gain_query))
    keys_low = low(rms_norm(keys_raw, gain_key))
    values_low = low(product(normed_low, w_value))
    places = jnp.arange(length)
    allowed = (places[:, None] >= places[None, :]) & (segment_ids[:, None] == segment_ids[None, :])

    def scores_of():
        raw = product_t(query_low, keys_low) * score_scale
        return jnp.where(allowed, raw, -1e30)

    scores = scores_of()
    largest = jnp.max(scores, axis=-1, keepdims=True)
    exponent = jnp.exp(scores - largest)
    total = jnp.sum(exponent, axis=-1, keepdims=True)
    log_total = largest + jnp.log(total)
    context_low = low(product(low(exponent / total), values_low))

    context = context_low.astype(f32)
    mine = jnp.concatenate([rows(context, 0, 1), rows(context, 0, 0)], axis=0)
    of_core = links.core(jnp.concatenate([rows(context, 1, 1), rows(context, 1, 0)], axis=0))
    of_y = links.y(jnp.concatenate([rows(context, 0, 0), rows(context, 0, 1)], axis=0))
    of_yc = links.y(jnp.concatenate([of_core[quarter:], of_core[:quarter]], axis=0))
    context_all = jnp.concatenate([low(mine), keep_low(of_core), keep_low(of_y), keep_low(of_yc)], axis=1)
    branch = product(context_all, w_out_all)
    hidden_rows = jnp.concatenate([rows(tokens, 0, 1), rows(tokens, 0, 0)], axis=0).astype(f32)
    middle_own = hidden_rows + rms_norm(branch, gain_attn_out)
    middle_core = links.core(middle_own)

    middles, normed_two, inners, parts = [], [], [], []
    saved = []
    for k in range(2):
        at = slice(k * quarter, (k + 1) * quarter)
        middle = jnp.concatenate([middle_own[at], middle_core[at]], axis=0)
        normed_k = low(rms_norm(middle, gain_ffn_in))
        gate, upward = product(normed_k, w_gate), product(normed_k, w_up)
        inner = low(activate(gate, upward))
        part = product(inner, w_down)
        middles.append(middle)
        normed_two.append(normed_k)
        saved.append((gate, upward))
        parts.append(part)
    normed_own = low(rms_norm(middle_own, gain_ffn_in)).astype(f32)
    other_own = links.z1(normed_own)
    other_core = links.core(other_own)
    normed_other = jnp.concatenate([keep_low(other_own), keep_low(other_core)], axis=0)

    def gather_quarters(parts):
        sums = [part[:quarter] + links.core(part[quarter:]) for part in parts]
        return sums[1] + links.y(sums[0])

    output_q = gather_quarters(parts)
    output_y = links.y(output_q)
    output_c = links.core(output_q)
    output_yc = links.core(output_y)
    outputs = [jnp.concatenate([output_y, output_yc], axis=0), jnp.concatenate([output_q, output_c], axis=0)]
    grad_out = cotangent.astype(f32)
    d_outputs, layer_pieces, grad_ffn_out = [], [], 0.0
    for k in range(2):
        dy_k = jnp.concatenate([rows(cotangent, 0, 1 - k), rows(cotangent, 1, 1 - k)], axis=0).astype(f32)
        layer_k = low(middles[k] + rms_norm(outputs[k], gain_ffn_out))
        d_k, gain_k = rms_back(outputs[k], gain_ffn_out, dy_k)
        grad_ffn_out = grad_ffn_out + gain_k
        d_outputs.append(low(d_k))
        layer_pieces.append(layer_k)
    layer_out = to_absolute(
        [
            [layer_pieces[1][:quarter], layer_pieces[0][:quarter]],
            [layer_pieces[1][quarter:], layer_pieces[0][quarter:]],
        ]
    )

    d_own_rows = [d[:quarter].astype(f32) for d in d_outputs]
    got_own = [links.z1(d_own_rows[1]), links.z1(d_own_rows[0])]
    got_core = [links.core(g) for g in got_own]
    d_other = jnp.concatenate(
        [keep_low(got_own[1]), keep_low(got_own[0]), keep_low(got_core[1]), keep_low(got_core[0])], axis=0
    )

    back_parts = []
    for k in range(2):
        gate, upward = saved[k]
        d_inner = product_t(d_outputs[k], w_down)
        _, pull = jax.vjp(activate, gate, upward)
        d_gate, d_up = pull(d_inner)
        back_parts.append(product_t(low(d_gate), w_gate) + product_t(low(d_up), w_up))
    d_normed_q = gather_quarters(back_parts)
    middle_q = middle_own[quarter:]
    branch_q = branch[quarter:]
    dy_q = rows(cotangent, 0, 0).astype(f32)
    d_mid, grad_ffn_in = rms_back(middle_q, gain_ffn_in, d_normed_q)
    d_middle = dy_q + d_mid
    d_branch, grad_attn_out = rms_back(branch_q, gain_attn_out, d_middle)
    d_branch_low = low(d_branch)
    d_context = low(product_t(d_branch_low, w_out_all)).astype(f32)
    heads = [d_context[:, i * head : (i + 1) * head] for i in range(4)]
    c_got = links.core(jnp.concatenate([heads[1], heads[3]], axis=1))
    y_got = links.y(jnp.concatenate([heads[2], c_got[:, head:]], axis=1))
    grad_context = keep_low(
        to_absolute([[heads[0], y_got[:, :head]], [c_got[:, :head], y_got[:, head:]]])
    )
    d_branch_own = d_branch_low.astype(f32)
    d_branch_y = links.y(d_branch_own)
    d_branch_c = links.core(d_branch_own)
    d_branch_yc = links.core(d_branch_y)
    d_branch_all = jnp.concatenate(
        [d_branch_low, keep_low(d_branch_y), keep_low(d_branch_c), keep_low(d_branch_yc)], axis=0
    )
    context_rel = jnp.concatenate(
        [rows(context_low, 0, 0), rows(context_low, 0, 1), rows(context_low, 1, 0), rows(context_low, 1, 1)], axis=0
    )
    grad_w_out_t = t_product(d_branch_all, context_rel)

    attn_prob = jnp.exp(scores_of() - log_total)
    prob_low = low(attn_prob)
    grad_prob = product_t(grad_context, values_low)
    grad_values = low(t_product(prob_low, grad_context))
    balance = jnp.sum(grad_prob * attn_prob, axis=-1, keepdims=True)
    grad_scores = low(attn_prob * (grad_prob - balance))
    grad_query_n = product(grad_scores, keys_low) * score_scale
    grad_keys_n = t_product(grad_scores, query_low) * score_scale
    d_query, grad_gain_query = rms_back(query_raw, gain_query, grad_query_n)
    d_keys, grad_gain_key = rms_back(keys_raw, gain_key, grad_keys_n)
    d_query, d_keys = low(d_query), low(d_keys)
    d_qkv = jnp.concatenate([d_query, d_keys, grad_values], axis=1)
    w_qkv = jnp.concatenate([w_query, w_key, w_value], axis=1)
    in_parts = []
    for k in range(2):
        rows_k = jnp.concatenate([rows(d_qkv, 0, 1 - k), rows(d_qkv, 1, 1 - k)], axis=0)
        in_parts.append(product_t(rows_k, w_qkv))
    d_normed_in = gather_quarters(in_parts)
    hidden_q = rows(tokens, 0, 0).astype(f32)
    d_in, grad_attn_in = rms_back(hidden_q, gain_attn_in, d_normed_in)
    input_q = low(d_middle + d_in)
    input_own = input_q.astype(f32)
    input_y = links.y(input_own)
    input_c = links.core(input_own)
    input_yc = links.core(input_y)
    input_grad = keep_low(to_absolute([[input_own, input_y], [input_c, input_yc]]))

    grad_qkv = t_product(normed_low, d_qkv)
    grad_w_query, grad_kv = grad_qkv[:, :head], grad_qkv[:, head:]
    kv_keep = jnp.where(c == 0, grad_kv[:, :head], grad_kv[:, head:])
    kv_send = jnp.where(c == 0, grad_kv[:, head:], grad_kv[:, :head])
    kv = kv_keep + links.core(kv_send)
    kv_half = head // 2
    kv_keep = jnp.where(y == 0, kv[:, :kv_half], kv[:, kv_half:])
    kv_send = jnp.where(y == 0, kv[:, kv_half:], kv[:, :kv_half])
    kv = kv_keep + links.y(kv_send)
    attn_grads = jnp.concatenate([grad_w_query, grad_w_out_t, kv], axis=1)

    normed_all = jnp.concatenate(
        [normed_two[0][:quarter], normed_two[1][:quarter], normed_two[0][quarter:], normed_two[1][quarter:], normed_other],
        axis=0,
    )
    d_all = jnp.concatenate(
        [d_outputs[0][:quarter], d_outputs[1][:quarter], d_outputs[0][quarter:], d_outputs[1][quarter:], d_other], axis=0
    )
    gate, upward = product(normed_all, wg_h), product(normed_all, wu_h)
    inner, pull = jax.vjp(activate, gate, upward)
    inner = low(inner)
    d_inner = product_t(d_all, wd_h)
    d_gate, d_up = pull(d_inner)
    ff_grads = [t_product(d_all, inner), t_product(normed_all, low(d_gate)), t_product(normed_all, low(d_up))]

    zh, zl = z // 2, z % 2

    def sum_x(grads, z_half):
        mine = lax.dynamic_index_in_dim(grads, z_half, 0, keepdims=False)
        acc = lax.dynamic_index_in_dim(mine, x, 1, keepdims=False)
        for step in range(1, nx):
            to = lax.dynamic_index_in_dim(mine, (x + step) % nx, 1, keepdims=False)
            acc = acc + links.x(to, step)
        return acc

    def scatter(grads):
        grads = grads.reshape(2, 2, nx, blk, grads.shape[1])
        far = sum_x(grads, 1 - zh)
        near = sum_x(grads, zh)
        return near + links.z2(far)

    ff_sums = []
    for grads in ff_grads:
        got = scatter(grads)
        own = lax.dynamic_index_in_dim(got, zl, 0, keepdims=False)
        other = links.z1(lax.dynamic_index_in_dim(got, 1 - zl, 0, keepdims=False))
        ff_sums.append(
            jnp.where(
                parity == 0, jnp.concatenate([own, other], axis=1), jnp.concatenate([other, own], axis=1)
            )
        )
    grad_w_down, grad_w_gate, grad_w_up = ff_sums[0].T, ff_sums[1], ff_sums[2]

    got = scatter(attn_grads)
    attn_sum = lax.dynamic_index_in_dim(got, zl, 0, keepdims=False) + links.z1(
        lax.dynamic_index_in_dim(got, 1 - zl, 0, keepdims=False)
    )
    grad_w_query = attn_sum[:, :head]
    grad_w_out = attn_sum[:, head : 2 * head].T
    kv_own = attn_sum[:, 2 * head :]
    kv_y = links.y(kv_own)
    kv_wide = jnp.where(y == 0, jnp.concatenate([kv_own, kv_y], axis=1), jnp.concatenate([kv_y, kv_own], axis=1))
    kv_c = links.core(kv_wide)
    grad_w_key = jnp.where(c == 0, kv_wide, kv_c)
    grad_w_value = jnp.where(c == 0, kv_c, kv_wide)

    small = jnp.concatenate(
        [
            grad_attn_in.reshape(links.dp_size, -1),
            grad_attn_out.reshape(links.dp_size, -1),
            grad_ffn_in.reshape(links.dp_size, -1),
            (grad_ffn_out * 0.25).reshape(links.dp_size, -1),
            grad_gain_query.reshape(links.dp_size, -1),
            grad_gain_key.reshape(links.dp_size, -1),
        ],
        axis=1,
    )
    small = small + links.core(small)
    small = small + links.y(small)
    small = small.reshape(2, 2, nx, 1, small.shape[1])
    acc = lax.dynamic_index_in_dim(small, x, 2, keepdims=False)
    for step in range(1, nx):
        acc = acc + links.x(lax.dynamic_index_in_dim(small, (x + step) % nx, 2, keepdims=False), step)
    acc = lax.dynamic_index_in_dim(acc, zh, 0, keepdims=False) + links.z2(
        lax.dynamic_index_in_dim(acc, 1 - zh, 0, keepdims=False)
    )
    acc = lax.dynamic_index_in_dim(acc, zl, 0, keepdims=False) + links.z1(
        lax.dynamic_index_in_dim(acc, 1 - zl, 0, keepdims=False)
    )
    acc = acc.reshape(-1)
    hb = head // links.dp_size
    return (
        layer_out,
        input_grad,
        grad_w_query,
        grad_w_key,
        grad_w_value,
        grad_w_out,
        grad_w_gate,
        grad_w_up,
        grad_w_down,
        acc[:blk],
        acc[blk : 2 * blk],
        acc[2 * blk : 3 * blk],
        acc[3 * blk : 4 * blk],
        acc[4 * blk : 4 * blk + hb],
        acc[4 * blk + hb :],
    )


def solution(mesh):
    links = Links(mesh)
    return jax.shard_map(
        functools.partial(body if links.nx == 2 else body_any, links),
        mesh=mesh,
        in_specs=(
            P("dp", None),
            P("dp"),
            P("dp", None),
            P(None, "tensor"),
            P(),
            P(),
            P("tensor", None),
            P(None, "tensor"),
            P(None, "tensor"),
            P("tensor", None),
            P(),
            P(),
            P(),
            P(),
            P(),
            P(),
        ),
        out_specs=(
            P("dp", None),
            P("dp", None),
            P("dp", "tensor"),
            P("dp", None),
            P("dp", None),
            P("tensor", "dp"),
            P("dp", "tensor"),
            P("dp", "tensor"),
            P("tensor", "dp"),
            P("dp"),
            P("dp"),
            P("dp"),
            P("dp"),
            P("dp"),
            P("dp"),
        ),
        check_vma=False,
    )
```

```python
import functools

import jax
import jax.numpy as jnp
from jax import lax
from jax.experimental import pallas as pl
from jax.experimental.pallas import tpu as pltpu
from jax.sharding import PartitionSpec as P

epsilon = 1e-06
score_scale = 0.0625
NZ = 4

f32 = jnp.float32
bf16 = jnp.bfloat16


def rms_norm(values, gain):
    inverse = lax.rsqrt(jnp.mean(values * values, axis=-1, keepdims=True) + epsilon)
    return values * inverse * (1.0 + gain)


def rms_back(values, gain, grad):
    inverse = lax.rsqrt(jnp.mean(values * values, axis=-1, keepdims=True) + epsilon)
    hat = values * inverse
    scaled = grad * (1.0 + gain)
    back = inverse * (scaled - hat * jnp.mean(scaled * hat, axis=-1, keepdims=True))
    return back, jnp.sum(grad * hat, axis=0)


def product(left, right):
    return jnp.dot(left, right, preferred_element_type=f32)


def product_t(left, right):
    return lax.dot_general(left, right, (((1,), (1,)), ((), ())), preferred_element_type=f32)


def t_product(left, right):
    return lax.dot_general(left, right, (((0,), (0,)), ((), ())), preferred_element_type=f32)


def activate(gate, upward):
    return jax.nn.gelu(gate, approximate=True) * upward


class Links:
    def __init__(self, mesh):
        self.dp_size = mesh.shape["dp"]
        self.nx = self.dp_size // NZ
        tensor = mesh.shape["tensor"]
        self.perm_core = [(t, t ^ 1) for t in range(tensor)]
        self.perm_y = [(t, t ^ 2) for t in range(tensor)]
        nx = self.nx
        self.perm_z1 = [(z * nx + x, (z ^ 1) * nx + x) for z in range(NZ) for x in range(nx)]
        self.perm_z2 = [(z * nx + x, (z ^ 2) * nx + x) for z in range(NZ) for x in range(nx)]

    def core(self, a):
        return lax.ppermute(a, "tensor", self.perm_core)

    def y(self, a):
        return lax.ppermute(a, "tensor", self.perm_y)

    def z1(self, a):
        return lax.ppermute(a, "dp", self.perm_z1)

    def z2(self, a):
        return lax.ppermute(a, "dp", self.perm_z2)

    def x(self, a, step):
        nx = self.nx
        return lax.ppermute(a, "dp", [(z * nx + x, z * nx + (x + step) % nx) for z in range(NZ) for x in range(nx)])


def low(a):
    return a.astype(bf16)


MESH = pl.DeviceIdType.MESH
ANY = pl.BlockSpec(memory_space=pl.ANY)
VMEM = pl.BlockSpec(memory_space=pltpu.VMEM)
TILE, HALF, QUARTER = 256, 128, 256
VMEM_LIMIT = 127 << 19


def spots(nx):
    dp, t = lax.axis_index("dp"), lax.axis_index("tensor")
    z, x = dp // nx, dp % nx
    near = {
        "c": {"tensor": t ^ 1},
        "y": {"tensor": t ^ 2},
        "z1": {"dp": (z ^ 1) * nx + x},
        "z2": {"dp": (z ^ 2) * nx + x},
        "x": {"dp": z * nx + (x ^ 1)},
    }
    return z, x, t // 2, t % 2, near


def remote(src, dst, sems, index, to):
    return pltpu.make_async_remote_copy(
        src_ref=src, dst_ref=dst, send_sem=sems[0].at[index], recv_sem=sems[1].at[index], device_id=to, device_id_type=MESH
    )


def greet(others):
    barrier = pltpu.get_barrier_semaphore()
    for other in others:
        pl.semaphore_signal(barrier, inc=1, device_id=other, device_id_type=MESH)
    pl.semaphore_wait(barrier, len(others))


def tile_row(c, y, i, dc):
    dy = 1 - i // 2
    return pl.multiple_of(((c ^ dc) * 2 + (y ^ dy)) * QUARTER + (i % 2) * HALF, HALF)


def gelu_parts(u):
    k = 0.7978845608028654
    square = u * u
    th = jnp.tanh(k * u * (1.0 + 0.044715 * square))
    side = 0.5 * (1.0 + th)
    return u * side, side + 0.5 * u * (1.0 - th * th) * (k * (1.0 + 3.0 * 0.044715 * square))


def gelu_tanh(u):
    return 0.5 * u * (1.0 + jnp.tanh(0.7978845608028654 * u * (1.0 + 0.044715 * (u * u))))


def gain_row(gains, k):
    return gains[k : k + 1, :]


def forward_kernel(
    nx,
    middle,
    cotangent,
    gains,
    w_gate,
    w_up,
    w_down,
    normed_hbm,
    other_hbm,
    d_out_hbm,
    d_own_hbm,
    d_first,
    layer_hbm,
    pair_own_hbm,
    for_gate_hbm,
    for_up_hbm,
    gain_grad,
    normed,
    other,
    d_out,
    d_own,
    layer_out,
    out,
    dy,
    inner,
    for_gate,
    for_up,
    part,
    from_core,
    from_y,
    z_stage,
    z_land,
    c_land,
    local,
    stores,
    tile_stores,
    c_send,
    c_recv,
    y_send,
    y_recv,
    z_send,
    z_recv,
):
    z, x, y, c, near = spots(nx)
    core, across, pair = near["c"], near["y"], near["z1"]
    cs, ys, zs = (c_send, c_recv), (y_send, y_recv), (z_send, z_recv)
    loads = []
    for i in range(4):
        for dc in range(2):
            copy = pltpu.make_async_copy(
                cotangent.at[pl.ds(tile_row(c, y, i, dc), HALF)],
                dy.at[pl.ds(i * TILE + dc * HALF, HALF)],
                local.at[i * 2 + dc],
            )
            copy.start()
            loads.append(copy)
    greet([core, across, pair])
    columns = w_gate.shape[0]
    cut = pl.cdiv(columns, TILE) * HALF
    for ref in (inner, for_gate, for_up):
        for slot in range(2):
            ref[slot, :, columns:] = jnp.zeros((TILE, 2 * cut - columns), bf16)

    def tile_puts(i):
        slot = i % 2
        at = pl.ds(pl.multiple_of(i * TILE, TILE), TILE)
        mine = pl.ds(pl.multiple_of(z % 2 * cut, HALF), cut)
        return [
            pltpu.make_async_copy(inner.at[slot, :, mine], pair_own_hbm.at[at], tile_stores.at[slot, 0]),
            pltpu.make_async_copy(for_gate.at[slot], for_gate_hbm.at[at], tile_stores.at[slot, 1]),
            pltpu.make_async_copy(for_up.at[slot], for_up_hbm.at[at], tile_stores.at[slot, 2]),
        ]

    def core_copy(i):
        return remote(part.at[i, pl.ds(HALF, HALF)], from_core.at[i], cs, i, core)

    def y_copy(h):
        return remote(part.at[h, pl.ds(0, HALF)], from_y.at[h], ys, h, across)

    def z_copy(i):
        return remote(z_stage.at[i], z_land.at[i], zs, i, pair)

    first_copy = remote(d_own.at[2], d_first, zs, 4, pair)

    def z_forward(i):
        return remote(z_land.at[i], c_land.at[i], cs, 8 + i, core)

    def step(i, carry):
        at = pl.ds(pl.multiple_of(i * TILE, TILE), TILE)
        m = middle[at, :]
        inverse = lax.rsqrt(jnp.mean(m * m, axis=-1, keepdims=True) + epsilon)
        n = (m * inverse * (1.0 + gain_row(gains, 2))).astype(bf16)
        normed[at, :] = n
        z_stage[i] = n[:HALF].astype(f32)
        z_copy(i).start()
        slot = i % 2

        @pl.when(i >= 2)
        def _():
            for copy in tile_puts(i - 2):
                copy.wait()

        for lo in range(0, columns, TILE):
            hi = min(lo + TILE, columns)
            g = product_t(n, w_gate[lo:hi, :])
            u = product_t(n, w_up[lo:hi, :])
            act, slope = gelu_parts(g)
            inner[slot, :, lo:hi] = (act * u).astype(bf16)
            for_gate[slot, :, lo:hi] = (u * slope).astype(bf16)
            for_up[slot, :, lo:hi] = act.astype(bf16)
        part[i] = product(inner[slot, :, :columns], w_down[...])
        for copy in tile_puts(i):
            copy.start()
        core_copy(i).start()
        core_copy(i).wait_recv()
        part[i, :HALF] = part[i, :HALF] + from_core[i]

        @pl.when(i < 2)
        def _():
            y_copy(i).start()

        return carry

    lax.fori_loop(0, 4, step, 0)
    out_copies = []

    def put(src, dst):
        copy = pltpu.make_async_copy(src, dst, stores.at[len(out_copies)])
        copy.start()
        out_copies.append(copy)

    put(normed, normed_hbm)
    for i in (2, 3):
        for copy in tile_puts(i):
            copy.wait()
    for copy in loads:
        copy.wait()
    gain_grad[...] = jnp.zeros_like(gain_grad)
    gain = 1.0 + gain_row(gains, 3)

    def finish(i, dc):
        lo = i * TILE + dc * HALF
        o, g = out[lo : lo + HALF, :], dy[lo : lo + HALF, :].astype(f32)
        inverse = lax.rsqrt(jnp.mean(o * o, axis=-1, keepdims=True) + epsilon)
        hat = o * inverse
        scaled = g * gain
        d = (inverse * (scaled - hat * jnp.mean(scaled * hat, axis=-1, keepdims=True))).astype(bf16)
        d_out[lo : lo + HALF, :] = d
        if dc == 0:
            d_own[i] = d.astype(f32)
            if i == 2:
                first_copy.start()
            put(d_own.at[i], d_own_hbm.at[i])
        gain_grad[...] = gain_grad[...] + jnp.sum((g * hat).reshape(HALF // 8, 8, g.shape[1]), axis=0)
        layer_out[pl.ds(tile_row(c, y, i, dc), HALF), :] = (middle[lo : lo + HALF, :] + hat * gain).astype(bf16)
        if dc == 1:
            put(d_out.at[pl.ds(i * TILE, TILE)], d_out_hbm.at[pl.ds(i * TILE, TILE)])

    def spread_y(h):
        return remote(out.at[pl.ds((2 + h) * TILE, HALF)], out.at[pl.ds(h * TILE, HALF)], ys, 2 + h, across)

    def spread_core(i):
        return remote(out.at[pl.ds(i * TILE, HALF)], out.at[pl.ds(i * TILE + HALF, HALF)], cs, 4 + i, core)

    for h in range(2):
        y_copy(h).wait_recv()
        lo = (2 + h) * TILE
        out[lo : lo + HALF, :] = part[2 + h, :HALF] + from_y[h]
        spread_y(h).start()
        spread_core(2 + h).start()
        finish(2 + h, 0)
        spread_core(2 + h).wait_recv()
        finish(2 + h, 1)

    def take(i):
        z_forward(i).wait_recv()
        other[i * TILE : i * TILE + HALF, :] = z_land[i].astype(bf16)
        other[i * TILE + HALF : (i + 1) * TILE, :] = c_land[i].astype(bf16)
        put(other.at[pl.ds(i * TILE, TILE)], other_hbm.at[pl.ds(i * TILE, TILE)])

    for i in range(3):
        z_copy(i).wait_recv()
        z_forward(i).start()
    for i in range(2):
        take(i)
    for h in range(2):
        spread_y(h).wait_recv()
        spread_core(h).start()
        finish(h, 0)
        spread_core(h).wait_recv()
        finish(h, 1)
    put(layer_out, layer_hbm)
    z_copy(3).wait_recv()
    z_forward(3).start()
    for i in range(2, 4):
        take(i)
    for i in range(4):
        core_copy(i).wait_send()
        z_copy(i).wait_send()
        z_forward(i).wait_send()
        spread_core(i).wait_send()
    for h in range(2):
        y_copy(h).wait_send()
        spread_y(h).wait_send()
    first_copy.wait()
    for copy in out_copies:
        copy.wait()


def dma(*counts):
    return [pltpu.SemaphoreType.DMA((n,)) for n in counts]


def feed_forward(nx, middle, cotangent, gains, w_gate, w_up, w_down):
    length, width = middle.shape
    columns = pl.cdiv(w_gate.shape[0], TILE) * TILE
    rows_low = jax.ShapeDtypeStruct((length, width), bf16)
    return pl.pallas_call(
        functools.partial(forward_kernel, nx),
        out_shape=(
            rows_low,
            rows_low,
            rows_low,
            jax.ShapeDtypeStruct((4, HALF, width), f32),
            jax.ShapeDtypeStruct((HALF, width), f32),
            rows_low,
            jax.ShapeDtypeStruct((length, columns // 2), bf16),
            jax.ShapeDtypeStruct((length, columns), bf16),
            jax.ShapeDtypeStruct((length, columns), bf16),
            jax.ShapeDtypeStruct((8, width), f32),
        ),
        in_specs=[VMEM, ANY] + [VMEM] * 4,
        out_specs=(ANY,) * 4 + (VMEM, ANY, ANY, ANY, ANY, VMEM),
        scratch_shapes=[pltpu.VMEM((length, width), bf16)] * 3
        + [
            pltpu.VMEM((4, HALF, width), f32),
            pltpu.VMEM((length, width), bf16),
            pltpu.VMEM((length, width), f32),
            pltpu.VMEM((length, width), bf16),
            pltpu.VMEM((2, TILE, columns), bf16),
            pltpu.VMEM((2, TILE, columns), bf16),
            pltpu.VMEM((2, TILE, columns), bf16),
            pltpu.VMEM((4, TILE, width), f32),
            pltpu.VMEM((4, HALF, width), f32),
            pltpu.VMEM((2, HALF, width), f32),
            pltpu.VMEM((4, HALF, width), f32),
            pltpu.VMEM((4, HALF, width), f32),
            pltpu.VMEM((4, HALF, width), f32),
        ]
        + dma(8, 14)
        + [pltpu.SemaphoreType.DMA((2, 3))]
        + dma(12, 12, 4, 4, 5, 5),
        compiler_params=pltpu.CompilerParams(collective_id=0, has_side_effects=True, vmem_limit_bytes=VMEM_LIMIT),
        name="feed_forward",
    )(middle, cotangent, gains, w_gate, w_up, w_down)


def back_kernel(
    nx,
    d_out_hbm,
    d_own_hbm,
    d_first_hbm,
    for_gate_hbm,
    for_up_hbm,
    other_hbm,
    w_gate_hbm,
    w_up_hbm,
    w_down_hbm,
    w_out_hbm,
    middle_hbm,
    branch_hbm,
    dy_hbm,
    gains,
    d_other,
    pair_in,
    pair_gates,
    grad_context,
    d_branch_out,
    d_middle_out,
    gain_grads,
    d_out,
    for_gate,
    for_up,
    other,
    w_gate,
    w_up,
    w_down,
    w_out,
    middle,
    branch,
    dy,
    gates,
    ups,
    inner,
    part,
    from_core,
    from_y,
    z_land,
    c_land,
    heads_c,
    heads_y,
    got_c,
    got_y,
    loads_sem,
    tiles_sem,
    stores_sem,
    c_send,
    c_recv,
    y_send,
    y_recv,
    z_send,
    z_recv,
):
    z, x, y, c, near = spots(nx)
    core, across, pair = near["c"], near["y"], near["z1"]
    cs, ys, zs = (c_send, c_recv), (y_send, y_recv), (z_send, z_recv)
    parity = z % 2
    real, columns = w_gate_hbm.shape[0], w_gate.shape[0]
    half = columns // 2
    head = heads_c.shape[2]
    own_row = pl.multiple_of((c * 2 + y) * QUARTER, QUARTER)
    sources = [
        (d_out_hbm, d_out),
        (w_gate_hbm, w_gate.at[pl.ds(0, real)]),
        (w_up_hbm, w_up.at[pl.ds(0, real)]),
        (w_down_hbm, w_down.at[pl.ds(0, real)]),
        (other_hbm, other),
        (w_out_hbm, w_out),
        (middle_hbm.at[pl.ds(2 * TILE, HALF)], middle.at[pl.ds(0, HALF)]),
        (middle_hbm.at[pl.ds(3 * TILE, HALF)], middle.at[pl.ds(HALF, HALF)]),
        (branch_hbm, branch),
        (dy_hbm.at[pl.ds(own_row, QUARTER)], dy),
        (d_first_hbm, z_land.at[2]),
    ]
    loads = [pltpu.make_async_copy(src, dst, loads_sem.at[k]) for k, (src, dst) in enumerate(sources)]
    for copy in loads:
        copy.start()
    if real < columns:
        for ref in (w_gate, w_up, w_down):
            ref[real:, :] = jnp.zeros((columns - real, ref.shape[1]), bf16)
    greet([core, across, pair])

    def core_copy(i):
        return remote(part.at[i, pl.ds(HALF, HALF)], from_core.at[i], cs, i, core)

    def y_copy(h):
        return remote(part.at[h, pl.ds(0, HALF)], from_y.at[h], ys, h, across)

    def z_copy(i):
        return remote(d_own_hbm.at[i], z_land.at[i], zs, i, pair)

    def z_forward(i):
        return remote(z_land.at[i], c_land.at[i], cs, 4 + i, core)

    for i in (3, 0, 1):
        z_copy(i).start()
    def tile_loads(i):
        slot = i % 2
        at = pl.ds(pl.multiple_of(i * TILE, TILE), TILE)
        return [
            pltpu.make_async_copy(for_gate_hbm.at[at], for_gate.at[slot], tiles_sem.at[slot, 0]),
            pltpu.make_async_copy(for_up_hbm.at[at], for_up.at[slot], tiles_sem.at[slot, 1]),
        ]

    for i in range(2):
        for copy in tile_loads(i):
            copy.start()
    for copy in loads[:4]:
        copy.wait()

    mine = pl.multiple_of(parity * half, HALF)

    def stores(i, base):
        slot = i % 2
        at = pl.ds(pl.multiple_of(base + i * TILE, TILE), TILE)
        pick = pl.ds(mine, half)
        first = []
        if base:
            first = [
                pltpu.make_async_copy(
                    inner.at[slot], pair_in.at[pl.ds(pl.multiple_of(i * TILE, TILE), TILE)], stores_sem.at[slot, 0]
                )
            ]
        return first + [
            pltpu.make_async_copy(gates.at[slot, :, pick], pair_gates.at[at, pl.ds(0, half)], stores_sem.at[slot, 1]),
            pltpu.make_async_copy(ups.at[slot, :, pick], pair_gates.at[at, pl.ds(half, half)], stores_sem.at[slot, 2]),
        ]

    def piece(n, d, slot, at, own):
        g = product_t(n, w_gate[at, :])
        u = product_t(n, w_up[at, :])
        di = product_t(d, w_down[at, :])
        act, slope = gelu_parts(g)
        inner[slot, :, own] = (act * u).astype(bf16)
        gates[slot, :, at] = (di * u * slope).astype(bf16)
        ups[slot, :, at] = (di * act).astype(bf16)

    def own_tile(i, carry):
        at = pl.ds(pl.multiple_of(i * TILE, TILE), TILE)
        slot = i % 2

        @pl.when(i >= 2)
        def _():
            for copy in stores(i - 2, 0):
                copy.wait()

        for copy in tile_loads(i):
            copy.wait()
        d = d_out[at, :]
        for lo in range(0, columns, TILE):
            cols = pl.ds(lo, TILE)
            di = product_t(d, w_down[cols, :])
            gates[slot, :, cols] = (di * for_gate[slot, :, cols].astype(f32)).astype(bf16)
            ups[slot, :, cols] = (di * for_up[slot, :, cols].astype(f32)).astype(bf16)

        @pl.when(i < 2)
        def _():
            for copy in tile_loads(i + 2):
                copy.start()

        for copy in stores(i, 0):
            copy.start()
        part[i] = product(gates[slot], w_gate[...]) + product(ups[slot], w_up[...])
        core_copy(i).start()
        core_copy(i).wait_recv()
        part[i, :HALF] = part[i, :HALF] + from_core[i]

        @pl.when(i < 2)
        def _():
            y_copy(i).start()

        return carry

    lax.fori_loop(0, 4, own_tile, 0)
    for copy in loads[4:]:
        copy.wait()

    def other_tile(n, carry):
        i, slot = (n + 2) % 4, n % 2

        @pl.when(n > 0)
        def _():
            z_copy(i).wait_recv()

        z_forward(i).start()

        @pl.when(n < 2)
        def _():
            for copy in stores(i, 0):
                copy.wait()

        @pl.when(n >= 2)
        def _():
            for copy in stores(n, d_out.shape[0]):
                copy.wait()

        z_forward(i).wait_recv()
        lo = pl.multiple_of(i * TILE, TILE)
        d_other[pl.ds(lo, HALF), :] = z_land[i].astype(bf16)
        d_other[pl.ds(lo + HALF, HALF), :] = c_land[i].astype(bf16)
        n, d = other[pl.ds(lo, TILE), :], d_other[pl.ds(lo, TILE), :]
        for off in range(0, half, TILE):
            size = min(TILE, half - off)
            piece(n, d, slot, pl.ds(pl.multiple_of(mine + off, HALF), size), pl.ds(off, size))
        for copy in stores(i, d_out.shape[0]):
            copy.start()
        return carry

    lax.fori_loop(0, 2, other_tile, 0)

    gain_grads[...] = jnp.zeros_like(gain_grads)

    def fold(a):
        return jnp.sum(a.reshape(a.shape[0] // 8, 8, a.shape[1]), axis=0)

    for h in range(2):
        y_copy(h).wait_recv()
        at = slice(h * HALF, (h + 1) * HALF)
        grad = part[2 + h, :HALF] + from_y[h]
        m = middle[at, :]
        inverse = lax.rsqrt(jnp.mean(m * m, axis=-1, keepdims=True) + epsilon)
        hat = m * inverse
        scaled = grad * (1.0 + gain_row(gains, 2))
        d_middle = dy[at, :].astype(f32) + inverse * (scaled - hat * jnp.mean(scaled * hat, axis=-1, keepdims=True))
        gain_grads[0] = gain_grads[0] + fold(grad * hat)
        d_middle_out[at, :] = d_middle
        b = branch[at, :]
        inverse = lax.rsqrt(jnp.mean(b * b, axis=-1, keepdims=True) + epsilon)
        hat = b * inverse
        scaled = d_middle * (1.0 + gain_row(gains, 1))
        d_low = (inverse * (scaled - hat * jnp.mean(scaled * hat, axis=-1, keepdims=True))).astype(bf16)
        gain_grads[1] = gain_grads[1] + fold(d_middle * hat)
        d_branch_out[at, :] = d_low.astype(f32)
        for k, (ref, slot) in enumerate([(None, 0), (heads_y, 0), (heads_c, 0), (heads_c, 1)]):
            piece_of = product_t(d_low, w_out[k * head : (k + 1) * head, :]).astype(bf16)
            if ref is None:
                grad_context[pl.ds(own_row + h * HALF, HALF), :] = piece_of
            else:
                ref[slot, at, :] = piece_of.astype(f32)
    to_core = remote(heads_c, got_c, cs, 8, core)
    to_core.start()
    to_core.wait_recv()
    heads_y[1] = got_c[1]
    to_y = remote(heads_y, got_y, ys, 2, across)
    to_y.start()
    grad_context[pl.ds(pl.multiple_of(((c ^ 1) * 2 + y) * QUARTER, QUARTER), QUARTER), :] = got_c[0].astype(bf16)

    lax.fori_loop(2, 4, other_tile, 0)
    to_y.wait_recv()
    grad_context[pl.ds(pl.multiple_of((c * 2 + (y ^ 1)) * QUARTER, QUARTER), QUARTER), :] = got_y[0].astype(bf16)
    grad_context[pl.ds(pl.multiple_of(((c ^ 1) * 2 + (y ^ 1)) * QUARTER, QUARTER), QUARTER), :] = got_y[1].astype(bf16)
    for i in (0, 1):
        for copy in stores(i, d_out.shape[0]):
            copy.wait()
    for i in (3, 0, 1):
        z_copy(i).wait_send()
    for i in range(4):
        core_copy(i).wait_send()
        z_forward(i).wait_send()
    for h in range(2):
        y_copy(h).wait_send()
    to_core.wait_send()
    to_y.wait_send()


def feed_back(nx, d_out, d_own, d_first, for_gate, for_up, other, w_gate, w_up, w_down, w_out, middle, branch, dy, gains):
    length, width = d_out.shape
    columns = pl.cdiv(w_gate.shape[0], TILE) * TILE
    head = w_out.shape[0] // 4
    return pl.pallas_call(
        functools.partial(back_kernel, nx),
        out_shape=(
            jax.ShapeDtypeStruct((length, width), bf16),
            jax.ShapeDtypeStruct((length, columns // 2), bf16),
            jax.ShapeDtypeStruct((2 * length, columns), bf16),
            jax.ShapeDtypeStruct((length, head), bf16),
            jax.ShapeDtypeStruct((QUARTER, width), f32),
            jax.ShapeDtypeStruct((QUARTER, width), f32),
            jax.ShapeDtypeStruct((2, 8, width), f32),
        ),
        in_specs=[ANY] * 13 + [VMEM],
        out_specs=(VMEM, ANY, ANY) + (VMEM,) * 4,
        scratch_shapes=[
            pltpu.VMEM((length, width), bf16),
            pltpu.VMEM((2, TILE, columns), bf16),
            pltpu.VMEM((2, TILE, columns), bf16),
            pltpu.VMEM((length, width), bf16),
            pltpu.VMEM((columns, width), bf16),
            pltpu.VMEM((columns, width), bf16),
            pltpu.VMEM((columns, width), bf16),
            pltpu.VMEM((4 * head, width), bf16),
            pltpu.VMEM((QUARTER, width), f32),
            pltpu.VMEM((QUARTER, width), f32),
            pltpu.VMEM((QUARTER, width), bf16),
            pltpu.VMEM((2, TILE, columns), bf16),
            pltpu.VMEM((2, TILE, columns), bf16),
            pltpu.VMEM((2, TILE, columns // 2), bf16),
            pltpu.VMEM((4, TILE, width), f32),
            pltpu.VMEM((4, HALF, width), f32),
            pltpu.VMEM((2, HALF, width), f32),
            pltpu.VMEM((4, HALF, width), f32),
            pltpu.VMEM((4, HALF, width), f32),
            pltpu.VMEM((2, QUARTER, head), f32),
            pltpu.VMEM((2, QUARTER, head), f32),
            pltpu.VMEM((2, QUARTER, head), f32),
            pltpu.VMEM((2, QUARTER, head), f32),
            pltpu.SemaphoreType.DMA((12,)),
            pltpu.SemaphoreType.DMA((2, 2)),
            pltpu.SemaphoreType.DMA((2, 3)),
        ]
        + dma(9, 9, 3, 3, 4, 4),
        compiler_params=pltpu.CompilerParams(collective_id=1, has_side_effects=True, vmem_limit_bytes=VMEM_LIMIT),
        name="feed_back",
    )(
        d_out,
        d_own,
        d_first,
        for_gate,
        for_up,
        other,
        w_gate,
        w_up,
        w_down,
        w_out,
        middle,
        branch,
        dy,
        gains,
    )


def visible_pairs(shape, i, segments):
    row = lax.broadcasted_iota(jnp.int32, shape, 0) + i * TILE
    col = lax.broadcasted_iota(jnp.int32, shape, 1)
    first = jnp.sum((segments[...] == 0).astype(jnp.int32), axis=1, keepdims=True)
    return (row >= col) & ((row < first) == (col < first))


def attention_kernel(
    nx,
    tokens,
    w_query,
    w_key,
    w_value,
    w_out,
    segments,
    gains,
    normed_hbm,
    query_hbm,
    keys_hbm,
    values_hbm,
    query_raw_hbm,
    keys_raw_hbm,
    log_total_hbm,
    context_hbm,
    w_out_all_hbm,
    middle,
    branch,
    normed,
    query,
    keys,
    values,
    query_raw,
    keys_raw,
    log_total,
    context,
    w_out_all,
    stores,
    out_own,
    out_land,
    context_own,
    context_core,
    context_land,
    context_all,
    c_send,
    c_recv,
    y_send,
    y_recv,
    x_send,
    x_recv,
):
    z, x, y, c, near = spots(nx)
    cs, ys, xs = (c_send, c_recv), (y_send, y_recv), (x_send, x_recv)
    length, width = tokens.shape
    head = w_query.shape[1]
    out_own[...] = w_out[...].astype(f32)
    greet([near[k] for k in ("c", "y", "x")])
    mine = pl.ds(pl.multiple_of(x * (head // 2), 8), head // 2)
    out_y = remote(out_own.at[mine], out_land.at[0, mine], ys, 0, near["y"])
    out_x = remote(out_land.at[0, mine], out_land.at[0, mine], xs, 0, near["x"])
    out_c = remote(out_own, out_land.at[1], cs, 0, near["c"])
    out_yc = remote(out_land.at[0], out_land.at[2], cs, 1, near["c"])
    out_y.start()
    out_c.start()
    w_out_all[:head, :] = w_out[...]

    def norm(v, gain):
        return v * lax.rsqrt(jnp.mean(v * v, axis=-1, keepdims=True) + epsilon) * (1.0 + gain)

    def inputs(i, carry):
        at = pl.ds(pl.multiple_of(i * TILE, TILE), TILE)
        n = norm(tokens[at, :].astype(f32), gain_row(gains, 0)).astype(bf16)
        normed[at, :] = n
        raw = product(n, w_query[...])
        query_raw[at, :] = raw
        query[at, :] = norm(raw, gain_row(gains, 4)[:, :head]).astype(bf16)
        raw = product(n, w_key[...])
        keys_raw[at, :] = raw
        keys[at, :] = norm(raw, gain_row(gains, 5)[:, :head]).astype(bf16)
        values[at, :] = product(n, w_value[...]).astype(bf16)
        return carry

    lax.fori_loop(0, length // TILE, inputs, 0)
    for i in range(length // TILE):
        at, seen = slice(i * TILE, (i + 1) * TILE), (i + 1) * TILE
        s = product_t(query[at, :], keys[:seen, :]) * score_scale
        s = jnp.where(visible_pairs(s.shape, i, segments), s, -1e30)
        largest = jnp.max(s, axis=-1, keepdims=True)
        e = jnp.exp(s - largest)
        total = jnp.sum(e, axis=-1, keepdims=True)
        log_total[at, :] = largest + jnp.log(total)
        low_context = product((e / total).astype(bf16), values[:seen, :]).astype(bf16)
        context[at, :] = low_context
        context_own[at, :] = low_context.astype(f32)

    out_copies = []

    def put(src, dst):
        copy = pltpu.make_async_copy(src, dst, stores.at[len(out_copies)])
        copy.start()
        out_copies.append(copy)

    span = length // 2
    to_core = remote(context_own.at[pl.ds(pl.multiple_of((1 - c) * span, span), span)], context_core, cs, 2, near["c"])
    to_core.start()

    def local(i, other):
        dy = 1 - i // 2
        return pl.multiple_of(((y ^ other) ^ dy) * QUARTER + (i % 2) * HALF, HALF)

    def context_copy(i, k):
        if k == 0:
            src = context_own.at[pl.ds(pl.multiple_of(c * span + local(i, 1), HALF), HALF)]
        else:
            src = context_core.at[pl.ds(local(i, 1), HALF)]
        return remote(src, context_land.at[k, i], ys, 1 + 2 * i + k, near["y"])

    context_copy(0, 0).start()
    for src, dst in (
        (normed, normed_hbm),
        (query, query_hbm),
        (keys, keys_hbm),
        (values, values_hbm),
        (query_raw, query_raw_hbm),
        (keys_raw, keys_raw_hbm),
        (log_total, log_total_hbm),
        (context, context_hbm),
    ):
        put(src, dst)
    out_y.wait_recv()
    out_x.start()
    to_core.wait_recv()
    for i in range(4):
        for k in range(2):
            if i + k > 0:
                context_copy(i, k).start()
    out_c.wait_recv()
    w_out_all[2 * head : 3 * head, :] = out_land[1].astype(bf16)
    for i in range(4):
        rows = pl.ds(i * HALF, HALF)
        context_all[rows, :head] = context[pl.ds(pl.multiple_of(c * span + local(i, 0), HALF), HALF), :]
        context_all[rows, 2 * head : 3 * head] = context_core[pl.ds(local(i, 0), HALF), :].astype(bf16)
    out_x.wait_recv()
    out_yc.start()
    w_out_all[head : 2 * head, :] = out_land[0].astype(bf16)
    out_yc.wait_recv()
    w_out_all[3 * head :, :] = out_land[2].astype(bf16)
    put(w_out_all, w_out_all_hbm)

    def middle_copy(i):
        at = pl.multiple_of(i * TILE, TILE)
        return remote(middle.at[pl.ds(at, HALF)], middle.at[pl.ds(at + HALF, HALF)], cs, 3 + i, near["c"])

    for i in range(4):
        rows = pl.ds(i * HALF, HALF)
        context_copy(i, 0).wait_recv()
        context_all[rows, head : 2 * head] = context_land[0, i].astype(bf16)
        context_copy(i, 1).wait_recv()
        context_all[rows, 3 * head :] = context_land[1, i].astype(bf16)
        b = product(context_all[rows, :], w_out_all[...])
        if i >= 2:
            branch[(i - 2) * HALF : (i - 1) * HALF, :] = b
        hidden = tokens[pl.ds(pl.multiple_of(c * span + local(i, 0), HALF), HALF), :].astype(f32)
        middle[i * TILE : i * TILE + HALF, :] = hidden + norm(b, gain_row(gains, 1))
        middle_copy(i).start()
    for i in range(4):
        middle_copy(i).wait()
        for k in range(2):
            context_copy(i, k).wait_send()
    for copy in (out_y, out_x, out_c, out_yc, to_core):
        copy.wait_send()
    for copy in out_copies:
        copy.wait()


def attend(nx, tokens, w_query, w_key, w_value, w_out, segment_ids, gains):
    length, width = tokens.shape
    head = w_query.shape[1]
    of_head = jax.ShapeDtypeStruct((length, head), bf16)
    raw = jax.ShapeDtypeStruct((length, head), f32)
    return pl.pallas_call(
        functools.partial(attention_kernel, nx),
        out_shape=(
            jax.ShapeDtypeStruct((length, width), bf16),
            of_head,
            of_head,
            of_head,
            raw,
            raw,
            jax.ShapeDtypeStruct((length, 1), f32),
            of_head,
            jax.ShapeDtypeStruct((4 * head, width), bf16),
            jax.ShapeDtypeStruct((length, width), f32),
            jax.ShapeDtypeStruct((QUARTER, width), f32),
        ),
        in_specs=[VMEM] * 7,
        out_specs=(ANY,) * 9 + (VMEM,) * 2,
        scratch_shapes=[
            pltpu.VMEM((length, width), bf16),
            pltpu.VMEM((length, head), bf16),
            pltpu.VMEM((length, head), bf16),
            pltpu.VMEM((length, head), bf16),
            pltpu.VMEM((length, head), f32),
            pltpu.VMEM((length, head), f32),
            pltpu.VMEM((length, 1), f32),
            pltpu.VMEM((length, head), bf16),
            pltpu.VMEM((4 * head, width), bf16),
            pltpu.SemaphoreType.DMA((9,)),
            pltpu.VMEM((head, width), f32),
            pltpu.VMEM((3, head, width), f32),
            pltpu.VMEM((length, head), f32),
            pltpu.VMEM((length // 2, head), f32),
            pltpu.VMEM((2, 4, HALF, head), f32),
            pltpu.VMEM((length // 2, 4 * head), bf16),
        ]
        + dma(7, 7, 9, 9, 1, 1),
        compiler_params=pltpu.CompilerParams(collective_id=3, has_side_effects=True, vmem_limit_bytes=VMEM_LIMIT),
        name="attend",
    )(
        tokens,
        w_query,
        w_key,
        w_value,
        w_out,
        segment_ids.reshape(1, length),
        gains,
    )


def reduce_kernel(
    nx,
    d_out_hbm,
    d_other_hbm,
    normed_hbm,
    other_hbm,
    pair_own_hbm,
    pair_other_hbm,
    pair_gates_hbm,
    d_branch_hbm,
    d_middle_hbm,
    tokens_hbm,
    normed_in_hbm,
    query_hbm,
    keys_hbm,
    values_hbm,
    query_raw_hbm,
    keys_raw_hbm,
    context_hbm,
    grad_context_hbm,
    w_query_hbm,
    w_key_hbm,
    w_value_hbm,
    log_total,
    segments,
    gain_rows,
    of_ffn_out,
    of_middle,
    ff_out,
    attn_out,
    kv_out,
    input_grad,
    gains,
    dw,
    x_land,
    z2_land,
    z1_land,
    from_core,
    from_y,
    branch_land,
    input_own,
    input_land,
    d_qkv,
    attn,
    attn_z1,
    attn_x,
    attn_z2,
    kv_core,
    kv_across,
    kv_own,
    kv_y,
    kv_wide,
    kv_wide_core,
    gains_land,
    loads,
    c_send,
    c_recv,
    y_send,
    y_recv,
    x_send,
    x_recv,
    z2_send,
    z2_recv,
    z1_send,
    z1_recv,
):
    z, x, y, c, near = spots(nx)
    zh, zl = z // 2, z % 2
    cs, ys, xs = (c_send, c_recv), (y_send, y_recv), (x_send, x_recv)
    z2s, z1s = (z2_send, z2_recv), (z1_send, z1_recv)
    length, width = d_out_hbm.shape
    half = pair_own_hbm.shape[1]
    head = query_hbm.shape[1]
    blk = x_land.shape[1]
    own_row = pl.multiple_of((c * 2 + y) * QUARTER, QUARTER)

    def block(a, b):
        return pl.ds(pl.multiple_of(b * blk, 8), blk)

    def quarter_rows(dc, dy):
        return pl.ds(pl.multiple_of(((c ^ dc) * 2 + (y ^ dy)) * QUARTER, QUARTER), QUARTER)

    greet([near[k] for k in ("c", "y", "x", "z2", "z1")])

    branch_y = remote(d_branch_hbm, branch_land.at[0], ys, 0, near["y"])
    branch_c = remote(d_branch_hbm, branch_land.at[1], cs, 0, near["c"])
    branch_fwd = remote(branch_land.at[0], branch_land.at[2], cs, 1, near["c"])
    branch_y.start()
    branch_c.start()

    def owner(j):
        return 2 * jnp.where(j < 2, 1 - zh, zh) + j % 2

    def x_copy(m, j):
        return remote(dw.at[m, block(dw, owner(j) * 2 + (1 - x))], x_land.at[m * 4 + j], xs, m * 4 + j, near["x"])

    def z2_copy(m, k):
        return remote(dw.at[m, block(dw, owner(k) * 2 + x)], z2_land.at[m * 2 + k], z2s, m * 2 + k, near["z2"])

    def z1_copy(m):
        return remote(dw.at[m, block(dw, (2 * zh + 1 - zl) * 2 + x)], z1_land.at[m], z1s, m, near["z1"])

    def start_x(*blocks):
        for m, j in blocks:
            x_copy(m, j).start()

    arrived = set()

    def wait_x(m, j):
        if (m, j) not in arrived:
            arrived.add((m, j))
            x_copy(m, j).wait_recv()

    def far(*blocks):
        for m, k in blocks:
            wait_x(m, k)
            rows = block(dw, owner(k) * 2 + x)
            dw[m, rows, :] = dw[m, rows, :] + x_land[m * 4 + k]
            z2_copy(m, k).start()

    def close(m):
        for k in range(2):
            wait_x(m, 2 + k)
            z2_copy(m, k).wait_recv()
            rows = block(dw, owner(2 + k) * 2 + x)
            dw[m, rows, :] = dw[m, rows, :] + x_land[m * 4 + 2 + k] + z2_land[m * 2 + k]
        z1_copy(m).start()
        ff_out[m, zl] = dw[m, block(dw, (2 * zh + zl) * 2 + x), :]

    def copies(pairs):
        started = [pltpu.make_async_copy(src, dst, loads.at[k]) for k, (src, dst) in enumerate(pairs)]
        for copy in started:
            copy.start()
        return started

    def weights(left, right):
        far_size = pl.cdiv(width // 2, HALF) * HALF
        far_at = pl.multiple_of((1 - zh) * (width - far_size), HALF)
        near_at = pl.multiple_of(zh * far_size, HALF)

        def form(m, lo, at, size):
            for off in range(0, size, 3 * HALF):
                rows = pl.ds(pl.multiple_of(at + off, HALF), min(3 * HALF, size - off))
                dw[m, rows, :] = t_product(left[:, rows], right[:, lo : lo + half])

        for copy in copies(
            [
                (d_out_hbm, left.at[pl.ds(0, length)]),
                (d_other_hbm, left.at[pl.ds(length, length)]),
                (pair_own_hbm, right.at[pl.ds(0, length), pl.ds(0, half)]),
                (pair_other_hbm, right.at[pl.ds(length, length), pl.ds(0, half)]),
            ]
        ):
            copy.wait()
        form(0, 0, far_at, far_size)
        start_x((0, 0), (0, 1))
        form(0, 0, near_at, width - far_size)
        for copy in copies(
            [
                (normed_hbm, left.at[pl.ds(0, length)]),
                (other_hbm, left.at[pl.ds(length, length)]),
                (pair_gates_hbm, right),
            ]
        ):
            copy.wait()
        for m in (1, 2):
            form(m, (m - 1) * half, far_at, far_size)
            start_x((m, 0), (m, 1))
        far((0, 0))
        for m in (1, 2):
            form(m, (m - 1) * half, near_at, width - far_size)
        start_x((0, 2), (0, 3), (1, 2), (1, 3))

    pl.run_scoped(weights, pltpu.VMEM((2 * length, width), bf16), pltpu.VMEM((2 * length, 2 * half), bf16))

    def total_of(a):
        return jnp.sum(a, axis=0, keepdims=True)

    gains[...] = jnp.zeros_like(gains)
    gains[1:2, :] = total_of(of_middle[1])
    gains[2:3, :] = total_of(of_middle[0])
    gains[3:4, :] = 0.25 * total_of(of_ffn_out[...])

    def back_norm(raw, gain, grad):
        inverse = lax.rsqrt(jnp.mean(raw * raw, axis=-1, keepdims=True) + epsilon)
        hat = raw * inverse
        scaled = grad * (1.0 + gain)
        return inverse * (scaled - hat * jnp.mean(scaled * hat, axis=-1, keepdims=True)), grad * hat

    def attention(query, keys, values, query_raw, keys_raw, grad_context, d_keys, d_values):
        for copy in copies(
            [
                (query_hbm, query),
                (keys_hbm, keys),
                (values_hbm, values),
                (query_raw_hbm, query_raw),
                (keys_raw_hbm, keys_raw),
                (grad_context_hbm, grad_context),
            ]
        ):
            copy.wait()
        d_keys[...] = jnp.zeros_like(d_keys)
        d_values[...] = jnp.zeros_like(d_values)
        for i in range(length // TILE):
            at, seen = slice(i * TILE, (i + 1) * TILE), (i + 1) * TILE
            q, k = query[at, :], keys[:seen, :]
            s = product_t(q, k) * score_scale
            p = jnp.exp(jnp.where(visible_pairs(s.shape, i, segments), s, -1e30) - log_total[at, :])
            g = grad_context[at, :]
            dp = product_t(g, values[:seen, :])
            balance = jnp.sum(dp * p, axis=-1, keepdims=True)
            ds = (p * (dp - balance)).astype(bf16)
            dq, of_gain = back_norm(query_raw[at, :], gain_row(gain_rows, 4)[:, :head], product(ds, k) * score_scale)
            d_qkv[at, :head] = dq.astype(bf16)
            gains[4:5, :head] = gains[4:5, :head] + jnp.sum(of_gain, axis=0, keepdims=True)
            d_keys[:seen, :] = d_keys[:seen, :] + t_product(ds, q)
            d_values[:seen, :] = d_values[:seen, :] + t_product(p.astype(bf16), g)
        for i in range(length // TILE):
            at = slice(i * TILE, (i + 1) * TILE)
            dk, of_gain = back_norm(keys_raw[at, :], gain_row(gain_rows, 5)[:, :head], d_keys[at, :] * score_scale)
            d_qkv[at, head : 2 * head] = dk.astype(bf16)
            gains[5:6, :head] = gains[5:6, :head] + jnp.sum(of_gain, axis=0, keepdims=True)
            d_qkv[at, 2 * head :] = d_values[at, :].astype(bf16)

    pl.run_scoped(
        attention,
        pltpu.VMEM((length, head), bf16),
        pltpu.VMEM((length, head), bf16),
        pltpu.VMEM((length, head), bf16),
        pltpu.VMEM((length, head), f32),
        pltpu.VMEM((length, head), f32),
        pltpu.VMEM((length, head), bf16),
        pltpu.VMEM((length, head), f32),
        pltpu.VMEM((length, head), f32),
    )
    far((0, 1))

    def attn_z1_copy(i):
        b = (2 * (i // 2) + 1 - zl) * 2 + i % 2
        return remote(attn.at[block(attn, b)], attn_z1.at[i], z1s, 3 + i, near["z1"])

    def attn_x_copy(j):
        b = (2 * (zh ^ j) + zl) * 2 + 1 - x
        return remote(attn.at[block(attn, b)], attn_x.at[j], xs, 12 + j, near["x"])

    attn_z2_copy = remote(attn.at[block(attn, (2 * (1 - zh) + zl) * 2 + x)], attn_z2, z2s, 6, near["z2"])

    input_y = remote(input_own, input_land.at[0], ys, 4, near["y"])
    input_c = remote(input_own, input_land.at[1], cs, 7, near["c"])
    input_fwd = remote(input_land.at[0], input_land.at[2], cs, 8, near["c"])

    hops = [
        remote(gains, gains_land.at[k], sems, index, near[to])
        for k, (sems, index, to) in enumerate([(cs, 10, "c"), (ys, 6, "y"), (xs, 14, "x"), (z1s, 7, "z1"), (z2s, 7, "z2")])
    ]

    def hop(k):
        hops[k].start()

    def arrive(k):
        hops[k].wait()
        gains[...] = gains[...] + gains_land[k]

    def rest(w_qkv, part, kv_halves):
        def of_inputs(normed_in, kv):
            for copy in copies([(normed_in_hbm, normed_in)]):
                copy.wait()
            for k in range(2):
                kv[k] = t_product(normed_in[...], d_qkv[:, (1 + k) * head : (2 + k) * head])
            to_core = remote(kv.at[1 - c], kv_core, cs, 6, near["c"])
            to_core.start()
            attn[:, :head] = t_product(normed_in[...], d_qkv[:, :head])
            to_core.wait_recv()
            for k in range(2):
                lanes = slice(k * (head // 2), (k + 1) * (head // 2))
                kv_halves[k] = kv[c, :, lanes] + kv_core[:, lanes]
            to_core.wait_send()

        pl.run_scoped(of_inputs, pltpu.VMEM((length, width), bf16), pltpu.VMEM((2, width, head), f32))
        to_y = remote(kv_halves.at[1 - y], kv_across, ys, 3, near["y"])
        to_y.start()
        for copy in copies(
            [
                (w_query_hbm, w_qkv.at[:, pl.ds(0, head)]),
                (w_key_hbm, w_qkv.at[:, pl.ds(head, head)]),
                (w_value_hbm, w_qkv.at[:, pl.ds(2 * head, head)]),
            ]
        ):
            copy.wait()

        def core_copy(i):
            return remote(part.at[i, pl.ds(HALF, HALF)], from_core.at[i], cs, 2 + i, near["c"])

        def y_copy(h):
            return remote(part.at[h, pl.ds(0, HALF)], from_y.at[h], ys, 1 + h, near["y"])

        def tile(i, carry):
            for dc in range(2):
                rows = d_qkv[pl.ds(tile_row(c, y, i, dc), HALF), :]
                part[i, dc * HALF : (dc + 1) * HALF] = product_t(rows, w_qkv[...])
            core_copy(i).start()
            core_copy(i).wait_recv()
            part[i, :HALF] = part[i, :HALF] + from_core[i]

            @pl.when(i < 2)
            def _():
                y_copy(i).start()

            return carry

        lax.fori_loop(0, 4, tile, 0)


        far((1, 0))

        def of_branch(context, d_branch, d_middle, tokens):
            waits = copies(
                [
                    (context_hbm, context),
                    (d_branch_hbm, d_branch),
                    (d_middle_hbm, d_middle),
                    (tokens_hbm.at[pl.ds(own_row, QUARTER)], tokens),
                ]
            )
            branch_y.wait_recv()
            branch_fwd.start()
            for copy in waits:
                copy.wait()
            acc = t_product(d_branch[...].astype(bf16), context[quarter_rows(0, 0), :])
            branch_c.wait_recv()
            branch_fwd.wait_recv()
            for k, (dc, dy) in enumerate([(0, 1), (1, 0), (1, 1)]):
                acc = acc + t_product(branch_land[k].astype(bf16), context[quarter_rows(dc, dy), :])
            attn[:, head : 2 * head] = acc
            far((1, 1))
            to_y.wait_recv()
            attn[:, 2 * head :] = kv_halves[y] + kv_across[...]
            for i in range(4):
                attn_z1_copy(i).start()
            far((2, 0), (2, 1))
            for h in range(2):
                y_copy(h).wait_recv()
                at = slice(h * HALF, (h + 1) * HALF)
                grad = part[2 + h, :HALF] + from_y[h]
                d_in, of_gain = back_norm(tokens[at, :].astype(f32), gain_row(gain_rows, 0), grad)
                gains[0:1, :] = gains[0:1, :] + jnp.sum(of_gain, axis=0, keepdims=True)
                d = (d_middle[at, :] + d_in).astype(bf16)
                input_grad[pl.ds(pl.multiple_of(own_row + h * HALF, HALF), HALF), :] = d
                input_own[at, :] = d.astype(f32)

        pl.run_scoped(
            of_branch,
            pltpu.VMEM((length, head), bf16),
            pltpu.VMEM((QUARTER, width), f32),
            pltpu.VMEM((QUARTER, width), f32),
            pltpu.VMEM((QUARTER, width), bf16),
        )
        hop(0)
        arrive(0)
        hop(1)
        input_y.start()
        input_c.start()
        for i in range(4):
            core_copy(i).wait_send()
        for h in range(2):
            y_copy(h).wait_send()
        to_y.wait_send()

    pl.run_scoped(
        rest,
        pltpu.VMEM((width, 3 * head), bf16),
        pltpu.VMEM((4, TILE, width), f32),
        pltpu.VMEM((2, width, head // 2), f32),
    )

    arrive(1)
    hop(2)
    close(0)
    input_y.wait_recv()
    input_fwd.start()
    input_grad[quarter_rows(0, 1), :] = input_land[0].astype(bf16)
    input_c.wait_recv()
    input_grad[quarter_rows(1, 0), :] = input_land[1].astype(bf16)
    close(1)
    for i in range(4):
        attn_z1_copy(i).wait_recv()
        rows = block(attn, (2 * (i // 2) + zl) * 2 + i % 2)
        attn[rows, :] = attn[rows, :] + attn_z1[i]
    for j in (1, 0):
        attn_x_copy(j).start()
    start_x((2, 2), (2, 3))
    input_fwd.wait_recv()
    input_grad[quarter_rows(1, 1), :] = input_land[2].astype(bf16)
    arrive(2)
    hop(3)
    for j in (1, 0):
        attn_x_copy(j).wait_recv()
        rows = block(attn, (2 * (zh ^ j) + zl) * 2 + x)
        attn[rows, :] = attn[rows, :] + attn_x[j]
        if j == 1:
            attn_z2_copy.start()
    arrive(3)
    hop(4)
    close(2)
    attn_z2_copy.wait_recv()
    total = attn[block(attn, (2 * zh + zl) * 2 + x), :] + attn_z2[...]
    attn_out[...] = total[:, : 2 * head]
    kv_own[...] = total[:, 2 * head :]
    wide_y = remote(kv_own, kv_y, ys, 5, near["y"])
    wide_y.start()
    wide_y.wait_recv()
    kv_wide[:, : head // 2] = jnp.where(y == 0, kv_own[...], kv_y[...])
    kv_wide[:, head // 2 :] = jnp.where(y == 0, kv_y[...], kv_own[...])
    wide_c = remote(kv_wide, kv_wide_core, cs, 9, near["c"])
    wide_c.start()
    wide_c.wait_recv()
    kv_out[c] = kv_wide[...]
    kv_out[1 - c] = kv_wide_core[...]
    arrive(4)
    for m in range(3):
        z1_copy(m).wait_recv()
        ff_out[m, 1 - zl] = z1_land[m]
    for m in range(3):
        for j in range(4):
            x_copy(m, j).wait_send()
        for k in range(2):
            z2_copy(m, k).wait_send()
        z1_copy(m).wait_send()
    for i in range(4):
        attn_z1_copy(i).wait_send()
    for j in range(2):
        attn_x_copy(j).wait_send()
    for copy in (attn_z2_copy, branch_y, branch_c, branch_fwd, input_y, input_c, input_fwd, wide_y, wide_c):
        copy.wait_send()


def reduce_all(nx, dp_size, whole, small):
    length, width = whole[0].shape
    half = whole[4].shape[1]
    head = whole[11].shape[1]
    blk = width // dp_size
    return pl.pallas_call(
        functools.partial(reduce_kernel, nx),
        out_shape=(
            jax.ShapeDtypeStruct((3, 2, blk, half), f32),
            jax.ShapeDtypeStruct((blk, 2 * head), f32),
            jax.ShapeDtypeStruct((2, blk, head), f32),
            jax.ShapeDtypeStruct((length, width), bf16),
            jax.ShapeDtypeStruct((8, width), f32),
        ),
        in_specs=[ANY] * len(whole) + [VMEM] * len(small),
        out_specs=(VMEM,) * 5,
        scratch_shapes=[
            pltpu.VMEM((3, width, half), f32),
            pltpu.VMEM((12, blk, half), f32),
            pltpu.VMEM((6, blk, half), f32),
            pltpu.VMEM((3, blk, half), f32),
            pltpu.VMEM((4, HALF, width), f32),
            pltpu.VMEM((2, HALF, width), f32),
            pltpu.VMEM((3, QUARTER, width), f32),
            pltpu.VMEM((QUARTER, width), f32),
            pltpu.VMEM((3, QUARTER, width), f32),
            pltpu.VMEM((length, 3 * head), bf16),
            pltpu.VMEM((width, 2 * head + head // 2), f32),
            pltpu.VMEM((4, blk, 2 * head + head // 2), f32),
            pltpu.VMEM((2, blk, 2 * head + head // 2), f32),
            pltpu.VMEM((blk, 2 * head + head // 2), f32),
            pltpu.VMEM((width, head), f32),
            pltpu.VMEM((width, head // 2), f32),
            pltpu.VMEM((blk, head // 2), f32),
            pltpu.VMEM((blk, head // 2), f32),
            pltpu.VMEM((blk, head), f32),
            pltpu.VMEM((blk, head), f32),
            pltpu.VMEM((5, 8, width), f32),
        ]
        + dma(6, 11, 11, 7, 7, 15, 15, 8, 8, 8, 8),
        compiler_params=pltpu.CompilerParams(collective_id=2, has_side_effects=True, vmem_limit_bytes=VMEM_LIMIT),
        name="reduce_all",
    )(*whole, *small)


def body(
    links,
    tokens,
    segment_ids,
    cotangent,
    w_query,
    w_key,
    w_value,
    w_out,
    w_gate,
    w_up,
    w_down,
    gain_attn_in,
    gain_attn_out,
    gain_ffn_in,
    gain_ffn_out,
    gain_query,
    gain_key,
):
    length, width = tokens.shape
    head = w_query.shape[1]
    columns = w_gate.shape[1]
    nx = links.nx
    blk = width // links.dp_size
    dp = lax.axis_index("dp")
    wg, wu = w_gate.T, w_up.T
    rest = jnp.zeros((width - head,), f32)
    flat = [gain_attn_in, gain_attn_out, gain_ffn_in, gain_ffn_out, gain_query, rest, gain_key, rest, jnp.zeros((2 * width,), f32)]
    gain_rows = jnp.concatenate(flat).reshape(8, width)
    (
        normed_low,
        query_low,
        keys_low,
        values_low,
        query_raw,
        keys_raw,
        log_total,
        context_low,
        w_out_all,
        middle,
        branch,
    ) = attend(
        nx, tokens, w_query, w_key, w_value, w_out, segment_ids, gain_rows
    )
    normed_two, normed_other, d_out, d_own, d_first, layer_out, pair_own, for_gate, for_up, of_ffn_out = feed_forward(
        nx, middle, cotangent, gain_rows, wg, wu, w_down
    )
    d_other, pair_other, pair_gates, grad_context, d_branch_own, d_middle, of_middle = feed_back(
        nx,
        d_out,
        d_own,
        d_first,
        for_gate,
        for_up,
        normed_other,
        wg,
        wu,
        w_down,
        w_out_all,
        middle,
        branch,
        cotangent,
        gain_rows,
    )
    ff, attn_sum, kv_sum, input_grad, gains = reduce_all(
        nx,
        links.dp_size,
        [
            d_out,
            d_other,
            normed_two,
            normed_other,
            pair_own,
            pair_other,
            pair_gates,
            d_branch_own,
            d_middle,
            tokens,
            normed_low,
            query_low,
            keys_low,
            values_low,
            query_raw,
            keys_raw,
            context_low,
            grad_context,
            w_query,
            w_key,
            w_value,
        ],
        [log_total, segment_ids.reshape(1, length), gain_rows, of_ffn_out, of_middle],
    )
    ff = jnp.concatenate([ff[:, 0], ff[:, 1, :, : columns - ff.shape[3]]], axis=2)
    part = lax.dynamic_slice_in_dim(gains, dp * blk, blk, 1)
    hb = head // links.dp_size
    head_part = lax.dynamic_slice_in_dim(gains, dp * hb, hb, 1)
    return (
        layer_out,
        input_grad,
        attn_sum[:, :head],
        kv_sum[0],
        kv_sum[1],
        attn_sum[:, head:].T,
        ff[1],
        ff[2],
        ff[0].T,
        part[0],
        part[1],
        part[2],
        part[3],
        head_part[4],
        head_part[5],
    )


def body_any(
    links,
    tokens,
    segment_ids,
    cotangent,
    w_query,
    w_key,
    w_value,
    w_out,
    w_gate,
    w_up,
    w_down,
    gain_attn_in,
    gain_attn_out,
    gain_ffn_in,
    gain_ffn_out,
    gain_query,
    gain_key,
):
    length, width = tokens.shape
    head = w_query.shape[1]
    quarter = length // 4
    half_ff = w_gate.shape[1] // 2
    nx = links.nx
    blk = width // links.dp_size
    dp, t = lax.axis_index("dp"), lax.axis_index("tensor")
    z, x = dp // nx, dp % nx
    y, c = t // 2, t % 2
    parity = z % 2
    one = jnp.where(segment_ids[0] < length, 1.0, 0.5).astype(f32)

    def keep_low(a):
        return (a * one).astype(bf16)

    def place(dc, dy):
        return ((c ^ dc) * 2 + (y ^ dy)) * quarter

    def rows(a, dc, dy):
        return lax.dynamic_slice_in_dim(a, place(dc, dy), quarter, 0)

    def to_absolute(pieces):
        stack = jnp.stack([pieces[0][0], pieces[0][1], pieces[1][0], pieces[1][1]])
        mine = c * 2 + y
        return jnp.concatenate([lax.dynamic_index_in_dim(stack, mine ^ b, 0, keepdims=False) for b in range(4)], axis=0)

    out_own = w_out.astype(f32)
    out_y = links.y(out_own)
    out_c = links.core(out_own)
    out_yc = links.core(out_y)
    w_out_all = jnp.concatenate([w_out, keep_low(out_c), keep_low(out_y), keep_low(out_yc)], axis=0)

    wg_h = jnp.where(parity == 0, w_gate[:, :half_ff], w_gate[:, half_ff:])
    wu_h = jnp.where(parity == 0, w_up[:, :half_ff], w_up[:, half_ff:])
    wd_h = jnp.where(parity == 0, w_down[:half_ff], w_down[half_ff:])

    hidden_in = tokens.astype(f32)
    normed_low = low(rms_norm(hidden_in, gain_attn_in))
    query_raw = product(normed_low, w_query)
    keys_raw = product(normed_low, w_key)
    query_low = low(rms_norm(query_raw, gain_query))
    keys_low = low(rms_norm(keys_raw, gain_key))
    values_low = low(product(normed_low, w_value))
    places = jnp.arange(length)
    allowed = (places[:, None] >= places[None, :]) & (segment_ids[:, None] == segment_ids[None, :])

    def scores_of():
        raw = product_t(query_low, keys_low) * score_scale
        return jnp.where(allowed, raw, -1e30)

    scores = scores_of()
    largest = jnp.max(scores, axis=-1, keepdims=True)
    exponent = jnp.exp(scores - largest)
    total = jnp.sum(exponent, axis=-1, keepdims=True)
    log_total = largest + jnp.log(total)
    context_low = low(product(low(exponent / total), values_low))

    context = context_low.astype(f32)
    mine = jnp.concatenate([rows(context, 0, 1), rows(context, 0, 0)], axis=0)
    of_core = links.core(jnp.concatenate([rows(context, 1, 1), rows(context, 1, 0)], axis=0))
    of_y = links.y(jnp.concatenate([rows(context, 0, 0), rows(context, 0, 1)], axis=0))
    of_yc = links.y(jnp.concatenate([of_core[quarter:], of_core[:quarter]], axis=0))
    context_all = jnp.concatenate([low(mine), keep_low(of_core), keep_low(of_y), keep_low(of_yc)], axis=1)
    branch = product(context_all, w_out_all)
    hidden_rows = jnp.concatenate([rows(tokens, 0, 1), rows(tokens, 0, 0)], axis=0).astype(f32)
    middle_own = hidden_rows + rms_norm(branch, gain_attn_out)
    middle_core = links.core(middle_own)

    middles, normed_two, inners, parts = [], [], [], []
    saved = []
    for k in range(2):
        at = slice(k * quarter, (k + 1) * quarter)
        middle = jnp.concatenate([middle_own[at], middle_core[at]], axis=0)
        normed_k = low(rms_norm(middle, gain_ffn_in))
        gate, upward = product(normed_k, w_gate), product(normed_k, w_up)
        inner = low(activate(gate, upward))
        part = product(inner, w_down)
        middles.append(middle)
        normed_two.append(normed_k)
        saved.append((gate, upward))
        parts.append(part)
    normed_own = low(rms_norm(middle_own, gain_ffn_in)).astype(f32)
    other_own = links.z1(normed_own)
    other_core = links.core(other_own)
    normed_other = jnp.concatenate([keep_low(other_own), keep_low(other_core)], axis=0)

    def gather_quarters(parts):
        sums = [part[:quarter] + links.core(part[quarter:]) for part in parts]
        return sums[1] + links.y(sums[0])

    output_q = gather_quarters(parts)
    output_y = links.y(output_q)
    output_c = links.core(output_q)
    output_yc = links.core(output_y)
    outputs = [jnp.concatenate([output_y, output_yc], axis=0), jnp.concatenate([output_q, output_c], axis=0)]
    grad_out = cotangent.astype(f32)
    d_outputs, layer_pieces, grad_ffn_out = [], [], 0.0
    for k in range(2):
        dy_k = jnp.concatenate([rows(cotangent, 0, 1 - k), rows(cotangent, 1, 1 - k)], axis=0).astype(f32)
        layer_k = low(middles[k] + rms_norm(outputs[k], gain_ffn_out))
        d_k, gain_k = rms_back(outputs[k], gain_ffn_out, dy_k)
        grad_ffn_out = grad_ffn_out + gain_k
        d_outputs.append(low(d_k))
        layer_pieces.append(layer_k)
    layer_out = to_absolute(
        [
            [layer_pieces[1][:quarter], layer_pieces[0][:quarter]],
            [layer_pieces[1][quarter:], layer_pieces[0][quarter:]],
        ]
    )

    d_own_rows = [d[:quarter].astype(f32) for d in d_outputs]
    got_own = [links.z1(d_own_rows[1]), links.z1(d_own_rows[0])]
    got_core = [links.core(g) for g in got_own]
    d_other = jnp.concatenate(
        [keep_low(got_own[1]), keep_low(got_own[0]), keep_low(got_core[1]), keep_low(got_core[0])], axis=0
    )

    back_parts = []
    for k in range(2):
        gate, upward = saved[k]
        d_inner = product_t(d_outputs[k], w_down)
        _, pull = jax.vjp(activate, gate, upward)
        d_gate, d_up = pull(d_inner)
        back_parts.append(product_t(low(d_gate), w_gate) + product_t(low(d_up), w_up))
    d_normed_q = gather_quarters(back_parts)
    middle_q = middle_own[quarter:]
    branch_q = branch[quarter:]
    dy_q = rows(cotangent, 0, 0).astype(f32)
    d_mid, grad_ffn_in = rms_back(middle_q, gain_ffn_in, d_normed_q)
    d_middle = dy_q + d_mid
    d_branch, grad_attn_out = rms_back(branch_q, gain_attn_out, d_middle)
    d_branch_low = low(d_branch)
    d_context = low(product_t(d_branch_low, w_out_all)).astype(f32)
    heads = [d_context[:, i * head : (i + 1) * head] for i in range(4)]
    c_got = links.core(jnp.concatenate([heads[1], heads[3]], axis=1))
    y_got = links.y(jnp.concatenate([heads[2], c_got[:, head:]], axis=1))
    grad_context = keep_low(
        to_absolute([[heads[0], y_got[:, :head]], [c_got[:, :head], y_got[:, head:]]])
    )
    d_branch_own = d_branch_low.astype(f32)
    d_branch_y = links.y(d_branch_own)
    d_branch_c = links.core(d_branch_own)
    d_branch_yc = links.core(d_branch_y)
    d_branch_all = jnp.concatenate(
        [d_branch_low, keep_low(d_branch_y), keep_low(d_branch_c), keep_low(d_branch_yc)], axis=0
    )
    context_rel = jnp.concatenate(
        [rows(context_low, 0, 0), rows(context_low, 0, 1), rows(context_low, 1, 0), rows(context_low, 1, 1)], axis=0
    )
    grad_w_out_t = t_product(d_branch_all, context_rel)

    attn_prob = jnp.exp(scores_of() - log_total)
    prob_low = low(attn_prob)
    grad_prob = product_t(grad_context, values_low)
    grad_values = low(t_product(prob_low, grad_context))
    balance = jnp.sum(grad_prob * attn_prob, axis=-1, keepdims=True)
    grad_scores = low(attn_prob * (grad_prob - balance))
    grad_query_n = product(grad_scores, keys_low) * score_scale
    grad_keys_n = t_product(grad_scores, query_low) * score_scale
    d_query, grad_gain_query = rms_back(query_raw, gain_query, grad_query_n)
    d_keys, grad_gain_key = rms_back(keys_raw, gain_key, grad_keys_n)
    d_query, d_keys = low(d_query), low(d_keys)
    d_qkv = jnp.concatenate([d_query, d_keys, grad_values], axis=1)
    w_qkv = jnp.concatenate([w_query, w_key, w_value], axis=1)
    in_parts = []
    for k in range(2):
        rows_k = jnp.concatenate([rows(d_qkv, 0, 1 - k), rows(d_qkv, 1, 1 - k)], axis=0)
        in_parts.append(product_t(rows_k, w_qkv))
    d_normed_in = gather_quarters(in_parts)
    hidden_q = rows(tokens, 0, 0).astype(f32)
    d_in, grad_attn_in = rms_back(hidden_q, gain_attn_in, d_normed_in)
    input_q = low(d_middle + d_in)
    input_own = input_q.astype(f32)
    input_y = links.y(input_own)
    input_c = links.core(input_own)
    input_yc = links.core(input_y)
    input_grad = keep_low(to_absolute([[input_own, input_y], [input_c, input_yc]]))

    grad_qkv = t_product(normed_low, d_qkv)
    grad_w_query, grad_kv = grad_qkv[:, :head], grad_qkv[:, head:]
    kv_keep = jnp.where(c == 0, grad_kv[:, :head], grad_kv[:, head:])
    kv_send = jnp.where(c == 0, grad_kv[:, head:], grad_kv[:, :head])
    kv = kv_keep + links.core(kv_send)
    kv_half = head // 2
    kv_keep = jnp.where(y == 0, kv[:, :kv_half], kv[:, kv_half:])
    kv_send = jnp.where(y == 0, kv[:, kv_half:], kv[:, :kv_half])
    kv = kv_keep + links.y(kv_send)
    attn_grads = jnp.concatenate([grad_w_query, grad_w_out_t, kv], axis=1)

    normed_all = jnp.concatenate(
        [normed_two[0][:quarter], normed_two[1][:quarter], normed_two[0][quarter:], normed_two[1][quarter:], normed_other],
        axis=0,
    )
    d_all = jnp.concatenate(
        [d_outputs[0][:quarter], d_outputs[1][:quarter], d_outputs[0][quarter:], d_outputs[1][quarter:], d_other], axis=0
    )
    gate, upward = product(normed_all, wg_h), product(normed_all, wu_h)
    inner, pull = jax.vjp(activate, gate, upward)
    inner = low(inner)
    d_inner = product_t(d_all, wd_h)
    d_gate, d_up = pull(d_inner)
    ff_grads = [t_product(d_all, inner), t_product(normed_all, low(d_gate)), t_product(normed_all, low(d_up))]

    zh, zl = z // 2, z % 2

    def sum_x(grads, z_half):
        mine = lax.dynamic_index_in_dim(grads, z_half, 0, keepdims=False)
        acc = lax.dynamic_index_in_dim(mine, x, 1, keepdims=False)
        for step in range(1, nx):
            to = lax.dynamic_index_in_dim(mine, (x + step) % nx, 1, keepdims=False)
            acc = acc + links.x(to, step)
        return acc

    def scatter(grads):
        grads = grads.reshape(2, 2, nx, blk, grads.shape[1])
        far = sum_x(grads, 1 - zh)
        near = sum_x(grads, zh)
        return near + links.z2(far)

    ff_sums = []
    for grads in ff_grads:
        got = scatter(grads)
        own = lax.dynamic_index_in_dim(got, zl, 0, keepdims=False)
        other = links.z1(lax.dynamic_index_in_dim(got, 1 - zl, 0, keepdims=False))
        ff_sums.append(
            jnp.where(
                parity == 0, jnp.concatenate([own, other], axis=1), jnp.concatenate([other, own], axis=1)
            )
        )
    grad_w_down, grad_w_gate, grad_w_up = ff_sums[0].T, ff_sums[1], ff_sums[2]

    got = scatter(attn_grads)
    attn_sum = lax.dynamic_index_in_dim(got, zl, 0, keepdims=False) + links.z1(
        lax.dynamic_index_in_dim(got, 1 - zl, 0, keepdims=False)
    )
    grad_w_query = attn_sum[:, :head]
    grad_w_out = attn_sum[:, head : 2 * head].T
    kv_own = attn_sum[:, 2 * head :]
    kv_y = links.y(kv_own)
    kv_wide = jnp.where(y == 0, jnp.concatenate([kv_own, kv_y], axis=1), jnp.concatenate([kv_y, kv_own], axis=1))
    kv_c = links.core(kv_wide)
    grad_w_key = jnp.where(c == 0, kv_wide, kv_c)
    grad_w_value = jnp.where(c == 0, kv_c, kv_wide)

    small = jnp.concatenate(
        [
            grad_attn_in.reshape(links.dp_size, -1),
            grad_attn_out.reshape(links.dp_size, -1),
            grad_ffn_in.reshape(links.dp_size, -1),
            (grad_ffn_out * 0.25).reshape(links.dp_size, -1),
            grad_gain_query.reshape(links.dp_size, -1),
            grad_gain_key.reshape(links.dp_size, -1),
        ],
        axis=1,
    )
    small = small + links.core(small)
    small = small + links.y(small)
    small = small.reshape(2, 2, nx, 1, small.shape[1])
    acc = lax.dynamic_index_in_dim(small, x, 2, keepdims=False)
    for step in range(1, nx):
        acc = acc + links.x(lax.dynamic_index_in_dim(small, (x + step) % nx, 2, keepdims=False), step)
    acc = lax.dynamic_index_in_dim(acc, zh, 0, keepdims=False) + links.z2(
        lax.dynamic_index_in_dim(acc, 1 - zh, 0, keepdims=False)
    )
    acc = lax.dynamic_index_in_dim(acc, zl, 0, keepdims=False) + links.z1(
        lax.dynamic_index_in_dim(acc, 1 - zl, 0, keepdims=False)
    )
    acc = acc.reshape(-1)
    hb = head // links.dp_size
    return (
        layer_out,
        input_grad,
        grad_w_query,
        grad_w_key,
        grad_w_value,
        grad_w_out,
        grad_w_gate,
        grad_w_up,
        grad_w_down,
        acc[:blk],
        acc[blk : 2 * blk],
        acc[2 * blk : 3 * blk],
        acc[3 * blk : 4 * blk],
        acc[4 * blk : 4 * blk + hb],
        acc[4 * blk + hb :],
    )


def solution(mesh):
    links = Links(mesh)
    return jax.shard_map(
        functools.partial(body if links.nx == 2 else body_any, links),
        mesh=mesh,
        in_specs=(
            P("dp", None),
            P("dp"),
            P("dp", None),
            P(None, "tensor"),
            P(),
            P(),
            P("tensor", None),
            P(None, "tensor"),
            P(None, "tensor"),
            P("tensor", None),
            P(),
            P(),
            P(),
            P(),
            P(),
            P(),
        ),
        out_specs=(
            P("dp", None),
            P("dp", None),
            P("dp", "tensor"),
            P("dp", None),
            P("dp", None),
            P("tensor", "dp"),
            P("dp", "tensor"),
            P("dp", "tensor"),
            P("tensor", "dp"),
            P("dp"),
            P("dp"),
            P("dp"),
            P("dp"),
            P("dp"),
            P("dp"),
        ),
        check_vma=False,
    )
```

```python
import functools

import jax
import jax.numpy as jnp
from jax import lax
from jax.experimental import pallas as pl
from jax.experimental.pallas import tpu as pltpu
from jax.sharding import PartitionSpec as P

epsilon = 1e-06
score_scale = 0.0625
NZ = 4

f32 = jnp.float32
bf16 = jnp.bfloat16


def rms_norm(values, gain):
    inverse = lax.rsqrt(jnp.mean(values * values, axis=-1, keepdims=True) + epsilon)
    return values * inverse * (1.0 + gain)


def rms_back(values, gain, grad):
    inverse = lax.rsqrt(jnp.mean(values * values, axis=-1, keepdims=True) + epsilon)
    hat = values * inverse
    scaled = grad * (1.0 + gain)
    back = inverse * (scaled - hat * jnp.mean(scaled * hat, axis=-1, keepdims=True))
    return back, jnp.sum(grad * hat, axis=0)


def product(left, right):
    return jnp.dot(left, right, preferred_element_type=f32)


def product_t(left, right):
    return lax.dot_general(left, right, (((1,), (1,)), ((), ())), preferred_element_type=f32)


def t_product(left, right):
    return lax.dot_general(left, right, (((0,), (0,)), ((), ())), preferred_element_type=f32)


def activate(gate, upward):
    return jax.nn.gelu(gate, approximate=True) * upward


class Links:
    def __init__(self, mesh):
        self.dp_size = mesh.shape["dp"]
        self.nx = self.dp_size // NZ
        tensor = mesh.shape["tensor"]
        self.perm_core = [(t, t ^ 1) for t in range(tensor)]
        self.perm_y = [(t, t ^ 2) for t in range(tensor)]
        nx = self.nx
        self.perm_z1 = [(z * nx + x, (z ^ 1) * nx + x) for z in range(NZ) for x in range(nx)]
        self.perm_z2 = [(z * nx + x, (z ^ 2) * nx + x) for z in range(NZ) for x in range(nx)]

    def core(self, a):
        return lax.ppermute(a, "tensor", self.perm_core)

    def y(self, a):
        return lax.ppermute(a, "tensor", self.perm_y)

    def z1(self, a):
        return lax.ppermute(a, "dp", self.perm_z1)

    def z2(self, a):
        return lax.ppermute(a, "dp", self.perm_z2)

    def x(self, a, step):
        nx = self.nx
        return lax.ppermute(a, "dp", [(z * nx + x, z * nx + (x + step) % nx) for z in range(NZ) for x in range(nx)])


def low(a):
    return a.astype(bf16)


MESH = pl.DeviceIdType.MESH
ANY = pl.BlockSpec(memory_space=pl.ANY)
VMEM = pl.BlockSpec(memory_space=pltpu.VMEM)
TILE, HALF, QUARTER = 256, 128, 256
VMEM_LIMIT = 127 << 19


def spots(nx):
    dp, t = lax.axis_index("dp"), lax.axis_index("tensor")
    z, x = dp // nx, dp % nx
    near = {
        "c": {"tensor": t ^ 1},
        "y": {"tensor": t ^ 2},
        "z1": {"dp": (z ^ 1) * nx + x},
        "z2": {"dp": (z ^ 2) * nx + x},
        "x": {"dp": z * nx + (x ^ 1)},
    }
    return z, x, t // 2, t % 2, near


def remote(src, dst, sems, index, to):
    return pltpu.make_async_remote_copy(
        src_ref=src, dst_ref=dst, send_sem=sems[0].at[index], recv_sem=sems[1].at[index], device_id=to, device_id_type=MESH
    )


def greet(others):
    barrier = pltpu.get_barrier_semaphore()
    for other in others:
        pl.semaphore_signal(barrier, inc=1, device_id=other, device_id_type=MESH)
    pl.semaphore_wait(barrier, len(others))


def tile_row(c, y, i, dc):
    dy = 1 - i // 2
    return pl.multiple_of(((c ^ dc) * 2 + (y ^ dy)) * QUARTER + (i % 2) * HALF, HALF)


def gelu_parts(u):
    k = 0.7978845608028654
    square = u * u
    th = jnp.tanh(k * u * (1.0 + 0.044715 * square))
    side = 0.5 * (1.0 + th)
    return u * side, side + 0.5 * u * (1.0 - th * th) * (k * (1.0 + 3.0 * 0.044715 * square))


def gelu_tanh(u):
    return 0.5 * u * (1.0 + jnp.tanh(0.7978845608028654 * u * (1.0 + 0.044715 * (u * u))))


def gain_row(gains, k):
    return gains[k : k + 1, :]


def forward_kernel(
    nx,
    middle,
    cotangent,
    gains,
    w_gate,
    w_up,
    w_down,
    normed_hbm,
    other_hbm,
    d_out_hbm,
    d_own_hbm,
    d_first,
    layer_hbm,
    pair_own_hbm,
    for_gate_hbm,
    for_up_hbm,
    gain_grad,
    normed,
    other,
    d_out,
    d_own,
    layer_out,
    out,
    dy,
    inner,
    for_gate,
    for_up,
    part,
    from_core,
    from_y,
    z_stage,
    z_land,
    c_land,
    local,
    stores,
    tile_stores,
    c_send,
    c_recv,
    y_send,
    y_recv,
    z_send,
    z_recv,
):
    z, x, y, c, near = spots(nx)
    core, across, pair = near["c"], near["y"], near["z1"]
    cs, ys, zs = (c_send, c_recv), (y_send, y_recv), (z_send, z_recv)
    loads = []
    for i in range(4):
        for dc in range(2):
            copy = pltpu.make_async_copy(
                cotangent.at[pl.ds(tile_row(c, y, i, dc), HALF)],
                dy.at[pl.ds(i * TILE + dc * HALF, HALF)],
                local.at[i * 2 + dc],
            )
            copy.start()
            loads.append(copy)
    greet([core, across, pair])
    columns = w_gate.shape[0]
    cut = pl.cdiv(columns, TILE) * HALF
    for ref in (inner, for_gate, for_up):
        for slot in range(2):
            ref[slot, :, columns:] = jnp.zeros((TILE, 2 * cut - columns), bf16)

    def tile_puts(i):
        slot = i % 2
        at = pl.ds(pl.multiple_of(i * TILE, TILE), TILE)
        mine = pl.ds(pl.multiple_of(z % 2 * cut, HALF), cut)
        return [
            pltpu.make_async_copy(inner.at[slot, :, mine], pair_own_hbm.at[at], tile_stores.at[slot, 0]),
            pltpu.make_async_copy(for_gate.at[slot], for_gate_hbm.at[at], tile_stores.at[slot, 1]),
            pltpu.make_async_copy(for_up.at[slot], for_up_hbm.at[at], tile_stores.at[slot, 2]),
        ]

    def core_copy(i):
        return remote(part.at[i, pl.ds(HALF, HALF)], from_core.at[i], cs, i, core)

    def y_copy(h):
        return remote(part.at[h, pl.ds(0, HALF)], from_y.at[h], ys, h, across)

    def z_copy(i):
        return remote(z_stage.at[i], z_land.at[i], zs, i, pair)

    first_copy = remote(d_own.at[2], d_first, zs, 4, pair)

    def z_forward(i):
        return remote(z_land.at[i], c_land.at[i], cs, 8 + i, core)

    def step(i, carry):
        at = pl.ds(pl.multiple_of(i * TILE, TILE), TILE)
        m = middle[at, :]
        inverse = lax.rsqrt(jnp.mean(m * m, axis=-1, keepdims=True) + epsilon)
        n = (m * inverse * (1.0 + gain_row(gains, 2))).astype(bf16)
        normed[at, :] = n
        z_stage[i] = n[:HALF].astype(f32)
        z_copy(i).start()
        slot = i % 2

        @pl.when(i >= 2)
        def _():
            for copy in tile_puts(i - 2):
                copy.wait()

        for lo in range(0, columns, TILE):
            hi = min(lo + TILE, columns)
            g = product_t(n, w_gate[lo:hi, :])
            u = product_t(n, w_up[lo:hi, :])
            act, slope = gelu_parts(g)
            inner[slot, :, lo:hi] = (act * u).astype(bf16)
            for_gate[slot, :, lo:hi] = (u * slope).astype(bf16)
            for_up[slot, :, lo:hi] = act.astype(bf16)
        part[i] = product(inner[slot, :, :columns], w_down[...])
        for copy in tile_puts(i):
            copy.start()
        core_copy(i).start()
        core_copy(i).wait_recv()
        part[i, :HALF] = part[i, :HALF] + from_core[i]

        @pl.when(i < 2)
        def _():
            y_copy(i).start()

        return carry

    lax.fori_loop(0, 4, step, 0)

    def tile_at(i):
        return pl.ds(pl.multiple_of(i * TILE, TILE), TILE)

    put_normed = pltpu.make_async_copy(normed, normed_hbm, stores.at[8])
    put_layer = pltpu.make_async_copy(layer_out, layer_hbm, stores.at[9])

    def put_own(i):
        return pltpu.make_async_copy(d_own.at[i], d_own_hbm.at[i], stores.at[i])

    def put_d(i):
        return pltpu.make_async_copy(d_out.at[tile_at(i)], d_out_hbm.at[tile_at(i)], stores.at[4 + i])

    def put_other(i):
        return pltpu.make_async_copy(other.at[tile_at(i)], other_hbm.at[tile_at(i)], stores.at[10 + i])

    put_normed.start()
    for i in (2, 3):
        for copy in tile_puts(i):
            copy.wait()
    for copy in loads:
        copy.wait()
    gain_grad[...] = jnp.zeros_like(gain_grad)
    gain = 1.0 + gain_row(gains, 3)

    def finish(i, dc):
        at = pl.ds(pl.multiple_of(i * TILE + dc * HALF, HALF), HALF)
        o, g = out[at, :], dy[at, :].astype(f32)
        inverse = lax.rsqrt(jnp.mean(o * o, axis=-1, keepdims=True) + epsilon)
        hat = o * inverse
        scaled = g * gain
        d = (inverse * (scaled - hat * jnp.mean(scaled * hat, axis=-1, keepdims=True))).astype(bf16)
        d_out[at, :] = d
        gain_grad[...] = gain_grad[...] + jnp.sum((g * hat).reshape(HALF // 8, 8, g.shape[1]), axis=0)
        layer_out[pl.ds(tile_row(c, y, i, dc), HALF), :] = (middle[at, :] + hat * gain).astype(bf16)
        return d

    def half_at(i, dc):
        return pl.ds(pl.multiple_of(i * TILE + dc * HALF, HALF), HALF)

    def spread_y(h):
        return remote(out.at[half_at(2 + h, 0)], out.at[half_at(h, 0)], ys, 2 + h, across)

    def spread_core(i):
        return remote(out.at[half_at(i, 0)], out.at[half_at(i, 1)], cs, 4 + i, core)

    def close_tile(n, carry):
        i = (n + 2) % 4

        @pl.when(n < 2)
        def _():
            y_copy(n).wait_recv()
            out[half_at(i, 0), :] = part[i, :HALF] + from_y[n]
            spread_y(n).start()

        @pl.when(n == 2)
        def _():
            for i in range(3):
                z_copy(i).wait_recv()
                z_forward(i).start()
            for i in range(2):
                take(i)

        @pl.when(n >= 2)
        def _():
            spread_y(i).wait_recv()

        spread_core(i).start()
        d_own[i] = finish(i, 0).astype(f32)

        @pl.when(n == 0)
        def _():
            first_copy.start()

        put_own(i).start()
        spread_core(i).wait_recv()
        finish(i, 1)
        put_d(i).start()
        return carry

    def take(i):
        z_forward(i).wait_recv()
        other[i * TILE : i * TILE + HALF, :] = z_land[i].astype(bf16)
        other[i * TILE + HALF : (i + 1) * TILE, :] = c_land[i].astype(bf16)
        put_other(i).start()

    lax.fori_loop(0, 4, close_tile, 0)
    put_layer.start()
    z_copy(3).wait_recv()
    z_forward(3).start()
    for i in range(2, 4):
        take(i)
    for i in range(4):
        core_copy(i).wait_send()
        z_copy(i).wait_send()
        z_forward(i).wait_send()
        spread_core(i).wait_send()
        put_own(i).wait()
        put_d(i).wait()
        put_other(i).wait()
    for h in range(2):
        y_copy(h).wait_send()
        spread_y(h).wait_send()
    put_normed.wait()
    put_layer.wait()
    first_copy.wait()


def dma(*counts):
    return [pltpu.SemaphoreType.DMA((n,)) for n in counts]


def feed_forward(nx, middle, cotangent, gains, w_gate, w_up, w_down):
    length, width = middle.shape
    columns = pl.cdiv(w_gate.shape[0], TILE) * TILE
    rows_low = jax.ShapeDtypeStruct((length, width), bf16)
    return pl.pallas_call(
        functools.partial(forward_kernel, nx),
        out_shape=(
            rows_low,
            rows_low,
            rows_low,
            jax.ShapeDtypeStruct((4, HALF, width), f32),
            jax.ShapeDtypeStruct((HALF, width), f32),
            rows_low,
            jax.ShapeDtypeStruct((length, columns // 2), bf16),
            jax.ShapeDtypeStruct((length, columns), bf16),
            jax.ShapeDtypeStruct((length, columns), bf16),
            jax.ShapeDtypeStruct((8, width), f32),
        ),
        in_specs=[VMEM, ANY] + [VMEM] * 4,
        out_specs=(ANY,) * 4 + (VMEM, ANY, ANY, ANY, ANY, VMEM),
        scratch_shapes=[pltpu.VMEM((length, width), bf16)] * 3
        + [
            pltpu.VMEM((4, HALF, width), f32),
            pltpu.VMEM((length, width), bf16),
            pltpu.VMEM((length, width), f32),
            pltpu.VMEM((length, width), bf16),
            pltpu.VMEM((2, TILE, columns), bf16),
            pltpu.VMEM((2, TILE, columns), bf16),
            pltpu.VMEM((2, TILE, columns), bf16),
            pltpu.VMEM((4, TILE, width), f32),
            pltpu.VMEM((4, HALF, width), f32),
            pltpu.VMEM((2, HALF, width), f32),
            pltpu.VMEM((4, HALF, width), f32),
            pltpu.VMEM((4, HALF, width), f32),
            pltpu.VMEM((4, HALF, width), f32),
        ]
        + dma(8, 14)
        + [pltpu.SemaphoreType.DMA((2, 3))]
        + dma(12, 12, 4, 4, 5, 5),
        compiler_params=pltpu.CompilerParams(collective_id=0, has_side_effects=True, vmem_limit_bytes=VMEM_LIMIT),
        name="feed_forward",
    )(middle, cotangent, gains, w_gate, w_up, w_down)


def back_kernel(
    nx,
    d_out_hbm,
    d_own_hbm,
    d_first_hbm,
    for_gate_hbm,
    for_up_hbm,
    other_hbm,
    w_gate_hbm,
    w_up_hbm,
    w_down_hbm,
    w_out_hbm,
    middle_hbm,
    branch_hbm,
    dy_hbm,
    gains,
    d_other,
    pair_in,
    pair_gates,
    heads,
    d_branch_out,
    d_middle_out,
    gain_grads,
    d_out,
    for_gate,
    for_up,
    other,
    w_gate,
    w_up,
    w_down,
    w_out,
    middle,
    branch,
    dy,
    gates,
    ups,
    inner,
    part,
    from_core,
    from_y,
    z_land,
    c_land,
    loads_sem,
    tiles_sem,
    stores_sem,
    c_send,
    c_recv,
    y_send,
    y_recv,
    z_send,
    z_recv,
):
    z, x, y, c, near = spots(nx)
    core, across, pair = near["c"], near["y"], near["z1"]
    cs, ys, zs = (c_send, c_recv), (y_send, y_recv), (z_send, z_recv)
    parity = z % 2
    real, columns = w_gate_hbm.shape[0], w_gate.shape[0]
    half = columns // 2
    head = heads.shape[2]
    own_row = pl.multiple_of((c * 2 + y) * QUARTER, QUARTER)
    sources = [
        (d_out_hbm, d_out),
        (w_gate_hbm, w_gate.at[pl.ds(0, real)]),
        (w_up_hbm, w_up.at[pl.ds(0, real)]),
        (w_down_hbm, w_down.at[pl.ds(0, real)]),
        (other_hbm, other),
        (w_out_hbm, w_out),
        (middle_hbm.at[pl.ds(2 * TILE, HALF)], middle.at[pl.ds(0, HALF)]),
        (middle_hbm.at[pl.ds(3 * TILE, HALF)], middle.at[pl.ds(HALF, HALF)]),
        (branch_hbm, branch),
        (dy_hbm.at[pl.ds(own_row, QUARTER)], dy),
        (d_first_hbm, z_land.at[2]),
    ]
    loads = [pltpu.make_async_copy(src, dst, loads_sem.at[k]) for k, (src, dst) in enumerate(sources)]
    for copy in loads:
        copy.start()
    if real < columns:
        for ref in (w_gate, w_up, w_down):
            ref[real:, :] = jnp.zeros((columns - real, ref.shape[1]), bf16)
    greet([core, across, pair])

    def core_copy(i):
        return remote(part.at[i, pl.ds(HALF, HALF)], from_core.at[i], cs, i, core)

    def y_copy(h):
        return remote(part.at[h, pl.ds(0, HALF)], from_y.at[h], ys, h, across)

    def z_copy(i):
        return remote(d_own_hbm.at[i], z_land.at[i], zs, i, pair)

    def z_forward(i):
        return remote(z_land.at[i], c_land.at[i], cs, 4 + i, core)

    for i in (3, 0, 1):
        z_copy(i).start()
    def tile_loads(i):
        slot = i % 2
        at = pl.ds(pl.multiple_of(i * TILE, TILE), TILE)
        return [
            pltpu.make_async_copy(for_gate_hbm.at[at], for_gate.at[slot], tiles_sem.at[slot, 0]),
            pltpu.make_async_copy(for_up_hbm.at[at], for_up.at[slot], tiles_sem.at[slot, 1]),
        ]

    for i in range(2):
        for copy in tile_loads(i):
            copy.start()
    for copy in loads[:4]:
        copy.wait()

    mine = pl.multiple_of(parity * half, HALF)

    def stores(i, base):
        slot = i % 2
        at = pl.ds(pl.multiple_of(base + i * TILE, TILE), TILE)
        pick = pl.ds(mine, half)
        first = []
        if base:
            first = [
                pltpu.make_async_copy(
                    inner.at[slot], pair_in.at[pl.ds(pl.multiple_of(i * TILE, TILE), TILE)], stores_sem.at[slot, 0]
                )
            ]
        return first + [
            pltpu.make_async_copy(gates.at[slot, :, pick], pair_gates.at[at, pl.ds(0, half)], stores_sem.at[slot, 1]),
            pltpu.make_async_copy(ups.at[slot, :, pick], pair_gates.at[at, pl.ds(half, half)], stores_sem.at[slot, 2]),
        ]

    def piece(n, d, slot, at, own):
        g = product_t(n, w_gate[at, :])
        u = product_t(n, w_up[at, :])
        di = product_t(d, w_down[at, :])
        act, slope = gelu_parts(g)
        inner[slot, :, own] = (act * u).astype(bf16)
        gates[slot, :, at] = (di * u * slope).astype(bf16)
        ups[slot, :, at] = (di * act).astype(bf16)

    def own_tile(i, carry):
        at = pl.ds(pl.multiple_of(i * TILE, TILE), TILE)
        slot = i % 2

        @pl.when(i >= 2)
        def _():
            for copy in stores(i - 2, 0):
                copy.wait()

        for copy in tile_loads(i):
            copy.wait()
        d = d_out[at, :]
        for lo in range(0, columns, TILE):
            cols = pl.ds(lo, TILE)
            di = product_t(d, w_down[cols, :])
            gates[slot, :, cols] = (di * for_gate[slot, :, cols].astype(f32)).astype(bf16)
            ups[slot, :, cols] = (di * for_up[slot, :, cols].astype(f32)).astype(bf16)

        @pl.when(i < 2)
        def _():
            for copy in tile_loads(i + 2):
                copy.start()

        for copy in stores(i, 0):
            copy.start()
        part[i] = product(gates[slot], w_gate[...]) + product(ups[slot], w_up[...])
        core_copy(i).start()
        core_copy(i).wait_recv()
        part[i, :HALF] = part[i, :HALF] + from_core[i]

        @pl.when(i < 2)
        def _():
            y_copy(i).start()

        return carry

    lax.fori_loop(0, 4, own_tile, 0)
    for copy in loads[4:]:
        copy.wait()

    def other_tile(n, carry):
        i, slot = (n + 2) % 4, n % 2

        @pl.when(n > 0)
        def _():
            z_copy(i).wait_recv()

        z_forward(i).start()

        @pl.when(n < 2)
        def _():
            for copy in stores(i, 0):
                copy.wait()

        @pl.when(n >= 2)
        def _():
            for copy in stores(n, d_out.shape[0]):
                copy.wait()

        z_forward(i).wait_recv()
        lo = pl.multiple_of(i * TILE, TILE)
        d_other[pl.ds(lo, HALF), :] = z_land[i].astype(bf16)
        d_other[pl.ds(lo + HALF, HALF), :] = c_land[i].astype(bf16)
        n, d = other[pl.ds(lo, TILE), :], d_other[pl.ds(lo, TILE), :]
        for off in range(0, half, TILE):
            size = min(TILE, half - off)
            piece(n, d, slot, pl.ds(pl.multiple_of(mine + off, HALF), size), pl.ds(off, size))
        for copy in stores(i, d_out.shape[0]):
            copy.start()
        return carry

    lax.fori_loop(0, 2, other_tile, 0)

    gain_grads[...] = jnp.zeros_like(gain_grads)

    def fold(a):
        return jnp.sum(a.reshape(a.shape[0] // 8, 8, a.shape[1]), axis=0)

    def of_quarter(h, carry):
        y_copy(h).wait_recv()
        at = pl.ds(pl.multiple_of(h * HALF, HALF), HALF)
        grad = part[2 + h, :HALF] + from_y[h]
        m = middle[at, :]
        inverse = lax.rsqrt(jnp.mean(m * m, axis=-1, keepdims=True) + epsilon)
        hat = m * inverse
        scaled = grad * (1.0 + gain_row(gains, 2))
        d_middle = dy[at, :].astype(f32) + inverse * (scaled - hat * jnp.mean(scaled * hat, axis=-1, keepdims=True))
        gain_grads[0] = gain_grads[0] + fold(grad * hat)
        d_middle_out[at, :] = d_middle
        b = branch[at, :]
        inverse = lax.rsqrt(jnp.mean(b * b, axis=-1, keepdims=True) + epsilon)
        hat = b * inverse
        scaled = d_middle * (1.0 + gain_row(gains, 1))
        d_low = (inverse * (scaled - hat * jnp.mean(scaled * hat, axis=-1, keepdims=True))).astype(bf16)
        gain_grads[1] = gain_grads[1] + fold(d_middle * hat)
        d_branch_out[at, :] = d_low.astype(f32)
        for k in range(4):
            heads[k, at, :] = product_t(d_low, w_out[k * head : (k + 1) * head, :]).astype(bf16).astype(f32)
        return carry

    lax.fori_loop(0, 2, of_quarter, 0)
    lax.fori_loop(2, 4, other_tile, 0)
    for i in (0, 1):
        for copy in stores(i, d_out.shape[0]):
            copy.wait()
    for i in (3, 0, 1):
        z_copy(i).wait_send()
    for i in range(4):
        core_copy(i).wait_send()
        z_forward(i).wait_send()
    for h in range(2):
        y_copy(h).wait_send()


def feed_back(nx, d_out, d_own, d_first, for_gate, for_up, other, w_gate, w_up, w_down, w_out, middle, branch, dy, gains):
    length, width = d_out.shape
    columns = pl.cdiv(w_gate.shape[0], TILE) * TILE
    head = w_out.shape[0] // 4
    return pl.pallas_call(
        functools.partial(back_kernel, nx),
        out_shape=(
            jax.ShapeDtypeStruct((length, width), bf16),
            jax.ShapeDtypeStruct((length, columns // 2), bf16),
            jax.ShapeDtypeStruct((2 * length, columns), bf16),
            jax.ShapeDtypeStruct((4, QUARTER, head), f32),
            jax.ShapeDtypeStruct((QUARTER, width), f32),
            jax.ShapeDtypeStruct((QUARTER, width), f32),
            jax.ShapeDtypeStruct((2, 8, width), f32),
        ),
        in_specs=[ANY] * 13 + [VMEM],
        out_specs=(VMEM, ANY, ANY) + (VMEM,) * 4,
        scratch_shapes=[
            pltpu.VMEM((length, width), bf16),
            pltpu.VMEM((2, TILE, columns), bf16),
            pltpu.VMEM((2, TILE, columns), bf16),
            pltpu.VMEM((length, width), bf16),
            pltpu.VMEM((columns, width), bf16),
            pltpu.VMEM((columns, width), bf16),
            pltpu.VMEM((columns, width), bf16),
            pltpu.VMEM((4 * head, width), bf16),
            pltpu.VMEM((QUARTER, width), f32),
            pltpu.VMEM((QUARTER, width), f32),
            pltpu.VMEM((QUARTER, width), bf16),
            pltpu.VMEM((2, TILE, columns), bf16),
            pltpu.VMEM((2, TILE, columns), bf16),
            pltpu.VMEM((2, TILE, columns // 2), bf16),
            pltpu.VMEM((4, TILE, width), f32),
            pltpu.VMEM((4, HALF, width), f32),
            pltpu.VMEM((2, HALF, width), f32),
            pltpu.VMEM((4, HALF, width), f32),
            pltpu.VMEM((4, HALF, width), f32),
            pltpu.SemaphoreType.DMA((12,)),
            pltpu.SemaphoreType.DMA((2, 2)),
            pltpu.SemaphoreType.DMA((2, 3)),
        ]
        + dma(8, 8, 2, 2, 4, 4),
        compiler_params=pltpu.CompilerParams(collective_id=1, has_side_effects=True, vmem_limit_bytes=VMEM_LIMIT),
        name="feed_back",
    )(
        d_out,
        d_own,
        d_first,
        for_gate,
        for_up,
        other,
        w_gate,
        w_up,
        w_down,
        w_out,
        middle,
        branch,
        dy,
        gains,
    )


def visible_pairs(shape, i, segments):
    row = lax.broadcasted_iota(jnp.int32, shape, 0) + i * TILE
    col = lax.broadcasted_iota(jnp.int32, shape, 1)
    first = jnp.sum((segments[...] == 0).astype(jnp.int32), axis=1, keepdims=True)
    return (row >= col) & ((row < first) == (col < first))


def attention_kernel(
    nx,
    tokens,
    w_query,
    w_key,
    w_value,
    w_out,
    segments,
    gain_0,
    gain_1,
    gain_2,
    gain_3,
    gain_4,
    gain_5,
    normed_hbm,
    query_hbm,
    keys_hbm,
    values_hbm,
    query_raw_hbm,
    keys_raw_hbm,
    log_total_hbm,
    context_hbm,
    w_out_all_hbm,
    middle,
    branch,
    gains,
    normed,
    query,
    keys,
    values,
    query_raw,
    keys_raw,
    log_total,
    context,
    w_out_all,
    stores,
    out_own,
    out_land,
    context_own,
    context_core,
    context_land,
    context_all,
    c_send,
    c_recv,
    y_send,
    y_recv,
    x_send,
    x_recv,
):
    z, x, y, c, near = spots(nx)
    cs, ys, xs = (c_send, c_recv), (y_send, y_recv), (x_send, x_recv)
    length, width = tokens.shape
    head = w_query.shape[1]
    given = (gain_0, gain_1, gain_2, gain_3, gain_4, gain_5)
    gain_loads = [
        pltpu.make_async_copy(ref, gains.at[k, pl.ds(0, ref.shape[0])], stores.at[k]) for k, ref in enumerate(given)
    ]
    for copy in gain_loads:
        copy.start()
    out_own[...] = w_out[...].astype(f32)
    greet([near[k] for k in ("c", "y", "x")])
    mine = pl.ds(pl.multiple_of(x * (head // 2), 8), head // 2)
    out_y = remote(out_own.at[mine], out_land.at[0, mine], ys, 0, near["y"])
    out_x = remote(out_land.at[0, mine], out_land.at[0, mine], xs, 0, near["x"])
    out_c = remote(out_own, out_land.at[1], cs, 0, near["c"])
    out_yc = remote(out_land.at[0], out_land.at[2], cs, 1, near["c"])
    out_y.start()
    out_c.start()
    w_out_all[:head, :] = w_out[...]

    for copy in gain_loads:
        copy.wait()

    def norm(v, gain):
        return v * lax.rsqrt(jnp.mean(v * v, axis=-1, keepdims=True) + epsilon) * (1.0 + gain)

    def inputs(i, carry):
        at = pl.ds(pl.multiple_of(i * TILE, TILE), TILE)
        n = norm(tokens[at, :].astype(f32), gain_row(gains, 0)).astype(bf16)
        normed[at, :] = n
        raw = product(n, w_query[...])
        query_raw[at, :] = raw
        query[at, :] = norm(raw, gain_row(gains, 4)[:, :head]).astype(bf16)
        raw = product(n, w_key[...])
        keys_raw[at, :] = raw
        keys[at, :] = norm(raw, gain_row(gains, 5)[:, :head]).astype(bf16)
        values[at, :] = product(n, w_value[...]).astype(bf16)
        return carry

    lax.fori_loop(0, length // TILE, inputs, 0)
    for i in range(length // TILE):
        at, seen = slice(i * TILE, (i + 1) * TILE), (i + 1) * TILE
        s = product_t(query[at, :], keys[:seen, :]) * score_scale
        s = jnp.where(visible_pairs(s.shape, i, segments), s, -1e30)
        largest = jnp.max(s, axis=-1, keepdims=True)
        e = jnp.exp(s - largest)
        total = jnp.sum(e, axis=-1, keepdims=True)
        log_total[at, :] = largest + jnp.log(total)
        low_context = product((e / total).astype(bf16), values[:seen, :]).astype(bf16)
        context[at, :] = low_context
        context_own[at, :] = low_context.astype(f32)

    out_copies = []

    def put(src, dst):
        copy = pltpu.make_async_copy(src, dst, stores.at[len(out_copies)])
        copy.start()
        out_copies.append(copy)

    span = length // 2
    to_core = remote(context_own.at[pl.ds(pl.multiple_of((1 - c) * span, span), span)], context_core, cs, 2, near["c"])
    to_core.start()

    def local(i, other):
        dy = 1 - i // 2
        return pl.multiple_of(((y ^ other) ^ dy) * QUARTER + (i % 2) * HALF, HALF)

    def context_copy(i, k):
        if k == 0:
            src = context_own.at[pl.ds(pl.multiple_of(c * span + local(i, 1), HALF), HALF)]
        else:
            src = context_core.at[pl.ds(local(i, 1), HALF)]
        return remote(src, context_land.at[k, i], ys, 1 + 2 * i + k, near["y"])

    context_copy(0, 0).start()
    for src, dst in (
        (normed, normed_hbm),
        (query, query_hbm),
        (keys, keys_hbm),
        (values, values_hbm),
        (query_raw, query_raw_hbm),
        (keys_raw, keys_raw_hbm),
        (log_total, log_total_hbm),
        (context, context_hbm),
    ):
        put(src, dst)
    out_y.wait_recv()
    out_x.start()
    to_core.wait_recv()
    for i in range(4):
        for k in range(2):
            if i + k > 0:
                context_copy(i, k).start()
    out_c.wait_recv()
    w_out_all[2 * head : 3 * head, :] = out_land[1].astype(bf16)
    for i in range(4):
        rows = pl.ds(i * HALF, HALF)
        context_all[rows, :head] = context[pl.ds(pl.multiple_of(c * span + local(i, 0), HALF), HALF), :]
        context_all[rows, 2 * head : 3 * head] = context_core[pl.ds(local(i, 0), HALF), :].astype(bf16)
    out_x.wait_recv()
    out_yc.start()
    w_out_all[head : 2 * head, :] = out_land[0].astype(bf16)
    out_yc.wait_recv()
    w_out_all[3 * head :, :] = out_land[2].astype(bf16)
    put(w_out_all, w_out_all_hbm)

    def middle_copy(i):
        at = pl.multiple_of(i * TILE, TILE)
        return remote(middle.at[pl.ds(at, HALF)], middle.at[pl.ds(at + HALF, HALF)], cs, 3 + i, near["c"])

    def middle_tile(i, carry):
        rows = pl.ds(pl.multiple_of(i * HALF, HALF), HALF)
        context_copy(i, 0).wait_recv()
        context_all[rows, head : 2 * head] = context_land[0, i].astype(bf16)
        context_copy(i, 1).wait_recv()
        context_all[rows, 3 * head :] = context_land[1, i].astype(bf16)
        b = product(context_all[rows, :], w_out_all[...])
        branch[i % 2] = b
        hidden = tokens[pl.ds(pl.multiple_of(c * span + local(i, 0), HALF), HALF), :].astype(f32)
        middle[pl.ds(pl.multiple_of(i * TILE, TILE), HALF), :] = hidden + norm(b, gain_row(gains, 1))
        middle_copy(i).start()
        return carry

    lax.fori_loop(0, 4, middle_tile, 0)
    for i in range(4):
        middle_copy(i).wait()
        for k in range(2):
            context_copy(i, k).wait_send()
    for copy in (out_y, out_x, out_c, out_yc, to_core):
        copy.wait_send()
    for copy in out_copies:
        copy.wait()


def attend(nx, tokens, w_query, w_key, w_value, w_out, segment_ids, *gains):
    length, width = tokens.shape
    head = w_query.shape[1]
    of_head = jax.ShapeDtypeStruct((length, head), bf16)
    raw = jax.ShapeDtypeStruct((length, head), f32)
    return pl.pallas_call(
        functools.partial(attention_kernel, nx),
        out_shape=(
            jax.ShapeDtypeStruct((length, width), bf16),
            of_head,
            of_head,
            of_head,
            raw,
            raw,
            jax.ShapeDtypeStruct((length, 1), f32),
            of_head,
            jax.ShapeDtypeStruct((4 * head, width), bf16),
            jax.ShapeDtypeStruct((length, width), f32),
            jax.ShapeDtypeStruct((2, HALF, width), f32),
            jax.ShapeDtypeStruct((8, width), f32),
        ),
        in_specs=[VMEM] * 6 + [ANY] * 6,
        out_specs=(ANY,) * 9 + (VMEM,) * 3,
        scratch_shapes=[
            pltpu.VMEM((length, width), bf16),
            pltpu.VMEM((length, head), bf16),
            pltpu.VMEM((length, head), bf16),
            pltpu.VMEM((length, head), bf16),
            pltpu.VMEM((length, head), f32),
            pltpu.VMEM((length, head), f32),
            pltpu.VMEM((length, 1), f32),
            pltpu.VMEM((length, head), bf16),
            pltpu.VMEM((4 * head, width), bf16),
            pltpu.SemaphoreType.DMA((9,)),
            pltpu.VMEM((head, width), f32),
            pltpu.VMEM((3, head, width), f32),
            pltpu.VMEM((length, head), f32),
            pltpu.VMEM((length // 2, head), f32),
            pltpu.VMEM((2, 4, HALF, head), f32),
            pltpu.VMEM((length // 2, 4 * head), bf16),
        ]
        + dma(7, 7, 9, 9, 1, 1),
        compiler_params=pltpu.CompilerParams(collective_id=3, has_side_effects=True, vmem_limit_bytes=VMEM_LIMIT),
        name="attend",
    )(
        tokens,
        w_query,
        w_key,
        w_value,
        w_out,
        segment_ids.reshape(1, length),
        *gains,
    )


def reduce_kernel(
    nx,
    d_out_hbm,
    d_other_hbm,
    normed_hbm,
    other_hbm,
    pair_own_hbm,
    pair_other_hbm,
    pair_gates_hbm,
    d_branch_hbm,
    d_middle_hbm,
    tokens_hbm,
    normed_in_hbm,
    query_hbm,
    keys_hbm,
    values_hbm,
    query_raw_hbm,
    keys_raw_hbm,
    context_hbm,
    heads_hbm,
    w_query_hbm,
    w_key_hbm,
    w_value_hbm,
    log_total,
    segments,
    gain_rows,
    of_ffn_out,
    of_middle,
    down_out,
    gate_out,
    up_out,
    query_out,
    out_out,
    key_out,
    value_out,
    input_grad,
    gains,
    input_stage,
    ff_stage,
    dw,
    x_land,
    z2_land,
    z1_land,
    from_core,
    from_y,
    branch_land,
    input_own,
    input_land,
    d_qkv,
    attn,
    attn_z1,
    attn_x,
    attn_z2,
    kv_core,
    kv_across,
    kv_own,
    kv_y,
    kv_wide,
    kv_wide_core,
    gains_land,
    heads_mine,
    heads_y,
    got_c,
    got_y,
    loads,
    c_send,
    c_recv,
    y_send,
    y_recv,
    x_send,
    x_recv,
    z2_send,
    z2_recv,
    z1_send,
    z1_recv,
):
    z, x, y, c, near = spots(nx)
    zh, zl = z // 2, z % 2
    cs, ys, xs = (c_send, c_recv), (y_send, y_recv), (x_send, x_recv)
    z2s, z1s = (z2_send, z2_recv), (z1_send, z1_recv)
    length, width = d_out_hbm.shape
    half = pair_own_hbm.shape[1]
    head = query_hbm.shape[1]
    blk = x_land.shape[1]
    own_row = pl.multiple_of((c * 2 + y) * QUARTER, QUARTER)

    def block(a, b):
        return pl.ds(pl.multiple_of(b * blk, 8), blk)

    def quarter_rows(dc, dy):
        return pl.ds(pl.multiple_of(((c ^ dc) * 2 + (y ^ dy)) * QUARTER, QUARTER), QUARTER)

    greet([near[k] for k in ("c", "y", "x", "z2", "z1")])

    heads_in = pltpu.make_async_copy(heads_hbm.at[0], heads_mine, loads.at[6])
    heads_in_y = pltpu.make_async_copy(heads_hbm.at[1], heads_y.at[0], loads.at[7])
    heads_c_copy = remote(heads_hbm.at[pl.ds(2, 2)], got_c, cs, 11, near["c"])
    heads_y_copy = remote(heads_y, got_y, ys, 7, near["y"])
    heads_c_copy.start()
    heads_in.start()
    heads_in_y.start()
    heads_c_copy.wait_recv()
    heads_in_y.wait()
    heads_y[1] = got_c[1]
    heads_y_copy.start()

    branch_y = remote(d_branch_hbm, branch_land.at[0], ys, 0, near["y"])
    branch_c = remote(d_branch_hbm, branch_land.at[1], cs, 0, near["c"])
    branch_fwd = remote(branch_land.at[0], branch_land.at[2], cs, 1, near["c"])
    branch_y.start()
    branch_c.start()

    def owner(j):
        return 2 * jnp.where(j < 2, 1 - zh, zh) + j % 2

    def x_copy(m, j):
        return remote(dw.at[m, block(dw, owner(j) * 2 + (1 - x))], x_land.at[m * 4 + j], xs, m * 4 + j, near["x"])

    def z2_copy(m, k):
        return remote(dw.at[m, block(dw, owner(k) * 2 + x)], z2_land.at[m * 2 + k], z2s, m * 2 + k, near["z2"])

    def z1_copy(m):
        return remote(dw.at[m, block(dw, (2 * zh + 1 - zl) * 2 + x)], z1_land.at[m], z1s, m, near["z1"])

    def start_x(*blocks):
        for m, j in blocks:
            x_copy(m, j).start()

    arrived = set()

    def wait_x(m, j):
        if (m, j) not in arrived:
            arrived.add((m, j))
            x_copy(m, j).wait_recv()

    def far(*blocks):
        for m, k in blocks:
            wait_x(m, k)
            rows = block(dw, owner(k) * 2 + x)
            dw[m, rows, :] = dw[m, rows, :] + x_land[m * 4 + k]
            z2_copy(m, k).start()

    def close(m):
        for k in range(2):
            wait_x(m, 2 + k)
            z2_copy(m, k).wait_recv()
            rows = block(dw, owner(2 + k) * 2 + x)
            dw[m, rows, :] = dw[m, rows, :] + x_land[m * 4 + 2 + k] + z2_land[m * 2 + k]
        z1_copy(m).start()

    def finish(m, ref):
        z1_copy(m).wait_recv()
        own, other = dw[m, block(dw, (2 * zh + zl) * 2 + x), :], z1_land[m]
        ff_stage[:, :half] = jnp.where(zl == 0, own, other)
        ff_stage[:, half:] = jnp.where(zl == 0, other, own)[:, : ref.shape[1] - half]
        copy = pltpu.make_async_copy(ff_stage, ref, loads.at[1])
        copy.start()
        copy.wait()

    def copies(pairs):
        started = [pltpu.make_async_copy(src, dst, loads.at[k]) for k, (src, dst) in enumerate(pairs)]
        for copy in started:
            copy.start()
        return started

    def weights(left, right):
        far_size = pl.cdiv(width // 2, HALF) * HALF
        far_at = pl.multiple_of((1 - zh) * (width - far_size), HALF)
        near_at = pl.multiple_of(zh * far_size, HALF)

        def form(m, lo, at, size):
            for off in range(0, size, 3 * HALF):
                rows = pl.ds(pl.multiple_of(at + off, HALF), min(3 * HALF, size - off))
                cols = pl.ds(pl.multiple_of(lo, HALF), half)
                dw[m, rows, :] = t_product(left[:, rows], right[:, cols])

        for copy in copies(
            [
                (d_out_hbm, left.at[pl.ds(0, length)]),
                (d_other_hbm, left.at[pl.ds(length, length)]),
                (pair_own_hbm, right.at[pl.ds(0, length), pl.ds(0, half)]),
                (pair_other_hbm, right.at[pl.ds(length, length), pl.ds(0, half)]),
            ]
        ):
            copy.wait()
        form(0, 0, far_at, far_size)
        start_x((0, 0), (0, 1))
        form(0, 0, near_at, width - far_size)
        for copy in copies(
            [
                (normed_hbm, left.at[pl.ds(0, length)]),
                (other_hbm, left.at[pl.ds(length, length)]),
                (pair_gates_hbm, right),
            ]
        ):
            copy.wait()
        def form_far(m, carry):
            form(m, (m - 1) * half, far_at, far_size)
            start_x((m, 0), (m, 1))
            return carry

        def form_near(m, carry):
            form(m, (m - 1) * half, near_at, width - far_size)
            return carry

        lax.fori_loop(1, 3, form_far, 0)
        far((0, 0))
        lax.fori_loop(1, 3, form_near, 0)
        start_x((0, 2), (0, 3), (1, 2), (1, 3), (2, 2), (2, 3))

    pl.run_scoped(weights, pltpu.VMEM((2 * length, width), bf16), pltpu.VMEM((2 * length, 2 * half), bf16))

    def total_of(a):
        return jnp.sum(a, axis=0, keepdims=True)

    gains[...] = jnp.zeros_like(gains)
    gains[1:2, :] = total_of(of_middle[1])
    gains[2:3, :] = total_of(of_middle[0])
    gains[3:4, :] = 0.25 * total_of(of_ffn_out[...])

    def back_norm(raw, gain, grad):
        inverse = lax.rsqrt(jnp.mean(raw * raw, axis=-1, keepdims=True) + epsilon)
        hat = raw * inverse
        scaled = grad * (1.0 + gain)
        return inverse * (scaled - hat * jnp.mean(scaled * hat, axis=-1, keepdims=True)), grad * hat

    def attention(query, keys, values, query_raw, keys_raw, grad_context, d_keys, d_values):
        for copy in copies(
            [
                (query_hbm, query),
                (keys_hbm, keys),
                (values_hbm, values),
                (query_raw_hbm, query_raw),
                (keys_raw_hbm, keys_raw),
            ]
        ):
            copy.wait()
        heads_in.wait()
        grad_context[quarter_rows(0, 0), :] = heads_mine[...].astype(bf16)
        grad_context[quarter_rows(1, 0), :] = got_c[0].astype(bf16)
        heads_y_copy.wait_recv()
        grad_context[quarter_rows(0, 1), :] = got_y[0].astype(bf16)
        grad_context[quarter_rows(1, 1), :] = got_y[1].astype(bf16)
        d_keys[...] = jnp.zeros_like(d_keys)
        d_values[...] = jnp.zeros_like(d_values)

        def back_tile(seen, i, carry):
            at = pl.ds(pl.multiple_of(i * TILE, TILE), TILE)
            q, k = query[at, :], keys[:seen, :]
            s = product_t(q, k) * score_scale
            p = jnp.exp(jnp.where(visible_pairs(s.shape, i, segments), s, -1e30) - log_total[at, :])
            g = grad_context[at, :]
            dp = product_t(g, values[:seen, :])
            balance = jnp.sum(dp * p, axis=-1, keepdims=True)
            ds = (p * (dp - balance)).astype(bf16)
            dq, of_gain = back_norm(query_raw[at, :], gain_row(gain_rows, 4)[:, :head], product(ds, k) * score_scale)
            d_qkv[at, :head] = dq.astype(bf16)
            gains[4:5, :head] = gains[4:5, :head] + jnp.sum(of_gain, axis=0, keepdims=True)
            d_keys[:seen, :] = d_keys[:seen, :] + t_product(ds, q)
            d_values[:seen, :] = d_values[:seen, :] + t_product(p.astype(bf16), g)
            return carry

        tiles = length // TILE
        lax.fori_loop(0, tiles // 2, functools.partial(back_tile, length // 2), 0)
        lax.fori_loop(tiles // 2, tiles, functools.partial(back_tile, length), 0)

        def keys_tile(i, carry):
            at = pl.ds(pl.multiple_of(i * TILE, TILE), TILE)
            dk, of_gain = back_norm(keys_raw[at, :], gain_row(gain_rows, 5)[:, :head], d_keys[at, :] * score_scale)
            d_qkv[at, head : 2 * head] = dk.astype(bf16)
            gains[5:6, :head] = gains[5:6, :head] + jnp.sum(of_gain, axis=0, keepdims=True)
            d_qkv[at, 2 * head :] = d_values[at, :].astype(bf16)
            return carry

        lax.fori_loop(0, tiles, keys_tile, 0)

    pl.run_scoped(
        attention,
        pltpu.VMEM((length, head), bf16),
        pltpu.VMEM((length, head), bf16),
        pltpu.VMEM((length, head), bf16),
        pltpu.VMEM((length, head), f32),
        pltpu.VMEM((length, head), f32),
        pltpu.VMEM((length, head), bf16),
        pltpu.VMEM((length, head), f32),
        pltpu.VMEM((length, head), f32),
    )
    far((0, 1))

    def put_input(dc, dy):
        copy = pltpu.make_async_copy(input_stage, input_grad.at[quarter_rows(dc, dy)], loads.at[0])
        copy.start()
        copy.wait()

    def attn_z1_copy(i):
        b = (2 * (i // 2) + 1 - zl) * 2 + i % 2
        return remote(attn.at[block(attn, b)], attn_z1.at[i], z1s, 3 + i, near["z1"])

    def attn_x_copy(j):
        b = (2 * (zh ^ j) + zl) * 2 + 1 - x
        return remote(attn.at[block(attn, b)], attn_x.at[j], xs, 12 + j, near["x"])

    attn_z2_copy = remote(attn.at[block(attn, (2 * (1 - zh) + zl) * 2 + x)], attn_z2, z2s, 6, near["z2"])

    input_y = remote(input_own, input_land.at[0], ys, 4, near["y"])
    input_c = remote(input_own, input_land.at[1], cs, 7, near["c"])
    input_fwd = remote(input_land.at[0], input_land.at[2], cs, 8, near["c"])

    hops = [
        remote(gains, gains_land.at[k], sems, index, near[to])
        for k, (sems, index, to) in enumerate([(cs, 10, "c"), (ys, 6, "y"), (xs, 14, "x"), (z1s, 7, "z1"), (z2s, 7, "z2")])
    ]

    def hop(k):
        hops[k].start()

    def arrive(k):
        hops[k].wait()
        gains[...] = gains[...] + gains_land[k]

    def rest(w_qkv, part, kv_halves):
        def of_inputs(normed_in, kv):
            for copy in copies([(normed_in_hbm, normed_in)]):
                copy.wait()
            for k in range(2):
                kv[k] = t_product(normed_in[...], d_qkv[:, (1 + k) * head : (2 + k) * head])
            to_core = remote(kv.at[1 - c], kv_core, cs, 6, near["c"])
            to_core.start()
            attn[:, :head] = t_product(normed_in[...], d_qkv[:, :head])
            to_core.wait_recv()
            for k in range(2):
                lanes = slice(k * (head // 2), (k + 1) * (head // 2))
                kv_halves[k] = kv[c, :, lanes] + kv_core[:, lanes]
            to_core.wait_send()

        pl.run_scoped(of_inputs, pltpu.VMEM((length, width), bf16), pltpu.VMEM((2, width, head), f32))
        to_y = remote(kv_halves.at[1 - y], kv_across, ys, 3, near["y"])
        to_y.start()
        for copy in copies(
            [
                (w_query_hbm, w_qkv.at[:, pl.ds(0, head)]),
                (w_key_hbm, w_qkv.at[:, pl.ds(head, head)]),
                (w_value_hbm, w_qkv.at[:, pl.ds(2 * head, head)]),
            ]
        ):
            copy.wait()

        def core_copy(i):
            return remote(part.at[i, pl.ds(HALF, HALF)], from_core.at[i], cs, 2 + i, near["c"])

        def y_copy(h):
            return remote(part.at[h, pl.ds(0, HALF)], from_y.at[h], ys, 1 + h, near["y"])

        def tile(i, carry):
            for dc in range(2):
                rows = d_qkv[pl.ds(tile_row(c, y, i, dc), HALF), :]
                part[i, dc * HALF : (dc + 1) * HALF] = product_t(rows, w_qkv[...])
            core_copy(i).start()
            core_copy(i).wait_recv()
            part[i, :HALF] = part[i, :HALF] + from_core[i]

            @pl.when(i < 2)
            def _():
                y_copy(i).start()

            return carry

        lax.fori_loop(0, 4, tile, 0)


        far((1, 0))

        def of_branch(context, d_branch, d_middle, tokens):
            waits = copies(
                [
                    (context_hbm, context),
                    (d_branch_hbm, d_branch),
                    (d_middle_hbm, d_middle),
                    (tokens_hbm.at[pl.ds(own_row, QUARTER)], tokens),
                ]
            )
            branch_y.wait_recv()
            branch_fwd.start()
            for copy in waits:
                copy.wait()
            acc = t_product(d_branch[...].astype(bf16), context[quarter_rows(0, 0), :])
            branch_c.wait_recv()
            branch_fwd.wait_recv()
            for k, (dc, dy) in enumerate([(0, 1), (1, 0), (1, 1)]):
                acc = acc + t_product(branch_land[k].astype(bf16), context[quarter_rows(dc, dy), :])
            attn[:, head : 2 * head] = acc
            far((1, 1))
            to_y.wait_recv()
            attn[:, 2 * head :] = kv_halves[y] + kv_across[...]
            for i in range(4):
                attn_z1_copy(i).start()
            far((2, 0), (2, 1))
            for h in range(2):
                y_copy(h).wait_recv()
                at = slice(h * HALF, (h + 1) * HALF)
                grad = part[2 + h, :HALF] + from_y[h]
                d_in, of_gain = back_norm(tokens[at, :].astype(f32), gain_row(gain_rows, 0), grad)
                gains[0:1, :] = gains[0:1, :] + jnp.sum(of_gain, axis=0, keepdims=True)
                d = (d_middle[at, :] + d_in).astype(bf16)
                input_stage[at, :] = d
                input_own[at, :] = d.astype(f32)

        pl.run_scoped(
            of_branch,
            pltpu.VMEM((length, head), bf16),
            pltpu.VMEM((QUARTER, width), f32),
            pltpu.VMEM((QUARTER, width), f32),
            pltpu.VMEM((QUARTER, width), bf16),
        )
        hop(0)
        arrive(0)
        hop(1)
        input_y.start()
        input_c.start()
        put_input(0, 0)
        for i in range(4):
            core_copy(i).wait_send()
        for h in range(2):
            y_copy(h).wait_send()
        to_y.wait_send()

    pl.run_scoped(
        rest,
        pltpu.VMEM((width, 3 * head), bf16),
        pltpu.VMEM((4, TILE, width), f32),
        pltpu.VMEM((2, width, head // 2), f32),
    )

    arrive(1)
    hop(2)
    close(0)
    input_y.wait_recv()
    input_fwd.start()
    input_stage[...] = input_land[0].astype(bf16)
    put_input(0, 1)
    input_c.wait_recv()
    input_stage[...] = input_land[1].astype(bf16)
    put_input(1, 0)
    close(1)
    for i in range(4):
        attn_z1_copy(i).wait_recv()
        rows = block(attn, (2 * (i // 2) + zl) * 2 + i % 2)
        attn[rows, :] = attn[rows, :] + attn_z1[i]
    for j in (1, 0):
        attn_x_copy(j).start()
    input_fwd.wait_recv()
    input_stage[...] = input_land[2].astype(bf16)
    put_input(1, 1)
    arrive(2)
    hop(3)
    for j in (1, 0):
        attn_x_copy(j).wait_recv()
        rows = block(attn, (2 * (zh ^ j) + zl) * 2 + x)
        attn[rows, :] = attn[rows, :] + attn_x[j]
        if j == 1:
            attn_z2_copy.start()
    arrive(3)
    hop(4)
    finish(0, down_out)
    finish(1, gate_out)
    close(2)
    attn_z2_copy.wait_recv()
    total = attn[block(attn, (2 * zh + zl) * 2 + x), :] + attn_z2[...]
    query_out[...] = total[:, :head]
    out_out[...] = total[:, head : 2 * head]
    kv_own[...] = total[:, 2 * head :]
    wide_y = remote(kv_own, kv_y, ys, 5, near["y"])
    wide_y.start()
    wide_y.wait_recv()
    kv_wide[:, : head // 2] = jnp.where(y == 0, kv_own[...], kv_y[...])
    kv_wide[:, head // 2 :] = jnp.where(y == 0, kv_y[...], kv_own[...])
    wide_c = remote(kv_wide, kv_wide_core, cs, 9, near["c"])
    wide_c.start()
    wide_c.wait_recv()
    key_out[...] = jnp.where(c == 0, kv_wide[...], kv_wide_core[...])
    value_out[...] = jnp.where(c == 0, kv_wide_core[...], kv_wide[...])
    arrive(4)
    finish(2, up_out)
    for m in range(3):
        for j in range(4):
            x_copy(m, j).wait_send()
        for k in range(2):
            z2_copy(m, k).wait_send()
        z1_copy(m).wait_send()
    for i in range(4):
        attn_z1_copy(i).wait_send()
    for j in range(2):
        attn_x_copy(j).wait_send()
    for copy in (attn_z2_copy, branch_y, branch_c, branch_fwd, input_y, input_c, input_fwd, wide_y, wide_c, heads_c_copy, heads_y_copy):
        copy.wait_send()


def reduce_all(nx, dp_size, columns, whole, small):
    length, width = whole[0].shape
    half = whole[4].shape[1]
    head = whole[11].shape[1]
    blk = width // dp_size
    return pl.pallas_call(
        functools.partial(reduce_kernel, nx),
        out_shape=(
            *[jax.ShapeDtypeStruct((blk, columns), f32)] * 3,
            *[jax.ShapeDtypeStruct((blk, head), f32)] * 4,
            jax.ShapeDtypeStruct((length, width), bf16),
            jax.ShapeDtypeStruct((8, width), f32),
        ),
        in_specs=[ANY] * len(whole) + [VMEM] * len(small),
        out_specs=(ANY,) * 3 + (VMEM,) * 4 + (ANY, VMEM),
        scratch_shapes=[
            pltpu.VMEM((QUARTER, width), bf16),
            pltpu.VMEM((blk, columns), f32),
            pltpu.VMEM((3, width, half), f32),
            pltpu.VMEM((12, blk, half), f32),
            pltpu.VMEM((6, blk, half), f32),
            pltpu.VMEM((3, blk, half), f32),
            pltpu.VMEM((4, HALF, width), f32),
            pltpu.VMEM((2, HALF, width), f32),
            pltpu.VMEM((3, QUARTER, width), f32),
            pltpu.VMEM((QUARTER, width), f32),
            pltpu.VMEM((3, QUARTER, width), f32),
            pltpu.VMEM((length, 3 * head), bf16),
            pltpu.VMEM((width, 2 * head + head // 2), f32),
            pltpu.VMEM((4, blk, 2 * head + head // 2), f32),
            pltpu.VMEM((2, blk, 2 * head + head // 2), f32),
            pltpu.VMEM((blk, 2 * head + head // 2), f32),
            pltpu.VMEM((width, head), f32),
            pltpu.VMEM((width, head // 2), f32),
            pltpu.VMEM((blk, head // 2), f32),
            pltpu.VMEM((blk, head // 2), f32),
            pltpu.VMEM((blk, head), f32),
            pltpu.VMEM((blk, head), f32),
            pltpu.VMEM((5, 8, width), f32),
            pltpu.VMEM((QUARTER, head), f32),
            pltpu.VMEM((2, QUARTER, head), f32),
            pltpu.VMEM((2, QUARTER, head), f32),
            pltpu.VMEM((2, QUARTER, head), f32),
        ]
        + dma(8, 12, 12, 8, 8, 15, 15, 8, 8, 8, 8),
        compiler_params=pltpu.CompilerParams(collective_id=2, has_side_effects=True, vmem_limit_bytes=VMEM_LIMIT),
        name="reduce_all",
    )(*whole, *small)


def settle_kernel(*refs):
    count = (len(refs) - 1) // 3
    sems = refs[-1]
    loads, puts = [], []
    for k in range(count):
        given, out, held = refs[k], refs[count + k], refs[2 * count + k]
        loads.append(pltpu.make_async_copy(given, held, sems.at[0, k]))
        puts.append(pltpu.make_async_copy(held, out, sems.at[1, k]))
    for copy in loads:
        copy.start()
    for load, put in zip(loads, puts):
        load.wait()
        put.start()
    for copy in puts:
        copy.wait()


def settle(*arrays):
    return pl.pallas_call(
        settle_kernel,
        out_shape=tuple(jax.ShapeDtypeStruct(a.shape, a.dtype) for a in arrays),
        in_specs=[ANY] * len(arrays),
        out_specs=(ANY,) * len(arrays),
        scratch_shapes=[pltpu.VMEM(a.shape, a.dtype) for a in arrays] + [pltpu.SemaphoreType.DMA((2, len(arrays)))],
        compiler_params=pltpu.CompilerParams(vmem_limit_bytes=VMEM_LIMIT),
        name="settle",
    )(*arrays)


def body(
    links,
    tokens,
    segment_ids,
    cotangent,
    w_query,
    w_key,
    w_value,
    w_out,
    w_gate,
    w_up,
    w_down,
    gain_attn_in,
    gain_attn_out,
    gain_ffn_in,
    gain_ffn_out,
    gain_query,
    gain_key,
):
    length, width = tokens.shape
    head = w_query.shape[1]
    columns = w_gate.shape[1]
    nx = links.nx
    blk = width // links.dp_size
    dp = lax.axis_index("dp")
    wg, wu = w_gate.T, w_up.T
    (
        normed_low,
        query_low,
        keys_low,
        values_low,
        query_raw,
        keys_raw,
        log_total,
        context_low,
        w_out_all,
        middle,
        branch,
        gain_rows,
    ) = attend(
        nx,
        tokens,
        w_query,
        w_key,
        w_value,
        w_out,
        segment_ids,
        gain_attn_in,
        gain_attn_out,
        gain_ffn_in,
        gain_ffn_out,
        gain_query,
        gain_key,
    )
    normed_two, normed_other, d_out, d_own, d_first, layer_out, pair_own, for_gate, for_up, of_ffn_out = feed_forward(
        nx, middle, cotangent, gain_rows, wg, wu, w_down
    )
    d_other, pair_other, pair_gates, heads, d_branch_own, d_middle, of_middle = feed_back(
        nx,
        d_out,
        d_own,
        d_first,
        for_gate,
        for_up,
        normed_other,
        wg,
        wu,
        w_down,
        w_out_all,
        middle,
        branch.reshape(QUARTER, width),
        cotangent,
        gain_rows,
    )
    *sums, gains = reduce_all(
        nx,
        links.dp_size,
        columns,
        [
            d_out,
            d_other,
            normed_two,
            normed_other,
            pair_own,
            pair_other,
            pair_gates,
            d_branch_own,
            d_middle,
            tokens,
            normed_low,
            query_low,
            keys_low,
            values_low,
            query_raw,
            keys_raw,
            context_low,
            heads,
            w_query,
            w_key,
            w_value,
        ],
        [log_total, segment_ids.reshape(1, length), gain_rows, of_ffn_out, of_middle],
    )
    layer_out, down_t, gate, up, query, out_t, key, value, input_grad = settle(layer_out, *sums)
    part = lax.dynamic_slice_in_dim(gains, dp * blk, blk, 1)
    hb = head // links.dp_size
    head_part = lax.dynamic_slice_in_dim(gains, dp * hb, hb, 1)
    return (
        layer_out,
        input_grad,
        query,
        key,
        value,
        out_t.T,
        gate,
        up,
        down_t.T,
        part[0],
        part[1],
        part[2],
        part[3],
        head_part[4],
        head_part[5],
    )


def body_any(
    links,
    tokens,
    segment_ids,
    cotangent,
    w_query,
    w_key,
    w_value,
    w_out,
    w_gate,
    w_up,
    w_down,
    gain_attn_in,
    gain_attn_out,
    gain_ffn_in,
    gain_ffn_out,
    gain_query,
    gain_key,
):
    length, width = tokens.shape
    head = w_query.shape[1]
    quarter = length // 4
    half_ff = w_gate.shape[1] // 2
    nx = links.nx
    blk = width // links.dp_size
    dp, t = lax.axis_index("dp"), lax.axis_index("tensor")
    z, x = dp // nx, dp % nx
    y, c = t // 2, t % 2
    parity = z % 2
    one = jnp.where(segment_ids[0] < length, 1.0, 0.5).astype(f32)

    def keep_low(a):
        return (a * one).astype(bf16)

    def place(dc, dy):
        return ((c ^ dc) * 2 + (y ^ dy)) * quarter

    def rows(a, dc, dy):
        return lax.dynamic_slice_in_dim(a, place(dc, dy), quarter, 0)

    def to_absolute(pieces):
        stack = jnp.stack([pieces[0][0], pieces[0][1], pieces[1][0], pieces[1][1]])
        mine = c * 2 + y
        return jnp.concatenate([lax.dynamic_index_in_dim(stack, mine ^ b, 0, keepdims=False) for b in range(4)], axis=0)

    out_own = w_out.astype(f32)
    out_y = links.y(out_own)
    out_c = links.core(out_own)
    out_yc = links.core(out_y)
    w_out_all = jnp.concatenate([w_out, keep_low(out_c), keep_low(out_y), keep_low(out_yc)], axis=0)

    wg_h = jnp.where(parity == 0, w_gate[:, :half_ff], w_gate[:, half_ff:])
    wu_h = jnp.where(parity == 0, w_up[:, :half_ff], w_up[:, half_ff:])
    wd_h = jnp.where(parity == 0, w_down[:half_ff], w_down[half_ff:])

    hidden_in = tokens.astype(f32)
    normed_low = low(rms_norm(hidden_in, gain_attn_in))
    query_raw = product(normed_low, w_query)
    keys_raw = product(normed_low, w_key)
    query_low = low(rms_norm(query_raw, gain_query))
    keys_low = low(rms_norm(keys_raw, gain_key))
    values_low = low(product(normed_low, w_value))
    places = jnp.arange(length)
    allowed = (places[:, None] >= places[None, :]) & (segment_ids[:, None] == segment_ids[None, :])

    def scores_of():
        raw = product_t(query_low, keys_low) * score_scale
        return jnp.where(allowed, raw, -1e30)

    scores = scores_of()
    largest = jnp.max(scores, axis=-1, keepdims=True)
    exponent = jnp.exp(scores - largest)
    total = jnp.sum(exponent, axis=-1, keepdims=True)
    log_total = largest + jnp.log(total)
    context_low = low(product(low(exponent / total), values_low))

    context = context_low.astype(f32)
    mine = jnp.concatenate([rows(context, 0, 1), rows(context, 0, 0)], axis=0)
    of_core = links.core(jnp.concatenate([rows(context, 1, 1), rows(context, 1, 0)], axis=0))
    of_y = links.y(jnp.concatenate([rows(context, 0, 0), rows(context, 0, 1)], axis=0))
    of_yc = links.y(jnp.concatenate([of_core[quarter:], of_core[:quarter]], axis=0))
    context_all = jnp.concatenate([low(mine), keep_low(of_core), keep_low(of_y), keep_low(of_yc)], axis=1)
    branch = product(context_all, w_out_all)
    hidden_rows = jnp.concatenate([rows(tokens, 0, 1), rows(tokens, 0, 0)], axis=0).astype(f32)
    middle_own = hidden_rows + rms_norm(branch, gain_attn_out)
    middle_core = links.core(middle_own)

    middles, normed_two, inners, parts = [], [], [], []
    saved = []
    for k in range(2):
        at = slice(k * quarter, (k + 1) * quarter)
        middle = jnp.concatenate([middle_own[at], middle_core[at]], axis=0)
        normed_k = low(rms_norm(middle, gain_ffn_in))
        gate, upward = product(normed_k, w_gate), product(normed_k, w_up)
        inner = low(activate(gate, upward))
        part = product(inner, w_down)
        middles.append(middle)
        normed_two.append(normed_k)
        saved.append((gate, upward))
        parts.append(part)
    normed_own = low(rms_norm(middle_own, gain_ffn_in)).astype(f32)
    other_own = links.z1(normed_own)
    other_core = links.core(other_own)
    normed_other = jnp.concatenate([keep_low(other_own), keep_low(other_core)], axis=0)

    def gather_quarters(parts):
        sums = [part[:quarter] + links.core(part[quarter:]) for part in parts]
        return sums[1] + links.y(sums[0])

    output_q = gather_quarters(parts)
    output_y = links.y(output_q)
    output_c = links.core(output_q)
    output_yc = links.core(output_y)
    outputs = [jnp.concatenate([output_y, output_yc], axis=0), jnp.concatenate([output_q, output_c], axis=0)]
    grad_out = cotangent.astype(f32)
    d_outputs, layer_pieces, grad_ffn_out = [], [], 0.0
    for k in range(2):
        dy_k = jnp.concatenate([rows(cotangent, 0, 1 - k), rows(cotangent, 1, 1 - k)], axis=0).astype(f32)
        layer_k = low(middles[k] + rms_norm(outputs[k], gain_ffn_out))
        d_k, gain_k = rms_back(outputs[k], gain_ffn_out, dy_k)
        grad_ffn_out = grad_ffn_out + gain_k
        d_outputs.append(low(d_k))
        layer_pieces.append(layer_k)
    layer_out = to_absolute(
        [
            [layer_pieces[1][:quarter], layer_pieces[0][:quarter]],
            [layer_pieces[1][quarter:], layer_pieces[0][quarter:]],
        ]
    )

    d_own_rows = [d[:quarter].astype(f32) for d in d_outputs]
    got_own = [links.z1(d_own_rows[1]), links.z1(d_own_rows[0])]
    got_core = [links.core(g) for g in got_own]
    d_other = jnp.concatenate(
        [keep_low(got_own[1]), keep_low(got_own[0]), keep_low(got_core[1]), keep_low(got_core[0])], axis=0
    )

    back_parts = []
    for k in range(2):
        gate, upward = saved[k]
        d_inner = product_t(d_outputs[k], w_down)
        _, pull = jax.vjp(activate, gate, upward)
        d_gate, d_up = pull(d_inner)
        back_parts.append(product_t(low(d_gate), w_gate) + product_t(low(d_up), w_up))
    d_normed_q = gather_quarters(back_parts)
    middle_q = middle_own[quarter:]
    branch_q = branch[quarter:]
    dy_q = rows(cotangent, 0, 0).astype(f32)
    d_mid, grad_ffn_in = rms_back(middle_q, gain_ffn_in, d_normed_q)
    d_middle = dy_q + d_mid
    d_branch, grad_attn_out = rms_back(branch_q, gain_attn_out, d_middle)
    d_branch_low = low(d_branch)
    d_context = low(product_t(d_branch_low, w_out_all)).astype(f32)
    heads = [d_context[:, i * head : (i + 1) * head] for i in range(4)]
    c_got = links.core(jnp.concatenate([heads[1], heads[3]], axis=1))
    y_got = links.y(jnp.concatenate([heads[2], c_got[:, head:]], axis=1))
    grad_context = keep_low(
        to_absolute([[heads[0], y_got[:, :head]], [c_got[:, :head], y_got[:, head:]]])
    )
    d_branch_own = d_branch_low.astype(f32)
    d_branch_y = links.y(d_branch_own)
    d_branch_c = links.core(d_branch_own)
    d_branch_yc = links.core(d_branch_y)
    d_branch_all = jnp.concatenate(
        [d_branch_low, keep_low(d_branch_y), keep_low(d_branch_c), keep_low(d_branch_yc)], axis=0
    )
    context_rel = jnp.concatenate(
        [rows(context_low, 0, 0), rows(context_low, 0, 1), rows(context_low, 1, 0), rows(context_low, 1, 1)], axis=0
    )
    grad_w_out_t = t_product(d_branch_all, context_rel)

    attn_prob = jnp.exp(scores_of() - log_total)
    prob_low = low(attn_prob)
    grad_prob = product_t(grad_context, values_low)
    grad_values = low(t_product(prob_low, grad_context))
    balance = jnp.sum(grad_prob * attn_prob, axis=-1, keepdims=True)
    grad_scores = low(attn_prob * (grad_prob - balance))
    grad_query_n = product(grad_scores, keys_low) * score_scale
    grad_keys_n = t_product(grad_scores, query_low) * score_scale
    d_query, grad_gain_query = rms_back(query_raw, gain_query, grad_query_n)
    d_keys, grad_gain_key = rms_back(keys_raw, gain_key, grad_keys_n)
    d_query, d_keys = low(d_query), low(d_keys)
    d_qkv = jnp.concatenate([d_query, d_keys, grad_values], axis=1)
    w_qkv = jnp.concatenate([w_query, w_key, w_value], axis=1)
    in_parts = []
    for k in range(2):
        rows_k = jnp.concatenate([rows(d_qkv, 0, 1 - k), rows(d_qkv, 1, 1 - k)], axis=0)
        in_parts.append(product_t(rows_k, w_qkv))
    d_normed_in = gather_quarters(in_parts)
    hidden_q = rows(tokens, 0, 0).astype(f32)
    d_in, grad_attn_in = rms_back(hidden_q, gain_attn_in, d_normed_in)
    input_q = low(d_middle + d_in)
    input_own = input_q.astype(f32)
    input_y = links.y(input_own)
    input_c = links.core(input_own)
    input_yc = links.core(input_y)
    input_grad = keep_low(to_absolute([[input_own, input_y], [input_c, input_yc]]))

    grad_qkv = t_product(normed_low, d_qkv)
    grad_w_query, grad_kv = grad_qkv[:, :head], grad_qkv[:, head:]
    kv_keep = jnp.where(c == 0, grad_kv[:, :head], grad_kv[:, head:])
    kv_send = jnp.where(c == 0, grad_kv[:, head:], grad_kv[:, :head])
    kv = kv_keep + links.core(kv_send)
    kv_half = head // 2
    kv_keep = jnp.where(y == 0, kv[:, :kv_half], kv[:, kv_half:])
    kv_send = jnp.where(y == 0, kv[:, kv_half:], kv[:, :kv_half])
    kv = kv_keep + links.y(kv_send)
    attn_grads = jnp.concatenate([grad_w_query, grad_w_out_t, kv], axis=1)

    normed_all = jnp.concatenate(
        [normed_two[0][:quarter], normed_two[1][:quarter], normed_two[0][quarter:], normed_two[1][quarter:], normed_other],
        axis=0,
    )
    d_all = jnp.concatenate(
        [d_outputs[0][:quarter], d_outputs[1][:quarter], d_outputs[0][quarter:], d_outputs[1][quarter:], d_other], axis=0
    )
    gate, upward = product(normed_all, wg_h), product(normed_all, wu_h)
    inner, pull = jax.vjp(activate, gate, upward)
    inner = low(inner)
    d_inner = product_t(d_all, wd_h)
    d_gate, d_up = pull(d_inner)
    ff_grads = [t_product(d_all, inner), t_product(normed_all, low(d_gate)), t_product(normed_all, low(d_up))]

    zh, zl = z // 2, z % 2

    def sum_x(grads, z_half):
        mine = lax.dynamic_index_in_dim(grads, z_half, 0, keepdims=False)
        acc = lax.dynamic_index_in_dim(mine, x, 1, keepdims=False)
        for step in range(1, nx):
            to = lax.dynamic_index_in_dim(mine, (x + step) % nx, 1, keepdims=False)
            acc = acc + links.x(to, step)
        return acc

    def scatter(grads):
        grads = grads.reshape(2, 2, nx, blk, grads.shape[1])
        far = sum_x(grads, 1 - zh)
        near = sum_x(grads, zh)
        return near + links.z2(far)

    ff_sums = []
    for grads in ff_grads:
        got = scatter(grads)
        own = lax.dynamic_index_in_dim(got, zl, 0, keepdims=False)
        other = links.z1(lax.dynamic_index_in_dim(got, 1 - zl, 0, keepdims=False))
        ff_sums.append(
            jnp.where(
                parity == 0, jnp.concatenate([own, other], axis=1), jnp.concatenate([other, own], axis=1)
            )
        )
    grad_w_down, grad_w_gate, grad_w_up = ff_sums[0].T, ff_sums[1], ff_sums[2]

    got = scatter(attn_grads)
    attn_sum = lax.dynamic_index_in_dim(got, zl, 0, keepdims=False) + links.z1(
        lax.dynamic_index_in_dim(got, 1 - zl, 0, keepdims=False)
    )
    grad_w_query = attn_sum[:, :head]
    grad_w_out = attn_sum[:, head : 2 * head].T
    kv_own = attn_sum[:, 2 * head :]
    kv_y = links.y(kv_own)
    kv_wide = jnp.where(y == 0, jnp.concatenate([kv_own, kv_y], axis=1), jnp.concatenate([kv_y, kv_own], axis=1))
    kv_c = links.core(kv_wide)
    grad_w_key = jnp.where(c == 0, kv_wide, kv_c)
    grad_w_value = jnp.where(c == 0, kv_c, kv_wide)

    small = jnp.concatenate(
        [
            grad_attn_in.reshape(links.dp_size, -1),
            grad_attn_out.reshape(links.dp_size, -1),
            grad_ffn_in.reshape(links.dp_size, -1),
            (grad_ffn_out * 0.25).reshape(links.dp_size, -1),
            grad_gain_query.reshape(links.dp_size, -1),
            grad_gain_key.reshape(links.dp_size, -1),
        ],
        axis=1,
    )
    small = small + links.core(small)
    small = small + links.y(small)
    small = small.reshape(2, 2, nx, 1, small.shape[1])
    acc = lax.dynamic_index_in_dim(small, x, 2, keepdims=False)
    for step in range(1, nx):
        acc = acc + links.x(lax.dynamic_index_in_dim(small, (x + step) % nx, 2, keepdims=False), step)
    acc = lax.dynamic_index_in_dim(acc, zh, 0, keepdims=False) + links.z2(
        lax.dynamic_index_in_dim(acc, 1 - zh, 0, keepdims=False)
    )
    acc = lax.dynamic_index_in_dim(acc, zl, 0, keepdims=False) + links.z1(
        lax.dynamic_index_in_dim(acc, 1 - zl, 0, keepdims=False)
    )
    acc = acc.reshape(-1)
    hb = head // links.dp_size
    return (
        layer_out,
        input_grad,
        grad_w_query,
        grad_w_key,
        grad_w_value,
        grad_w_out,
        grad_w_gate,
        grad_w_up,
        grad_w_down,
        acc[:blk],
        acc[blk : 2 * blk],
        acc[2 * blk : 3 * blk],
        acc[3 * blk : 4 * blk],
        acc[4 * blk : 4 * blk + hb],
        acc[4 * blk + hb :],
    )


def solution(mesh):
    links = Links(mesh)
    return jax.shard_map(
        functools.partial(body if links.nx == 2 else body_any, links),
        mesh=mesh,
        in_specs=(
            P("dp", None),
            P("dp"),
            P("dp", None),
            P(None, "tensor"),
            P(),
            P(),
            P("tensor", None),
            P(None, "tensor"),
            P(None, "tensor"),
            P("tensor", None),
            P(),
            P(),
            P(),
            P(),
            P(),
            P(),
        ),
        out_specs=(
            P("dp", None),
            P("dp", None),
            P("dp", "tensor"),
            P("dp", None),
            P("dp", None),
            P("tensor", "dp"),
            P("dp", "tensor"),
            P("dp", "tensor"),
            P("tensor", "dp"),
            P("dp"),
            P("dp"),
            P("dp"),
            P("dp"),
            P("dp"),
            P("dp"),
        ),
        check_vma=False,
    )
```

```python
import functools

import jax
import jax.numpy as jnp
from jax import lax
from jax.experimental import pallas as pl
from jax.experimental.pallas import tpu as pltpu
from jax.sharding import PartitionSpec as P

epsilon = 1e-06
score_scale = 0.0625
NZ = 4

f32 = jnp.float32
bf16 = jnp.bfloat16


def rms_norm(values, gain):
    inverse = lax.rsqrt(jnp.mean(values * values, axis=-1, keepdims=True) + epsilon)
    return values * inverse * (1.0 + gain)


def rms_back(values, gain, grad):
    inverse = lax.rsqrt(jnp.mean(values * values, axis=-1, keepdims=True) + epsilon)
    hat = values * inverse
    scaled = grad * (1.0 + gain)
    back = inverse * (scaled - hat * jnp.mean(scaled * hat, axis=-1, keepdims=True))
    return back, jnp.sum(grad * hat, axis=0)


def product(left, right):
    return jnp.dot(left, right, preferred_element_type=f32)


def product_t(left, right):
    return lax.dot_general(left, right, (((1,), (1,)), ((), ())), preferred_element_type=f32)


def t_product(left, right):
    return lax.dot_general(left, right, (((0,), (0,)), ((), ())), preferred_element_type=f32)


def activate(gate, upward):
    return jax.nn.gelu(gate, approximate=True) * upward


class Links:
    def __init__(self, mesh):
        self.dp_size = mesh.shape["dp"]
        self.nx = self.dp_size // NZ
        tensor = mesh.shape["tensor"]
        self.perm_core = [(t, t ^ 1) for t in range(tensor)]
        self.perm_y = [(t, t ^ 2) for t in range(tensor)]
        nx = self.nx
        self.perm_z1 = [(z * nx + x, (z ^ 1) * nx + x) for z in range(NZ) for x in range(nx)]
        self.perm_z2 = [(z * nx + x, (z ^ 2) * nx + x) for z in range(NZ) for x in range(nx)]

    def core(self, a):
        return lax.ppermute(a, "tensor", self.perm_core)

    def y(self, a):
        return lax.ppermute(a, "tensor", self.perm_y)

    def z1(self, a):
        return lax.ppermute(a, "dp", self.perm_z1)

    def z2(self, a):
        return lax.ppermute(a, "dp", self.perm_z2)

    def x(self, a, step):
        nx = self.nx
        return lax.ppermute(a, "dp", [(z * nx + x, z * nx + (x + step) % nx) for z in range(NZ) for x in range(nx)])


def low(a):
    return a.astype(bf16)


MESH = pl.DeviceIdType.MESH
ANY = pl.BlockSpec(memory_space=pl.ANY)
VMEM = pl.BlockSpec(memory_space=pltpu.VMEM)
TILE, HALF, QUARTER = 256, 128, 256
VMEM_LIMIT = 127 << 19


def spots(nx):
    dp, t = lax.axis_index("dp"), lax.axis_index("tensor")
    z, x = dp // nx, dp % nx
    near = {
        "c": {"tensor": t ^ 1},
        "y": {"tensor": t ^ 2},
        "z1": {"dp": (z ^ 1) * nx + x},
        "z2": {"dp": (z ^ 2) * nx + x},
        "x": {"dp": z * nx + (x ^ 1)},
    }
    return z, x, t // 2, t % 2, near


def remote(src, dst, sems, index, to):
    return pltpu.make_async_remote_copy(
        src_ref=src, dst_ref=dst, send_sem=sems[0].at[index], recv_sem=sems[1].at[index], device_id=to, device_id_type=MESH
    )


def greet(others):
    barrier = pltpu.get_barrier_semaphore()
    for other in others:
        pl.semaphore_signal(barrier, inc=1, device_id=other, device_id_type=MESH)
    pl.semaphore_wait(barrier, len(others))


def tile_row(c, y, i, dc):
    dy = 1 - i // 2
    return pl.multiple_of(((c ^ dc) * 2 + (y ^ dy)) * QUARTER + (i % 2) * HALF, HALF)


def gelu_parts(u):
    k = 0.7978845608028654
    square = u * u
    th = jnp.tanh(k * u * (1.0 + 0.044715 * square))
    side = 0.5 * (1.0 + th)
    return u * side, side + 0.5 * u * (1.0 - th * th) * (k * (1.0 + 3.0 * 0.044715 * square))


def gelu_tanh(u):
    return 0.5 * u * (1.0 + jnp.tanh(0.7978845608028654 * u * (1.0 + 0.044715 * (u * u))))


def gain_row(gains, k):
    return gains[k : k + 1, :]


def forward_kernel(
    nx,
    middle,
    cotangent,
    gains,
    w_gate,
    w_up,
    w_down,
    normed_hbm,
    other_hbm,
    d_out_hbm,
    d_own_hbm,
    d_first,
    layer_hbm,
    pair_own_hbm,
    for_gate_hbm,
    for_up_hbm,
    gain_grad,
    normed,
    other,
    d_out,
    d_own,
    layer_out,
    out,
    dy,
    inner,
    for_gate,
    for_up,
    part,
    from_core,
    from_y,
    z_stage,
    z_land,
    c_land,
    local,
    stores,
    tile_stores,
    c_send,
    c_recv,
    y_send,
    y_recv,
    z_send,
    z_recv,
):
    z, x, y, c, near = spots(nx)
    core, across, pair = near["c"], near["y"], near["z1"]
    cs, ys, zs = (c_send, c_recv), (y_send, y_recv), (z_send, z_recv)
    loads = []
    for i in range(4):
        for dc in range(2):
            copy = pltpu.make_async_copy(
                cotangent.at[pl.ds(tile_row(c, y, i, dc), HALF)],
                dy.at[pl.ds(i * TILE + dc * HALF, HALF)],
                local.at[i * 2 + dc],
            )
            copy.start()
            loads.append(copy)
    greet([core, across, pair])
    columns = w_gate.shape[0]
    cut = pl.cdiv(columns, TILE) * HALF
    for ref in (inner, for_gate, for_up):
        for slot in range(2):
            ref[slot, :, columns:] = jnp.zeros((TILE, 2 * cut - columns), bf16)

    def tile_puts(i):
        slot = i % 2
        at = pl.ds(pl.multiple_of(i * TILE, TILE), TILE)
        mine = pl.ds(pl.multiple_of(z % 2 * cut, HALF), cut)
        return [
            pltpu.make_async_copy(inner.at[slot, :, mine], pair_own_hbm.at[at], tile_stores.at[slot, 0]),
            pltpu.make_async_copy(for_gate.at[slot], for_gate_hbm.at[at], tile_stores.at[slot, 1]),
            pltpu.make_async_copy(for_up.at[slot], for_up_hbm.at[at], tile_stores.at[slot, 2]),
        ]

    def core_copy(i):
        return remote(part.at[i, pl.ds(HALF, HALF)], from_core.at[i], cs, i, core)

    def y_copy(h):
        return remote(part.at[h, pl.ds(0, HALF)], from_y.at[h], ys, h, across)

    def z_copy(i):
        return remote(z_stage.at[i], z_land.at[i], zs, i, pair)

    first_copy = remote(d_own.at[2], d_first, zs, 4, pair)

    def z_forward(i):
        return remote(z_land.at[i], c_land.at[i], cs, 8 + i, core)

    def step(i, carry):
        at = pl.ds(pl.multiple_of(i * TILE, TILE), TILE)
        m = middle[at, :]
        inverse = lax.rsqrt(jnp.mean(m * m, axis=-1, keepdims=True) + epsilon)
        n = (m * inverse * (1.0 + gain_row(gains, 2))).astype(bf16)
        normed[at, :] = n
        z_stage[i] = n[:HALF].astype(f32)
        z_copy(i).start()
        slot = i % 2

        @pl.when(i >= 2)
        def _():
            for copy in tile_puts(i - 2):
                copy.wait()

        for lo in range(0, columns, TILE):
            hi = min(lo + TILE, columns)
            g = product_t(n, w_gate[lo:hi, :])
            u = product_t(n, w_up[lo:hi, :])
            act, slope = gelu_parts(g)
            inner[slot, :, lo:hi] = (act * u).astype(bf16)
            for_gate[slot, :, lo:hi] = (u * slope).astype(bf16)
            for_up[slot, :, lo:hi] = act.astype(bf16)
        part[i] = product(inner[slot, :, :columns], w_down[...])
        for copy in tile_puts(i):
            copy.start()
        core_copy(i).start()
        core_copy(i).wait_recv()
        part[i, :HALF] = part[i, :HALF] + from_core[i]

        @pl.when(i < 2)
        def _():
            y_copy(i).start()

        return carry

    lax.fori_loop(0, 4, step, 0)

    def tile_at(i):
        return pl.ds(pl.multiple_of(i * TILE, TILE), TILE)

    put_normed = pltpu.make_async_copy(normed, normed_hbm, stores.at[8])
    put_layer = pltpu.make_async_copy(layer_out, layer_hbm, stores.at[9])

    def put_own(i):
        return pltpu.make_async_copy(d_own.at[i], d_own_hbm.at[i], stores.at[i])

    def put_d(i):
        return pltpu.make_async_copy(d_out.at[tile_at(i)], d_out_hbm.at[tile_at(i)], stores.at[4 + i])

    def put_other(i):
        return pltpu.make_async_copy(other.at[tile_at(i)], other_hbm.at[tile_at(i)], stores.at[10 + i])

    put_normed.start()
    for i in (2, 3):
        for copy in tile_puts(i):
            copy.wait()
    for copy in loads:
        copy.wait()
    gain_grad[...] = jnp.zeros_like(gain_grad)
    gain = 1.0 + gain_row(gains, 3)

    def finish(i, dc):
        at = pl.ds(pl.multiple_of(i * TILE + dc * HALF, HALF), HALF)
        o, g = out[at, :], dy[at, :].astype(f32)
        inverse = lax.rsqrt(jnp.mean(o * o, axis=-1, keepdims=True) + epsilon)
        hat = o * inverse
        scaled = g * gain
        d = (inverse * (scaled - hat * jnp.mean(scaled * hat, axis=-1, keepdims=True))).astype(bf16)
        d_out[at, :] = d
        gain_grad[...] = gain_grad[...] + jnp.sum((g * hat).reshape(HALF // 8, 8, g.shape[1]), axis=0)
        layer_out[pl.ds(tile_row(c, y, i, dc), HALF), :] = (middle[at, :] + hat * gain).astype(bf16)
        return d

    def half_at(i, dc):
        return pl.ds(pl.multiple_of(i * TILE + dc * HALF, HALF), HALF)

    def spread_y(h):
        return remote(out.at[half_at(2 + h, 0)], out.at[half_at(h, 0)], ys, 2 + h, across)

    def spread_core(i):
        return remote(out.at[half_at(i, 0)], out.at[half_at(i, 1)], cs, 4 + i, core)

    def close_tile(n, carry):
        i = (n + 2) % 4

        @pl.when(n < 2)
        def _():
            y_copy(n).wait_recv()
            out[half_at(i, 0), :] = part[i, :HALF] + from_y[n]
            spread_y(n).start()

        @pl.when(n == 2)
        def _():
            for i in range(3):
                z_copy(i).wait_recv()
                z_forward(i).start()
            for i in range(2):
                take(i)

        @pl.when(n >= 2)
        def _():
            spread_y(i).wait_recv()

        spread_core(i).start()
        d_own[i] = finish(i, 0).astype(f32)

        @pl.when(n == 0)
        def _():
            first_copy.start()

        put_own(i).start()
        spread_core(i).wait_recv()
        finish(i, 1)
        put_d(i).start()
        return carry

    def take(i):
        z_forward(i).wait_recv()
        other[i * TILE : i * TILE + HALF, :] = z_land[i].astype(bf16)
        other[i * TILE + HALF : (i + 1) * TILE, :] = c_land[i].astype(bf16)
        put_other(i).start()

    lax.fori_loop(0, 4, close_tile, 0)
    put_layer.start()
    z_copy(3).wait_recv()
    z_forward(3).start()
    for i in range(2, 4):
        take(i)
    for i in range(4):
        core_copy(i).wait_send()
        z_copy(i).wait_send()
        z_forward(i).wait_send()
        spread_core(i).wait_send()
        put_own(i).wait()
        put_d(i).wait()
        put_other(i).wait()
    for h in range(2):
        y_copy(h).wait_send()
        spread_y(h).wait_send()
    put_normed.wait()
    put_layer.wait()
    first_copy.wait()


def dma(*counts):
    return [pltpu.SemaphoreType.DMA((n,)) for n in counts]


def feed_forward(nx, middle, cotangent, gains, w_gate, w_up, w_down):
    length, width = middle.shape
    columns = pl.cdiv(w_gate.shape[0], TILE) * TILE
    rows_low = jax.ShapeDtypeStruct((length, width), bf16)
    return pl.pallas_call(
        functools.partial(forward_kernel, nx),
        out_shape=(
            rows_low,
            rows_low,
            rows_low,
            jax.ShapeDtypeStruct((4, HALF, width), f32),
            jax.ShapeDtypeStruct((HALF, width), f32),
            rows_low,
            jax.ShapeDtypeStruct((length, columns // 2), bf16),
            jax.ShapeDtypeStruct((length, columns), bf16),
            jax.ShapeDtypeStruct((length, columns), bf16),
            jax.ShapeDtypeStruct((8, width), f32),
        ),
        in_specs=[VMEM, ANY] + [VMEM] * 4,
        out_specs=(ANY,) * 4 + (VMEM, ANY, ANY, ANY, ANY, VMEM),
        scratch_shapes=[pltpu.VMEM((length, width), bf16)] * 3
        + [
            pltpu.VMEM((4, HALF, width), f32),
            pltpu.VMEM((length, width), bf16),
            pltpu.VMEM((length, width), f32),
            pltpu.VMEM((length, width), bf16),
            pltpu.VMEM((2, TILE, columns), bf16),
            pltpu.VMEM((2, TILE, columns), bf16),
            pltpu.VMEM((2, TILE, columns), bf16),
            pltpu.VMEM((4, TILE, width), f32),
            pltpu.VMEM((4, HALF, width), f32),
            pltpu.VMEM((2, HALF, width), f32),
            pltpu.VMEM((4, HALF, width), f32),
            pltpu.VMEM((4, HALF, width), f32),
            pltpu.VMEM((4, HALF, width), f32),
        ]
        + dma(8, 14)
        + [pltpu.SemaphoreType.DMA((2, 3))]
        + dma(12, 12, 4, 4, 5, 5),
        compiler_params=pltpu.CompilerParams(collective_id=0, has_side_effects=True, vmem_limit_bytes=VMEM_LIMIT),
        name="feed_forward",
    )(middle, cotangent, gains, w_gate, w_up, w_down)


def back_kernel(
    nx,
    d_out_hbm,
    d_own_hbm,
    d_first_hbm,
    for_gate_hbm,
    for_up_hbm,
    other_hbm,
    w_gate_hbm,
    w_up_hbm,
    w_down_hbm,
    w_out_hbm,
    middle_hbm,
    branch_hbm,
    dy_hbm,
    gains,
    d_other,
    pair_in,
    pair_gates,
    heads,
    d_branch_out,
    d_middle_out,
    gain_grads,
    d_out,
    for_gate,
    for_up,
    other,
    w_gate,
    w_up,
    w_down,
    w_out,
    middle,
    branch,
    dy,
    gates,
    ups,
    inner,
    part,
    from_core,
    from_y,
    z_land,
    c_land,
    loads_sem,
    tiles_sem,
    stores_sem,
    c_send,
    c_recv,
    y_send,
    y_recv,
    z_send,
    z_recv,
):
    z, x, y, c, near = spots(nx)
    core, across, pair = near["c"], near["y"], near["z1"]
    cs, ys, zs = (c_send, c_recv), (y_send, y_recv), (z_send, z_recv)
    parity = z % 2
    real, columns = w_gate_hbm.shape[0], w_gate.shape[0]
    half = columns // 2
    head = heads.shape[2]
    own_row = pl.multiple_of((c * 2 + y) * QUARTER, QUARTER)
    sources = [
        (d_out_hbm, d_out),
        (w_gate_hbm, w_gate.at[pl.ds(0, real)]),
        (w_up_hbm, w_up.at[pl.ds(0, real)]),
        (w_down_hbm, w_down.at[pl.ds(0, real)]),
        (other_hbm, other),
        (w_out_hbm, w_out),
        (middle_hbm.at[pl.ds(2 * TILE, HALF)], middle.at[pl.ds(0, HALF)]),
        (middle_hbm.at[pl.ds(3 * TILE, HALF)], middle.at[pl.ds(HALF, HALF)]),
        (branch_hbm, branch),
        (dy_hbm.at[pl.ds(own_row, QUARTER)], dy),
        (d_first_hbm, z_land.at[2]),
    ]
    loads = [pltpu.make_async_copy(src, dst, loads_sem.at[k]) for k, (src, dst) in enumerate(sources)]
    for copy in loads:
        copy.start()
    if real < columns:
        for ref in (w_gate, w_up, w_down):
            ref[real:, :] = jnp.zeros((columns - real, ref.shape[1]), bf16)
    greet([core, across, pair])

    def core_copy(i):
        return remote(part.at[i, pl.ds(HALF, HALF)], from_core.at[i], cs, i, core)

    def y_copy(h):
        return remote(part.at[h, pl.ds(0, HALF)], from_y.at[h], ys, h, across)

    def z_copy(i):
        return remote(d_own_hbm.at[i], z_land.at[i], zs, i, pair)

    def z_forward(i):
        return remote(z_land.at[i], c_land.at[i], cs, 4 + i, core)

    for i in (3, 0, 1):
        z_copy(i).start()
    def tile_loads(i):
        slot = i % 2
        at = pl.ds(pl.multiple_of(i * TILE, TILE), TILE)
        return [
            pltpu.make_async_copy(for_gate_hbm.at[at], for_gate.at[slot], tiles_sem.at[slot, 0]),
            pltpu.make_async_copy(for_up_hbm.at[at], for_up.at[slot], tiles_sem.at[slot, 1]),
        ]

    for i in range(2):
        for copy in tile_loads(i):
            copy.start()
    for copy in loads[:4]:
        copy.wait()

    mine = pl.multiple_of(parity * half, HALF)

    def stores(i, base):
        slot = i % 2
        at = pl.ds(pl.multiple_of(base + i * TILE, TILE), TILE)
        pick = pl.ds(mine, half)
        first = []
        if base:
            first = [
                pltpu.make_async_copy(
                    inner.at[slot], pair_in.at[pl.ds(pl.multiple_of(i * TILE, TILE), TILE)], stores_sem.at[slot, 0]
                )
            ]
        return first + [
            pltpu.make_async_copy(gates.at[slot, :, pick], pair_gates.at[at, pl.ds(0, half)], stores_sem.at[slot, 1]),
            pltpu.make_async_copy(ups.at[slot, :, pick], pair_gates.at[at, pl.ds(half, half)], stores_sem.at[slot, 2]),
        ]

    def piece(n, d, slot, at, own):
        g = product_t(n, w_gate[at, :])
        u = product_t(n, w_up[at, :])
        di = product_t(d, w_down[at, :])
        act, slope = gelu_parts(g)
        inner[slot, :, own] = (act * u).astype(bf16)
        gates[slot, :, at] = (di * u * slope).astype(bf16)
        ups[slot, :, at] = (di * act).astype(bf16)

    def own_tile(i, carry):
        at = pl.ds(pl.multiple_of(i * TILE, TILE), TILE)
        slot = i % 2

        @pl.when(i >= 2)
        def _():
            for copy in stores(i - 2, 0):
                copy.wait()

        for copy in tile_loads(i):
            copy.wait()
        d = d_out[at, :]
        for lo in range(0, columns, TILE):
            cols = pl.ds(lo, TILE)
            di = product_t(d, w_down[cols, :])
            gates[slot, :, cols] = (di * for_gate[slot, :, cols].astype(f32)).astype(bf16)
            ups[slot, :, cols] = (di * for_up[slot, :, cols].astype(f32)).astype(bf16)

        @pl.when(i < 2)
        def _():
            for copy in tile_loads(i + 2):
                copy.start()

        for copy in stores(i, 0):
            copy.start()
        part[i] = product(gates[slot], w_gate[...]) + product(ups[slot], w_up[...])
        core_copy(i).start()
        core_copy(i).wait_recv()
        part[i, :HALF] = part[i, :HALF] + from_core[i]

        @pl.when(i < 2)
        def _():
            y_copy(i).start()

        return carry

    lax.fori_loop(0, 4, own_tile, 0)
    for copy in loads[4:]:
        copy.wait()

    def other_tile(n, carry):
        i, slot = (n + 2) % 4, n % 2

        @pl.when(n > 0)
        def _():
            z_copy(i).wait_recv()

        z_forward(i).start()

        @pl.when(n < 2)
        def _():
            for copy in stores(i, 0):
                copy.wait()

        @pl.when(n >= 2)
        def _():
            for copy in stores(n, d_out.shape[0]):
                copy.wait()

        z_forward(i).wait_recv()
        lo = pl.multiple_of(i * TILE, TILE)
        d_other[pl.ds(lo, HALF), :] = z_land[i].astype(bf16)
        d_other[pl.ds(lo + HALF, HALF), :] = c_land[i].astype(bf16)
        n, d = other[pl.ds(lo, TILE), :], d_other[pl.ds(lo, TILE), :]
        for off in range(0, half, TILE):
            size = min(TILE, half - off)
            piece(n, d, slot, pl.ds(pl.multiple_of(mine + off, HALF), size), pl.ds(off, size))
        for copy in stores(i, d_out.shape[0]):
            copy.start()
        return carry

    lax.fori_loop(0, 3, other_tile, 0)

    gain_grads[...] = jnp.zeros_like(gain_grads)

    def fold(a):
        return jnp.sum(a.reshape(a.shape[0] // 8, 8, a.shape[1]), axis=0)

    def of_quarter(h, carry):
        y_copy(h).wait_recv()
        at = pl.ds(pl.multiple_of(h * HALF, HALF), HALF)
        grad = part[2 + h, :HALF] + from_y[h]
        m = middle[at, :]
        inverse = lax.rsqrt(jnp.mean(m * m, axis=-1, keepdims=True) + epsilon)
        hat = m * inverse
        scaled = grad * (1.0 + gain_row(gains, 2))
        d_middle = dy[at, :].astype(f32) + inverse * (scaled - hat * jnp.mean(scaled * hat, axis=-1, keepdims=True))
        gain_grads[0] = gain_grads[0] + fold(grad * hat)
        d_middle_out[at, :] = d_middle
        b = branch[at, :]
        inverse = lax.rsqrt(jnp.mean(b * b, axis=-1, keepdims=True) + epsilon)
        hat = b * inverse
        scaled = d_middle * (1.0 + gain_row(gains, 1))
        d_low = (inverse * (scaled - hat * jnp.mean(scaled * hat, axis=-1, keepdims=True))).astype(bf16)
        gain_grads[1] = gain_grads[1] + fold(d_middle * hat)
        d_branch_out[at, :] = d_low.astype(f32)
        for k in range(4):
            heads[k, at, :] = product_t(d_low, w_out[k * head : (k + 1) * head, :]).astype(bf16).astype(f32)
        return carry

    lax.fori_loop(0, 2, of_quarter, 0)
    lax.fori_loop(3, 4, other_tile, 0)
    for i in (0, 1):
        for copy in stores(i, d_out.shape[0]):
            copy.wait()
    for i in (3, 0, 1):
        z_copy(i).wait_send()
    for i in range(4):
        core_copy(i).wait_send()
        z_forward(i).wait_send()
    for h in range(2):
        y_copy(h).wait_send()


def feed_back(nx, d_out, d_own, d_first, for_gate, for_up, other, w_gate, w_up, w_down, w_out, middle, branch, dy, gains):
    length, width = d_out.shape
    columns = pl.cdiv(w_gate.shape[0], TILE) * TILE
    head = w_out.shape[0] // 4
    return pl.pallas_call(
        functools.partial(back_kernel, nx),
        out_shape=(
            jax.ShapeDtypeStruct((length, width), bf16),
            jax.ShapeDtypeStruct((length, columns // 2), bf16),
            jax.ShapeDtypeStruct((2 * length, columns), bf16),
            jax.ShapeDtypeStruct((4, QUARTER, head), f32),
            jax.ShapeDtypeStruct((QUARTER, width), f32),
            jax.ShapeDtypeStruct((QUARTER, width), f32),
            jax.ShapeDtypeStruct((2, 8, width), f32),
        ),
        in_specs=[ANY] * 13 + [VMEM],
        out_specs=(VMEM, ANY, ANY) + (VMEM,) * 4,
        scratch_shapes=[
            pltpu.VMEM((length, width), bf16),
            pltpu.VMEM((2, TILE, columns), bf16),
            pltpu.VMEM((2, TILE, columns), bf16),
            pltpu.VMEM((length, width), bf16),
            pltpu.VMEM((columns, width), bf16),
            pltpu.VMEM((columns, width), bf16),
            pltpu.VMEM((columns, width), bf16),
            pltpu.VMEM((4 * head, width), bf16),
            pltpu.VMEM((QUARTER, width), f32),
            pltpu.VMEM((QUARTER, width), f32),
            pltpu.VMEM((QUARTER, width), bf16),
            pltpu.VMEM((2, TILE, columns), bf16),
            pltpu.VMEM((2, TILE, columns), bf16),
            pltpu.VMEM((2, TILE, columns // 2), bf16),
            pltpu.VMEM((4, TILE, width), f32),
            pltpu.VMEM((4, HALF, width), f32),
            pltpu.VMEM((2, HALF, width), f32),
            pltpu.VMEM((4, HALF, width), f32),
            pltpu.VMEM((4, HALF, width), f32),
            pltpu.SemaphoreType.DMA((12,)),
            pltpu.SemaphoreType.DMA((2, 2)),
            pltpu.SemaphoreType.DMA((2, 3)),
        ]
        + dma(8, 8, 2, 2, 4, 4),
        compiler_params=pltpu.CompilerParams(collective_id=1, has_side_effects=True, vmem_limit_bytes=VMEM_LIMIT),
        name="feed_back",
    )(
        d_out,
        d_own,
        d_first,
        for_gate,
        for_up,
        other,
        w_gate,
        w_up,
        w_down,
        w_out,
        middle,
        branch,
        dy,
        gains,
    )


def visible_pairs(shape, i, segments):
    row = lax.broadcasted_iota(jnp.int32, shape, 0) + i * TILE
    col = lax.broadcasted_iota(jnp.int32, shape, 1)
    first = jnp.sum((segments[...] == 0).astype(jnp.int32), axis=1, keepdims=True)
    return (row >= col) & ((row < first) == (col < first))


def attention_kernel(
    nx,
    tokens,
    w_query,
    w_key,
    w_value,
    w_out,
    segments,
    gain_0,
    gain_1,
    gain_2,
    gain_3,
    gain_4,
    gain_5,
    normed_hbm,
    query_hbm,
    keys_hbm,
    values_hbm,
    query_raw_hbm,
    keys_raw_hbm,
    log_total_hbm,
    context_hbm,
    w_out_all_hbm,
    middle,
    branch,
    gains,
    normed,
    query,
    keys,
    values,
    query_raw,
    keys_raw,
    log_total,
    context,
    w_out_all,
    stores,
    out_own,
    out_land,
    context_own,
    context_core,
    context_land,
    context_all,
    c_send,
    c_recv,
    y_send,
    y_recv,
    x_send,
    x_recv,
):
    z, x, y, c, near = spots(nx)
    cs, ys, xs = (c_send, c_recv), (y_send, y_recv), (x_send, x_recv)
    length, width = tokens.shape
    head = w_query.shape[1]
    given = (gain_0, gain_1, gain_2, gain_3, gain_4, gain_5)
    gain_loads = [
        pltpu.make_async_copy(ref, gains.at[k, pl.ds(0, ref.shape[0])], stores.at[k]) for k, ref in enumerate(given)
    ]
    for copy in gain_loads:
        copy.start()
    out_own[...] = w_out[...].astype(f32)
    greet([near[k] for k in ("c", "y", "x")])
    mine = pl.ds(pl.multiple_of(x * (head // 2), 8), head // 2)
    out_y = remote(out_own.at[mine], out_land.at[0, mine], ys, 0, near["y"])
    out_x = remote(out_land.at[0, mine], out_land.at[0, mine], xs, 0, near["x"])
    out_c = remote(out_own, out_land.at[1], cs, 0, near["c"])
    out_yc = remote(out_land.at[0], out_land.at[2], cs, 1, near["c"])
    out_y.start()
    out_c.start()
    w_out_all[:head, :] = w_out[...]

    for copy in gain_loads:
        copy.wait()

    def norm(v, gain):
        return v * lax.rsqrt(jnp.mean(v * v, axis=-1, keepdims=True) + epsilon) * (1.0 + gain)

    def inputs(i, carry):
        at = pl.ds(pl.multiple_of(i * TILE, TILE), TILE)
        n = norm(tokens[at, :].astype(f32), gain_row(gains, 0)).astype(bf16)
        normed[at, :] = n
        raw = product(n, w_query[...])
        query_raw[at, :] = raw
        query[at, :] = norm(raw, gain_row(gains, 4)[:, :head]).astype(bf16)
        raw = product(n, w_key[...])
        keys_raw[at, :] = raw
        keys[at, :] = norm(raw, gain_row(gains, 5)[:, :head]).astype(bf16)
        values[at, :] = product(n, w_value[...]).astype(bf16)
        return carry

    lax.fori_loop(0, length // TILE, inputs, 0)
    for i in range(length // TILE):
        at, seen = slice(i * TILE, (i + 1) * TILE), (i + 1) * TILE
        s = product_t(query[at, :], keys[:seen, :]) * score_scale
        s = jnp.where(visible_pairs(s.shape, i, segments), s, -1e30)
        largest = jnp.max(s, axis=-1, keepdims=True)
        e = jnp.exp(s - largest)
        total = jnp.sum(e, axis=-1, keepdims=True)
        log_total[at, :] = largest + jnp.log(total)
        low_context = product((e / total).astype(bf16), values[:seen, :]).astype(bf16)
        context[at, :] = low_context
        context_own[at, :] = low_context.astype(f32)

    out_copies = []

    def put(src, dst):
        copy = pltpu.make_async_copy(src, dst, stores.at[len(out_copies)])
        copy.start()
        out_copies.append(copy)

    span = length // 2
    to_core = remote(context_own.at[pl.ds(pl.multiple_of((1 - c) * span, span), span)], context_core, cs, 2, near["c"])
    to_core.start()

    def local(i, other):
        dy = 1 - i // 2
        return pl.multiple_of(((y ^ other) ^ dy) * QUARTER + (i % 2) * HALF, HALF)

    def context_copy(i, k):
        if k == 0:
            src = context_own.at[pl.ds(pl.multiple_of(c * span + local(i, 1), HALF), HALF)]
        else:
            src = context_core.at[pl.ds(local(i, 1), HALF)]
        return remote(src, context_land.at[k, i], ys, 1 + 2 * i + k, near["y"])

    context_copy(0, 0).start()
    for src, dst in (
        (normed, normed_hbm),
        (query, query_hbm),
        (keys, keys_hbm),
        (values, values_hbm),
        (query_raw, query_raw_hbm),
        (keys_raw, keys_raw_hbm),
        (log_total, log_total_hbm),
        (context, context_hbm),
    ):
        put(src, dst)
    out_y.wait_recv()
    out_x.start()
    to_core.wait_recv()
    for i in range(4):
        for k in range(2):
            if i + k > 0:
                context_copy(i, k).start()
    out_c.wait_recv()
    w_out_all[2 * head : 3 * head, :] = out_land[1].astype(bf16)
    for i in range(4):
        rows = pl.ds(i * HALF, HALF)
        context_all[rows, :head] = context[pl.ds(pl.multiple_of(c * span + local(i, 0), HALF), HALF), :]
        context_all[rows, 2 * head : 3 * head] = context_core[pl.ds(local(i, 0), HALF), :].astype(bf16)
    out_x.wait_recv()
    out_yc.start()
    w_out_all[head : 2 * head, :] = out_land[0].astype(bf16)
    out_yc.wait_recv()
    w_out_all[3 * head :, :] = out_land[2].astype(bf16)
    put(w_out_all, w_out_all_hbm)

    def middle_copy(i):
        at = pl.multiple_of(i * TILE, TILE)
        return remote(middle.at[pl.ds(at, HALF)], middle.at[pl.ds(at + HALF, HALF)], cs, 3 + i, near["c"])

    def middle_tile(i, carry):
        rows = pl.ds(pl.multiple_of(i * HALF, HALF), HALF)
        context_copy(i, 0).wait_recv()
        context_all[rows, head : 2 * head] = context_land[0, i].astype(bf16)
        context_copy(i, 1).wait_recv()
        context_all[rows, 3 * head :] = context_land[1, i].astype(bf16)
        b = product(context_all[rows, :], w_out_all[...])
        branch[i % 2] = b
        hidden = tokens[pl.ds(pl.multiple_of(c * span + local(i, 0), HALF), HALF), :].astype(f32)
        middle[pl.ds(pl.multiple_of(i * TILE, TILE), HALF), :] = hidden + norm(b, gain_row(gains, 1))
        middle_copy(i).start()
        return carry

    lax.fori_loop(0, 4, middle_tile, 0)
    for i in range(4):
        middle_copy(i).wait()
        for k in range(2):
            context_copy(i, k).wait_send()
    for copy in (out_y, out_x, out_c, out_yc, to_core):
        copy.wait_send()
    for copy in out_copies:
        copy.wait()


def attend(nx, tokens, w_query, w_key, w_value, w_out, segment_ids, *gains):
    length, width = tokens.shape
    head = w_query.shape[1]
    of_head = jax.ShapeDtypeStruct((length, head), bf16)
    raw = jax.ShapeDtypeStruct((length, head), f32)
    return pl.pallas_call(
        functools.partial(attention_kernel, nx),
        out_shape=(
            jax.ShapeDtypeStruct((length, width), bf16),
            of_head,
            of_head,
            of_head,
            raw,
            raw,
            jax.ShapeDtypeStruct((length, 1), f32),
            of_head,
            jax.ShapeDtypeStruct((4 * head, width), bf16),
            jax.ShapeDtypeStruct((length, width), f32),
            jax.ShapeDtypeStruct((2, HALF, width), f32),
            jax.ShapeDtypeStruct((8, width), f32),
        ),
        in_specs=[VMEM] * 6 + [ANY] * 6,
        out_specs=(ANY,) * 9 + (VMEM,) * 3,
        scratch_shapes=[
            pltpu.VMEM((length, width), bf16),
            pltpu.VMEM((length, head), bf16),
            pltpu.VMEM((length, head), bf16),
            pltpu.VMEM((length, head), bf16),
            pltpu.VMEM((length, head), f32),
            pltpu.VMEM((length, head), f32),
            pltpu.VMEM((length, 1), f32),
            pltpu.VMEM((length, head), bf16),
            pltpu.VMEM((4 * head, width), bf16),
            pltpu.SemaphoreType.DMA((9,)),
            pltpu.VMEM((head, width), f32),
            pltpu.VMEM((3, head, width), f32),
            pltpu.VMEM((length, head), f32),
            pltpu.VMEM((length // 2, head), f32),
            pltpu.VMEM((2, 4, HALF, head), f32),
            pltpu.VMEM((length // 2, 4 * head), bf16),
        ]
        + dma(7, 7, 9, 9, 1, 1),
        compiler_params=pltpu.CompilerParams(collective_id=3, has_side_effects=True, vmem_limit_bytes=VMEM_LIMIT),
        name="attend",
    )(
        tokens,
        w_query,
        w_key,
        w_value,
        w_out,
        segment_ids.reshape(1, length),
        *gains,
    )


def reduce_kernel(
    nx,
    d_out_hbm,
    d_other_hbm,
    normed_hbm,
    other_hbm,
    pair_own_hbm,
    pair_other_hbm,
    pair_gates_hbm,
    d_branch_hbm,
    d_middle_hbm,
    tokens_hbm,
    normed_in_hbm,
    query_hbm,
    keys_hbm,
    values_hbm,
    query_raw_hbm,
    keys_raw_hbm,
    context_hbm,
    heads_hbm,
    w_query_hbm,
    w_key_hbm,
    w_value_hbm,
    log_total,
    segments,
    gain_rows,
    of_ffn_out,
    of_middle,
    down_out,
    gate_out,
    up_out,
    query_out,
    out_out,
    key_out,
    value_out,
    input_grad,
    gains,
    input_stage,
    ff_stage,
    dw,
    x_land,
    z2_land,
    z1_land,
    from_core,
    from_y,
    branch_land,
    input_own,
    input_land,
    d_qkv,
    attn,
    attn_z1,
    attn_x,
    attn_z2,
    kv_core,
    kv_across,
    kv_own,
    kv_y,
    kv_wide,
    kv_wide_core,
    gains_land,
    heads_mine,
    heads_y,
    got_c,
    got_y,
    loads,
    c_send,
    c_recv,
    y_send,
    y_recv,
    x_send,
    x_recv,
    z2_send,
    z2_recv,
    z1_send,
    z1_recv,
):
    z, x, y, c, near = spots(nx)
    zh, zl = z // 2, z % 2
    cs, ys, xs = (c_send, c_recv), (y_send, y_recv), (x_send, x_recv)
    z2s, z1s = (z2_send, z2_recv), (z1_send, z1_recv)
    length, width = d_out_hbm.shape
    half = pair_own_hbm.shape[1]
    head = query_hbm.shape[1]
    blk = x_land.shape[1]
    own_row = pl.multiple_of((c * 2 + y) * QUARTER, QUARTER)

    def block(a, b):
        return pl.ds(pl.multiple_of(b * blk, 8), blk)

    def quarter_rows(dc, dy):
        return pl.ds(pl.multiple_of(((c ^ dc) * 2 + (y ^ dy)) * QUARTER, QUARTER), QUARTER)

    greet([near[k] for k in ("c", "y", "x", "z2", "z1")])

    heads_in = pltpu.make_async_copy(heads_hbm.at[0], heads_mine, loads.at[6])
    heads_in_y = pltpu.make_async_copy(heads_hbm.at[1], heads_y.at[0], loads.at[7])
    heads_c_copy = remote(heads_hbm.at[pl.ds(2, 2)], got_c, cs, 11, near["c"])
    heads_y_copy = remote(heads_y, got_y, ys, 7, near["y"])
    heads_c_copy.start()
    heads_in.start()
    heads_in_y.start()
    heads_c_copy.wait_recv()
    heads_in_y.wait()
    heads_y[1] = got_c[1]
    heads_y_copy.start()

    branch_y = remote(d_branch_hbm, branch_land.at[0], ys, 0, near["y"])
    branch_c = remote(d_branch_hbm, branch_land.at[1], cs, 0, near["c"])
    branch_fwd = remote(branch_land.at[0], branch_land.at[2], cs, 1, near["c"])
    branch_y.start()
    branch_c.start()

    def place(n):
        return n // 2 * 2 + (1 - zl if n % 2 == 0 else zl)

    def owner(n):
        return 2 * (1 - zh if n < 2 else zh) + (1 - zl if n % 2 == 0 else zl)

    def x_copy(m, n):
        slot = m * 4 + place(n)
        return remote(dw.at[m, block(dw, owner(n) * 2 + (1 - x))], x_land.at[slot], xs, slot, near["x"])

    def z2_copy(m, n):
        slot = m * 2 + place(n)
        return remote(dw.at[m, block(dw, owner(n) * 2 + x)], z2_land.at[slot], z2s, slot, near["z2"])

    def z1_copy(m):
        return remote(dw.at[m, block(dw, (2 * zh + 1 - zl) * 2 + x)], z1_land.at[m], z1s, m, near["z1"])

    def start_x(*blocks):
        for m, j in blocks:
            x_copy(m, j).start()

    arrived = set()

    def wait_x(m, j):
        if (m, j) not in arrived:
            arrived.add((m, j))
            x_copy(m, j).wait_recv()

    inner = (z == 1) | (z == 2)

    def far(*blocks):
        for m, k in blocks:
            wait_x(m, k)
            rows = block(dw, owner(k) * 2 + x)
            dw[m, rows, :] = dw[m, rows, :] + x_land[m * 4 + place(k)]

            @pl.when(inner)
            def _():
                z2_copy(m, k).start()

    def outer(m, k):
        @pl.when(jnp.logical_not(inner))
        def _():
            z2_copy(m, k).start()

    def close(m):
        for k in range(2):
            wait_x(m, 2 + k)
            z2_copy(m, k).wait_recv()
            rows = block(dw, owner(2 + k) * 2 + x)
            dw[m, rows, :] = dw[m, rows, :] + x_land[m * 4 + place(2 + k)] + z2_land[m * 2 + place(k)]
            if k == 0:
                z1_copy(m).start()

    def finish(m, ref):
        z1_copy(m).wait_recv()
        own, other = dw[m, block(dw, (2 * zh + zl) * 2 + x), :], z1_land[m]
        ff_stage[:, :half] = jnp.where(zl == 0, own, other)
        ff_stage[:, half:] = jnp.where(zl == 0, other, own)[:, : ref.shape[1] - half]
        copy = pltpu.make_async_copy(ff_stage, ref, loads.at[1])
        copy.start()
        copy.wait()

    def copies(pairs):
        started = [pltpu.make_async_copy(src, dst, loads.at[k]) for k, (src, dst) in enumerate(pairs)]
        for copy in started:
            copy.start()
        return started

    def weights(left, right):
        far_size = pl.cdiv(width // 2, HALF) * HALF
        far_at = pl.multiple_of((1 - zh) * (width - far_size), HALF)
        near_at = pl.multiple_of(zh * far_size, HALF)

        def form(m, lo, at, size):
            for off in range(0, size, 3 * HALF):
                rows = pl.ds(pl.multiple_of(at + off, HALF), min(3 * HALF, size - off))
                cols = pl.ds(pl.multiple_of(lo, HALF), half)
                dw[m, rows, :] = t_product(left[:, rows], right[:, cols])

        for copy in copies(
            [
                (d_out_hbm, left.at[pl.ds(0, length)]),
                (d_other_hbm, left.at[pl.ds(length, length)]),
                (pair_own_hbm, right.at[pl.ds(0, length), pl.ds(0, half)]),
                (pair_other_hbm, right.at[pl.ds(length, length), pl.ds(0, half)]),
            ]
        ):
            copy.wait()
        form(0, 0, far_at, far_size)
        start_x((0, 0), (0, 1))
        form(0, 0, near_at, width - far_size)
        for copy in copies(
            [
                (normed_hbm, left.at[pl.ds(0, length)]),
                (other_hbm, left.at[pl.ds(length, length)]),
                (pair_gates_hbm, right),
            ]
        ):
            copy.wait()
        def form_far(m, carry):
            form(m, (m - 1) * half, far_at, far_size)
            start_x((m, 0), (m, 1))
            return carry

        def form_near(m, carry):
            form(m, (m - 1) * half, near_at, width - far_size)
            return carry

        lax.fori_loop(1, 3, form_far, 0)
        far((0, 0))
        outer(0, 0)
        lax.fori_loop(1, 3, form_near, 0)
        start_x((0, 2), (0, 3), (1, 2), (1, 3), (2, 2), (2, 3))

    pl.run_scoped(weights, pltpu.VMEM((2 * length, width), bf16), pltpu.VMEM((2 * length, 2 * half), bf16))

    def total_of(a):
        return jnp.sum(a, axis=0, keepdims=True)

    gains[...] = jnp.zeros_like(gains)
    gains[1:2, :] = total_of(of_middle[1])
    gains[2:3, :] = total_of(of_middle[0])
    gains[3:4, :] = 0.25 * total_of(of_ffn_out[...])

    def back_norm(raw, gain, grad):
        inverse = lax.rsqrt(jnp.mean(raw * raw, axis=-1, keepdims=True) + epsilon)
        hat = raw * inverse
        scaled = grad * (1.0 + gain)
        return inverse * (scaled - hat * jnp.mean(scaled * hat, axis=-1, keepdims=True)), grad * hat

    def attention(query, keys, values, query_raw, keys_raw, grad_context, d_keys, d_values):
        for copy in copies(
            [
                (query_hbm, query),
                (keys_hbm, keys),
                (values_hbm, values),
                (query_raw_hbm, query_raw),
                (keys_raw_hbm, keys_raw),
            ]
        ):
            copy.wait()
        heads_in.wait()
        grad_context[quarter_rows(0, 0), :] = heads_mine[...].astype(bf16)
        grad_context[quarter_rows(1, 0), :] = got_c[0].astype(bf16)
        heads_y_copy.wait_recv()
        grad_context[quarter_rows(0, 1), :] = got_y[0].astype(bf16)
        grad_context[quarter_rows(1, 1), :] = got_y[1].astype(bf16)
        d_keys[...] = jnp.zeros_like(d_keys)
        d_values[...] = jnp.zeros_like(d_values)

        def back_tile(seen, i, carry):
            at = pl.ds(pl.multiple_of(i * TILE, TILE), TILE)
            q, k = query[at, :], keys[:seen, :]
            s = product_t(q, k) * score_scale
            p = jnp.exp(jnp.where(visible_pairs(s.shape, i, segments), s, -1e30) - log_total[at, :])
            g = grad_context[at, :]
            dp = product_t(g, values[:seen, :])
            balance = jnp.sum(dp * p, axis=-1, keepdims=True)
            ds = (p * (dp - balance)).astype(bf16)
            dq, of_gain = back_norm(query_raw[at, :], gain_row(gain_rows, 4)[:, :head], product(ds, k) * score_scale)
            d_qkv[at, :head] = dq.astype(bf16)
            gains[4:5, :head] = gains[4:5, :head] + jnp.sum(of_gain, axis=0, keepdims=True)
            d_keys[:seen, :] = d_keys[:seen, :] + t_product(ds, q)
            d_values[:seen, :] = d_values[:seen, :] + t_product(p.astype(bf16), g)
            return carry

        tiles = length // TILE
        lax.fori_loop(0, tiles // 2, functools.partial(back_tile, length // 2), 0)
        lax.fori_loop(tiles // 2, tiles, functools.partial(back_tile, length), 0)

        def keys_tile(i, carry):
            at = pl.ds(pl.multiple_of(i * TILE, TILE), TILE)
            dk, of_gain = back_norm(keys_raw[at, :], gain_row(gain_rows, 5)[:, :head], d_keys[at, :] * score_scale)
            d_qkv[at, head : 2 * head] = dk.astype(bf16)
            gains[5:6, :head] = gains[5:6, :head] + jnp.sum(of_gain, axis=0, keepdims=True)
            d_qkv[at, 2 * head :] = d_values[at, :].astype(bf16)
            return carry

        lax.fori_loop(0, tiles, keys_tile, 0)

    pl.run_scoped(
        attention,
        pltpu.VMEM((length, head), bf16),
        pltpu.VMEM((length, head), bf16),
        pltpu.VMEM((length, head), bf16),
        pltpu.VMEM((length, head), f32),
        pltpu.VMEM((length, head), f32),
        pltpu.VMEM((length, head), bf16),
        pltpu.VMEM((length, head), f32),
        pltpu.VMEM((length, head), f32),
    )
    far((0, 1))

    def put_input(dc, dy):
        copy = pltpu.make_async_copy(input_stage, input_grad.at[quarter_rows(dc, dy)], loads.at[0])
        copy.start()
        copy.wait()

    def attn_z1_copy(i):
        b = (2 * (i // 2) + 1 - zl) * 2 + i % 2
        return remote(attn.at[block(attn, b)], attn_z1.at[i], z1s, 3 + i, near["z1"])

    def attn_x_copy(j):
        b = (2 * (zh ^ j) + zl) * 2 + 1 - x
        return remote(attn.at[block(attn, b)], attn_x.at[j], xs, 12 + j, near["x"])

    attn_z2_copy = remote(attn.at[block(attn, (2 * (1 - zh) + zl) * 2 + x)], attn_z2, z2s, 6, near["z2"])

    input_y = remote(input_own, input_land.at[0], ys, 4, near["y"])
    input_c = remote(input_own, input_land.at[1], cs, 7, near["c"])
    input_fwd = remote(input_land.at[0], input_land.at[2], cs, 8, near["c"])

    hops = [
        remote(gains, gains_land.at[k], sems, index, near[to])
        for k, (sems, index, to) in enumerate([(cs, 10, "c"), (ys, 6, "y"), (xs, 14, "x"), (z1s, 7, "z1"), (z2s, 7, "z2")])
    ]

    def hop(k):
        hops[k].start()

    def arrive(k):
        hops[k].wait()
        gains[...] = gains[...] + gains_land[k]

    def rest(w_qkv, part, kv_halves):
        def of_inputs(normed_in, kv):
            for copy in copies([(normed_in_hbm, normed_in)]):
                copy.wait()
            for k in range(2):
                kv[k] = t_product(normed_in[...], d_qkv[:, (1 + k) * head : (2 + k) * head])
            to_core = remote(kv.at[1 - c], kv_core, cs, 6, near["c"])
            to_core.start()
            attn[:, :head] = t_product(normed_in[...], d_qkv[:, :head])
            to_core.wait_recv()
            for k in range(2):
                lanes = slice(k * (head // 2), (k + 1) * (head // 2))
                kv_halves[k] = kv[c, :, lanes] + kv_core[:, lanes]
            to_core.wait_send()

        pl.run_scoped(of_inputs, pltpu.VMEM((length, width), bf16), pltpu.VMEM((2, width, head), f32))
        to_y = remote(kv_halves.at[1 - y], kv_across, ys, 3, near["y"])
        to_y.start()
        for copy in copies(
            [
                (w_query_hbm, w_qkv.at[:, pl.ds(0, head)]),
                (w_key_hbm, w_qkv.at[:, pl.ds(head, head)]),
                (w_value_hbm, w_qkv.at[:, pl.ds(2 * head, head)]),
            ]
        ):
            copy.wait()

        def core_copy(i):
            return remote(part.at[i, pl.ds(HALF, HALF)], from_core.at[i], cs, 2 + i, near["c"])

        def y_copy(h):
            return remote(part.at[h, pl.ds(0, HALF)], from_y.at[h], ys, 1 + h, near["y"])

        def tile(i, carry):
            for dc in range(2):
                rows = d_qkv[pl.ds(tile_row(c, y, i, dc), HALF), :]
                part[i, dc * HALF : (dc + 1) * HALF] = product_t(rows, w_qkv[...])
            core_copy(i).start()
            core_copy(i).wait_recv()
            part[i, :HALF] = part[i, :HALF] + from_core[i]

            @pl.when(i < 2)
            def _():
                y_copy(i).start()

            return carry

        lax.fori_loop(0, 4, tile, 0)


        far((1, 0))
        outer(0, 1)

        def of_branch(context, d_branch, d_middle, tokens):
            waits = copies(
                [
                    (context_hbm, context),
                    (d_branch_hbm, d_branch),
                    (d_middle_hbm, d_middle),
                    (tokens_hbm.at[pl.ds(own_row, QUARTER)], tokens),
                ]
            )
            branch_y.wait_recv()
            branch_fwd.start()
            for copy in waits:
                copy.wait()
            acc = t_product(d_branch[...].astype(bf16), context[quarter_rows(0, 0), :])
            branch_c.wait_recv()
            branch_fwd.wait_recv()
            for k, (dc, dy) in enumerate([(0, 1), (1, 0), (1, 1)]):
                acc = acc + t_product(branch_land[k].astype(bf16), context[quarter_rows(dc, dy), :])
            attn[:, head : 2 * head] = acc
            far((1, 1))
            to_y.wait_recv()
            attn[:, 2 * head :] = kv_halves[y] + kv_across[...]
            for i in range(4):
                attn_z1_copy(i).start()
            far((2, 0), (2, 1))
            outer(1, 0)
            for h in range(2):
                y_copy(h).wait_recv()
                at = slice(h * HALF, (h + 1) * HALF)
                grad = part[2 + h, :HALF] + from_y[h]
                d_in, of_gain = back_norm(tokens[at, :].astype(f32), gain_row(gain_rows, 0), grad)
                gains[0:1, :] = gains[0:1, :] + jnp.sum(of_gain, axis=0, keepdims=True)
                d = (d_middle[at, :] + d_in).astype(bf16)
                input_stage[at, :] = d
                input_own[at, :] = d.astype(f32)

        pl.run_scoped(
            of_branch,
            pltpu.VMEM((length, head), bf16),
            pltpu.VMEM((QUARTER, width), f32),
            pltpu.VMEM((QUARTER, width), f32),
            pltpu.VMEM((QUARTER, width), bf16),
        )
        hop(0)
        arrive(0)
        hop(1)
        input_y.start()
        input_c.start()
        outer(1, 1)
        put_input(0, 0)
        for i in range(4):
            core_copy(i).wait_send()
        for h in range(2):
            y_copy(h).wait_send()
        to_y.wait_send()

    pl.run_scoped(
        rest,
        pltpu.VMEM((width, 3 * head), bf16),
        pltpu.VMEM((4, TILE, width), f32),
        pltpu.VMEM((2, width, head // 2), f32),
    )

    arrive(1)
    hop(2)
    close(0)
    outer(2, 0)
    input_y.wait_recv()
    input_fwd.start()
    input_stage[...] = input_land[0].astype(bf16)
    put_input(0, 1)
    input_c.wait_recv()
    input_stage[...] = input_land[1].astype(bf16)
    put_input(1, 0)
    close(1)
    outer(2, 1)
    for i in range(4):
        attn_z1_copy(i).wait_recv()
        rows = block(attn, (2 * (i // 2) + zl) * 2 + i % 2)
        attn[rows, :] = attn[rows, :] + attn_z1[i]
    for j in (1, 0):
        attn_x_copy(j).start()
    input_fwd.wait_recv()
    input_stage[...] = input_land[2].astype(bf16)
    put_input(1, 1)
    arrive(2)
    hop(3)
    for j in (1, 0):
        attn_x_copy(j).wait_recv()
        rows = block(attn, (2 * (zh ^ j) + zl) * 2 + x)
        attn[rows, :] = attn[rows, :] + attn_x[j]
        if j == 1:
            attn_z2_copy.start()
    close(2)
    finish(0, down_out)
    finish(1, gate_out)
    attn_z2_copy.wait_recv()
    total = attn[block(attn, (2 * zh + zl) * 2 + x), :] + attn_z2[...]
    query_out[...] = total[:, :head]
    out_out[...] = total[:, head : 2 * head]
    kv_own[...] = total[:, 2 * head :]
    wide_y = remote(kv_own, kv_y, ys, 5, near["y"])
    wide_y.start()
    arrive(3)
    hop(4)
    wide_y.wait_recv()
    kv_wide[:, : head // 2] = jnp.where(y == 0, kv_own[...], kv_y[...])
    kv_wide[:, head // 2 :] = jnp.where(y == 0, kv_y[...], kv_own[...])
    wide_c = remote(kv_wide, kv_wide_core, cs, 9, near["c"])
    wide_c.start()
    wide_c.wait_recv()
    key_out[...] = jnp.where(c == 0, kv_wide[...], kv_wide_core[...])
    value_out[...] = jnp.where(c == 0, kv_wide_core[...], kv_wide[...])
    arrive(4)
    finish(2, up_out)
    for m in range(3):
        for j in range(4):
            x_copy(m, j).wait_send()
        for k in range(2):
            z2_copy(m, k).wait_send()
        z1_copy(m).wait_send()
    for i in range(4):
        attn_z1_copy(i).wait_send()
    for j in range(2):
        attn_x_copy(j).wait_send()
    for copy in (attn_z2_copy, branch_y, branch_c, branch_fwd, input_y, input_c, input_fwd, wide_y, wide_c, heads_c_copy, heads_y_copy):
        copy.wait_send()


def reduce_all(nx, dp_size, columns, whole, small):
    length, width = whole[0].shape
    half = whole[4].shape[1]
    head = whole[11].shape[1]
    blk = width // dp_size
    return pl.pallas_call(
        functools.partial(reduce_kernel, nx),
        out_shape=(
            *[jax.ShapeDtypeStruct((blk, columns), f32)] * 3,
            *[jax.ShapeDtypeStruct((blk, head), f32)] * 4,
            jax.ShapeDtypeStruct((length, width), bf16),
            jax.ShapeDtypeStruct((8, width), f32),
        ),
        in_specs=[ANY] * len(whole) + [VMEM] * len(small),
        out_specs=(ANY,) * 3 + (VMEM,) * 4 + (ANY, VMEM),
        scratch_shapes=[
            pltpu.VMEM((QUARTER, width), bf16),
            pltpu.VMEM((blk, columns), f32),
            pltpu.VMEM((3, width, half), f32),
            pltpu.VMEM((12, blk, half), f32),
            pltpu.VMEM((6, blk, half), f32),
            pltpu.VMEM((3, blk, half), f32),
            pltpu.VMEM((4, HALF, width), f32),
            pltpu.VMEM((2, HALF, width), f32),
            pltpu.VMEM((3, QUARTER, width), f32),
            pltpu.VMEM((QUARTER, width), f32),
            pltpu.VMEM((3, QUARTER, width), f32),
            pltpu.VMEM((length, 3 * head), bf16),
            pltpu.VMEM((width, 2 * head + head // 2), f32),
            pltpu.VMEM((4, blk, 2 * head + head // 2), f32),
            pltpu.VMEM((2, blk, 2 * head + head // 2), f32),
            pltpu.VMEM((blk, 2 * head + head // 2), f32),
            pltpu.VMEM((width, head), f32),
            pltpu.VMEM((width, head // 2), f32),
            pltpu.VMEM((blk, head // 2), f32),
            pltpu.VMEM((blk, head // 2), f32),
            pltpu.VMEM((blk, head), f32),
            pltpu.VMEM((blk, head), f32),
            pltpu.VMEM((5, 8, width), f32),
            pltpu.VMEM((QUARTER, head), f32),
            pltpu.VMEM((2, QUARTER, head), f32),
            pltpu.VMEM((2, QUARTER, head), f32),
            pltpu.VMEM((2, QUARTER, head), f32),
        ]
        + dma(8, 12, 12, 8, 8, 15, 15, 8, 8, 8, 8),
        compiler_params=pltpu.CompilerParams(collective_id=2, has_side_effects=True, vmem_limit_bytes=VMEM_LIMIT),
        name="reduce_all",
    )(*whole, *small)


def settle_kernel(*refs):
    count = (len(refs) - 1) // 3
    sems = refs[-1]
    loads, puts = [], []
    for k in range(count):
        given, out, held = refs[k], refs[count + k], refs[2 * count + k]
        loads.append(pltpu.make_async_copy(given, held, sems.at[0, k]))
        puts.append(pltpu.make_async_copy(held, out, sems.at[1, k]))
    for copy in loads:
        copy.start()
    for load, put in zip(loads, puts):
        load.wait()
        put.start()
    for copy in puts:
        copy.wait()


def settle(*arrays):
    return pl.pallas_call(
        settle_kernel,
        out_shape=tuple(jax.ShapeDtypeStruct(a.shape, a.dtype) for a in arrays),
        in_specs=[ANY] * len(arrays),
        out_specs=(ANY,) * len(arrays),
        scratch_shapes=[pltpu.VMEM(a.shape, a.dtype) for a in arrays] + [pltpu.SemaphoreType.DMA((2, len(arrays)))],
        compiler_params=pltpu.CompilerParams(vmem_limit_bytes=VMEM_LIMIT),
        name="settle",
    )(*arrays)


def body(
    links,
    tokens,
    segment_ids,
    cotangent,
    w_query,
    w_key,
    w_value,
    w_out,
    w_gate,
    w_up,
    w_down,
    gain_attn_in,
    gain_attn_out,
    gain_ffn_in,
    gain_ffn_out,
    gain_query,
    gain_key,
):
    length, width = tokens.shape
    head = w_query.shape[1]
    columns = w_gate.shape[1]
    nx = links.nx
    blk = width // links.dp_size
    dp = lax.axis_index("dp")
    wg, wu = w_gate.T, w_up.T
    (
        normed_low,
        query_low,
        keys_low,
        values_low,
        query_raw,
        keys_raw,
        log_total,
        context_low,
        w_out_all,
        middle,
        branch,
        gain_rows,
    ) = attend(
        nx,
        tokens,
        w_query,
        w_key,
        w_value,
        w_out,
        segment_ids,
        gain_attn_in,
        gain_attn_out,
        gain_ffn_in,
        gain_ffn_out,
        gain_query,
        gain_key,
    )
    normed_two, normed_other, d_out, d_own, d_first, layer_out, pair_own, for_gate, for_up, of_ffn_out = feed_forward(
        nx, middle, cotangent, gain_rows, wg, wu, w_down
    )
    d_other, pair_other, pair_gates, heads, d_branch_own, d_middle, of_middle = feed_back(
        nx,
        d_out,
        d_own,
        d_first,
        for_gate,
        for_up,
        normed_other,
        wg,
        wu,
        w_down,
        w_out_all,
        middle,
        branch.reshape(QUARTER, width),
        cotangent,
        gain_rows,
    )
    *sums, gains = reduce_all(
        nx,
        links.dp_size,
        columns,
        [
            d_out,
            d_other,
            normed_two,
            normed_other,
            pair_own,
            pair_other,
            pair_gates,
            d_branch_own,
            d_middle,
            tokens,
            normed_low,
            query_low,
            keys_low,
            values_low,
            query_raw,
            keys_raw,
            context_low,
            heads,
            w_query,
            w_key,
            w_value,
        ],
        [log_total, segment_ids.reshape(1, length), gain_rows, of_ffn_out, of_middle],
    )
    layer_out, down_t, gate, up, query, out_t, key, value, input_grad = settle(layer_out, *sums)
    part = lax.dynamic_slice_in_dim(gains, dp * blk, blk, 1)
    hb = head // links.dp_size
    head_part = lax.dynamic_slice_in_dim(gains, dp * hb, hb, 1)
    return (
        layer_out,
        input_grad,
        query,
        key,
        value,
        out_t.T,
        gate,
        up,
        down_t.T,
        part[0],
        part[1],
        part[2],
        part[3],
        head_part[4],
        head_part[5],
    )


def body_any(
    links,
    tokens,
    segment_ids,
    cotangent,
    w_query,
    w_key,
    w_value,
    w_out,
    w_gate,
    w_up,
    w_down,
    gain_attn_in,
    gain_attn_out,
    gain_ffn_in,
    gain_ffn_out,
    gain_query,
    gain_key,
):
    length, width = tokens.shape
    head = w_query.shape[1]
    quarter = length // 4
    half_ff = w_gate.shape[1] // 2
    nx = links.nx
    blk = width // links.dp_size
    dp, t = lax.axis_index("dp"), lax.axis_index("tensor")
    z, x = dp // nx, dp % nx
    y, c = t // 2, t % 2
    parity = z % 2
    one = jnp.where(segment_ids[0] < length, 1.0, 0.5).astype(f32)

    def keep_low(a):
        return (a * one).astype(bf16)

    def place(dc, dy):
        return ((c ^ dc) * 2 + (y ^ dy)) * quarter

    def rows(a, dc, dy):
        return lax.dynamic_slice_in_dim(a, place(dc, dy), quarter, 0)

    def to_absolute(pieces):
        stack = jnp.stack([pieces[0][0], pieces[0][1], pieces[1][0], pieces[1][1]])
        mine = c * 2 + y
        return jnp.concatenate([lax.dynamic_index_in_dim(stack, mine ^ b, 0, keepdims=False) for b in range(4)], axis=0)

    out_own = w_out.astype(f32)
    out_y = links.y(out_own)
    out_c = links.core(out_own)
    out_yc = links.core(out_y)
    w_out_all = jnp.concatenate([w_out, keep_low(out_c), keep_low(out_y), keep_low(out_yc)], axis=0)

    wg_h = jnp.where(parity == 0, w_gate[:, :half_ff], w_gate[:, half_ff:])
    wu_h = jnp.where(parity == 0, w_up[:, :half_ff], w_up[:, half_ff:])
    wd_h = jnp.where(parity == 0, w_down[:half_ff], w_down[half_ff:])

    hidden_in = tokens.astype(f32)
    normed_low = low(rms_norm(hidden_in, gain_attn_in))
    query_raw = product(normed_low, w_query)
    keys_raw = product(normed_low, w_key)
    query_low = low(rms_norm(query_raw, gain_query))
    keys_low = low(rms_norm(keys_raw, gain_key))
    values_low = low(product(normed_low, w_value))
    places = jnp.arange(length)
    allowed = (places[:, None] >= places[None, :]) & (segment_ids[:, None] == segment_ids[None, :])

    def scores_of():
        raw = product_t(query_low, keys_low) * score_scale
        return jnp.where(allowed, raw, -1e30)

    scores = scores_of()
    largest = jnp.max(scores, axis=-1, keepdims=True)
    exponent = jnp.exp(scores - largest)
    total = jnp.sum(exponent, axis=-1, keepdims=True)
    log_total = largest + jnp.log(total)
    context_low = low(product(low(exponent / total), values_low))

    context = context_low.astype(f32)
    mine = jnp.concatenate([rows(context, 0, 1), rows(context, 0, 0)], axis=0)
    of_core = links.core(jnp.concatenate([rows(context, 1, 1), rows(context, 1, 0)], axis=0))
    of_y = links.y(jnp.concatenate([rows(context, 0, 0), rows(context, 0, 1)], axis=0))
    of_yc = links.y(jnp.concatenate([of_core[quarter:], of_core[:quarter]], axis=0))
    context_all = jnp.concatenate([low(mine), keep_low(of_core), keep_low(of_y), keep_low(of_yc)], axis=1)
    branch = product(context_all, w_out_all)
    hidden_rows = jnp.concatenate([rows(tokens, 0, 1), rows(tokens, 0, 0)], axis=0).astype(f32)
    middle_own = hidden_rows + rms_norm(branch, gain_attn_out)
    middle_core = links.core(middle_own)

    middles, normed_two, inners, parts = [], [], [], []
    saved = []
    for k in range(2):
        at = slice(k * quarter, (k + 1) * quarter)
        middle = jnp.concatenate([middle_own[at], middle_core[at]], axis=0)
        normed_k = low(rms_norm(middle, gain_ffn_in))
        gate, upward = product(normed_k, w_gate), product(normed_k, w_up)
        inner = low(activate(gate, upward))
        part = product(inner, w_down)
        middles.append(middle)
        normed_two.append(normed_k)
        saved.append((gate, upward))
        parts.append(part)
    normed_own = low(rms_norm(middle_own, gain_ffn_in)).astype(f32)
    other_own = links.z1(normed_own)
    other_core = links.core(other_own)
    normed_other = jnp.concatenate([keep_low(other_own), keep_low(other_core)], axis=0)

    def gather_quarters(parts):
        sums = [part[:quarter] + links.core(part[quarter:]) for part in parts]
        return sums[1] + links.y(sums[0])

    output_q = gather_quarters(parts)
    output_y = links.y(output_q)
    output_c = links.core(output_q)
    output_yc = links.core(output_y)
    outputs = [jnp.concatenate([output_y, output_yc], axis=0), jnp.concatenate([output_q, output_c], axis=0)]
    grad_out = cotangent.astype(f32)
    d_outputs, layer_pieces, grad_ffn_out = [], [], 0.0
    for k in range(2):
        dy_k = jnp.concatenate([rows(cotangent, 0, 1 - k), rows(cotangent, 1, 1 - k)], axis=0).astype(f32)
        layer_k = low(middles[k] + rms_norm(outputs[k], gain_ffn_out))
        d_k, gain_k = rms_back(outputs[k], gain_ffn_out, dy_k)
        grad_ffn_out = grad_ffn_out + gain_k
        d_outputs.append(low(d_k))
        layer_pieces.append(layer_k)
    layer_out = to_absolute(
        [
            [layer_pieces[1][:quarter], layer_pieces[0][:quarter]],
            [layer_pieces[1][quarter:], layer_pieces[0][quarter:]],
        ]
    )

    d_own_rows = [d[:quarter].astype(f32) for d in d_outputs]
    got_own = [links.z1(d_own_rows[1]), links.z1(d_own_rows[0])]
    got_core = [links.core(g) for g in got_own]
    d_other = jnp.concatenate(
        [keep_low(got_own[1]), keep_low(got_own[0]), keep_low(got_core[1]), keep_low(got_core[0])], axis=0
    )

    back_parts = []
    for k in range(2):
        gate, upward = saved[k]
        d_inner = product_t(d_outputs[k], w_down)
        _, pull = jax.vjp(activate, gate, upward)
        d_gate, d_up = pull(d_inner)
        back_parts.append(product_t(low(d_gate), w_gate) + product_t(low(d_up), w_up))
    d_normed_q = gather_quarters(back_parts)
    middle_q = middle_own[quarter:]
    branch_q = branch[quarter:]
    dy_q = rows(cotangent, 0, 0).astype(f32)
    d_mid, grad_ffn_in = rms_back(middle_q, gain_ffn_in, d_normed_q)
    d_middle = dy_q + d_mid
    d_branch, grad_attn_out = rms_back(branch_q, gain_attn_out, d_middle)
    d_branch_low = low(d_branch)
    d_context = low(product_t(d_branch_low, w_out_all)).astype(f32)
    heads = [d_context[:, i * head : (i + 1) * head] for i in range(4)]
    c_got = links.core(jnp.concatenate([heads[1], heads[3]], axis=1))
    y_got = links.y(jnp.concatenate([heads[2], c_got[:, head:]], axis=1))
    grad_context = keep_low(
        to_absolute([[heads[0], y_got[:, :head]], [c_got[:, :head], y_got[:, head:]]])
    )
    d_branch_own = d_branch_low.astype(f32)
    d_branch_y = links.y(d_branch_own)
    d_branch_c = links.core(d_branch_own)
    d_branch_yc = links.core(d_branch_y)
    d_branch_all = jnp.concatenate(
        [d_branch_low, keep_low(d_branch_y), keep_low(d_branch_c), keep_low(d_branch_yc)], axis=0
    )
    context_rel = jnp.concatenate(
        [rows(context_low, 0, 0), rows(context_low, 0, 1), rows(context_low, 1, 0), rows(context_low, 1, 1)], axis=0
    )
    grad_w_out_t = t_product(d_branch_all, context_rel)

    attn_prob = jnp.exp(scores_of() - log_total)
    prob_low = low(attn_prob)
    grad_prob = product_t(grad_context, values_low)
    grad_values = low(t_product(prob_low, grad_context))
    balance = jnp.sum(grad_prob * attn_prob, axis=-1, keepdims=True)
    grad_scores = low(attn_prob * (grad_prob - balance))
    grad_query_n = product(grad_scores, keys_low) * score_scale
    grad_keys_n = t_product(grad_scores, query_low) * score_scale
    d_query, grad_gain_query = rms_back(query_raw, gain_query, grad_query_n)
    d_keys, grad_gain_key = rms_back(keys_raw, gain_key, grad_keys_n)
    d_query, d_keys = low(d_query), low(d_keys)
    d_qkv = jnp.concatenate([d_query, d_keys, grad_values], axis=1)
    w_qkv = jnp.concatenate([w_query, w_key, w_value], axis=1)
    in_parts = []
    for k in range(2):
        rows_k = jnp.concatenate([rows(d_qkv, 0, 1 - k), rows(d_qkv, 1, 1 - k)], axis=0)
        in_parts.append(product_t(rows_k, w_qkv))
    d_normed_in = gather_quarters(in_parts)
    hidden_q = rows(tokens, 0, 0).astype(f32)
    d_in, grad_attn_in = rms_back(hidden_q, gain_attn_in, d_normed_in)
    input_q = low(d_middle + d_in)
    input_own = input_q.astype(f32)
    input_y = links.y(input_own)
    input_c = links.core(input_own)
    input_yc = links.core(input_y)
    input_grad = keep_low(to_absolute([[input_own, input_y], [input_c, input_yc]]))

    grad_qkv = t_product(normed_low, d_qkv)
    grad_w_query, grad_kv = grad_qkv[:, :head], grad_qkv[:, head:]
    kv_keep = jnp.where(c == 0, grad_kv[:, :head], grad_kv[:, head:])
    kv_send = jnp.where(c == 0, grad_kv[:, head:], grad_kv[:, :head])
    kv = kv_keep + links.core(kv_send)
    kv_half = head // 2
    kv_keep = jnp.where(y == 0, kv[:, :kv_half], kv[:, kv_half:])
    kv_send = jnp.where(y == 0, kv[:, kv_half:], kv[:, :kv_half])
    kv = kv_keep + links.y(kv_send)
    attn_grads = jnp.concatenate([grad_w_query, grad_w_out_t, kv], axis=1)

    normed_all = jnp.concatenate(
        [normed_two[0][:quarter], normed_two[1][:quarter], normed_two[0][quarter:], normed_two[1][quarter:], normed_other],
        axis=0,
    )
    d_all = jnp.concatenate(
        [d_outputs[0][:quarter], d_outputs[1][:quarter], d_outputs[0][quarter:], d_outputs[1][quarter:], d_other], axis=0
    )
    gate, upward = product(normed_all, wg_h), product(normed_all, wu_h)
    inner, pull = jax.vjp(activate, gate, upward)
    inner = low(inner)
    d_inner = product_t(d_all, wd_h)
    d_gate, d_up = pull(d_inner)
    ff_grads = [t_product(d_all, inner), t_product(normed_all, low(d_gate)), t_product(normed_all, low(d_up))]

    zh, zl = z // 2, z % 2

    def sum_x(grads, z_half):
        mine = lax.dynamic_index_in_dim(grads, z_half, 0, keepdims=False)
        acc = lax.dynamic_index_in_dim(mine, x, 1, keepdims=False)
        for step in range(1, nx):
            to = lax.dynamic_index_in_dim(mine, (x + step) % nx, 1, keepdims=False)
            acc = acc + links.x(to, step)
        return acc

    def scatter(grads):
        grads = grads.reshape(2, 2, nx, blk, grads.shape[1])
        far = sum_x(grads, 1 - zh)
        near = sum_x(grads, zh)
        return near + links.z2(far)

    ff_sums = []
    for grads in ff_grads:
        got = scatter(grads)
        own = lax.dynamic_index_in_dim(got, zl, 0, keepdims=False)
        other = links.z1(lax.dynamic_index_in_dim(got, 1 - zl, 0, keepdims=False))
        ff_sums.append(
            jnp.where(
                parity == 0, jnp.concatenate([own, other], axis=1), jnp.concatenate([other, own], axis=1)
            )
        )
    grad_w_down, grad_w_gate, grad_w_up = ff_sums[0].T, ff_sums[1], ff_sums[2]

    got = scatter(attn_grads)
    attn_sum = lax.dynamic_index_in_dim(got, zl, 0, keepdims=False) + links.z1(
        lax.dynamic_index_in_dim(got, 1 - zl, 0, keepdims=False)
    )
    grad_w_query = attn_sum[:, :head]
    grad_w_out = attn_sum[:, head : 2 * head].T
    kv_own = attn_sum[:, 2 * head :]
    kv_y = links.y(kv_own)
    kv_wide = jnp.where(y == 0, jnp.concatenate([kv_own, kv_y], axis=1), jnp.concatenate([kv_y, kv_own], axis=1))
    kv_c = links.core(kv_wide)
    grad_w_key = jnp.where(c == 0, kv_wide, kv_c)
    grad_w_value = jnp.where(c == 0, kv_c, kv_wide)

    small = jnp.concatenate(
        [
            grad_attn_in.reshape(links.dp_size, -1),
            grad_attn_out.reshape(links.dp_size, -1),
            grad_ffn_in.reshape(links.dp_size, -1),
            (grad_ffn_out * 0.25).reshape(links.dp_size, -1),
            grad_gain_query.reshape(links.dp_size, -1),
            grad_gain_key.reshape(links.dp_size, -1),
        ],
        axis=1,
    )
    small = small + links.core(small)
    small = small + links.y(small)
    small = small.reshape(2, 2, nx, 1, small.shape[1])
    acc = lax.dynamic_index_in_dim(small, x, 2, keepdims=False)
    for step in range(1, nx):
        acc = acc + links.x(lax.dynamic_index_in_dim(small, (x + step) % nx, 2, keepdims=False), step)
    acc = lax.dynamic_index_in_dim(acc, zh, 0, keepdims=False) + links.z2(
        lax.dynamic_index_in_dim(acc, 1 - zh, 0, keepdims=False)
    )
    acc = lax.dynamic_index_in_dim(acc, zl, 0, keepdims=False) + links.z1(
        lax.dynamic_index_in_dim(acc, 1 - zl, 0, keepdims=False)
    )
    acc = acc.reshape(-1)
    hb = head // links.dp_size
    return (
        layer_out,
        input_grad,
        grad_w_query,
        grad_w_key,
        grad_w_value,
        grad_w_out,
        grad_w_gate,
        grad_w_up,
        grad_w_down,
        acc[:blk],
        acc[blk : 2 * blk],
        acc[2 * blk : 3 * blk],
        acc[3 * blk : 4 * blk],
        acc[4 * blk : 4 * blk + hb],
        acc[4 * blk + hb :],
    )


def solution(mesh):
    links = Links(mesh)
    return jax.shard_map(
        functools.partial(body if links.nx == 2 else body_any, links),
        mesh=mesh,
        in_specs=(
            P("dp", None),
            P("dp"),
            P("dp", None),
            P(None, "tensor"),
            P(),
            P(),
            P("tensor", None),
            P(None, "tensor"),
            P(None, "tensor"),
            P("tensor", None),
            P(),
            P(),
            P(),
            P(),
            P(),
            P(),
        ),
        out_specs=(
            P("dp", None),
            P("dp", None),
            P("dp", "tensor"),
            P("dp", None),
            P("dp", None),
            P("tensor", "dp"),
            P("dp", "tensor"),
            P("dp", "tensor"),
            P("tensor", "dp"),
            P("dp"),
            P("dp"),
            P("dp"),
            P("dp"),
            P("dp"),
            P("dp"),
        ),
        check_vma=False,
    )
```

```python
import functools

import jax
import jax.numpy as jnp
from jax import lax
from jax.experimental import pallas as pl
from jax.experimental.pallas import tpu as pltpu
from jax.sharding import PartitionSpec as P

epsilon = 1e-06
score_scale = 0.0625
NZ = 4

f32 = jnp.float32
bf16 = jnp.bfloat16


def rms_norm(values, gain):
    inverse = lax.rsqrt(jnp.mean(values * values, axis=-1, keepdims=True) + epsilon)
    return values * inverse * (1.0 + gain)


def rms_back(values, gain, grad):
    inverse = lax.rsqrt(jnp.mean(values * values, axis=-1, keepdims=True) + epsilon)
    hat = values * inverse
    scaled = grad * (1.0 + gain)
    back = inverse * (scaled - hat * jnp.mean(scaled * hat, axis=-1, keepdims=True))
    return back, jnp.sum(grad * hat, axis=0)


def product(left, right):
    return jnp.dot(left, right, preferred_element_type=f32)


def product_t(left, right):
    return lax.dot_general(left, right, (((1,), (1,)), ((), ())), preferred_element_type=f32)


def t_product(left, right):
    return lax.dot_general(left, right, (((0,), (0,)), ((), ())), preferred_element_type=f32)


def activate(gate, upward):
    return jax.nn.gelu(gate, approximate=True) * upward


class Links:
    def __init__(self, mesh):
        self.dp_size = mesh.shape["dp"]
        self.nx = self.dp_size // NZ
        tensor = mesh.shape["tensor"]
        self.perm_core = [(t, t ^ 1) for t in range(tensor)]
        self.perm_y = [(t, t ^ 2) for t in range(tensor)]
        nx = self.nx
        self.perm_z1 = [(z * nx + x, (z ^ 1) * nx + x) for z in range(NZ) for x in range(nx)]
        self.perm_z2 = [(z * nx + x, (z ^ 2) * nx + x) for z in range(NZ) for x in range(nx)]

    def core(self, a):
        return lax.ppermute(a, "tensor", self.perm_core)

    def y(self, a):
        return lax.ppermute(a, "tensor", self.perm_y)

    def z1(self, a):
        return lax.ppermute(a, "dp", self.perm_z1)

    def z2(self, a):
        return lax.ppermute(a, "dp", self.perm_z2)

    def x(self, a, step):
        nx = self.nx
        return lax.ppermute(a, "dp", [(z * nx + x, z * nx + (x + step) % nx) for z in range(NZ) for x in range(nx)])


def low(a):
    return a.astype(bf16)


MESH = pl.DeviceIdType.MESH
ANY = pl.BlockSpec(memory_space=pl.ANY)
VMEM = pl.BlockSpec(memory_space=pltpu.VMEM)
TILE, HALF, QUARTER = 256, 128, 256
VMEM_LIMIT = 127 << 19


def spots(nx):
    dp, t = lax.axis_index("dp"), lax.axis_index("tensor")
    z, x = dp // nx, dp % nx
    near = {
        "c": {"tensor": t ^ 1},
        "y": {"tensor": t ^ 2},
        "z1": {"dp": (z ^ 1) * nx + x},
        "z2": {"dp": (z ^ 2) * nx + x},
        "x": {"dp": z * nx + (x ^ 1)},
    }
    return z, x, t // 2, t % 2, near


def remote(src, dst, sems, index, to):
    return pltpu.make_async_remote_copy(
        src_ref=src, dst_ref=dst, send_sem=sems[0].at[index], recv_sem=sems[1].at[index], device_id=to, device_id_type=MESH
    )


def greet(others):
    barrier = pltpu.get_barrier_semaphore()
    for other in others:
        pl.semaphore_signal(barrier, inc=1, device_id=other, device_id_type=MESH)
    pl.semaphore_wait(barrier, len(others))


def tile_row(c, y, i, dc):
    dy = 1 - i // 2
    return pl.multiple_of(((c ^ dc) * 2 + (y ^ dy)) * QUARTER + (i % 2) * HALF, HALF)


def gelu_parts(u):
    k = 0.7978845608028654
    square = u * u
    th = jnp.tanh(k * u * (1.0 + 0.044715 * square))
    side = 0.5 * (1.0 + th)
    return u * side, side + 0.5 * u * (1.0 - th * th) * (k * (1.0 + 3.0 * 0.044715 * square))


def gelu_tanh(u):
    return 0.5 * u * (1.0 + jnp.tanh(0.7978845608028654 * u * (1.0 + 0.044715 * (u * u))))


def gain_row(gains, k):
    return gains[k : k + 1, :]


def forward_kernel(
    nx,
    middle_hbm,
    cotangent,
    gains,
    w_gate_hbm,
    w_up_hbm,
    w_down_hbm,
    normed_hbm,
    other_hbm,
    d_out_hbm,
    d_own_hbm,
    d_first,
    layer_hbm,
    pair_own_hbm,
    for_gate_hbm,
    for_up_hbm,
    gain_grad,
    middle,
    w_gate,
    w_up,
    w_down,
    normed,
    other,
    d_out,
    d_own,
    layer_out,
    out,
    dy,
    inner,
    for_gate,
    for_up,
    part,
    from_core,
    from_y,
    z_stage,
    z_land,
    c_land,
    local,
    stores,
    tile_stores,
    c_send,
    c_recv,
    y_send,
    y_recv,
    z_send,
    z_recv,
):
    z, x, y, c, near = spots(nx)
    core, across, pair = near["c"], near["y"], near["z1"]
    cs, ys, zs = (c_send, c_recv), (y_send, y_recv), (z_send, z_recv)
    first = [
        pltpu.make_async_copy(src, dst, local.at[8 + k])
        for k, (src, dst) in enumerate(
            [(middle_hbm, middle), (w_gate_hbm, w_gate), (w_up_hbm, w_up), (w_down_hbm, w_down)]
        )
    ]
    for copy in first:
        copy.start()
    loads = []
    for i in range(4):
        for dc in range(2):
            copy = pltpu.make_async_copy(
                cotangent.at[pl.ds(tile_row(c, y, i, dc), HALF)],
                dy.at[pl.ds(i * TILE + dc * HALF, HALF)],
                local.at[i * 2 + dc],
            )
            copy.start()
            loads.append(copy)
    greet([core, across, pair])
    columns = w_gate.shape[0]
    cut = pl.cdiv(columns, TILE) * HALF
    for ref in (inner, for_gate, for_up):
        for slot in range(2):
            ref[slot, :, columns:] = jnp.zeros((TILE, 2 * cut - columns), bf16)

    def tile_puts(i):
        slot = i % 2
        at = pl.ds(pl.multiple_of(i * TILE, TILE), TILE)
        mine = pl.ds(pl.multiple_of(z % 2 * cut, HALF), cut)
        return [
            pltpu.make_async_copy(inner.at[slot, :, mine], pair_own_hbm.at[at], tile_stores.at[slot, 0]),
            pltpu.make_async_copy(for_gate.at[slot], for_gate_hbm.at[at], tile_stores.at[slot, 1]),
            pltpu.make_async_copy(for_up.at[slot], for_up_hbm.at[at], tile_stores.at[slot, 2]),
        ]

    def core_copy(i):
        return remote(part.at[i, pl.ds(HALF, HALF)], from_core.at[i], cs, i, core)

    def y_copy(h):
        return remote(part.at[h, pl.ds(0, HALF)], from_y.at[h], ys, h, across)

    def z_copy(i):
        return remote(z_stage.at[i], z_land.at[i], zs, i, pair)

    first_copy = remote(d_own.at[2], d_first, zs, 4, pair)

    def z_forward(i):
        return remote(z_land.at[i], c_land.at[i], cs, 8 + i, core)

    def norm_tile(i, carry):
        at = pl.ds(pl.multiple_of(i * TILE, TILE), TILE)
        m = middle[at, :]
        inverse = lax.rsqrt(jnp.mean(m * m, axis=-1, keepdims=True) + epsilon)
        n = (m * inverse * (1.0 + gain_row(gains, 2))).astype(bf16)
        normed[at, :] = n
        z_stage[i] = n[:HALF].astype(f32)
        z_copy(i).start()
        return carry

    first[0].wait()
    lax.fori_loop(0, 4, norm_tile, 0)
    for copy in first[1:]:
        copy.wait()

    def step(i, carry):
        at = pl.ds(pl.multiple_of(i * TILE, TILE), TILE)
        n = normed[at, :]
        slot = i % 2

        @pl.when(i >= 2)
        def _():
            for copy in tile_puts(i - 2):
                copy.wait()

        for lo in range(0, columns, TILE):
            hi = min(lo + TILE, columns)
            g = product_t(n, w_gate[lo:hi, :])
            u = product_t(n, w_up[lo:hi, :])
            act, slope = gelu_parts(g)
            inner[slot, :, lo:hi] = (act * u).astype(bf16)
            for_gate[slot, :, lo:hi] = (u * slope).astype(bf16)
            for_up[slot, :, lo:hi] = act.astype(bf16)
        part[i] = product(inner[slot, :, :columns], w_down[...])
        for copy in tile_puts(i):
            copy.start()
        core_copy(i).start()
        core_copy(i).wait_recv()
        part[i, :HALF] = part[i, :HALF] + from_core[i]

        @pl.when(i < 2)
        def _():
            y_copy(i).start()

        return carry

    lax.fori_loop(0, 4, step, 0)

    def tile_at(i):
        return pl.ds(pl.multiple_of(i * TILE, TILE), TILE)

    put_normed = pltpu.make_async_copy(normed, normed_hbm, stores.at[8])
    put_layer = pltpu.make_async_copy(layer_out, layer_hbm, stores.at[9])

    def put_own(i):
        return pltpu.make_async_copy(d_own.at[i], d_own_hbm.at[i], stores.at[i])

    def put_d(i):
        return pltpu.make_async_copy(d_out.at[tile_at(i)], d_out_hbm.at[tile_at(i)], stores.at[4 + i])

    def put_other(i):
        return pltpu.make_async_copy(other.at[tile_at(i)], other_hbm.at[tile_at(i)], stores.at[10 + i])

    put_normed.start()
    for i in (2, 3):
        for copy in tile_puts(i):
            copy.wait()
    for copy in loads:
        copy.wait()
    gain_grad[...] = jnp.zeros_like(gain_grad)
    gain = 1.0 + gain_row(gains, 3)

    def finish(i, dc):
        at = pl.ds(pl.multiple_of(i * TILE + dc * HALF, HALF), HALF)
        o, g = out[at, :], dy[at, :].astype(f32)
        inverse = lax.rsqrt(jnp.mean(o * o, axis=-1, keepdims=True) + epsilon)
        hat = o * inverse
        scaled = g * gain
        d = (inverse * (scaled - hat * jnp.mean(scaled * hat, axis=-1, keepdims=True))).astype(bf16)
        d_out[at, :] = d
        gain_grad[...] = gain_grad[...] + jnp.sum((g * hat).reshape(HALF // 8, 8, g.shape[1]), axis=0)
        layer_out[pl.ds(tile_row(c, y, i, dc), HALF), :] = (middle[at, :] + hat * gain).astype(bf16)
        return d

    def half_at(i, dc):
        return pl.ds(pl.multiple_of(i * TILE + dc * HALF, HALF), HALF)

    def spread_y(h):
        return remote(out.at[half_at(2 + h, 0)], out.at[half_at(h, 0)], ys, 2 + h, across)

    def spread_core(i):
        return remote(out.at[half_at(i, 0)], out.at[half_at(i, 1)], cs, 4 + i, core)

    def close_tile(n, carry):
        i = (n + 2) % 4

        @pl.when(n < 2)
        def _():
            y_copy(n).wait_recv()
            out[half_at(i, 0), :] = part[i, :HALF] + from_y[n]
            spread_y(n).start()

        @pl.when(n == 2)
        def _():
            for i in range(3):
                z_copy(i).wait_recv()
                z_forward(i).start()
            for i in range(2):
                take(i)

        @pl.when(n >= 2)
        def _():
            spread_y(i).wait_recv()

        spread_core(i).start()
        d_own[i] = finish(i, 0).astype(f32)

        @pl.when(n == 0)
        def _():
            first_copy.start()

        put_own(i).start()
        spread_core(i).wait_recv()
        finish(i, 1)
        put_d(i).start()
        return carry

    def take(i):
        z_forward(i).wait_recv()
        other[i * TILE : i * TILE + HALF, :] = z_land[i].astype(bf16)
        other[i * TILE + HALF : (i + 1) * TILE, :] = c_land[i].astype(bf16)
        put_other(i).start()

    lax.fori_loop(0, 4, close_tile, 0)
    put_layer.start()
    z_copy(3).wait_recv()
    z_forward(3).start()
    for i in range(2, 4):
        take(i)
    for i in range(4):
        core_copy(i).wait_send()
        z_copy(i).wait_send()
        z_forward(i).wait_send()
        spread_core(i).wait_send()
        put_own(i).wait()
        put_d(i).wait()
        put_other(i).wait()
    for h in range(2):
        y_copy(h).wait_send()
        spread_y(h).wait_send()
    put_normed.wait()
    put_layer.wait()
    first_copy.wait()


def dma(*counts):
    return [pltpu.SemaphoreType.DMA((n,)) for n in counts]


def feed_forward(nx, middle, cotangent, gains, w_gate, w_up, w_down):
    length, width = middle.shape
    columns = pl.cdiv(w_gate.shape[0], TILE) * TILE
    rows_low = jax.ShapeDtypeStruct((length, width), bf16)
    return pl.pallas_call(
        functools.partial(forward_kernel, nx),
        out_shape=(
            rows_low,
            rows_low,
            rows_low,
            jax.ShapeDtypeStruct((4, HALF, width), f32),
            jax.ShapeDtypeStruct((HALF, width), f32),
            rows_low,
            jax.ShapeDtypeStruct((length, columns // 2), bf16),
            jax.ShapeDtypeStruct((length, columns), bf16),
            jax.ShapeDtypeStruct((length, columns), bf16),
            jax.ShapeDtypeStruct((8, width), f32),
        ),
        in_specs=[ANY, ANY, VMEM] + [ANY] * 3,
        out_specs=(ANY,) * 4 + (VMEM, ANY, ANY, ANY, ANY, VMEM),
        scratch_shapes=[pltpu.VMEM((length, width), f32)]
        + [pltpu.VMEM(w_gate.shape, bf16)] * 3
        + [pltpu.VMEM((length, width), bf16)] * 3
        + [
            pltpu.VMEM((4, HALF, width), f32),
            pltpu.VMEM((length, width), bf16),
            pltpu.VMEM((length, width), f32),
            pltpu.VMEM((length, width), bf16),
            pltpu.VMEM((2, TILE, columns), bf16),
            pltpu.VMEM((2, TILE, columns), bf16),
            pltpu.VMEM((2, TILE, columns), bf16),
            pltpu.VMEM((4, TILE, width), f32),
            pltpu.VMEM((4, HALF, width), f32),
            pltpu.VMEM((2, HALF, width), f32),
            pltpu.VMEM((4, HALF, width), f32),
            pltpu.VMEM((4, HALF, width), f32),
            pltpu.VMEM((4, HALF, width), f32),
        ]
        + dma(12, 14)
        + [pltpu.SemaphoreType.DMA((2, 3))]
        + dma(12, 12, 4, 4, 5, 5),
        compiler_params=pltpu.CompilerParams(collective_id=0, has_side_effects=True, vmem_limit_bytes=VMEM_LIMIT),
        name="feed_forward",
    )(middle, cotangent, gains, w_gate, w_up, w_down)


def back_kernel(
    nx,
    d_out_hbm,
    d_own_hbm,
    d_first_hbm,
    for_gate_hbm,
    for_up_hbm,
    other_hbm,
    w_gate_hbm,
    w_up_hbm,
    w_down_hbm,
    w_out_hbm,
    middle_hbm,
    branch_hbm,
    dy_hbm,
    gains,
    d_other,
    pair_in,
    pair_gates,
    heads,
    d_branch_out,
    d_middle_out,
    gain_grads,
    d_out,
    for_gate,
    for_up,
    other,
    w_gate,
    w_up,
    w_down,
    w_out,
    middle,
    branch,
    dy,
    gates,
    ups,
    inner,
    part,
    from_core,
    from_y,
    z_land,
    c_land,
    loads_sem,
    tiles_sem,
    stores_sem,
    c_send,
    c_recv,
    y_send,
    y_recv,
    z_send,
    z_recv,
):
    z, x, y, c, near = spots(nx)
    core, across, pair = near["c"], near["y"], near["z1"]
    cs, ys, zs = (c_send, c_recv), (y_send, y_recv), (z_send, z_recv)
    parity = z % 2
    real, columns = w_gate_hbm.shape[0], w_gate.shape[0]
    half = columns // 2
    head = heads.shape[2]
    own_row = pl.multiple_of((c * 2 + y) * QUARTER, QUARTER)
    sources = [
        (d_out_hbm, d_out),
        (w_gate_hbm, w_gate.at[pl.ds(0, real)]),
        (w_up_hbm, w_up.at[pl.ds(0, real)]),
        (w_down_hbm, w_down.at[pl.ds(0, real)]),
        (other_hbm, other),
        (w_out_hbm, w_out),
        (middle_hbm.at[pl.ds(2 * TILE, HALF)], middle.at[pl.ds(0, HALF)]),
        (middle_hbm.at[pl.ds(3 * TILE, HALF)], middle.at[pl.ds(HALF, HALF)]),
        (branch_hbm, branch),
        (dy_hbm.at[pl.ds(own_row, QUARTER)], dy),
        (d_first_hbm, z_land.at[2]),
    ]
    loads = [pltpu.make_async_copy(src, dst, loads_sem.at[k]) for k, (src, dst) in enumerate(sources)]
    for copy in loads:
        copy.start()
    if real < columns:
        for ref in (w_gate, w_up, w_down):
            ref[real:, :] = jnp.zeros((columns - real, ref.shape[1]), bf16)
    greet([core, across, pair])

    def core_copy(i):
        return remote(part.at[i, pl.ds(HALF, HALF)], from_core.at[i], cs, i, core)

    def y_copy(h):
        return remote(part.at[h, pl.ds(0, HALF)], from_y.at[h], ys, h, across)

    def z_copy(i):
        return remote(d_own_hbm.at[i], z_land.at[i], zs, i, pair)

    def z_forward(i):
        return remote(z_land.at[i], c_land.at[i], cs, 4 + i, core)

    for i in (3, 0, 1):
        z_copy(i).start()
    def tile_loads(i):
        slot = i % 2
        at = pl.ds(pl.multiple_of(i * TILE, TILE), TILE)
        return [
            pltpu.make_async_copy(for_gate_hbm.at[at], for_gate.at[slot], tiles_sem.at[slot, 0]),
            pltpu.make_async_copy(for_up_hbm.at[at], for_up.at[slot], tiles_sem.at[slot, 1]),
        ]

    for i in range(2):
        for copy in tile_loads(i):
            copy.start()
    for copy in loads[:4]:
        copy.wait()

    mine = pl.multiple_of(parity * half, HALF)

    def stores(i, base):
        slot = i % 2
        at = pl.ds(pl.multiple_of(base + i * TILE, TILE), TILE)
        pick = pl.ds(mine, half)
        first = []
        if base:
            first = [
                pltpu.make_async_copy(
                    inner.at[slot], pair_in.at[pl.ds(pl.multiple_of(i * TILE, TILE), TILE)], stores_sem.at[slot, 0]
                )
            ]
        return first + [
            pltpu.make_async_copy(gates.at[slot, :, pick], pair_gates.at[at, pl.ds(0, half)], stores_sem.at[slot, 1]),
            pltpu.make_async_copy(ups.at[slot, :, pick], pair_gates.at[at, pl.ds(half, half)], stores_sem.at[slot, 2]),
        ]

    def piece(n, d, slot, at, own):
        g = product_t(n, w_gate[at, :])
        u = product_t(n, w_up[at, :])
        di = product_t(d, w_down[at, :])
        act, slope = gelu_parts(g)
        inner[slot, :, own] = (act * u).astype(bf16)
        gates[slot, :, at] = (di * u * slope).astype(bf16)
        ups[slot, :, at] = (di * act).astype(bf16)

    def own_tile(i, carry):
        at = pl.ds(pl.multiple_of(i * TILE, TILE), TILE)
        slot = i % 2

        @pl.when(i >= 2)
        def _():
            for copy in stores(i - 2, 0):
                copy.wait()

        for copy in tile_loads(i):
            copy.wait()
        d = d_out[at, :]
        for lo in range(0, columns, TILE):
            cols = pl.ds(lo, TILE)
            di = product_t(d, w_down[cols, :])
            gates[slot, :, cols] = (di * for_gate[slot, :, cols].astype(f32)).astype(bf16)
            ups[slot, :, cols] = (di * for_up[slot, :, cols].astype(f32)).astype(bf16)

        @pl.when(i < 2)
        def _():
            for copy in tile_loads(i + 2):
                copy.start()

        for copy in stores(i, 0):
            copy.start()
        part[i] = product(gates[slot], w_gate[...]) + product(ups[slot], w_up[...])
        core_copy(i).start()

        @pl.when(i >= 1)
        def _():
            both(i - 1)

        return carry

    def both(i):
        core_copy(i).wait_recv()
        part[i, :HALF] = part[i, :HALF] + from_core[i]

        @pl.when(i < 2)
        def _():
            y_copy(i).start()

    lax.fori_loop(0, 4, own_tile, 0)
    for copy in loads[4:]:
        copy.wait()

    def other_tile(n, carry):
        i, slot = (n + 2) % 4, n % 2

        @pl.when(n > 0)
        def _():
            z_copy(i).wait_recv()

        @pl.when(n >= 1)
        def _():
            z_forward(i).start()

        @pl.when(n < 2)
        def _():
            for copy in stores(i, 0):
                copy.wait()

        @pl.when(n >= 2)
        def _():
            for copy in stores(n, d_out.shape[0]):
                copy.wait()

        z_forward(i).wait_recv()
        lo = pl.multiple_of(i * TILE, TILE)
        d_other[pl.ds(lo, HALF), :] = z_land[i].astype(bf16)
        d_other[pl.ds(lo + HALF, HALF), :] = c_land[i].astype(bf16)
        n, d = other[pl.ds(lo, TILE), :], d_other[pl.ds(lo, TILE), :]
        for off in range(0, half, TILE):
            size = min(TILE, half - off)
            piece(n, d, slot, pl.ds(pl.multiple_of(mine + off, HALF), size), pl.ds(off, size))
        for copy in stores(i, d_out.shape[0]):
            copy.start()
        return carry

    z_forward(2).start()
    both(jnp.int32(3))
    lax.fori_loop(0, 3, other_tile, 0)

    gain_grads[...] = jnp.zeros_like(gain_grads)

    def fold(a):
        return jnp.sum(a.reshape(a.shape[0] // 8, 8, a.shape[1]), axis=0)

    def of_quarter(h, carry):
        y_copy(h).wait_recv()
        at = pl.ds(pl.multiple_of(h * HALF, HALF), HALF)
        grad = part[2 + h, :HALF] + from_y[h]
        m = middle[at, :]
        inverse = lax.rsqrt(jnp.mean(m * m, axis=-1, keepdims=True) + epsilon)
        hat = m * inverse
        scaled = grad * (1.0 + gain_row(gains, 2))
        d_middle = dy[at, :].astype(f32) + inverse * (scaled - hat * jnp.mean(scaled * hat, axis=-1, keepdims=True))
        gain_grads[0] = gain_grads[0] + fold(grad * hat)
        d_middle_out[at, :] = d_middle
        b = branch[at, :]
        inverse = lax.rsqrt(jnp.mean(b * b, axis=-1, keepdims=True) + epsilon)
        hat = b * inverse
        scaled = d_middle * (1.0 + gain_row(gains, 1))
        d_low = (inverse * (scaled - hat * jnp.mean(scaled * hat, axis=-1, keepdims=True))).astype(bf16)
        gain_grads[1] = gain_grads[1] + fold(d_middle * hat)
        d_branch_out[at, :] = d_low.astype(f32)
        for k in range(4):
            heads[k, at, :] = product_t(d_low, w_out[k * head : (k + 1) * head, :]).astype(bf16).astype(f32)
        return carry

    lax.fori_loop(0, 2, of_quarter, 0)
    lax.fori_loop(3, 4, other_tile, 0)
    for i in (0, 1):
        for copy in stores(i, d_out.shape[0]):
            copy.wait()
    for i in (3, 0, 1):
        z_copy(i).wait_send()
    for i in range(4):
        core_copy(i).wait_send()
        z_forward(i).wait_send()
    for h in range(2):
        y_copy(h).wait_send()


def feed_back(nx, d_out, d_own, d_first, for_gate, for_up, other, w_gate, w_up, w_down, w_out, middle, branch, dy, gains):
    length, width = d_out.shape
    columns = pl.cdiv(w_gate.shape[0], TILE) * TILE
    head = w_out.shape[0] // 4
    return pl.pallas_call(
        functools.partial(back_kernel, nx),
        out_shape=(
            jax.ShapeDtypeStruct((length, width), bf16),
            jax.ShapeDtypeStruct((length, columns // 2), bf16),
            jax.ShapeDtypeStruct((2 * length, columns), bf16),
            jax.ShapeDtypeStruct((4, QUARTER, head), f32),
            jax.ShapeDtypeStruct((QUARTER, width), f32),
            jax.ShapeDtypeStruct((QUARTER, width), f32),
            jax.ShapeDtypeStruct((2, 8, width), f32),
        ),
        in_specs=[ANY] * 13 + [VMEM],
        out_specs=(VMEM, ANY, ANY) + (VMEM,) * 4,
        scratch_shapes=[
            pltpu.VMEM((length, width), bf16),
            pltpu.VMEM((2, TILE, columns), bf16),
            pltpu.VMEM((2, TILE, columns), bf16),
            pltpu.VMEM((length, width), bf16),
            pltpu.VMEM((columns, width), bf16),
            pltpu.VMEM((columns, width), bf16),
            pltpu.VMEM((columns, width), bf16),
            pltpu.VMEM((4 * head, width), bf16),
            pltpu.VMEM((QUARTER, width), f32),
            pltpu.VMEM((QUARTER, width), f32),
            pltpu.VMEM((QUARTER, width), bf16),
            pltpu.VMEM((2, TILE, columns), bf16),
            pltpu.VMEM((2, TILE, columns), bf16),
            pltpu.VMEM((2, TILE, columns // 2), bf16),
            pltpu.VMEM((4, TILE, width), f32),
            pltpu.VMEM((4, HALF, width), f32),
            pltpu.VMEM((2, HALF, width), f32),
            pltpu.VMEM((4, HALF, width), f32),
            pltpu.VMEM((4, HALF, width), f32),
            pltpu.SemaphoreType.DMA((12,)),
            pltpu.SemaphoreType.DMA((2, 2)),
            pltpu.SemaphoreType.DMA((2, 3)),
        ]
        + dma(8, 8, 2, 2, 4, 4),
        compiler_params=pltpu.CompilerParams(collective_id=1, has_side_effects=True, vmem_limit_bytes=VMEM_LIMIT),
        name="feed_back",
    )(
        d_out,
        d_own,
        d_first,
        for_gate,
        for_up,
        other,
        w_gate,
        w_up,
        w_down,
        w_out,
        middle,
        branch,
        dy,
        gains,
    )


def visible_pairs(shape, i, segments):
    row = lax.broadcasted_iota(jnp.int32, shape, 0) + i * TILE
    col = lax.broadcasted_iota(jnp.int32, shape, 1)
    first = jnp.sum((segments[...] == 0).astype(jnp.int32), axis=1, keepdims=True)
    return (row >= col) & ((row < first) == (col < first))


def attention_kernel(
    nx,
    tokens,
    w_query,
    w_key,
    w_value,
    w_out,
    segments,
    gain_0,
    gain_1,
    gain_2,
    gain_3,
    gain_4,
    gain_5,
    normed_hbm,
    query_hbm,
    keys_hbm,
    values_hbm,
    query_raw_hbm,
    keys_raw_hbm,
    log_total_hbm,
    context_hbm,
    w_out_all_hbm,
    middle,
    branch,
    gains,
    normed,
    query,
    keys,
    values,
    query_raw,
    keys_raw,
    log_total,
    context,
    w_out_all,
    stores,
    out_own,
    out_land,
    context_own,
    context_core,
    context_land,
    context_all,
    c_send,
    c_recv,
    y_send,
    y_recv,
    x_send,
    x_recv,
):
    z, x, y, c, near = spots(nx)
    cs, ys, xs = (c_send, c_recv), (y_send, y_recv), (x_send, x_recv)
    length, width = tokens.shape
    head = w_query.shape[1]
    given = (gain_0, gain_1, gain_2, gain_3, gain_4, gain_5)
    gain_loads = [
        pltpu.make_async_copy(ref, gains.at[k, pl.ds(0, ref.shape[0])], stores.at[k]) for k, ref in enumerate(given)
    ]
    for copy in gain_loads:
        copy.start()
    out_own[...] = w_out[...].astype(f32)
    greet([near[k] for k in ("c", "y", "x")])
    mine = pl.ds(pl.multiple_of(x * (head // 2), 8), head // 2)
    out_y = remote(out_own.at[mine], out_land.at[0, mine], ys, 0, near["y"])
    out_x = remote(out_land.at[0, mine], out_land.at[0, mine], xs, 0, near["x"])
    out_c = remote(out_own, out_land.at[1], cs, 0, near["c"])
    out_yc = remote(out_land.at[0], out_land.at[2], cs, 1, near["c"])
    out_y.start()
    out_c.start()
    w_out_all[:head, :] = w_out[...]

    for copy in gain_loads:
        copy.wait()

    def norm(v, gain):
        return v * lax.rsqrt(jnp.mean(v * v, axis=-1, keepdims=True) + epsilon) * (1.0 + gain)

    def inputs(i, carry):
        at = pl.ds(pl.multiple_of(i * TILE, TILE), TILE)
        n = norm(tokens[at, :].astype(f32), gain_row(gains, 0)).astype(bf16)
        normed[at, :] = n
        raw = product(n, w_query[...])
        query_raw[at, :] = raw
        query[at, :] = norm(raw, gain_row(gains, 4)[:, :head]).astype(bf16)
        raw = product(n, w_key[...])
        keys_raw[at, :] = raw
        keys[at, :] = norm(raw, gain_row(gains, 5)[:, :head]).astype(bf16)
        values[at, :] = product(n, w_value[...]).astype(bf16)
        return carry

    lax.fori_loop(0, length // TILE, inputs, 0)
    for i in range(length // TILE):
        at, seen = slice(i * TILE, (i + 1) * TILE), (i + 1) * TILE
        s = product_t(query[at, :], keys[:seen, :]) * score_scale
        s = jnp.where(visible_pairs(s.shape, i, segments), s, -1e30)
        largest = jnp.max(s, axis=-1, keepdims=True)
        e = jnp.exp(s - largest)
        total = jnp.sum(e, axis=-1, keepdims=True)
        log_total[at, :] = largest + jnp.log(total)
        low_context = product((e / total).astype(bf16), values[:seen, :]).astype(bf16)
        context[at, :] = low_context
        context_own[at, :] = low_context.astype(f32)

    out_copies = []

    def put(src, dst):
        copy = pltpu.make_async_copy(src, dst, stores.at[len(out_copies)])
        copy.start()
        out_copies.append(copy)

    span = length // 2
    to_core = remote(context_own.at[pl.ds(pl.multiple_of((1 - c) * span, span), span)], context_core, cs, 2, near["c"])
    to_core.start()

    def local(i, other):
        dy = 1 - i // 2
        return pl.multiple_of(((y ^ other) ^ dy) * QUARTER + (i % 2) * HALF, HALF)

    def context_copy(i, k):
        if k == 0:
            src = context_own.at[pl.ds(pl.multiple_of(c * span + local(i, 1), HALF), HALF)]
        else:
            src = context_core.at[pl.ds(local(i, 1), HALF)]
        return remote(src, context_land.at[k, i], ys, 1 + 2 * i + k, near["y"])

    context_copy(0, 0).start()
    for src, dst in (
        (normed, normed_hbm),
        (query, query_hbm),
        (keys, keys_hbm),
        (values, values_hbm),
        (query_raw, query_raw_hbm),
        (keys_raw, keys_raw_hbm),
        (log_total, log_total_hbm),
        (context, context_hbm),
    ):
        put(src, dst)
    out_y.wait_recv()
    out_x.start()
    to_core.wait_recv()
    for i in range(4):
        for k in range(2):
            if i + k > 0:
                context_copy(i, k).start()
    out_c.wait_recv()
    w_out_all[2 * head : 3 * head, :] = out_land[1].astype(bf16)
    for i in range(4):
        rows = pl.ds(i * HALF, HALF)
        context_all[rows, :head] = context[pl.ds(pl.multiple_of(c * span + local(i, 0), HALF), HALF), :]
        context_all[rows, 2 * head : 3 * head] = context_core[pl.ds(local(i, 0), HALF), :].astype(bf16)
    out_x.wait_recv()
    out_yc.start()
    w_out_all[head : 2 * head, :] = out_land[0].astype(bf16)
    out_yc.wait_recv()
    w_out_all[3 * head :, :] = out_land[2].astype(bf16)
    put(w_out_all, w_out_all_hbm)

    def middle_copy(i):
        at = pl.multiple_of(i * TILE, TILE)
        return remote(middle.at[pl.ds(at, HALF)], middle.at[pl.ds(at + HALF, HALF)], cs, 3 + i, near["c"])

    def middle_tile(i, carry):
        rows = pl.ds(pl.multiple_of(i * HALF, HALF), HALF)
        context_copy(i, 0).wait_recv()
        context_all[rows, head : 2 * head] = context_land[0, i].astype(bf16)
        context_copy(i, 1).wait_recv()
        context_all[rows, 3 * head :] = context_land[1, i].astype(bf16)
        b = product(context_all[rows, :], w_out_all[...])
        branch[i % 2] = b
        hidden = tokens[pl.ds(pl.multiple_of(c * span + local(i, 0), HALF), HALF), :].astype(f32)
        middle[pl.ds(pl.multiple_of(i * TILE, TILE), HALF), :] = hidden + norm(b, gain_row(gains, 1))
        middle_copy(i).start()
        return carry

    lax.fori_loop(0, 4, middle_tile, 0)
    for i in range(4):
        middle_copy(i).wait()
        for k in range(2):
            context_copy(i, k).wait_send()
    for copy in (out_y, out_x, out_c, out_yc, to_core):
        copy.wait_send()
    for copy in out_copies:
        copy.wait()


def attend(nx, tokens, w_query, w_key, w_value, w_out, segment_ids, *gains):
    length, width = tokens.shape
    head = w_query.shape[1]
    of_head = jax.ShapeDtypeStruct((length, head), bf16)
    raw = jax.ShapeDtypeStruct((length, head), f32)
    return pl.pallas_call(
        functools.partial(attention_kernel, nx),
        out_shape=(
            jax.ShapeDtypeStruct((length, width), bf16),
            of_head,
            of_head,
            of_head,
            raw,
            raw,
            jax.ShapeDtypeStruct((length, 1), f32),
            of_head,
            jax.ShapeDtypeStruct((4 * head, width), bf16),
            jax.ShapeDtypeStruct((length, width), f32),
            jax.ShapeDtypeStruct((2, HALF, width), f32),
            jax.ShapeDtypeStruct((8, width), f32),
        ),
        in_specs=[VMEM] * 6 + [ANY] * 6,
        out_specs=(ANY,) * 9 + (VMEM,) * 3,
        scratch_shapes=[
            pltpu.VMEM((length, width), bf16),
            pltpu.VMEM((length, head), bf16),
            pltpu.VMEM((length, head), bf16),
            pltpu.VMEM((length, head), bf16),
            pltpu.VMEM((length, head), f32),
            pltpu.VMEM((length, head), f32),
            pltpu.VMEM((length, 1), f32),
            pltpu.VMEM((length, head), bf16),
            pltpu.VMEM((4 * head, width), bf16),
            pltpu.SemaphoreType.DMA((9,)),
            pltpu.VMEM((head, width), f32),
            pltpu.VMEM((3, head, width), f32),
            pltpu.VMEM((length, head), f32),
            pltpu.VMEM((length // 2, head), f32),
            pltpu.VMEM((2, 4, HALF, head), f32),
            pltpu.VMEM((length // 2, 4 * head), bf16),
        ]
        + dma(7, 7, 9, 9, 1, 1),
        compiler_params=pltpu.CompilerParams(collective_id=3, has_side_effects=True, vmem_limit_bytes=VMEM_LIMIT),
        name="attend",
    )(
        tokens,
        w_query,
        w_key,
        w_value,
        w_out,
        segment_ids.reshape(1, length),
        *gains,
    )


def reduce_kernel(
    nx,
    d_out_hbm,
    d_other_hbm,
    normed_hbm,
    other_hbm,
    pair_own_hbm,
    pair_other_hbm,
    pair_gates_hbm,
    d_branch_hbm,
    d_middle_hbm,
    tokens_hbm,
    normed_in_hbm,
    query_hbm,
    keys_hbm,
    values_hbm,
    query_raw_hbm,
    keys_raw_hbm,
    context_hbm,
    heads_hbm,
    w_query_hbm,
    w_key_hbm,
    w_value_hbm,
    log_total,
    segments,
    gain_rows,
    of_ffn_out,
    of_middle,
    down_out,
    gate_out,
    up_out,
    query_out,
    out_out,
    key_out,
    value_out,
    input_grad,
    gains,
    input_stage,
    ff_stage,
    dw,
    x_land,
    z2_land,
    z1_land,
    from_core,
    from_y,
    branch_land,
    input_own,
    input_land,
    d_qkv,
    attn,
    attn_z1,
    attn_x,
    attn_z2,
    kv_core,
    kv_across,
    kv_own,
    kv_y,
    kv_wide,
    kv_wide_core,
    gains_land,
    heads_mine,
    heads_y,
    got_c,
    got_y,
    loads,
    c_send,
    c_recv,
    y_send,
    y_recv,
    x_send,
    x_recv,
    z2_send,
    z2_recv,
    z1_send,
    z1_recv,
):
    z, x, y, c, near = spots(nx)
    zh, zl = z // 2, z % 2
    cs, ys, xs = (c_send, c_recv), (y_send, y_recv), (x_send, x_recv)
    z2s, z1s = (z2_send, z2_recv), (z1_send, z1_recv)
    length, width = d_out_hbm.shape
    half = pair_own_hbm.shape[1]
    head = query_hbm.shape[1]
    blk = x_land.shape[1]
    own_row = pl.multiple_of((c * 2 + y) * QUARTER, QUARTER)

    def block(a, b):
        return pl.ds(pl.multiple_of(b * blk, 8), blk)

    def quarter_rows(dc, dy):
        return pl.ds(pl.multiple_of(((c ^ dc) * 2 + (y ^ dy)) * QUARTER, QUARTER), QUARTER)

    heads_in = pltpu.make_async_copy(heads_hbm.at[0], heads_mine, loads.at[6])
    heads_in_y = pltpu.make_async_copy(heads_hbm.at[1], heads_y.at[0], loads.at[7])
    heads_c_copy = remote(heads_hbm.at[pl.ds(2, 2)], got_c, cs, 11, near["c"])
    heads_y_copy = remote(heads_y, got_y, ys, 7, near["y"])

    branch_y = remote(d_branch_hbm, branch_land.at[0], ys, 0, near["y"])
    branch_c = remote(d_branch_hbm, branch_land.at[1], cs, 0, near["c"])
    branch_fwd = remote(branch_land.at[0], branch_land.at[2], cs, 1, near["c"])

    def place(n):
        return n // 2 * 2 + (1 - zl if n % 2 == 0 else zl)

    def owner(n):
        return 2 * (1 - zh if n < 2 else zh) + (1 - zl if n % 2 == 0 else zl)

    def x_copy(m, n):
        slot = m * 4 + place(n)
        return remote(dw.at[m, block(dw, owner(n) * 2 + (1 - x))], x_land.at[slot], xs, slot, near["x"])

    def z2_copy(m, n):
        slot = m * 2 + place(n)
        return remote(dw.at[m, block(dw, owner(n) * 2 + x)], z2_land.at[slot], z2s, slot, near["z2"])

    def z1_copy(m):
        return remote(dw.at[m, block(dw, (2 * zh + 1 - zl) * 2 + x)], z1_land.at[m], z1s, m, near["z1"])

    def start_x(*blocks):
        for m, j in blocks:
            x_copy(m, j).start()

    arrived = set()

    def wait_x(m, j):
        if (m, j) not in arrived:
            arrived.add((m, j))
            x_copy(m, j).wait_recv()

    inner = (z == 1) | (z == 2)

    def far(*blocks):
        for m, k in blocks:
            wait_x(m, k)
            rows = block(dw, owner(k) * 2 + x)
            dw[m, rows, :] = dw[m, rows, :] + x_land[m * 4 + place(k)]

            @pl.when(inner)
            def _():
                z2_copy(m, k).start()

    def outer(m, k):
        @pl.when(jnp.logical_not(inner))
        def _():
            z2_copy(m, k).start()

    def close(m):
        for k in range(2):
            wait_x(m, 2 + k)
            z2_copy(m, k).wait_recv()
            rows = block(dw, owner(2 + k) * 2 + x)
            dw[m, rows, :] = dw[m, rows, :] + x_land[m * 4 + place(2 + k)] + z2_land[m * 2 + place(k)]
            if k == 0:
                z1_copy(m).start()

    def finish(m, ref):
        z1_copy(m).wait_recv()
        own, other = dw[m, block(dw, (2 * zh + zl) * 2 + x), :], z1_land[m]
        ff_stage[:, :half] = jnp.where(zl == 0, own, other)
        ff_stage[:, half:] = jnp.where(zl == 0, other, own)[:, : ref.shape[1] - half]
        copy = pltpu.make_async_copy(ff_stage, ref, loads.at[1])
        copy.start()
        copy.wait()

    def copies(pairs):
        started = [pltpu.make_async_copy(src, dst, loads.at[k]) for k, (src, dst) in enumerate(pairs)]
        for copy in started:
            copy.start()
        return started

    def weights(left, right):
        far_size = pl.cdiv(width // 2, HALF) * HALF
        far_at = pl.multiple_of((1 - zh) * (width - far_size), HALF)
        near_at = pl.multiple_of(zh * far_size, HALF)

        def form(m, lo, at, size):
            for off in range(0, size, 3 * HALF):
                rows = pl.ds(pl.multiple_of(at + off, HALF), min(3 * HALF, size - off))
                cols = pl.ds(pl.multiple_of(lo, HALF), half)
                dw[m, rows, :] = t_product(left[:, rows], right[:, cols])

        waits = copies(
            [
                (d_out_hbm, left.at[pl.ds(0, length)]),
                (d_other_hbm, left.at[pl.ds(length, length)]),
                (pair_own_hbm, right.at[pl.ds(0, length), pl.ds(0, half)]),
                (pair_other_hbm, right.at[pl.ds(length, length), pl.ds(0, half)]),
            ]
        )
        heads_in.start()
        heads_in_y.start()
        greet([near[k] for k in ("c", "y", "x", "z2", "z1")])
        heads_c_copy.start()
        for copy in waits:
            copy.wait()
        form(0, 0, far_at, far_size)
        start_x((0, 0), (0, 1))
        heads_c_copy.wait_recv()
        heads_in_y.wait()
        heads_y[1] = got_c[1]
        heads_y_copy.start()
        branch_y.start()
        branch_c.start()
        form(0, 0, near_at, width - far_size)
        for copy in copies(
            [
                (normed_hbm, left.at[pl.ds(0, length)]),
                (other_hbm, left.at[pl.ds(length, length)]),
                (pair_gates_hbm, right),
            ]
        ):
            copy.wait()
        def form_far(m, carry):
            form(m, (m - 1) * half, far_at, far_size)
            start_x((m, 0), (m, 1))
            return carry

        def form_near(m, carry):
            form(m, (m - 1) * half, near_at, width - far_size)
            return carry

        lax.fori_loop(1, 3, form_far, 0)
        far((0, 0))
        outer(0, 0)
        lax.fori_loop(1, 3, form_near, 0)
        start_x((0, 2), (0, 3), (1, 2), (1, 3), (2, 2), (2, 3))

    pl.run_scoped(weights, pltpu.VMEM((2 * length, width), bf16), pltpu.VMEM((2 * length, 2 * half), bf16))

    def total_of(a):
        return jnp.sum(a, axis=0, keepdims=True)

    gains[...] = jnp.zeros_like(gains)
    gains[1:2, :] = total_of(of_middle[1])
    gains[2:3, :] = total_of(of_middle[0])
    gains[3:4, :] = 0.25 * total_of(of_ffn_out[...])

    def back_norm(raw, gain, grad):
        inverse = lax.rsqrt(jnp.mean(raw * raw, axis=-1, keepdims=True) + epsilon)
        hat = raw * inverse
        scaled = grad * (1.0 + gain)
        return inverse * (scaled - hat * jnp.mean(scaled * hat, axis=-1, keepdims=True)), grad * hat

    def attention(query, keys, values, query_raw, keys_raw, grad_context, d_keys, d_values):
        for copy in copies(
            [
                (query_hbm, query),
                (keys_hbm, keys),
                (values_hbm, values),
                (query_raw_hbm, query_raw),
                (keys_raw_hbm, keys_raw),
            ]
        ):
            copy.wait()
        heads_in.wait()
        grad_context[quarter_rows(0, 0), :] = heads_mine[...].astype(bf16)
        grad_context[quarter_rows(1, 0), :] = got_c[0].astype(bf16)
        heads_y_copy.wait_recv()
        grad_context[quarter_rows(0, 1), :] = got_y[0].astype(bf16)
        grad_context[quarter_rows(1, 1), :] = got_y[1].astype(bf16)
        d_keys[...] = jnp.zeros_like(d_keys)
        d_values[...] = jnp.zeros_like(d_values)

        def back_tile(seen, i, carry):
            at = pl.ds(pl.multiple_of(i * TILE, TILE), TILE)
            q, k = query[at, :], keys[:seen, :]
            s = product_t(q, k) * score_scale
            p = jnp.exp(jnp.where(visible_pairs(s.shape, i, segments), s, -1e30) - log_total[at, :])
            g = grad_context[at, :]
            dp = product_t(g, values[:seen, :])
            balance = jnp.sum(dp * p, axis=-1, keepdims=True)
            ds = (p * (dp - balance)).astype(bf16)
            dq, of_gain = back_norm(query_raw[at, :], gain_row(gain_rows, 4)[:, :head], product(ds, k) * score_scale)
            d_qkv[at, :head] = dq.astype(bf16)
            gains[4:5, :head] = gains[4:5, :head] + jnp.sum(of_gain, axis=0, keepdims=True)
            d_keys[:seen, :] = d_keys[:seen, :] + t_product(ds, q)
            d_values[:seen, :] = d_values[:seen, :] + t_product(p.astype(bf16), g)
            return carry

        tiles = length // TILE
        lax.fori_loop(0, tiles // 2, functools.partial(back_tile, length // 2), 0)
        lax.fori_loop(tiles // 2, tiles, functools.partial(back_tile, length), 0)

        def keys_tile(i, carry):
            at = pl.ds(pl.multiple_of(i * TILE, TILE), TILE)
            dk, of_gain = back_norm(keys_raw[at, :], gain_row(gain_rows, 5)[:, :head], d_keys[at, :] * score_scale)
            d_qkv[at, head : 2 * head] = dk.astype(bf16)
            gains[5:6, :head] = gains[5:6, :head] + jnp.sum(of_gain, axis=0, keepdims=True)
            d_qkv[at, 2 * head :] = d_values[at, :].astype(bf16)
            return carry

        lax.fori_loop(0, tiles, keys_tile, 0)

    pl.run_scoped(
        attention,
        pltpu.VMEM((length, head), bf16),
        pltpu.VMEM((length, head), bf16),
        pltpu.VMEM((length, head), bf16),
        pltpu.VMEM((length, head), f32),
        pltpu.VMEM((length, head), f32),
        pltpu.VMEM((length, head), bf16),
        pltpu.VMEM((length, head), f32),
        pltpu.VMEM((length, head), f32),
    )
    far((0, 1))

    def put_input(dc, dy):
        copy = pltpu.make_async_copy(input_stage, input_grad.at[quarter_rows(dc, dy)], loads.at[0])
        copy.start()
        copy.wait()

    def attn_z1_copy(i):
        b = (2 * (i // 2) + 1 - zl) * 2 + i % 2
        return remote(attn.at[block(attn, b)], attn_z1.at[i], z1s, 3 + i, near["z1"])

    def attn_x_copy(j):
        b = (2 * (zh ^ j) + zl) * 2 + 1 - x
        return remote(attn.at[block(attn, b)], attn_x.at[j], xs, 12 + j, near["x"])

    attn_z2_copy = remote(attn.at[block(attn, (2 * (1 - zh) + zl) * 2 + x)], attn_z2, z2s, 6, near["z2"])

    input_y = remote(input_own, input_land.at[0], ys, 4, near["y"])
    input_c = remote(input_own, input_land.at[1], cs, 7, near["c"])
    input_fwd = remote(input_land.at[0], input_land.at[2], cs, 8, near["c"])

    hops = [
        remote(gains, gains_land.at[k], sems, index, near[to])
        for k, (sems, index, to) in enumerate([(cs, 10, "c"), (ys, 6, "y"), (xs, 14, "x"), (z1s, 7, "z1"), (z2s, 7, "z2")])
    ]

    def hop(k):
        hops[k].start()

    def arrive(k):
        hops[k].wait()
        gains[...] = gains[...] + gains_land[k]

    def rest(w_qkv, part, kv_halves):
        def of_inputs(normed_in, kv):
            for copy in copies([(normed_in_hbm, normed_in)]):
                copy.wait()
            for k in range(2):
                kv[k] = t_product(normed_in[...], d_qkv[:, (1 + k) * head : (2 + k) * head])
            to_core = remote(kv.at[1 - c], kv_core, cs, 6, near["c"])
            to_core.start()
            attn[:, :head] = t_product(normed_in[...], d_qkv[:, :head])
            to_core.wait_recv()
            for k in range(2):
                lanes = slice(k * (head // 2), (k + 1) * (head // 2))
                kv_halves[k] = kv[c, :, lanes] + kv_core[:, lanes]
            to_core.wait_send()

        pl.run_scoped(of_inputs, pltpu.VMEM((length, width), bf16), pltpu.VMEM((2, width, head), f32))
        to_y = remote(kv_halves.at[1 - y], kv_across, ys, 3, near["y"])
        to_y.start()
        for copy in copies(
            [
                (w_query_hbm, w_qkv.at[:, pl.ds(0, head)]),
                (w_key_hbm, w_qkv.at[:, pl.ds(head, head)]),
                (w_value_hbm, w_qkv.at[:, pl.ds(2 * head, head)]),
            ]
        ):
            copy.wait()

        def core_copy(i):
            return remote(part.at[i, pl.ds(HALF, HALF)], from_core.at[i], cs, 2 + i, near["c"])

        def y_copy(h):
            return remote(part.at[h, pl.ds(0, HALF)], from_y.at[h], ys, 1 + h, near["y"])

        def tile(i, carry):
            for dc in range(2):
                rows = d_qkv[pl.ds(tile_row(c, y, i, dc), HALF), :]
                part[i, dc * HALF : (dc + 1) * HALF] = product_t(rows, w_qkv[...])
            core_copy(i).start()
            core_copy(i).wait_recv()
            part[i, :HALF] = part[i, :HALF] + from_core[i]

            @pl.when(i < 2)
            def _():
                y_copy(i).start()

            return carry

        lax.fori_loop(0, 4, tile, 0)


        far((1, 0))
        outer(0, 1)

        def of_branch(context, d_branch, d_middle, tokens):
            waits = copies(
                [
                    (context_hbm, context),
                    (d_branch_hbm, d_branch),
                    (d_middle_hbm, d_middle),
                    (tokens_hbm.at[pl.ds(own_row, QUARTER)], tokens),
                ]
            )
            branch_y.wait_recv()
            branch_fwd.start()
            for copy in waits:
                copy.wait()
            acc = t_product(d_branch[...].astype(bf16), context[quarter_rows(0, 0), :])
            branch_c.wait_recv()
            branch_fwd.wait_recv()
            for k, (dc, dy) in enumerate([(0, 1), (1, 0), (1, 1)]):
                acc = acc + t_product(branch_land[k].astype(bf16), context[quarter_rows(dc, dy), :])
            attn[:, head : 2 * head] = acc
            far((1, 1))
            to_y.wait_recv()
            attn[:, 2 * head :] = kv_halves[y] + kv_across[...]
            for i in range(4):
                attn_z1_copy(i).start()
            far((2, 0), (2, 1))
            outer(1, 0)
            for h in range(2):
                y_copy(h).wait_recv()
                at = slice(h * HALF, (h + 1) * HALF)
                grad = part[2 + h, :HALF] + from_y[h]
                d_in, of_gain = back_norm(tokens[at, :].astype(f32), gain_row(gain_rows, 0), grad)
                gains[0:1, :] = gains[0:1, :] + jnp.sum(of_gain, axis=0, keepdims=True)
                d = (d_middle[at, :] + d_in).astype(bf16)
                input_stage[at, :] = d
                input_own[at, :] = d.astype(f32)

        pl.run_scoped(
            of_branch,
            pltpu.VMEM((length, head), bf16),
            pltpu.VMEM((QUARTER, width), f32),
            pltpu.VMEM((QUARTER, width), f32),
            pltpu.VMEM((QUARTER, width), bf16),
        )
        hop(0)
        arrive(0)
        hop(1)
        input_y.start()
        input_c.start()
        outer(1, 1)
        put_input(0, 0)
        for i in range(4):
            core_copy(i).wait_send()
        for h in range(2):
            y_copy(h).wait_send()
        to_y.wait_send()

    pl.run_scoped(
        rest,
        pltpu.VMEM((width, 3 * head), bf16),
        pltpu.VMEM((4, TILE, width), f32),
        pltpu.VMEM((2, width, head // 2), f32),
    )

    arrive(1)
    hop(2)
    close(0)
    outer(2, 0)
    input_y.wait_recv()
    input_fwd.start()
    input_stage[...] = input_land[0].astype(bf16)
    put_input(0, 1)
    input_c.wait_recv()
    input_stage[...] = input_land[1].astype(bf16)
    put_input(1, 0)
    close(1)
    outer(2, 1)
    for i in range(4):
        attn_z1_copy(i).wait_recv()
        rows = block(attn, (2 * (i // 2) + zl) * 2 + i % 2)
        attn[rows, :] = attn[rows, :] + attn_z1[i]
    for j in (1, 0):
        attn_x_copy(j).start()
    input_fwd.wait_recv()
    input_stage[...] = input_land[2].astype(bf16)
    put_input(1, 1)
    arrive(2)
    hop(3)
    for j in (1, 0):
        attn_x_copy(j).wait_recv()
        rows = block(attn, (2 * (zh ^ j) + zl) * 2 + x)
        attn[rows, :] = attn[rows, :] + attn_x[j]
        if j == 1:
            attn_z2_copy.start()
    close(2)
    finish(0, down_out)
    finish(1, gate_out)
    attn_z2_copy.wait_recv()
    total = attn[block(attn, (2 * zh + zl) * 2 + x), :] + attn_z2[...]
    query_out[...] = total[:, :head]
    out_out[...] = total[:, head : 2 * head]
    kv_own[...] = total[:, 2 * head :]
    wide_y = remote(kv_own, kv_y, ys, 5, near["y"])
    wide_y.start()
    arrive(3)
    hop(4)
    wide_y.wait_recv()
    kv_wide[:, : head // 2] = jnp.where(y == 0, kv_own[...], kv_y[...])
    kv_wide[:, head // 2 :] = jnp.where(y == 0, kv_y[...], kv_own[...])
    wide_c = remote(kv_wide, kv_wide_core, cs, 9, near["c"])
    wide_c.start()
    wide_c.wait_recv()
    key_out[...] = jnp.where(c == 0, kv_wide[...], kv_wide_core[...])
    value_out[...] = jnp.where(c == 0, kv_wide_core[...], kv_wide[...])
    arrive(4)
    finish(2, up_out)
    for m in range(3):
        for j in range(4):
            x_copy(m, j).wait_send()
        for k in range(2):
            z2_copy(m, k).wait_send()
        z1_copy(m).wait_send()
    for i in range(4):
        attn_z1_copy(i).wait_send()
    for j in range(2):
        attn_x_copy(j).wait_send()
    for copy in (attn_z2_copy, branch_y, branch_c, branch_fwd, input_y, input_c, input_fwd, wide_y, wide_c, heads_c_copy, heads_y_copy):
        copy.wait_send()


def reduce_all(nx, dp_size, columns, whole, small):
    length, width = whole[0].shape
    half = whole[4].shape[1]
    head = whole[11].shape[1]
    blk = width // dp_size
    return pl.pallas_call(
        functools.partial(reduce_kernel, nx),
        out_shape=(
            *[jax.ShapeDtypeStruct((blk, columns), f32)] * 3,
            *[jax.ShapeDtypeStruct((blk, head), f32)] * 4,
            jax.ShapeDtypeStruct((length, width), bf16),
            jax.ShapeDtypeStruct((8, width), f32),
        ),
        in_specs=[ANY] * len(whole) + [VMEM] * len(small),
        out_specs=(ANY,) * 3 + (VMEM,) * 4 + (ANY, VMEM),
        scratch_shapes=[
            pltpu.VMEM((QUARTER, width), bf16),
            pltpu.VMEM((blk, columns), f32),
            pltpu.VMEM((3, width, half), f32),
            pltpu.VMEM((12, blk, half), f32),
            pltpu.VMEM((6, blk, half), f32),
            pltpu.VMEM((3, blk, half), f32),
            pltpu.VMEM((4, HALF, width), f32),
            pltpu.VMEM((2, HALF, width), f32),
            pltpu.VMEM((3, QUARTER, width), f32),
            pltpu.VMEM((QUARTER, width), f32),
            pltpu.VMEM((3, QUARTER, width), f32),
            pltpu.VMEM((length, 3 * head), bf16),
            pltpu.VMEM((width, 2 * head + head // 2), f32),
            pltpu.VMEM((4, blk, 2 * head + head // 2), f32),
            pltpu.VMEM((2, blk, 2 * head + head // 2), f32),
            pltpu.VMEM((blk, 2 * head + head // 2), f32),
            pltpu.VMEM((width, head), f32),
            pltpu.VMEM((width, head // 2), f32),
            pltpu.VMEM((blk, head // 2), f32),
            pltpu.VMEM((blk, head // 2), f32),
            pltpu.VMEM((blk, head), f32),
            pltpu.VMEM((blk, head), f32),
            pltpu.VMEM((5, 8, width), f32),
            pltpu.VMEM((QUARTER, head), f32),
            pltpu.VMEM((2, QUARTER, head), f32),
            pltpu.VMEM((2, QUARTER, head), f32),
            pltpu.VMEM((2, QUARTER, head), f32),
        ]
        + dma(8, 12, 12, 8, 8, 15, 15, 8, 8, 8, 8),
        compiler_params=pltpu.CompilerParams(collective_id=2, has_side_effects=True, vmem_limit_bytes=VMEM_LIMIT),
        name="reduce_all",
    )(*whole, *small)


def settle_kernel(*refs):
    count = (len(refs) - 1) // 3
    sems = refs[-1]
    loads, puts = [], []
    for k in range(count):
        given, out, held = refs[k], refs[count + k], refs[2 * count + k]
        loads.append(pltpu.make_async_copy(given, held, sems.at[0, k]))
        puts.append(pltpu.make_async_copy(held, out, sems.at[1, k]))
    for copy in loads:
        copy.start()
    for load, put in zip(loads, puts):
        load.wait()
        put.start()
    for copy in puts:
        copy.wait()


def settle(*arrays):
    return pl.pallas_call(
        settle_kernel,
        out_shape=tuple(jax.ShapeDtypeStruct(a.shape, a.dtype) for a in arrays),
        in_specs=[ANY] * len(arrays),
        out_specs=(ANY,) * len(arrays),
        scratch_shapes=[pltpu.VMEM(a.shape, a.dtype) for a in arrays] + [pltpu.SemaphoreType.DMA((2, len(arrays)))],
        compiler_params=pltpu.CompilerParams(vmem_limit_bytes=VMEM_LIMIT),
        name="settle",
    )(*arrays)


def body(
    links,
    tokens,
    segment_ids,
    cotangent,
    w_query,
    w_key,
    w_value,
    w_out,
    w_gate,
    w_up,
    w_down,
    gain_attn_in,
    gain_attn_out,
    gain_ffn_in,
    gain_ffn_out,
    gain_query,
    gain_key,
):
    length, width = tokens.shape
    head = w_query.shape[1]
    columns = w_gate.shape[1]
    nx = links.nx
    blk = width // links.dp_size
    dp = lax.axis_index("dp")
    wg, wu = w_gate.T, w_up.T
    (
        normed_low,
        query_low,
        keys_low,
        values_low,
        query_raw,
        keys_raw,
        log_total,
        context_low,
        w_out_all,
        middle,
        branch,
        gain_rows,
    ) = attend(
        nx,
        tokens,
        w_query,
        w_key,
        w_value,
        w_out,
        segment_ids,
        gain_attn_in,
        gain_attn_out,
        gain_ffn_in,
        gain_ffn_out,
        gain_query,
        gain_key,
    )
    normed_two, normed_other, d_out, d_own, d_first, layer_out, pair_own, for_gate, for_up, of_ffn_out = feed_forward(
        nx, middle, cotangent, gain_rows, wg, wu, w_down
    )
    d_other, pair_other, pair_gates, heads, d_branch_own, d_middle, of_middle = feed_back(
        nx,
        d_out,
        d_own,
        d_first,
        for_gate,
        for_up,
        normed_other,
        wg,
        wu,
        w_down,
        w_out_all,
        middle,
        branch.reshape(QUARTER, width),
        cotangent,
        gain_rows,
    )
    *sums, gains = reduce_all(
        nx,
        links.dp_size,
        columns,
        [
            d_out,
            d_other,
            normed_two,
            normed_other,
            pair_own,
            pair_other,
            pair_gates,
            d_branch_own,
            d_middle,
            tokens,
            normed_low,
            query_low,
            keys_low,
            values_low,
            query_raw,
            keys_raw,
            context_low,
            heads,
            w_query,
            w_key,
            w_value,
        ],
        [log_total, segment_ids.reshape(1, length), gain_rows, of_ffn_out, of_middle],
    )
    layer_out, down_t, gate, up, query, out_t, key, value, input_grad = settle(layer_out, *sums)
    part = lax.dynamic_slice_in_dim(gains, dp * blk, blk, 1)
    hb = head // links.dp_size
    head_part = lax.dynamic_slice_in_dim(gains, dp * hb, hb, 1)
    return (
        layer_out,
        input_grad,
        query,
        key,
        value,
        out_t.T,
        gate,
        up,
        down_t.T,
        part[0],
        part[1],
        part[2],
        part[3],
        head_part[4],
        head_part[5],
    )


def body_any(
    links,
    tokens,
    segment_ids,
    cotangent,
    w_query,
    w_key,
    w_value,
    w_out,
    w_gate,
    w_up,
    w_down,
    gain_attn_in,
    gain_attn_out,
    gain_ffn_in,
    gain_ffn_out,
    gain_query,
    gain_key,
):
    length, width = tokens.shape
    head = w_query.shape[1]
    quarter = length // 4
    half_ff = w_gate.shape[1] // 2
    nx = links.nx
    blk = width // links.dp_size
    dp, t = lax.axis_index("dp"), lax.axis_index("tensor")
    z, x = dp // nx, dp % nx
    y, c = t // 2, t % 2
    parity = z % 2
    one = jnp.where(segment_ids[0] < length, 1.0, 0.5).astype(f32)

    def keep_low(a):
        return (a * one).astype(bf16)

    def place(dc, dy):
        return ((c ^ dc) * 2 + (y ^ dy)) * quarter

    def rows(a, dc, dy):
        return lax.dynamic_slice_in_dim(a, place(dc, dy), quarter, 0)

    def to_absolute(pieces):
        stack = jnp.stack([pieces[0][0], pieces[0][1], pieces[1][0], pieces[1][1]])
        mine = c * 2 + y
        return jnp.concatenate([lax.dynamic_index_in_dim(stack, mine ^ b, 0, keepdims=False) for b in range(4)], axis=0)

    out_own = w_out.astype(f32)
    out_y = links.y(out_own)
    out_c = links.core(out_own)
    out_yc = links.core(out_y)
    w_out_all = jnp.concatenate([w_out, keep_low(out_c), keep_low(out_y), keep_low(out_yc)], axis=0)

    wg_h = jnp.where(parity == 0, w_gate[:, :half_ff], w_gate[:, half_ff:])
    wu_h = jnp.where(parity == 0, w_up[:, :half_ff], w_up[:, half_ff:])
    wd_h = jnp.where(parity == 0, w_down[:half_ff], w_down[half_ff:])

    hidden_in = tokens.astype(f32)
    normed_low = low(rms_norm(hidden_in, gain_attn_in))
    query_raw = product(normed_low, w_query)
    keys_raw = product(normed_low, w_key)
    query_low = low(rms_norm(query_raw, gain_query))
    keys_low = low(rms_norm(keys_raw, gain_key))
    values_low = low(product(normed_low, w_value))
    places = jnp.arange(length)
    allowed = (places[:, None] >= places[None, :]) & (segment_ids[:, None] == segment_ids[None, :])

    def scores_of():
        raw = product_t(query_low, keys_low) * score_scale
        return jnp.where(allowed, raw, -1e30)

    scores = scores_of()
    largest = jnp.max(scores, axis=-1, keepdims=True)
    exponent = jnp.exp(scores - largest)
    total = jnp.sum(exponent, axis=-1, keepdims=True)
    log_total = largest + jnp.log(total)
    context_low = low(product(low(exponent / total), values_low))

    context = context_low.astype(f32)
    mine = jnp.concatenate([rows(context, 0, 1), rows(context, 0, 0)], axis=0)
    of_core = links.core(jnp.concatenate([rows(context, 1, 1), rows(context, 1, 0)], axis=0))
    of_y = links.y(jnp.concatenate([rows(context, 0, 0), rows(context, 0, 1)], axis=0))
    of_yc = links.y(jnp.concatenate([of_core[quarter:], of_core[:quarter]], axis=0))
    context_all = jnp.concatenate([low(mine), keep_low(of_core), keep_low(of_y), keep_low(of_yc)], axis=1)
    branch = product(context_all, w_out_all)
    hidden_rows = jnp.concatenate([rows(tokens, 0, 1), rows(tokens, 0, 0)], axis=0).astype(f32)
    middle_own = hidden_rows + rms_norm(branch, gain_attn_out)
    middle_core = links.core(middle_own)

    middles, normed_two, inners, parts = [], [], [], []
    saved = []
    for k in range(2):
        at = slice(k * quarter, (k + 1) * quarter)
        middle = jnp.concatenate([middle_own[at], middle_core[at]], axis=0)
        normed_k = low(rms_norm(middle, gain_ffn_in))
        gate, upward = product(normed_k, w_gate), product(normed_k, w_up)
        inner = low(activate(gate, upward))
        part = product(inner, w_down)
        middles.append(middle)
        normed_two.append(normed_k)
        saved.append((gate, upward))
        parts.append(part)
    normed_own = low(rms_norm(middle_own, gain_ffn_in)).astype(f32)
    other_own = links.z1(normed_own)
    other_core = links.core(other_own)
    normed_other = jnp.concatenate([keep_low(other_own), keep_low(other_core)], axis=0)

    def gather_quarters(parts):
        sums = [part[:quarter] + links.core(part[quarter:]) for part in parts]
        return sums[1] + links.y(sums[0])

    output_q = gather_quarters(parts)
    output_y = links.y(output_q)
    output_c = links.core(output_q)
    output_yc = links.core(output_y)
    outputs = [jnp.concatenate([output_y, output_yc], axis=0), jnp.concatenate([output_q, output_c], axis=0)]
    grad_out = cotangent.astype(f32)
    d_outputs, layer_pieces, grad_ffn_out = [], [], 0.0
    for k in range(2):
        dy_k = jnp.concatenate([rows(cotangent, 0, 1 - k), rows(cotangent, 1, 1 - k)], axis=0).astype(f32)
        layer_k = low(middles[k] + rms_norm(outputs[k], gain_ffn_out))
        d_k, gain_k = rms_back(outputs[k], gain_ffn_out, dy_k)
        grad_ffn_out = grad_ffn_out + gain_k
        d_outputs.append(low(d_k))
        layer_pieces.append(layer_k)
    layer_out = to_absolute(
        [
            [layer_pieces[1][:quarter], layer_pieces[0][:quarter]],
            [layer_pieces[1][quarter:], layer_pieces[0][quarter:]],
        ]
    )

    d_own_rows = [d[:quarter].astype(f32) for d in d_outputs]
    got_own = [links.z1(d_own_rows[1]), links.z1(d_own_rows[0])]
    got_core = [links.core(g) for g in got_own]
    d_other = jnp.concatenate(
        [keep_low(got_own[1]), keep_low(got_own[0]), keep_low(got_core[1]), keep_low(got_core[0])], axis=0
    )

    back_parts = []
    for k in range(2):
        gate, upward = saved[k]
        d_inner = product_t(d_outputs[k], w_down)
        _, pull = jax.vjp(activate, gate, upward)
        d_gate, d_up = pull(d_inner)
        back_parts.append(product_t(low(d_gate), w_gate) + product_t(low(d_up), w_up))
    d_normed_q = gather_quarters(back_parts)
    middle_q = middle_own[quarter:]
    branch_q = branch[quarter:]
    dy_q = rows(cotangent, 0, 0).astype(f32)
    d_mid, grad_ffn_in = rms_back(middle_q, gain_ffn_in, d_normed_q)
    d_middle = dy_q + d_mid
    d_branch, grad_attn_out = rms_back(branch_q, gain_attn_out, d_middle)
    d_branch_low = low(d_branch)
    d_context = low(product_t(d_branch_low, w_out_all)).astype(f32)
    heads = [d_context[:, i * head : (i + 1) * head] for i in range(4)]
    c_got = links.core(jnp.concatenate([heads[1], heads[3]], axis=1))
    y_got = links.y(jnp.concatenate([heads[2], c_got[:, head:]], axis=1))
    grad_context = keep_low(
        to_absolute([[heads[0], y_got[:, :head]], [c_got[:, :head], y_got[:, head:]]])
    )
    d_branch_own = d_branch_low.astype(f32)
    d_branch_y = links.y(d_branch_own)
    d_branch_c = links.core(d_branch_own)
    d_branch_yc = links.core(d_branch_y)
    d_branch_all = jnp.concatenate(
        [d_branch_low, keep_low(d_branch_y), keep_low(d_branch_c), keep_low(d_branch_yc)], axis=0
    )
    context_rel = jnp.concatenate(
        [rows(context_low, 0, 0), rows(context_low, 0, 1), rows(context_low, 1, 0), rows(context_low, 1, 1)], axis=0
    )
    grad_w_out_t = t_product(d_branch_all, context_rel)

    attn_prob = jnp.exp(scores_of() - log_total)
    prob_low = low(attn_prob)
    grad_prob = product_t(grad_context, values_low)
    grad_values = low(t_product(prob_low, grad_context))
    balance = jnp.sum(grad_prob * attn_prob, axis=-1, keepdims=True)
    grad_scores = low(attn_prob * (grad_prob - balance))
    grad_query_n = product(grad_scores, keys_low) * score_scale
    grad_keys_n = t_product(grad_scores, query_low) * score_scale
    d_query, grad_gain_query = rms_back(query_raw, gain_query, grad_query_n)
    d_keys, grad_gain_key = rms_back(keys_raw, gain_key, grad_keys_n)
    d_query, d_keys = low(d_query), low(d_keys)
    d_qkv = jnp.concatenate([d_query, d_keys, grad_values], axis=1)
    w_qkv = jnp.concatenate([w_query, w_key, w_value], axis=1)
    in_parts = []
    for k in range(2):
        rows_k = jnp.concatenate([rows(d_qkv, 0, 1 - k), rows(d_qkv, 1, 1 - k)], axis=0)
        in_parts.append(product_t(rows_k, w_qkv))
    d_normed_in = gather_quarters(in_parts)
    hidden_q = rows(tokens, 0, 0).astype(f32)
    d_in, grad_attn_in = rms_back(hidden_q, gain_attn_in, d_normed_in)
    input_q = low(d_middle + d_in)
    input_own = input_q.astype(f32)
    input_y = links.y(input_own)
    input_c = links.core(input_own)
    input_yc = links.core(input_y)
    input_grad = keep_low(to_absolute([[input_own, input_y], [input_c, input_yc]]))

    grad_qkv = t_product(normed_low, d_qkv)
    grad_w_query, grad_kv = grad_qkv[:, :head], grad_qkv[:, head:]
    kv_keep = jnp.where(c == 0, grad_kv[:, :head], grad_kv[:, head:])
    kv_send = jnp.where(c == 0, grad_kv[:, head:], grad_kv[:, :head])
    kv = kv_keep + links.core(kv_send)
    kv_half = head // 2
    kv_keep = jnp.where(y == 0, kv[:, :kv_half], kv[:, kv_half:])
    kv_send = jnp.where(y == 0, kv[:, kv_half:], kv[:, :kv_half])
    kv = kv_keep + links.y(kv_send)
    attn_grads = jnp.concatenate([grad_w_query, grad_w_out_t, kv], axis=1)

    normed_all = jnp.concatenate(
        [normed_two[0][:quarter], normed_two[1][:quarter], normed_two[0][quarter:], normed_two[1][quarter:], normed_other],
        axis=0,
    )
    d_all = jnp.concatenate(
        [d_outputs[0][:quarter], d_outputs[1][:quarter], d_outputs[0][quarter:], d_outputs[1][quarter:], d_other], axis=0
    )
    gate, upward = product(normed_all, wg_h), product(normed_all, wu_h)
    inner, pull = jax.vjp(activate, gate, upward)
    inner = low(inner)
    d_inner = product_t(d_all, wd_h)
    d_gate, d_up = pull(d_inner)
    ff_grads = [t_product(d_all, inner), t_product(normed_all, low(d_gate)), t_product(normed_all, low(d_up))]

    zh, zl = z // 2, z % 2

    def sum_x(grads, z_half):
        mine = lax.dynamic_index_in_dim(grads, z_half, 0, keepdims=False)
        acc = lax.dynamic_index_in_dim(mine, x, 1, keepdims=False)
        for step in range(1, nx):
            to = lax.dynamic_index_in_dim(mine, (x + step) % nx, 1, keepdims=False)
            acc = acc + links.x(to, step)
        return acc

    def scatter(grads):
        grads = grads.reshape(2, 2, nx, blk, grads.shape[1])
        far = sum_x(grads, 1 - zh)
        near = sum_x(grads, zh)
        return near + links.z2(far)

    ff_sums = []
    for grads in ff_grads:
        got = scatter(grads)
        own = lax.dynamic_index_in_dim(got, zl, 0, keepdims=False)
        other = links.z1(lax.dynamic_index_in_dim(got, 1 - zl, 0, keepdims=False))
        ff_sums.append(
            jnp.where(
                parity == 0, jnp.concatenate([own, other], axis=1), jnp.concatenate([other, own], axis=1)
            )
        )
    grad_w_down, grad_w_gate, grad_w_up = ff_sums[0].T, ff_sums[1], ff_sums[2]

    got = scatter(attn_grads)
    attn_sum = lax.dynamic_index_in_dim(got, zl, 0, keepdims=False) + links.z1(
        lax.dynamic_index_in_dim(got, 1 - zl, 0, keepdims=False)
    )
    grad_w_query = attn_sum[:, :head]
    grad_w_out = attn_sum[:, head : 2 * head].T
    kv_own = attn_sum[:, 2 * head :]
    kv_y = links.y(kv_own)
    kv_wide = jnp.where(y == 0, jnp.concatenate([kv_own, kv_y], axis=1), jnp.concatenate([kv_y, kv_own], axis=1))
    kv_c = links.core(kv_wide)
    grad_w_key = jnp.where(c == 0, kv_wide, kv_c)
    grad_w_value = jnp.where(c == 0, kv_c, kv_wide)

    small = jnp.concatenate(
        [
            grad_attn_in.reshape(links.dp_size, -1),
            grad_attn_out.reshape(links.dp_size, -1),
            grad_ffn_in.reshape(links.dp_size, -1),
            (grad_ffn_out * 0.25).reshape(links.dp_size, -1),
            grad_gain_query.reshape(links.dp_size, -1),
            grad_gain_key.reshape(links.dp_size, -1),
        ],
        axis=1,
    )
    small = small + links.core(small)
    small = small + links.y(small)
    small = small.reshape(2, 2, nx, 1, small.shape[1])
    acc = lax.dynamic_index_in_dim(small, x, 2, keepdims=False)
    for step in range(1, nx):
        acc = acc + links.x(lax.dynamic_index_in_dim(small, (x + step) % nx, 2, keepdims=False), step)
    acc = lax.dynamic_index_in_dim(acc, zh, 0, keepdims=False) + links.z2(
        lax.dynamic_index_in_dim(acc, 1 - zh, 0, keepdims=False)
    )
    acc = lax.dynamic_index_in_dim(acc, zl, 0, keepdims=False) + links.z1(
        lax.dynamic_index_in_dim(acc, 1 - zl, 0, keepdims=False)
    )
    acc = acc.reshape(-1)
    hb = head // links.dp_size
    return (
        layer_out,
        input_grad,
        grad_w_query,
        grad_w_key,
        grad_w_value,
        grad_w_out,
        grad_w_gate,
        grad_w_up,
        grad_w_down,
        acc[:blk],
        acc[blk : 2 * blk],
        acc[2 * blk : 3 * blk],
        acc[3 * blk : 4 * blk],
        acc[4 * blk : 4 * blk + hb],
        acc[4 * blk + hb :],
    )


def solution(mesh):
    links = Links(mesh)
    return jax.shard_map(
        functools.partial(body if links.nx == 2 else body_any, links),
        mesh=mesh,
        in_specs=(
            P("dp", None),
            P("dp"),
            P("dp", None),
            P(None, "tensor"),
            P(),
            P(),
            P("tensor", None),
            P(None, "tensor"),
            P(None, "tensor"),
            P("tensor", None),
            P(),
            P(),
            P(),
            P(),
            P(),
            P(),
        ),
        out_specs=(
            P("dp", None),
            P("dp", None),
            P("dp", "tensor"),
            P("dp", None),
            P("dp", None),
            P("tensor", "dp"),
            P("dp", "tensor"),
            P("dp", "tensor"),
            P("tensor", "dp"),
            P("dp"),
            P("dp"),
            P("dp"),
            P("dp"),
            P("dp"),
            P("dp"),
        ),
        check_vma=False,
    )
```

```python
import functools

import jax
import jax.numpy as jnp
from jax import lax
from jax.experimental import pallas as pl
from jax.experimental.pallas import tpu as pltpu
from jax.sharding import PartitionSpec as P

epsilon = 1e-06
score_scale = 0.0625
NZ = 4

f32 = jnp.float32
bf16 = jnp.bfloat16


def rms_norm(values, gain):
    inverse = lax.rsqrt(jnp.mean(values * values, axis=-1, keepdims=True) + epsilon)
    return values * inverse * (1.0 + gain)


def rms_back(values, gain, grad):
    inverse = lax.rsqrt(jnp.mean(values * values, axis=-1, keepdims=True) + epsilon)
    hat = values * inverse
    scaled = grad * (1.0 + gain)
    back = inverse * (scaled - hat * jnp.mean(scaled * hat, axis=-1, keepdims=True))
    return back, jnp.sum(grad * hat, axis=0)


def product(left, right):
    return jnp.dot(left, right, preferred_element_type=f32)


def product_t(left, right):
    return lax.dot_general(left, right, (((1,), (1,)), ((), ())), preferred_element_type=f32)


def t_product(left, right):
    return lax.dot_general(left, right, (((0,), (0,)), ((), ())), preferred_element_type=f32)


def activate(gate, upward):
    return jax.nn.gelu(gate, approximate=True) * upward


class Links:
    def __init__(self, mesh):
        self.dp_size = mesh.shape["dp"]
        self.nx = self.dp_size // NZ
        tensor = mesh.shape["tensor"]
        self.perm_core = [(t, t ^ 1) for t in range(tensor)]
        self.perm_y = [(t, t ^ 2) for t in range(tensor)]
        nx = self.nx
        self.perm_z1 = [(z * nx + x, (z ^ 1) * nx + x) for z in range(NZ) for x in range(nx)]
        self.perm_z2 = [(z * nx + x, (z ^ 2) * nx + x) for z in range(NZ) for x in range(nx)]

    def core(self, a):
        return lax.ppermute(a, "tensor", self.perm_core)

    def y(self, a):
        return lax.ppermute(a, "tensor", self.perm_y)

    def z1(self, a):
        return lax.ppermute(a, "dp", self.perm_z1)

    def z2(self, a):
        return lax.ppermute(a, "dp", self.perm_z2)

    def x(self, a, step):
        nx = self.nx
        return lax.ppermute(a, "dp", [(z * nx + x, z * nx + (x + step) % nx) for z in range(NZ) for x in range(nx)])


def low(a):
    return a.astype(bf16)


MESH = pl.DeviceIdType.MESH
ANY = pl.BlockSpec(memory_space=pl.ANY)
VMEM = pl.BlockSpec(memory_space=pltpu.VMEM)
TILE, HALF, QUARTER = 256, 128, 256
VMEM_LIMIT = 127 << 19


def spots(nx):
    dp, t = lax.axis_index("dp"), lax.axis_index("tensor")
    z, x = dp // nx, dp % nx
    near = {
        "c": {"tensor": t ^ 1},
        "y": {"tensor": t ^ 2},
        "z1": {"dp": (z ^ 1) * nx + x},
        "z2": {"dp": (z ^ 2) * nx + x},
        "x": {"dp": z * nx + (x ^ 1)},
    }
    return z, x, t // 2, t % 2, near


def remote(src, dst, sems, index, to):
    return pltpu.make_async_remote_copy(
        src_ref=src, dst_ref=dst, send_sem=sems[0].at[index], recv_sem=sems[1].at[index], device_id=to, device_id_type=MESH
    )


def greet(others):
    barrier = pltpu.get_barrier_semaphore()
    for other in others:
        pl.semaphore_signal(barrier, inc=1, device_id=other, device_id_type=MESH)
    pl.semaphore_wait(barrier, len(others))


def tile_row(c, y, i, dc):
    dy = 1 - i // 2
    return pl.multiple_of(((c ^ dc) * 2 + (y ^ dy)) * QUARTER + (i % 2) * HALF, HALF)


def gelu_parts(u):
    k = 0.7978845608028654
    square = u * u
    th = jnp.tanh(k * u * (1.0 + 0.044715 * square))
    side = 0.5 * (1.0 + th)
    return u * side, side + 0.5 * u * (1.0 - th * th) * (k * (1.0 + 3.0 * 0.044715 * square))


def gelu_tanh(u):
    return 0.5 * u * (1.0 + jnp.tanh(0.7978845608028654 * u * (1.0 + 0.044715 * (u * u))))


def gain_row(gains, k):
    return gains[k : k + 1, :]


def forward_kernel(
    nx,
    middle_hbm,
    cotangent,
    gains,
    w_gate_hbm,
    w_up_hbm,
    w_down_hbm,
    normed_hbm,
    other_hbm,
    d_out_hbm,
    d_own_hbm,
    d_first,
    layer_hbm,
    pair_own_hbm,
    for_gate_hbm,
    for_up_hbm,
    gain_grad,
    middle,
    w_gate,
    w_up,
    w_down,
    normed,
    other,
    d_out,
    d_own,
    layer_out,
    out,
    dy,
    inner,
    for_gate,
    for_up,
    part,
    from_core,
    from_y,
    z_stage,
    z_land,
    c_land,
    local,
    stores,
    tile_stores,
    c_send,
    c_recv,
    y_send,
    y_recv,
    z_send,
    z_recv,
):
    z, x, y, c, near = spots(nx)
    core, across, pair = near["c"], near["y"], near["z1"]
    cs, ys, zs = (c_send, c_recv), (y_send, y_recv), (z_send, z_recv)
    first = [
        pltpu.make_async_copy(src, dst, local.at[8 + k])
        for k, (src, dst) in enumerate(
            [(middle_hbm, middle), (w_gate_hbm, w_gate), (w_up_hbm, w_up), (w_down_hbm, w_down)]
        )
    ]
    for copy in first:
        copy.start()
    loads = []
    for i in range(4):
        for dc in range(2):
            copy = pltpu.make_async_copy(
                cotangent.at[pl.ds(tile_row(c, y, i, dc), HALF)],
                dy.at[pl.ds(i * TILE + dc * HALF, HALF)],
                local.at[i * 2 + dc],
            )
            copy.start()
            loads.append(copy)
    greet([core, across, pair])
    columns = w_gate.shape[0]
    cut = pl.cdiv(columns, TILE) * HALF
    for ref in (inner, for_gate, for_up):
        for slot in range(2):
            ref[slot, :, columns:] = jnp.zeros((TILE, 2 * cut - columns), bf16)

    def tile_puts(i):
        slot = i % 2
        at = pl.ds(pl.multiple_of(i * TILE, TILE), TILE)
        mine = pl.ds(pl.multiple_of(z % 2 * cut, HALF), cut)
        return [
            pltpu.make_async_copy(inner.at[slot, :, mine], pair_own_hbm.at[at], tile_stores.at[slot, 0]),
            pltpu.make_async_copy(for_gate.at[slot], for_gate_hbm.at[at], tile_stores.at[slot, 1]),
            pltpu.make_async_copy(for_up.at[slot], for_up_hbm.at[at], tile_stores.at[slot, 2]),
        ]

    def core_copy(i):
        return remote(part.at[i, pl.ds(HALF, HALF)], from_core.at[i], cs, i, core)

    def y_copy(h):
        return remote(part.at[h, pl.ds(0, HALF)], from_y.at[h], ys, h, across)

    def z_copy(i):
        return remote(z_stage.at[i], z_land.at[i], zs, i, pair)

    first_copy = remote(d_own.at[2], d_first, zs, 4, pair)

    def z_forward(i):
        return remote(z_land.at[i], c_land.at[i], cs, 8 + i, core)

    def norm_tile(i, carry):
        at = pl.ds(pl.multiple_of(i * TILE, TILE), TILE)
        m = middle[at, :]
        inverse = lax.rsqrt(jnp.mean(m * m, axis=-1, keepdims=True) + epsilon)
        n = (m * inverse * (1.0 + gain_row(gains, 2))).astype(bf16)
        normed[at, :] = n
        z_stage[i] = n[:HALF].astype(f32)
        z_copy(i).start()
        return carry

    first[0].wait()
    lax.fori_loop(0, 4, norm_tile, 0)
    for copy in first[1:]:
        copy.wait()

    def step(i, carry):
        at = pl.ds(pl.multiple_of(i * TILE, TILE), TILE)
        n = normed[at, :]
        slot = i % 2

        @pl.when(i >= 2)
        def _():
            for copy in tile_puts(i - 2):
                copy.wait()

        for lo in range(0, columns, TILE):
            hi = min(lo + TILE, columns)
            g = product_t(n, w_gate[lo:hi, :])
            u = product_t(n, w_up[lo:hi, :])
            act, slope = gelu_parts(g)
            inner[slot, :, lo:hi] = (act * u).astype(bf16)
            for_gate[slot, :, lo:hi] = (u * slope).astype(bf16)
            for_up[slot, :, lo:hi] = act.astype(bf16)
        part[i] = product(inner[slot, :, :columns], w_down[...])
        for copy in tile_puts(i):
            copy.start()
        core_copy(i).start()
        core_copy(i).wait_recv()
        part[i, :HALF] = part[i, :HALF] + from_core[i]

        @pl.when(i < 2)
        def _():
            y_copy(i).start()

        return carry

    lax.fori_loop(0, 4, step, 0)

    def tile_at(i):
        return pl.ds(pl.multiple_of(i * TILE, TILE), TILE)

    put_normed = pltpu.make_async_copy(normed, normed_hbm, stores.at[8])
    put_layer = pltpu.make_async_copy(layer_out, layer_hbm, stores.at[9])

    def put_own(i):
        return pltpu.make_async_copy(d_own.at[i], d_own_hbm.at[i], stores.at[i])

    def put_d(i):
        return pltpu.make_async_copy(d_out.at[tile_at(i)], d_out_hbm.at[tile_at(i)], stores.at[4 + i])

    def put_other(i):
        return pltpu.make_async_copy(other.at[tile_at(i)], other_hbm.at[tile_at(i)], stores.at[10 + i])

    put_normed.start()
    for i in (2, 3):
        for copy in tile_puts(i):
            copy.wait()
    for copy in loads:
        copy.wait()
    gain_grad[...] = jnp.zeros_like(gain_grad)
    gain = 1.0 + gain_row(gains, 3)

    def finish(i, dc):
        at = pl.ds(pl.multiple_of(i * TILE + dc * HALF, HALF), HALF)
        o, g = out[at, :], dy[at, :].astype(f32)
        inverse = lax.rsqrt(jnp.mean(o * o, axis=-1, keepdims=True) + epsilon)
        hat = o * inverse
        scaled = g * gain
        d = (inverse * (scaled - hat * jnp.mean(scaled * hat, axis=-1, keepdims=True))).astype(bf16)
        d_out[at, :] = d
        gain_grad[...] = gain_grad[...] + jnp.sum((g * hat).reshape(HALF // 8, 8, g.shape[1]), axis=0)
        layer_out[pl.ds(tile_row(c, y, i, dc), HALF), :] = (middle[at, :] + hat * gain).astype(bf16)
        return d

    def half_at(i, dc):
        return pl.ds(pl.multiple_of(i * TILE + dc * HALF, HALF), HALF)

    def spread_y(h):
        return remote(out.at[half_at(2 + h, 0)], out.at[half_at(h, 0)], ys, 2 + h, across)

    def spread_core(i):
        return remote(out.at[half_at(i, 0)], out.at[half_at(i, 1)], cs, 4 + i, core)

    def close_tile(n, carry):
        i = (n + 2) % 4

        @pl.when(n < 2)
        def _():
            y_copy(n).wait_recv()
            out[half_at(i, 0), :] = part[i, :HALF] + from_y[n]
            spread_y(n).start()

        @pl.when(n == 2)
        def _():
            for i in range(3):
                z_copy(i).wait_recv()
                z_forward(i).start()
            for i in range(2):
                take(i)

        @pl.when(n >= 2)
        def _():
            spread_y(i).wait_recv()

        spread_core(i).start()
        d_own[i] = finish(i, 0).astype(f32)

        @pl.when(n == 0)
        def _():
            first_copy.start()

        put_own(i).start()
        spread_core(i).wait_recv()
        finish(i, 1)
        put_d(i).start()
        return carry

    def take(i):
        z_forward(i).wait_recv()
        other[i * TILE : i * TILE + HALF, :] = z_land[i].astype(bf16)
        other[i * TILE + HALF : (i + 1) * TILE, :] = c_land[i].astype(bf16)
        put_other(i).start()

    lax.fori_loop(0, 4, close_tile, 0)
    put_layer.start()
    z_copy(3).wait_recv()
    z_forward(3).start()
    for i in range(2, 4):
        take(i)
    for i in range(4):
        core_copy(i).wait_send()
        z_copy(i).wait_send()
        z_forward(i).wait_send()
        spread_core(i).wait_send()
        put_own(i).wait()
        put_d(i).wait()
        put_other(i).wait()
    for h in range(2):
        y_copy(h).wait_send()
        spread_y(h).wait_send()
    put_normed.wait()
    put_layer.wait()
    first_copy.wait()


def dma(*counts):
    return [pltpu.SemaphoreType.DMA((n,)) for n in counts]


def feed_forward(nx, middle, cotangent, gains, w_gate, w_up, w_down):
    length, width = middle.shape
    columns = pl.cdiv(w_gate.shape[0], TILE) * TILE
    rows_low = jax.ShapeDtypeStruct((length, width), bf16)
    return pl.pallas_call(
        functools.partial(forward_kernel, nx),
        out_shape=(
            rows_low,
            rows_low,
            rows_low,
            jax.ShapeDtypeStruct((4, HALF, width), f32),
            jax.ShapeDtypeStruct((HALF, width), f32),
            rows_low,
            jax.ShapeDtypeStruct((length, columns // 2), bf16),
            jax.ShapeDtypeStruct((length, columns), bf16),
            jax.ShapeDtypeStruct((length, columns), bf16),
            jax.ShapeDtypeStruct((8, width), f32),
        ),
        in_specs=[ANY, ANY, VMEM] + [ANY] * 3,
        out_specs=(ANY,) * 4 + (VMEM, ANY, ANY, ANY, ANY, VMEM),
        scratch_shapes=[pltpu.VMEM((length, width), f32)]
        + [pltpu.VMEM(w_gate.shape, bf16)] * 3
        + [pltpu.VMEM((length, width), bf16)] * 3
        + [
            pltpu.VMEM((4, HALF, width), f32),
            pltpu.VMEM((length, width), bf16),
            pltpu.VMEM((length, width), f32),
            pltpu.VMEM((length, width), bf16),
            pltpu.VMEM((2, TILE, columns), bf16),
            pltpu.VMEM((2, TILE, columns), bf16),
            pltpu.VMEM((2, TILE, columns), bf16),
            pltpu.VMEM((4, TILE, width), f32),
            pltpu.VMEM((4, HALF, width), f32),
            pltpu.VMEM((2, HALF, width), f32),
            pltpu.VMEM((4, HALF, width), f32),
            pltpu.VMEM((4, HALF, width), f32),
            pltpu.VMEM((4, HALF, width), f32),
        ]
        + dma(12, 14)
        + [pltpu.SemaphoreType.DMA((2, 3))]
        + dma(12, 12, 4, 4, 5, 5),
        compiler_params=pltpu.CompilerParams(collective_id=0, has_side_effects=True, vmem_limit_bytes=VMEM_LIMIT),
        name="feed_forward",
    )(middle, cotangent, gains, w_gate, w_up, w_down)


def back_kernel(
    nx,
    d_out_hbm,
    d_own_hbm,
    d_first_hbm,
    for_gate_hbm,
    for_up_hbm,
    other_hbm,
    w_gate_hbm,
    w_up_hbm,
    w_down_hbm,
    w_out_hbm,
    middle_hbm,
    branch_hbm,
    dy_hbm,
    gains,
    d_other_hbm,
    pair_in,
    pair_gates,
    heads_hbm,
    d_branch_hbm,
    d_middle_hbm,
    gain_grads,
    d_other,
    heads,
    d_branch_out,
    d_middle_out,
    puts_sem,
    d_out,
    for_gate,
    for_up,
    other,
    w_gate,
    w_up,
    w_down,
    w_out,
    middle,
    branch,
    dy,
    gates,
    ups,
    inner,
    part,
    from_core,
    from_y,
    z_land,
    c_land,
    loads_sem,
    tiles_sem,
    stores_sem,
    c_send,
    c_recv,
    y_send,
    y_recv,
    z_send,
    z_recv,
):
    z, x, y, c, near = spots(nx)
    core, across, pair = near["c"], near["y"], near["z1"]
    cs, ys, zs = (c_send, c_recv), (y_send, y_recv), (z_send, z_recv)
    parity = z % 2
    real, columns = w_gate_hbm.shape[0], w_gate.shape[0]
    half = columns // 2
    head = heads.shape[2]
    own_row = pl.multiple_of((c * 2 + y) * QUARTER, QUARTER)
    sources = [
        (d_out_hbm, d_out),
        (w_gate_hbm, w_gate.at[pl.ds(0, real)]),
        (w_up_hbm, w_up.at[pl.ds(0, real)]),
        (w_down_hbm, w_down.at[pl.ds(0, real)]),
        (other_hbm, other),
        (w_out_hbm, w_out),
        (middle_hbm.at[pl.ds(2 * TILE, HALF)], middle.at[pl.ds(0, HALF)]),
        (middle_hbm.at[pl.ds(3 * TILE, HALF)], middle.at[pl.ds(HALF, HALF)]),
        (branch_hbm, branch),
        (dy_hbm.at[pl.ds(own_row, QUARTER)], dy),
        (d_first_hbm, z_land.at[2]),
    ]
    loads = [pltpu.make_async_copy(src, dst, loads_sem.at[k]) for k, (src, dst) in enumerate(sources)]
    for copy in loads:
        copy.start()
    if real < columns:
        for ref in (w_gate, w_up, w_down):
            ref[real:, :] = jnp.zeros((columns - real, ref.shape[1]), bf16)
    greet([core, across, pair])

    def core_copy(i):
        return remote(part.at[i, pl.ds(HALF, HALF)], from_core.at[i], cs, i, core)

    def y_copy(h):
        return remote(part.at[h, pl.ds(0, HALF)], from_y.at[h], ys, h, across)

    def z_copy(i):
        return remote(d_own_hbm.at[i], z_land.at[i], zs, i, pair)

    def z_forward(i):
        return remote(z_land.at[i], c_land.at[i], cs, 4 + i, core)

    for i in (3, 0, 1):
        z_copy(i).start()
    def tile_loads(i):
        slot = i % 2
        at = pl.ds(pl.multiple_of(i * TILE, TILE), TILE)
        return [
            pltpu.make_async_copy(for_gate_hbm.at[at], for_gate.at[slot], tiles_sem.at[slot, 0]),
            pltpu.make_async_copy(for_up_hbm.at[at], for_up.at[slot], tiles_sem.at[slot, 1]),
        ]

    for i in range(2):
        for copy in tile_loads(i):
            copy.start()
    for copy in loads[:4]:
        copy.wait()

    mine = pl.multiple_of(parity * half, HALF)

    def stores(i, base):
        slot = i % 2
        at = pl.ds(pl.multiple_of(base + i * TILE, TILE), TILE)
        pick = pl.ds(mine, half)
        first = []
        if base:
            first = [
                pltpu.make_async_copy(
                    inner.at[slot], pair_in.at[pl.ds(pl.multiple_of(i * TILE, TILE), TILE)], stores_sem.at[slot, 0]
                )
            ]
        return first + [
            pltpu.make_async_copy(gates.at[slot, :, pick], pair_gates.at[at, pl.ds(0, half)], stores_sem.at[slot, 1]),
            pltpu.make_async_copy(ups.at[slot, :, pick], pair_gates.at[at, pl.ds(half, half)], stores_sem.at[slot, 2]),
        ]

    def piece(n, d, slot, at, own):
        g = product_t(n, w_gate[at, :])
        u = product_t(n, w_up[at, :])
        di = product_t(d, w_down[at, :])
        act, slope = gelu_parts(g)
        inner[slot, :, own] = (act * u).astype(bf16)
        gates[slot, :, at] = (di * u * slope).astype(bf16)
        ups[slot, :, at] = (di * act).astype(bf16)

    def own_tile(i, carry):
        at = pl.ds(pl.multiple_of(i * TILE, TILE), TILE)
        slot = i % 2

        @pl.when(i >= 2)
        def _():
            for copy in stores(i - 2, 0):
                copy.wait()

        for copy in tile_loads(i):
            copy.wait()
        d = d_out[at, :]
        for lo in range(0, columns, TILE):
            cols = pl.ds(lo, TILE)
            di = product_t(d, w_down[cols, :])
            gates[slot, :, cols] = (di * for_gate[slot, :, cols].astype(f32)).astype(bf16)
            ups[slot, :, cols] = (di * for_up[slot, :, cols].astype(f32)).astype(bf16)

        @pl.when(i < 2)
        def _():
            for copy in tile_loads(i + 2):
                copy.start()

        for copy in stores(i, 0):
            copy.start()
        part[i] = product(gates[slot], w_gate[...]) + product(ups[slot], w_up[...])
        core_copy(i).start()

        @pl.when(i >= 1)
        def _():
            both(i - 1)

        return carry

    def both(i):
        core_copy(i).wait_recv()
        part[i, :HALF] = part[i, :HALF] + from_core[i]

        @pl.when(i < 2)
        def _():
            y_copy(i).start()

    lax.fori_loop(0, 4, own_tile, 0)
    for copy in loads[4:]:
        copy.wait()

    def put_other(i):
        at = pl.ds(pl.multiple_of(i * TILE, TILE), TILE)
        return pltpu.make_async_copy(d_other.at[at], d_other_hbm.at[at], puts_sem.at[i])

    puts = [
        pltpu.make_async_copy(src, dst, puts_sem.at[4 + k])
        for k, (src, dst) in enumerate(
            [(heads, heads_hbm), (d_branch_out, d_branch_hbm), (d_middle_out, d_middle_hbm)]
        )
    ]

    def other_tile(n, carry):
        i, slot = (n + 2) % 4, n % 2

        @pl.when(n > 0)
        def _():
            z_copy(i).wait_recv()

        @pl.when(n >= 1)
        def _():
            z_forward(i).start()

        @pl.when(n < 2)
        def _():
            for copy in stores(i, 0):
                copy.wait()

        @pl.when(n >= 2)
        def _():
            for copy in stores(n, d_out.shape[0]):
                copy.wait()

        z_forward(i).wait_recv()
        lo = pl.multiple_of(i * TILE, TILE)
        d_other[pl.ds(lo, HALF), :] = z_land[i].astype(bf16)
        d_other[pl.ds(lo + HALF, HALF), :] = c_land[i].astype(bf16)
        put_other(i).start()
        n, d = other[pl.ds(lo, TILE), :], d_other[pl.ds(lo, TILE), :]
        for off in range(0, half, TILE):
            size = min(TILE, half - off)
            piece(n, d, slot, pl.ds(pl.multiple_of(mine + off, HALF), size), pl.ds(off, size))
        for copy in stores(i, d_out.shape[0]):
            copy.start()
        return carry

    z_forward(2).start()
    both(jnp.int32(3))
    lax.fori_loop(0, 3, other_tile, 0)

    gain_grads[...] = jnp.zeros_like(gain_grads)

    def fold(a):
        return jnp.sum(a.reshape(a.shape[0] // 8, 8, a.shape[1]), axis=0)

    def of_quarter(h, carry):
        y_copy(h).wait_recv()
        at = pl.ds(pl.multiple_of(h * HALF, HALF), HALF)
        grad = part[2 + h, :HALF] + from_y[h]
        m = middle[at, :]
        inverse = lax.rsqrt(jnp.mean(m * m, axis=-1, keepdims=True) + epsilon)
        hat = m * inverse
        scaled = grad * (1.0 + gain_row(gains, 2))
        d_middle = dy[at, :].astype(f32) + inverse * (scaled - hat * jnp.mean(scaled * hat, axis=-1, keepdims=True))
        gain_grads[0] = gain_grads[0] + fold(grad * hat)
        d_middle_out[at, :] = d_middle
        b = branch[at, :]
        inverse = lax.rsqrt(jnp.mean(b * b, axis=-1, keepdims=True) + epsilon)
        hat = b * inverse
        scaled = d_middle * (1.0 + gain_row(gains, 1))
        d_low = (inverse * (scaled - hat * jnp.mean(scaled * hat, axis=-1, keepdims=True))).astype(bf16)
        gain_grads[1] = gain_grads[1] + fold(d_middle * hat)
        d_branch_out[at, :] = d_low.astype(f32)
        for k in range(4):
            heads[k, at, :] = product_t(d_low, w_out[k * head : (k + 1) * head, :]).astype(bf16).astype(f32)
        return carry

    lax.fori_loop(0, 2, of_quarter, 0)
    for copy in puts:
        copy.start()
    lax.fori_loop(3, 4, other_tile, 0)
    for i in (0, 1):
        for copy in stores(i, d_out.shape[0]):
            copy.wait()
    for copy in puts + [put_other(i) for i in range(4)]:
        copy.wait()
    for i in (3, 0, 1):
        z_copy(i).wait_send()
    for i in range(4):
        core_copy(i).wait_send()
        z_forward(i).wait_send()
    for h in range(2):
        y_copy(h).wait_send()


def feed_back(nx, d_out, d_own, d_first, for_gate, for_up, other, w_gate, w_up, w_down, w_out, middle, branch, dy, gains):
    length, width = d_out.shape
    columns = pl.cdiv(w_gate.shape[0], TILE) * TILE
    head = w_out.shape[0] // 4
    return pl.pallas_call(
        functools.partial(back_kernel, nx),
        out_shape=(
            jax.ShapeDtypeStruct((length, width), bf16),
            jax.ShapeDtypeStruct((length, columns // 2), bf16),
            jax.ShapeDtypeStruct((2 * length, columns), bf16),
            jax.ShapeDtypeStruct((4, QUARTER, head), f32),
            jax.ShapeDtypeStruct((QUARTER, width), f32),
            jax.ShapeDtypeStruct((QUARTER, width), f32),
            jax.ShapeDtypeStruct((2, 8, width), f32),
        ),
        in_specs=[ANY] * 13 + [VMEM],
        out_specs=(ANY,) * 6 + (VMEM,),
        scratch_shapes=[
            pltpu.VMEM((length, width), bf16),
            pltpu.VMEM((4, QUARTER, head), f32),
            pltpu.VMEM((QUARTER, width), f32),
            pltpu.VMEM((QUARTER, width), f32),
            pltpu.SemaphoreType.DMA((7,)),
            pltpu.VMEM((length, width), bf16),
            pltpu.VMEM((2, TILE, columns), bf16),
            pltpu.VMEM((2, TILE, columns), bf16),
            pltpu.VMEM((length, width), bf16),
            pltpu.VMEM((columns, width), bf16),
            pltpu.VMEM((columns, width), bf16),
            pltpu.VMEM((columns, width), bf16),
            pltpu.VMEM((4 * head, width), bf16),
            pltpu.VMEM((QUARTER, width), f32),
            pltpu.VMEM((QUARTER, width), f32),
            pltpu.VMEM((QUARTER, width), bf16),
            pltpu.VMEM((2, TILE, columns), bf16),
            pltpu.VMEM((2, TILE, columns), bf16),
            pltpu.VMEM((2, TILE, columns // 2), bf16),
            pltpu.VMEM((4, TILE, width), f32),
            pltpu.VMEM((4, HALF, width), f32),
            pltpu.VMEM((2, HALF, width), f32),
            pltpu.VMEM((4, HALF, width), f32),
            pltpu.VMEM((4, HALF, width), f32),
            pltpu.SemaphoreType.DMA((12,)),
            pltpu.SemaphoreType.DMA((2, 2)),
            pltpu.SemaphoreType.DMA((2, 3)),
        ]
        + dma(8, 8, 2, 2, 4, 4),
        compiler_params=pltpu.CompilerParams(collective_id=1, has_side_effects=True, vmem_limit_bytes=VMEM_LIMIT),
        name="feed_back",
    )(
        d_out,
        d_own,
        d_first,
        for_gate,
        for_up,
        other,
        w_gate,
        w_up,
        w_down,
        w_out,
        middle,
        branch,
        dy,
        gains,
    )


def visible_pairs(shape, i, segments):
    row = lax.broadcasted_iota(jnp.int32, shape, 0) + i * TILE
    col = lax.broadcasted_iota(jnp.int32, shape, 1)
    first = jnp.sum((segments[...] == 0).astype(jnp.int32), axis=1, keepdims=True)
    return (row >= col) & ((row < first) == (col < first))


def attention_kernel(
    nx,
    tokens,
    w_query,
    w_key,
    w_value,
    w_out,
    segments,
    gain_0,
    gain_1,
    gain_2,
    gain_3,
    gain_4,
    gain_5,
    normed_hbm,
    query_hbm,
    keys_hbm,
    values_hbm,
    query_raw_hbm,
    keys_raw_hbm,
    log_total_hbm,
    context_hbm,
    w_out_all_hbm,
    middle_hbm,
    branch,
    gains,
    middle,
    normed,
    query,
    keys,
    values,
    query_raw,
    keys_raw,
    log_total,
    context,
    w_out_all,
    stores,
    out_own,
    out_land,
    context_own,
    context_core,
    context_land,
    context_all,
    c_send,
    c_recv,
    y_send,
    y_recv,
    x_send,
    x_recv,
):
    z, x, y, c, near = spots(nx)
    cs, ys, xs = (c_send, c_recv), (y_send, y_recv), (x_send, x_recv)
    length, width = tokens.shape
    head = w_query.shape[1]
    given = (gain_0, gain_1, gain_2, gain_3, gain_4, gain_5)
    gain_loads = [
        pltpu.make_async_copy(ref, gains.at[k, pl.ds(0, ref.shape[0])], stores.at[k]) for k, ref in enumerate(given)
    ]
    for copy in gain_loads:
        copy.start()
    out_own[...] = w_out[...].astype(f32)
    greet([near[k] for k in ("c", "y", "x")])
    mine = pl.ds(pl.multiple_of(x * (head // 2), 8), head // 2)
    out_y = remote(out_own.at[mine], out_land.at[0, mine], ys, 0, near["y"])
    out_x = remote(out_land.at[0, mine], out_land.at[0, mine], xs, 0, near["x"])
    out_c = remote(out_own, out_land.at[1], cs, 0, near["c"])
    out_yc = remote(out_land.at[0], out_land.at[2], cs, 1, near["c"])
    out_y.start()
    out_c.start()
    w_out_all[:head, :] = w_out[...]

    for copy in gain_loads:
        copy.wait()

    def norm(v, gain):
        return v * lax.rsqrt(jnp.mean(v * v, axis=-1, keepdims=True) + epsilon) * (1.0 + gain)

    def inputs(i, carry):
        at = pl.ds(pl.multiple_of(i * TILE, TILE), TILE)
        n = norm(tokens[at, :].astype(f32), gain_row(gains, 0)).astype(bf16)
        normed[at, :] = n
        raw = product(n, w_query[...])
        query_raw[at, :] = raw
        query[at, :] = norm(raw, gain_row(gains, 4)[:, :head]).astype(bf16)
        raw = product(n, w_key[...])
        keys_raw[at, :] = raw
        keys[at, :] = norm(raw, gain_row(gains, 5)[:, :head]).astype(bf16)
        values[at, :] = product(n, w_value[...]).astype(bf16)
        return carry

    lax.fori_loop(0, length // TILE, inputs, 0)
    for i in range(length // TILE):
        at, seen = slice(i * TILE, (i + 1) * TILE), (i + 1) * TILE
        s = product_t(query[at, :], keys[:seen, :]) * score_scale
        s = jnp.where(visible_pairs(s.shape, i, segments), s, -1e30)
        largest = jnp.max(s, axis=-1, keepdims=True)
        e = jnp.exp(s - largest)
        total = jnp.sum(e, axis=-1, keepdims=True)
        log_total[at, :] = largest + jnp.log(total)
        low_context = product((e / total).astype(bf16), values[:seen, :]).astype(bf16)
        context[at, :] = low_context
        context_own[at, :] = low_context.astype(f32)

    out_copies = []

    def put(src, dst):
        copy = pltpu.make_async_copy(src, dst, stores.at[len(out_copies)])
        copy.start()
        out_copies.append(copy)

    span = length // 2
    to_core = remote(context_own.at[pl.ds(pl.multiple_of((1 - c) * span, span), span)], context_core, cs, 2, near["c"])
    to_core.start()

    def local(i, other):
        dy = 1 - i // 2
        return pl.multiple_of(((y ^ other) ^ dy) * QUARTER + (i % 2) * HALF, HALF)

    def context_copy(i, k):
        if k == 0:
            src = context_own.at[pl.ds(pl.multiple_of(c * span + local(i, 1), HALF), HALF)]
        else:
            src = context_core.at[pl.ds(local(i, 1), HALF)]
        return remote(src, context_land.at[k, i], ys, 1 + 2 * i + k, near["y"])

    context_copy(0, 0).start()
    for src, dst in (
        (normed, normed_hbm),
        (query, query_hbm),
        (keys, keys_hbm),
        (values, values_hbm),
        (query_raw, query_raw_hbm),
        (keys_raw, keys_raw_hbm),
        (log_total, log_total_hbm),
        (context, context_hbm),
    ):
        put(src, dst)
    out_y.wait_recv()
    out_x.start()
    to_core.wait_recv()
    for i in range(4):
        for k in range(2):
            if i + k > 0:
                context_copy(i, k).start()
    out_c.wait_recv()
    w_out_all[2 * head : 3 * head, :] = out_land[1].astype(bf16)
    for i in range(4):
        rows = pl.ds(i * HALF, HALF)
        context_all[rows, :head] = context[pl.ds(pl.multiple_of(c * span + local(i, 0), HALF), HALF), :]
        context_all[rows, 2 * head : 3 * head] = context_core[pl.ds(local(i, 0), HALF), :].astype(bf16)
    out_x.wait_recv()
    out_yc.start()
    w_out_all[head : 2 * head, :] = out_land[0].astype(bf16)
    out_yc.wait_recv()
    w_out_all[3 * head :, :] = out_land[2].astype(bf16)
    put(w_out_all, w_out_all_hbm)

    def middle_copy(i):
        at = pl.multiple_of(i * TILE, TILE)
        return remote(middle.at[pl.ds(at, HALF)], middle.at[pl.ds(at + HALF, HALF)], cs, 3 + i, near["c"])

    def middle_tile(i, carry):
        rows = pl.ds(pl.multiple_of(i * HALF, HALF), HALF)
        context_copy(i, 0).wait_recv()
        context_all[rows, head : 2 * head] = context_land[0, i].astype(bf16)
        context_copy(i, 1).wait_recv()
        context_all[rows, 3 * head :] = context_land[1, i].astype(bf16)
        b = product(context_all[rows, :], w_out_all[...])
        branch[i % 2] = b
        hidden = tokens[pl.ds(pl.multiple_of(c * span + local(i, 0), HALF), HALF), :].astype(f32)
        middle[pl.ds(pl.multiple_of(i * TILE, TILE), HALF), :] = hidden + norm(b, gain_row(gains, 1))
        middle_copy(i).start()
        return carry

    lax.fori_loop(0, 4, middle_tile, 0)
    for i in range(4):
        middle_copy(i).wait()
        put(middle.at[pl.ds(i * TILE, TILE)], middle_hbm.at[pl.ds(i * TILE, TILE)])
        for k in range(2):
            context_copy(i, k).wait_send()
    for copy in (out_y, out_x, out_c, out_yc, to_core):
        copy.wait_send()
    for copy in out_copies:
        copy.wait()


def attend(nx, tokens, w_query, w_key, w_value, w_out, segment_ids, *gains):
    length, width = tokens.shape
    head = w_query.shape[1]
    of_head = jax.ShapeDtypeStruct((length, head), bf16)
    raw = jax.ShapeDtypeStruct((length, head), f32)
    return pl.pallas_call(
        functools.partial(attention_kernel, nx),
        out_shape=(
            jax.ShapeDtypeStruct((length, width), bf16),
            of_head,
            of_head,
            of_head,
            raw,
            raw,
            jax.ShapeDtypeStruct((length, 1), f32),
            of_head,
            jax.ShapeDtypeStruct((4 * head, width), bf16),
            jax.ShapeDtypeStruct((length, width), f32),
            jax.ShapeDtypeStruct((2, HALF, width), f32),
            jax.ShapeDtypeStruct((8, width), f32),
        ),
        in_specs=[VMEM] * 6 + [ANY] * 6,
        out_specs=(ANY,) * 10 + (VMEM,) * 2,
        scratch_shapes=[
            pltpu.VMEM((length, width), f32),
            pltpu.VMEM((length, width), bf16),
            pltpu.VMEM((length, head), bf16),
            pltpu.VMEM((length, head), bf16),
            pltpu.VMEM((length, head), bf16),
            pltpu.VMEM((length, head), f32),
            pltpu.VMEM((length, head), f32),
            pltpu.VMEM((length, 1), f32),
            pltpu.VMEM((length, head), bf16),
            pltpu.VMEM((4 * head, width), bf16),
            pltpu.SemaphoreType.DMA((13,)),
            pltpu.VMEM((head, width), f32),
            pltpu.VMEM((3, head, width), f32),
            pltpu.VMEM((length, head), f32),
            pltpu.VMEM((length // 2, head), f32),
            pltpu.VMEM((2, 4, HALF, head), f32),
            pltpu.VMEM((length // 2, 4 * head), bf16),
        ]
        + dma(7, 7, 9, 9, 1, 1),
        compiler_params=pltpu.CompilerParams(collective_id=3, has_side_effects=True, vmem_limit_bytes=VMEM_LIMIT),
        name="attend",
    )(
        tokens,
        w_query,
        w_key,
        w_value,
        w_out,
        segment_ids.reshape(1, length),
        *gains,
    )


def reduce_kernel(
    nx,
    d_out_hbm,
    d_other_hbm,
    normed_hbm,
    other_hbm,
    pair_own_hbm,
    pair_other_hbm,
    pair_gates_hbm,
    d_branch_hbm,
    d_middle_hbm,
    tokens_hbm,
    normed_in_hbm,
    query_hbm,
    keys_hbm,
    values_hbm,
    query_raw_hbm,
    keys_raw_hbm,
    context_hbm,
    heads_hbm,
    w_query_hbm,
    w_key_hbm,
    w_value_hbm,
    log_total,
    segments,
    gain_rows,
    of_ffn_out,
    of_middle,
    down_out,
    gate_out,
    up_out,
    query_out,
    out_out,
    key_out,
    value_out,
    input_grad,
    gains,
    input_stage,
    ff_stage,
    dw,
    x_land,
    z2_land,
    z1_land,
    from_core,
    from_y,
    branch_land,
    input_own,
    input_land,
    d_qkv,
    attn,
    attn_z1,
    attn_x,
    attn_z2,
    kv_core,
    kv_across,
    kv_own,
    kv_y,
    kv_wide,
    kv_wide_core,
    gains_land,
    heads_mine,
    heads_y,
    got_c,
    got_y,
    loads,
    c_send,
    c_recv,
    y_send,
    y_recv,
    x_send,
    x_recv,
    z2_send,
    z2_recv,
    z1_send,
    z1_recv,
):
    z, x, y, c, near = spots(nx)
    zh, zl = z // 2, z % 2
    cs, ys, xs = (c_send, c_recv), (y_send, y_recv), (x_send, x_recv)
    z2s, z1s = (z2_send, z2_recv), (z1_send, z1_recv)
    length, width = d_out_hbm.shape
    half = pair_own_hbm.shape[1]
    head = query_hbm.shape[1]
    blk = x_land.shape[1]
    own_row = pl.multiple_of((c * 2 + y) * QUARTER, QUARTER)

    def block(a, b):
        return pl.ds(pl.multiple_of(b * blk, 8), blk)

    def quarter_rows(dc, dy):
        return pl.ds(pl.multiple_of(((c ^ dc) * 2 + (y ^ dy)) * QUARTER, QUARTER), QUARTER)

    heads_in = pltpu.make_async_copy(heads_hbm.at[0], heads_mine, loads.at[6])
    heads_in_y = pltpu.make_async_copy(heads_hbm.at[1], heads_y.at[0], loads.at[7])
    heads_c_copy = remote(heads_hbm.at[pl.ds(2, 2)], got_c, cs, 11, near["c"])
    heads_y_copy = remote(heads_y, got_y, ys, 7, near["y"])

    branch_y = remote(d_branch_hbm, branch_land.at[0], ys, 0, near["y"])
    branch_c = remote(d_branch_hbm, branch_land.at[1], cs, 0, near["c"])
    branch_fwd = remote(branch_land.at[0], branch_land.at[2], cs, 1, near["c"])

    def place(n):
        return n // 2 * 2 + (1 - zl if n % 2 == 0 else zl)

    def owner(n):
        return 2 * (1 - zh if n < 2 else zh) + (1 - zl if n % 2 == 0 else zl)

    def x_copy(m, n):
        slot = m * 4 + place(n)
        return remote(dw.at[m, block(dw, owner(n) * 2 + (1 - x))], x_land.at[slot], xs, slot, near["x"])

    def z2_copy(m, n):
        slot = m * 2 + place(n)
        return remote(dw.at[m, block(dw, owner(n) * 2 + x)], z2_land.at[slot], z2s, slot, near["z2"])

    def z1_copy(m):
        return remote(dw.at[m, block(dw, (2 * zh + 1 - zl) * 2 + x)], z1_land.at[m], z1s, m, near["z1"])

    def start_x(*blocks):
        for m, j in blocks:
            x_copy(m, j).start()

    arrived = set()

    def wait_x(m, j):
        if (m, j) not in arrived:
            arrived.add((m, j))
            x_copy(m, j).wait_recv()

    inner = (z == 1) | (z == 2)

    def far(*blocks):
        for m, k in blocks:
            wait_x(m, k)
            rows = block(dw, owner(k) * 2 + x)
            dw[m, rows, :] = dw[m, rows, :] + x_land[m * 4 + place(k)]

            @pl.when(inner)
            def _():
                z2_copy(m, k).start()

    def outer(m, k):
        @pl.when(jnp.logical_not(inner))
        def _():
            z2_copy(m, k).start()

    def close(m):
        for k in range(2):
            wait_x(m, 2 + k)
            z2_copy(m, k).wait_recv()
            rows = block(dw, owner(2 + k) * 2 + x)
            dw[m, rows, :] = dw[m, rows, :] + x_land[m * 4 + place(2 + k)] + z2_land[m * 2 + place(k)]
            if k == 0:
                z1_copy(m).start()

    def finish(m, ref):
        z1_copy(m).wait_recv()
        own, other = dw[m, block(dw, (2 * zh + zl) * 2 + x), :], z1_land[m]
        ff_stage[:, :half] = jnp.where(zl == 0, own, other)
        ff_stage[:, half:] = jnp.where(zl == 0, other, own)[:, : ref.shape[1] - half]
        copy = pltpu.make_async_copy(ff_stage, ref, loads.at[1])
        copy.start()
        copy.wait()

    def copies(pairs):
        started = [pltpu.make_async_copy(src, dst, loads.at[k]) for k, (src, dst) in enumerate(pairs)]
        for copy in started:
            copy.start()
        return started

    def weights(left, right):
        far_size = pl.cdiv(width // 2, HALF) * HALF
        far_at = pl.multiple_of((1 - zh) * (width - far_size), HALF)
        near_at = pl.multiple_of(zh * far_size, HALF)

        def piece(m, lo, at, size):
            rows = pl.ds(pl.multiple_of(at, HALF), size)
            cols = pl.ds(pl.multiple_of(lo, HALF), half)
            dw[m, rows, :] = t_product(left[:, rows], right[:, cols])

        def form(m, lo, at, size):
            for off in range(0, size, 2 * HALF):
                piece(m, lo, at + off, 2 * HALF)

        first_at = owner(0) * 2 * blk // HALF * HALF
        second_at = jnp.where(first_at == far_at, far_at + 3 * HALF, far_at)

        def form_first(m, lo):
            piece(m, lo, first_at, 3 * HALF)
            start_x((m, 0))
            piece(m, lo, second_at, far_size - 3 * HALF)

        waits = copies(
            [
                (d_out_hbm, left.at[pl.ds(0, length)]),
                (d_other_hbm, left.at[pl.ds(length, length)]),
                (pair_own_hbm, right.at[pl.ds(0, length), pl.ds(0, half)]),
                (pair_other_hbm, right.at[pl.ds(length, length), pl.ds(0, half)]),
            ]
        )
        heads_in.start()
        heads_in_y.start()
        greet([near[k] for k in ("c", "y", "x", "z2", "z1")])
        heads_c_copy.start()
        for copy in waits:
            copy.wait()
        form_first(0, 0)
        start_x((0, 1))
        heads_c_copy.wait_recv()
        heads_in_y.wait()
        heads_y[1] = got_c[1]
        heads_y_copy.start()
        branch_y.start()
        branch_c.start()
        form(0, 0, near_at, width - far_size)
        for copy in copies(
            [
                (normed_hbm, left.at[pl.ds(0, length)]),
                (other_hbm, left.at[pl.ds(length, length)]),
                (pair_gates_hbm, right),
            ]
        ):
            copy.wait()
        def form_far(m, carry):
            form_first(m, (m - 1) * half)
            start_x((m, 1))
            return carry

        def form_near(m, carry):
            form(m, (m - 1) * half, near_at, width - far_size)
            return carry

        lax.fori_loop(1, 3, form_far, 0)
        far((0, 0))
        outer(0, 0)
        lax.fori_loop(1, 3, form_near, 0)
        start_x((0, 2), (0, 3), (1, 2), (1, 3), (2, 2), (2, 3))

    pl.run_scoped(weights, pltpu.VMEM((2 * length, width), bf16), pltpu.VMEM((2 * length, 2 * half), bf16))

    def total_of(a):
        return jnp.sum(a, axis=0, keepdims=True)

    gains[...] = jnp.zeros_like(gains)
    gains[1:2, :] = total_of(of_middle[1])
    gains[2:3, :] = total_of(of_middle[0])
    gains[3:4, :] = 0.25 * total_of(of_ffn_out[...])

    def back_norm(raw, gain, grad):
        inverse = lax.rsqrt(jnp.mean(raw * raw, axis=-1, keepdims=True) + epsilon)
        hat = raw * inverse
        scaled = grad * (1.0 + gain)
        return inverse * (scaled - hat * jnp.mean(scaled * hat, axis=-1, keepdims=True)), grad * hat

    def attention(query, keys, values, query_raw, keys_raw, grad_context, d_keys, d_values):
        for copy in copies(
            [
                (query_hbm, query),
                (keys_hbm, keys),
                (values_hbm, values),
                (query_raw_hbm, query_raw),
                (keys_raw_hbm, keys_raw),
            ]
        ):
            copy.wait()
        heads_in.wait()
        grad_context[quarter_rows(0, 0), :] = heads_mine[...].astype(bf16)
        grad_context[quarter_rows(1, 0), :] = got_c[0].astype(bf16)
        heads_y_copy.wait_recv()
        grad_context[quarter_rows(0, 1), :] = got_y[0].astype(bf16)
        grad_context[quarter_rows(1, 1), :] = got_y[1].astype(bf16)
        d_keys[...] = jnp.zeros_like(d_keys)
        d_values[...] = jnp.zeros_like(d_values)

        def back_tile(seen, i, carry):
            at = pl.ds(pl.multiple_of(i * TILE, TILE), TILE)
            q, k = query[at, :], keys[:seen, :]
            s = product_t(q, k) * score_scale
            p = jnp.exp(jnp.where(visible_pairs(s.shape, i, segments), s, -1e30) - log_total[at, :])
            g = grad_context[at, :]
            dp = product_t(g, values[:seen, :])
            balance = jnp.sum(dp * p, axis=-1, keepdims=True)
            ds = (p * (dp - balance)).astype(bf16)
            dq, of_gain = back_norm(query_raw[at, :], gain_row(gain_rows, 4)[:, :head], product(ds, k) * score_scale)
            d_qkv[at, :head] = dq.astype(bf16)
            gains[4:5, :head] = gains[4:5, :head] + jnp.sum(of_gain, axis=0, keepdims=True)
            d_keys[:seen, :] = d_keys[:seen, :] + t_product(ds, q)
            d_values[:seen, :] = d_values[:seen, :] + t_product(p.astype(bf16), g)
            return carry

        tiles = length // TILE
        lax.fori_loop(0, tiles // 2, functools.partial(back_tile, length // 2), 0)
        lax.fori_loop(tiles // 2, tiles, functools.partial(back_tile, length), 0)

        def keys_tile(i, carry):
            at = pl.ds(pl.multiple_of(i * TILE, TILE), TILE)
            dk, of_gain = back_norm(keys_raw[at, :], gain_row(gain_rows, 5)[:, :head], d_keys[at, :] * score_scale)
            d_qkv[at, head : 2 * head] = dk.astype(bf16)
            gains[5:6, :head] = gains[5:6, :head] + jnp.sum(of_gain, axis=0, keepdims=True)
            d_qkv[at, 2 * head :] = d_values[at, :].astype(bf16)
            return carry

        lax.fori_loop(0, tiles, keys_tile, 0)

    pl.run_scoped(
        attention,
        pltpu.VMEM((length, head), bf16),
        pltpu.VMEM((length, head), bf16),
        pltpu.VMEM((length, head), bf16),
        pltpu.VMEM((length, head), f32),
        pltpu.VMEM((length, head), f32),
        pltpu.VMEM((length, head), bf16),
        pltpu.VMEM((length, head), f32),
        pltpu.VMEM((length, head), f32),
    )
    far((0, 1))

    def put_input(dc, dy):
        copy = pltpu.make_async_copy(input_stage, input_grad.at[quarter_rows(dc, dy)], loads.at[0])
        copy.start()
        copy.wait()

    def attn_z1_copy(i):
        b = (2 * (i // 2) + 1 - zl) * 2 + i % 2
        return remote(attn.at[block(attn, b)], attn_z1.at[i], z1s, 3 + i, near["z1"])

    def attn_x_copy(j):
        b = (2 * (zh ^ j) + zl) * 2 + 1 - x
        return remote(attn.at[block(attn, b)], attn_x.at[j], xs, 12 + j, near["x"])

    attn_z2_copy = remote(attn.at[block(attn, (2 * (1 - zh) + zl) * 2 + x)], attn_z2, z2s, 6, near["z2"])

    input_y = remote(input_own, input_land.at[0], ys, 4, near["y"])
    input_c = remote(input_own, input_land.at[1], cs, 7, near["c"])
    input_fwd = remote(input_land.at[0], input_land.at[2], cs, 8, near["c"])

    hops = [
        remote(gains, gains_land.at[k], sems, index, near[to])
        for k, (sems, index, to) in enumerate([(cs, 10, "c"), (ys, 6, "y"), (xs, 14, "x"), (z1s, 7, "z1"), (z2s, 7, "z2")])
    ]

    def hop(k):
        hops[k].start()

    def arrive(k):
        hops[k].wait()
        gains[...] = gains[...] + gains_land[k]

    def rest(w_qkv, part, kv_halves):
        def of_inputs(normed_in, kv):
            for copy in copies([(normed_in_hbm, normed_in)]):
                copy.wait()
            for k in range(2):
                kv[k] = t_product(normed_in[...], d_qkv[:, (1 + k) * head : (2 + k) * head])
            to_core = remote(kv.at[1 - c], kv_core, cs, 6, near["c"])
            to_core.start()
            attn[:, :head] = t_product(normed_in[...], d_qkv[:, :head])
            to_core.wait_recv()
            for k in range(2):
                lanes = slice(k * (head // 2), (k + 1) * (head // 2))
                kv_halves[k] = kv[c, :, lanes] + kv_core[:, lanes]
            to_core.wait_send()

        pl.run_scoped(of_inputs, pltpu.VMEM((length, width), bf16), pltpu.VMEM((2, width, head), f32))
        to_y = remote(kv_halves.at[1 - y], kv_across, ys, 3, near["y"])
        to_y.start()
        for copy in copies(
            [
                (w_query_hbm, w_qkv.at[:, pl.ds(0, head)]),
                (w_key_hbm, w_qkv.at[:, pl.ds(head, head)]),
                (w_value_hbm, w_qkv.at[:, pl.ds(2 * head, head)]),
            ]
        ):
            copy.wait()

        def core_copy(i):
            return remote(part.at[i, pl.ds(HALF, HALF)], from_core.at[i], cs, 2 + i, near["c"])

        def y_copy(h):
            return remote(part.at[h, pl.ds(0, HALF)], from_y.at[h], ys, 1 + h, near["y"])

        def tile(i, carry):
            for dc in range(2):
                rows = d_qkv[pl.ds(tile_row(c, y, i, dc), HALF), :]
                part[i, dc * HALF : (dc + 1) * HALF] = product_t(rows, w_qkv[...])
            core_copy(i).start()
            core_copy(i).wait_recv()
            part[i, :HALF] = part[i, :HALF] + from_core[i]

            @pl.when(i < 2)
            def _():
                y_copy(i).start()

            return carry

        lax.fori_loop(0, 4, tile, 0)


        far((1, 0))
        outer(0, 1)

        def of_branch(context, d_branch, d_middle, tokens):
            waits = copies(
                [
                    (context_hbm, context),
                    (d_branch_hbm, d_branch),
                    (d_middle_hbm, d_middle),
                    (tokens_hbm.at[pl.ds(own_row, QUARTER)], tokens),
                ]
            )
            branch_y.wait_recv()
            branch_fwd.start()
            for copy in waits:
                copy.wait()
            acc = t_product(d_branch[...].astype(bf16), context[quarter_rows(0, 0), :])
            branch_c.wait_recv()
            branch_fwd.wait_recv()
            for k, (dc, dy) in enumerate([(0, 1), (1, 0), (1, 1)]):
                acc = acc + t_product(branch_land[k].astype(bf16), context[quarter_rows(dc, dy), :])
            attn[:, head : 2 * head] = acc
            far((1, 1))
            to_y.wait_recv()
            attn[:, 2 * head :] = kv_halves[y] + kv_across[...]
            for i in range(4):
                attn_z1_copy(i).start()
            far((2, 0), (2, 1))
            outer(1, 0)
            for h in range(2):
                y_copy(h).wait_recv()
                at = slice(h * HALF, (h + 1) * HALF)
                grad = part[2 + h, :HALF] + from_y[h]
                d_in, of_gain = back_norm(tokens[at, :].astype(f32), gain_row(gain_rows, 0), grad)
                gains[0:1, :] = gains[0:1, :] + jnp.sum(of_gain, axis=0, keepdims=True)
                d = (d_middle[at, :] + d_in).astype(bf16)
                input_stage[at, :] = d
                input_own[at, :] = d.astype(f32)

        pl.run_scoped(
            of_branch,
            pltpu.VMEM((length, head), bf16),
            pltpu.VMEM((QUARTER, width), f32),
            pltpu.VMEM((QUARTER, width), f32),
            pltpu.VMEM((QUARTER, width), bf16),
        )
        hop(0)
        arrive(0)
        hop(1)
        input_y.start()
        input_c.start()
        outer(1, 1)
        put_input(0, 0)
        for i in range(4):
            core_copy(i).wait_send()
        for h in range(2):
            y_copy(h).wait_send()
        to_y.wait_send()

    pl.run_scoped(
        rest,
        pltpu.VMEM((width, 3 * head), bf16),
        pltpu.VMEM((4, TILE, width), f32),
        pltpu.VMEM((2, width, head // 2), f32),
    )

    arrive(1)
    hop(2)
    close(0)
    outer(2, 0)
    input_y.wait_recv()
    input_fwd.start()
    input_stage[...] = input_land[0].astype(bf16)
    put_input(0, 1)
    input_c.wait_recv()
    input_stage[...] = input_land[1].astype(bf16)
    put_input(1, 0)
    close(1)
    outer(2, 1)
    for i in range(4):
        attn_z1_copy(i).wait_recv()
        rows = block(attn, (2 * (i // 2) + zl) * 2 + i % 2)
        attn[rows, :] = attn[rows, :] + attn_z1[i]
    for j in (1, 0):
        attn_x_copy(j).start()
    input_fwd.wait_recv()
    input_stage[...] = input_land[2].astype(bf16)
    put_input(1, 1)
    arrive(2)
    hop(3)
    for j in (1, 0):
        attn_x_copy(j).wait_recv()
        rows = block(attn, (2 * (zh ^ j) + zl) * 2 + x)
        attn[rows, :] = attn[rows, :] + attn_x[j]
        if j == 1:
            attn_z2_copy.start()
    close(2)
    finish(0, down_out)
    finish(1, gate_out)
    attn_z2_copy.wait_recv()
    total = attn[block(attn, (2 * zh + zl) * 2 + x), :] + attn_z2[...]
    query_out[...] = total[:, :head]
    out_out[...] = total[:, head : 2 * head]
    kv_own[...] = total[:, 2 * head :]
    wide_y = remote(kv_own, kv_y, ys, 5, near["y"])
    wide_y.start()
    arrive(3)
    hop(4)
    wide_y.wait_recv()
    kv_wide[:, : head // 2] = jnp.where(y == 0, kv_own[...], kv_y[...])
    kv_wide[:, head // 2 :] = jnp.where(y == 0, kv_y[...], kv_own[...])
    wide_c = remote(kv_wide, kv_wide_core, cs, 9, near["c"])
    wide_c.start()
    wide_c.wait_recv()
    key_out[...] = jnp.where(c == 0, kv_wide[...], kv_wide_core[...])
    value_out[...] = jnp.where(c == 0, kv_wide_core[...], kv_wide[...])
    arrive(4)
    finish(2, up_out)
    for m in range(3):
        for j in range(4):
            x_copy(m, j).wait_send()
        for k in range(2):
            z2_copy(m, k).wait_send()
        z1_copy(m).wait_send()
    for i in range(4):
        attn_z1_copy(i).wait_send()
    for j in range(2):
        attn_x_copy(j).wait_send()
    for copy in (attn_z2_copy, branch_y, branch_c, branch_fwd, input_y, input_c, input_fwd, wide_y, wide_c, heads_c_copy, heads_y_copy):
        copy.wait_send()


def reduce_all(nx, dp_size, columns, whole, small):
    length, width = whole[0].shape
    half = whole[4].shape[1]
    head = whole[11].shape[1]
    blk = width // dp_size
    return pl.pallas_call(
        functools.partial(reduce_kernel, nx),
        out_shape=(
            *[jax.ShapeDtypeStruct((blk, columns), f32)] * 3,
            *[jax.ShapeDtypeStruct((blk, head), f32)] * 4,
            jax.ShapeDtypeStruct((length, width), bf16),
            jax.ShapeDtypeStruct((8, width), f32),
        ),
        in_specs=[ANY] * len(whole) + [VMEM] * len(small),
        out_specs=(ANY,) * 3 + (VMEM,) * 4 + (ANY, VMEM),
        scratch_shapes=[
            pltpu.VMEM((QUARTER, width), bf16),
            pltpu.VMEM((blk, columns), f32),
            pltpu.VMEM((3, width, half), f32),
            pltpu.VMEM((12, blk, half), f32),
            pltpu.VMEM((6, blk, half), f32),
            pltpu.VMEM((3, blk, half), f32),
            pltpu.VMEM((4, HALF, width), f32),
            pltpu.VMEM((2, HALF, width), f32),
            pltpu.VMEM((3, QUARTER, width), f32),
            pltpu.VMEM((QUARTER, width), f32),
            pltpu.VMEM((3, QUARTER, width), f32),
            pltpu.VMEM((length, 3 * head), bf16),
            pltpu.VMEM((width, 2 * head + head // 2), f32),
            pltpu.VMEM((4, blk, 2 * head + head // 2), f32),
            pltpu.VMEM((2, blk, 2 * head + head // 2), f32),
            pltpu.VMEM((blk, 2 * head + head // 2), f32),
            pltpu.VMEM((width, head), f32),
            pltpu.VMEM((width, head // 2), f32),
            pltpu.VMEM((blk, head // 2), f32),
            pltpu.VMEM((blk, head // 2), f32),
            pltpu.VMEM((blk, head), f32),
            pltpu.VMEM((blk, head), f32),
            pltpu.VMEM((5, 8, width), f32),
            pltpu.VMEM((QUARTER, head), f32),
            pltpu.VMEM((2, QUARTER, head), f32),
            pltpu.VMEM((2, QUARTER, head), f32),
            pltpu.VMEM((2, QUARTER, head), f32),
        ]
        + dma(8, 12, 12, 8, 8, 15, 15, 8, 8, 8, 8),
        compiler_params=pltpu.CompilerParams(collective_id=2, has_side_effects=True, vmem_limit_bytes=VMEM_LIMIT),
        name="reduce_all",
    )(*whole, *small)


def settle_kernel(*refs):
    count = (len(refs) - 1) // 3
    sems = refs[-1]
    loads, puts = [], []
    for k in range(count):
        given, out, held = refs[k], refs[count + k], refs[2 * count + k]
        loads.append(pltpu.make_async_copy(given, held, sems.at[0, k]))
        puts.append(pltpu.make_async_copy(held, out, sems.at[1, k]))
    for copy in loads:
        copy.start()
    for load, put in zip(loads, puts):
        load.wait()
        put.start()
    for copy in puts:
        copy.wait()


def settle(*arrays):
    return pl.pallas_call(
        settle_kernel,
        out_shape=tuple(jax.ShapeDtypeStruct(a.shape, a.dtype) for a in arrays),
        in_specs=[ANY] * len(arrays),
        out_specs=(ANY,) * len(arrays),
        scratch_shapes=[pltpu.VMEM(a.shape, a.dtype) for a in arrays] + [pltpu.SemaphoreType.DMA((2, len(arrays)))],
        compiler_params=pltpu.CompilerParams(vmem_limit_bytes=VMEM_LIMIT),
        name="settle",
    )(*arrays)


def body(
    links,
    tokens,
    segment_ids,
    cotangent,
    w_query,
    w_key,
    w_value,
    w_out,
    w_gate,
    w_up,
    w_down,
    gain_attn_in,
    gain_attn_out,
    gain_ffn_in,
    gain_ffn_out,
    gain_query,
    gain_key,
):
    length, width = tokens.shape
    head = w_query.shape[1]
    columns = w_gate.shape[1]
    nx = links.nx
    blk = width // links.dp_size
    dp = lax.axis_index("dp")
    wg, wu = w_gate.T, w_up.T
    (
        normed_low,
        query_low,
        keys_low,
        values_low,
        query_raw,
        keys_raw,
        log_total,
        context_low,
        w_out_all,
        middle,
        branch,
        gain_rows,
    ) = attend(
        nx,
        tokens,
        w_query,
        w_key,
        w_value,
        w_out,
        segment_ids,
        gain_attn_in,
        gain_attn_out,
        gain_ffn_in,
        gain_ffn_out,
        gain_query,
        gain_key,
    )
    normed_two, normed_other, d_out, d_own, d_first, layer_out, pair_own, for_gate, for_up, of_ffn_out = feed_forward(
        nx, middle, cotangent, gain_rows, wg, wu, w_down
    )
    d_other, pair_other, pair_gates, heads, d_branch_own, d_middle, of_middle = feed_back(
        nx,
        d_out,
        d_own,
        d_first,
        for_gate,
        for_up,
        normed_other,
        wg,
        wu,
        w_down,
        w_out_all,
        middle,
        branch.reshape(QUARTER, width),
        cotangent,
        gain_rows,
    )
    *sums, gains = reduce_all(
        nx,
        links.dp_size,
        columns,
        [
            d_out,
            d_other,
            normed_two,
            normed_other,
            pair_own,
            pair_other,
            pair_gates,
            d_branch_own,
            d_middle,
            tokens,
            normed_low,
            query_low,
            keys_low,
            values_low,
            query_raw,
            keys_raw,
            context_low,
            heads,
            w_query,
            w_key,
            w_value,
        ],
        [log_total, segment_ids.reshape(1, length), gain_rows, of_ffn_out, of_middle],
    )
    layer_out, down_t, gate, up, query, out_t, key, value, input_grad = settle(layer_out, *sums)
    part = lax.dynamic_slice_in_dim(gains, dp * blk, blk, 1)
    hb = head // links.dp_size
    head_part = lax.dynamic_slice_in_dim(gains, dp * hb, hb, 1)
    return (
        layer_out,
        input_grad,
        query,
        key,
        value,
        out_t.T,
        gate,
        up,
        down_t.T,
        part[0],
        part[1],
        part[2],
        part[3],
        head_part[4],
        head_part[5],
    )


def body_any(
    links,
    tokens,
    segment_ids,
    cotangent,
    w_query,
    w_key,
    w_value,
    w_out,
    w_gate,
    w_up,
    w_down,
    gain_attn_in,
    gain_attn_out,
    gain_ffn_in,
    gain_ffn_out,
    gain_query,
    gain_key,
):
    length, width = tokens.shape
    head = w_query.shape[1]
    quarter = length // 4
    half_ff = w_gate.shape[1] // 2
    nx = links.nx
    blk = width // links.dp_size
    dp, t = lax.axis_index("dp"), lax.axis_index("tensor")
    z, x = dp // nx, dp % nx
    y, c = t // 2, t % 2
    parity = z % 2
    one = jnp.where(segment_ids[0] < length, 1.0, 0.5).astype(f32)

    def keep_low(a):
        return (a * one).astype(bf16)

    def place(dc, dy):
        return ((c ^ dc) * 2 + (y ^ dy)) * quarter

    def rows(a, dc, dy):
        return lax.dynamic_slice_in_dim(a, place(dc, dy), quarter, 0)

    def to_absolute(pieces):
        stack = jnp.stack([pieces[0][0], pieces[0][1], pieces[1][0], pieces[1][1]])
        mine = c * 2 + y
        return jnp.concatenate([lax.dynamic_index_in_dim(stack, mine ^ b, 0, keepdims=False) for b in range(4)], axis=0)

    out_own = w_out.astype(f32)
    out_y = links.y(out_own)
    out_c = links.core(out_own)
    out_yc = links.core(out_y)
    w_out_all = jnp.concatenate([w_out, keep_low(out_c), keep_low(out_y), keep_low(out_yc)], axis=0)

    wg_h = jnp.where(parity == 0, w_gate[:, :half_ff], w_gate[:, half_ff:])
    wu_h = jnp.where(parity == 0, w_up[:, :half_ff], w_up[:, half_ff:])
    wd_h = jnp.where(parity == 0, w_down[:half_ff], w_down[half_ff:])

    hidden_in = tokens.astype(f32)
    normed_low = low(rms_norm(hidden_in, gain_attn_in))
    query_raw = product(normed_low, w_query)
    keys_raw = product(normed_low, w_key)
    query_low = low(rms_norm(query_raw, gain_query))
    keys_low = low(rms_norm(keys_raw, gain_key))
    values_low = low(product(normed_low, w_value))
    places = jnp.arange(length)
    allowed = (places[:, None] >= places[None, :]) & (segment_ids[:, None] == segment_ids[None, :])

    def scores_of():
        raw = product_t(query_low, keys_low) * score_scale
        return jnp.where(allowed, raw, -1e30)

    scores = scores_of()
    largest = jnp.max(scores, axis=-1, keepdims=True)
    exponent = jnp.exp(scores - largest)
    total = jnp.sum(exponent, axis=-1, keepdims=True)
    log_total = largest + jnp.log(total)
    context_low = low(product(low(exponent / total), values_low))

    context = context_low.astype(f32)
    mine = jnp.concatenate([rows(context, 0, 1), rows(context, 0, 0)], axis=0)
    of_core = links.core(jnp.concatenate([rows(context, 1, 1), rows(context, 1, 0)], axis=0))
    of_y = links.y(jnp.concatenate([rows(context, 0, 0), rows(context, 0, 1)], axis=0))
    of_yc = links.y(jnp.concatenate([of_core[quarter:], of_core[:quarter]], axis=0))
    context_all = jnp.concatenate([low(mine), keep_low(of_core), keep_low(of_y), keep_low(of_yc)], axis=1)
    branch = product(context_all, w_out_all)
    hidden_rows = jnp.concatenate([rows(tokens, 0, 1), rows(tokens, 0, 0)], axis=0).astype(f32)
    middle_own = hidden_rows + rms_norm(branch, gain_attn_out)
    middle_core = links.core(middle_own)

    middles, normed_two, inners, parts = [], [], [], []
    saved = []
    for k in range(2):
        at = slice(k * quarter, (k + 1) * quarter)
        middle = jnp.concatenate([middle_own[at], middle_core[at]], axis=0)
        normed_k = low(rms_norm(middle, gain_ffn_in))
        gate, upward = product(normed_k, w_gate), product(normed_k, w_up)
        inner = low(activate(gate, upward))
        part = product(inner, w_down)
        middles.append(middle)
        normed_two.append(normed_k)
        saved.append((gate, upward))
        parts.append(part)
    normed_own = low(rms_norm(middle_own, gain_ffn_in)).astype(f32)
    other_own = links.z1(normed_own)
    other_core = links.core(other_own)
    normed_other = jnp.concatenate([keep_low(other_own), keep_low(other_core)], axis=0)

    def gather_quarters(parts):
        sums = [part[:quarter] + links.core(part[quarter:]) for part in parts]
        return sums[1] + links.y(sums[0])

    output_q = gather_quarters(parts)
    output_y = links.y(output_q)
    output_c = links.core(output_q)
    output_yc = links.core(output_y)
    outputs = [jnp.concatenate([output_y, output_yc], axis=0), jnp.concatenate([output_q, output_c], axis=0)]
    grad_out = cotangent.astype(f32)
    d_outputs, layer_pieces, grad_ffn_out = [], [], 0.0
    for k in range(2):
        dy_k = jnp.concatenate([rows(cotangent, 0, 1 - k), rows(cotangent, 1, 1 - k)], axis=0).astype(f32)
        layer_k = low(middles[k] + rms_norm(outputs[k], gain_ffn_out))
        d_k, gain_k = rms_back(outputs[k], gain_ffn_out, dy_k)
        grad_ffn_out = grad_ffn_out + gain_k
        d_outputs.append(low(d_k))
        layer_pieces.append(layer_k)
    layer_out = to_absolute(
        [
            [layer_pieces[1][:quarter], layer_pieces[0][:quarter]],
            [layer_pieces[1][quarter:], layer_pieces[0][quarter:]],
        ]
    )

    d_own_rows = [d[:quarter].astype(f32) for d in d_outputs]
    got_own = [links.z1(d_own_rows[1]), links.z1(d_own_rows[0])]
    got_core = [links.core(g) for g in got_own]
    d_other = jnp.concatenate(
        [keep_low(got_own[1]), keep_low(got_own[0]), keep_low(got_core[1]), keep_low(got_core[0])], axis=0
    )

    back_parts = []
    for k in range(2):
        gate, upward = saved[k]
        d_inner = product_t(d_outputs[k], w_down)
        _, pull = jax.vjp(activate, gate, upward)
        d_gate, d_up = pull(d_inner)
        back_parts.append(product_t(low(d_gate), w_gate) + product_t(low(d_up), w_up))
    d_normed_q = gather_quarters(back_parts)
    middle_q = middle_own[quarter:]
    branch_q = branch[quarter:]
    dy_q = rows(cotangent, 0, 0).astype(f32)
    d_mid, grad_ffn_in = rms_back(middle_q, gain_ffn_in, d_normed_q)
    d_middle = dy_q + d_mid
    d_branch, grad_attn_out = rms_back(branch_q, gain_attn_out, d_middle)
    d_branch_low = low(d_branch)
    d_context = low(product_t(d_branch_low, w_out_all)).astype(f32)
    heads = [d_context[:, i * head : (i + 1) * head] for i in range(4)]
    c_got = links.core(jnp.concatenate([heads[1], heads[3]], axis=1))
    y_got = links.y(jnp.concatenate([heads[2], c_got[:, head:]], axis=1))
    grad_context = keep_low(
        to_absolute([[heads[0], y_got[:, :head]], [c_got[:, :head], y_got[:, head:]]])
    )
    d_branch_own = d_branch_low.astype(f32)
    d_branch_y = links.y(d_branch_own)
    d_branch_c = links.core(d_branch_own)
    d_branch_yc = links.core(d_branch_y)
    d_branch_all = jnp.concatenate(
        [d_branch_low, keep_low(d_branch_y), keep_low(d_branch_c), keep_low(d_branch_yc)], axis=0
    )
    context_rel = jnp.concatenate(
        [rows(context_low, 0, 0), rows(context_low, 0, 1), rows(context_low, 1, 0), rows(context_low, 1, 1)], axis=0
    )
    grad_w_out_t = t_product(d_branch_all, context_rel)

    attn_prob = jnp.exp(scores_of() - log_total)
    prob_low = low(attn_prob)
    grad_prob = product_t(grad_context, values_low)
    grad_values = low(t_product(prob_low, grad_context))
    balance = jnp.sum(grad_prob * attn_prob, axis=-1, keepdims=True)
    grad_scores = low(attn_prob * (grad_prob - balance))
    grad_query_n = product(grad_scores, keys_low) * score_scale
    grad_keys_n = t_product(grad_scores, query_low) * score_scale
    d_query, grad_gain_query = rms_back(query_raw, gain_query, grad_query_n)
    d_keys, grad_gain_key = rms_back(keys_raw, gain_key, grad_keys_n)
    d_query, d_keys = low(d_query), low(d_keys)
    d_qkv = jnp.concatenate([d_query, d_keys, grad_values], axis=1)
    w_qkv = jnp.concatenate([w_query, w_key, w_value], axis=1)
    in_parts = []
    for k in range(2):
        rows_k = jnp.concatenate([rows(d_qkv, 0, 1 - k), rows(d_qkv, 1, 1 - k)], axis=0)
        in_parts.append(product_t(rows_k, w_qkv))
    d_normed_in = gather_quarters(in_parts)
    hidden_q = rows(tokens, 0, 0).astype(f32)
    d_in, grad_attn_in = rms_back(hidden_q, gain_attn_in, d_normed_in)
    input_q = low(d_middle + d_in)
    input_own = input_q.astype(f32)
    input_y = links.y(input_own)
    input_c = links.core(input_own)
    input_yc = links.core(input_y)
    input_grad = keep_low(to_absolute([[input_own, input_y], [input_c, input_yc]]))

    grad_qkv = t_product(normed_low, d_qkv)
    grad_w_query, grad_kv = grad_qkv[:, :head], grad_qkv[:, head:]
    kv_keep = jnp.where(c == 0, grad_kv[:, :head], grad_kv[:, head:])
    kv_send = jnp.where(c == 0, grad_kv[:, head:], grad_kv[:, :head])
    kv = kv_keep + links.core(kv_send)
    kv_half = head // 2
    kv_keep = jnp.where(y == 0, kv[:, :kv_half], kv[:, kv_half:])
    kv_send = jnp.where(y == 0, kv[:, kv_half:], kv[:, :kv_half])
    kv = kv_keep + links.y(kv_send)
    attn_grads = jnp.concatenate([grad_w_query, grad_w_out_t, kv], axis=1)

    normed_all = jnp.concatenate(
        [normed_two[0][:quarter], normed_two[1][:quarter], normed_two[0][quarter:], normed_two[1][quarter:], normed_other],
        axis=0,
    )
    d_all = jnp.concatenate(
        [d_outputs[0][:quarter], d_outputs[1][:quarter], d_outputs[0][quarter:], d_outputs[1][quarter:], d_other], axis=0
    )
    gate, upward = product(normed_all, wg_h), product(normed_all, wu_h)
    inner, pull = jax.vjp(activate, gate, upward)
    inner = low(inner)
    d_inner = product_t(d_all, wd_h)
    d_gate, d_up = pull(d_inner)
    ff_grads = [t_product(d_all, inner), t_product(normed_all, low(d_gate)), t_product(normed_all, low(d_up))]

    zh, zl = z // 2, z % 2

    def sum_x(grads, z_half):
        mine = lax.dynamic_index_in_dim(grads, z_half, 0, keepdims=False)
        acc = lax.dynamic_index_in_dim(mine, x, 1, keepdims=False)
        for step in range(1, nx):
            to = lax.dynamic_index_in_dim(mine, (x + step) % nx, 1, keepdims=False)
            acc = acc + links.x(to, step)
        return acc

    def scatter(grads):
        grads = grads.reshape(2, 2, nx, blk, grads.shape[1])
        far = sum_x(grads, 1 - zh)
        near = sum_x(grads, zh)
        return near + links.z2(far)

    ff_sums = []
    for grads in ff_grads:
        got = scatter(grads)
        own = lax.dynamic_index_in_dim(got, zl, 0, keepdims=False)
        other = links.z1(lax.dynamic_index_in_dim(got, 1 - zl, 0, keepdims=False))
        ff_sums.append(
            jnp.where(
                parity == 0, jnp.concatenate([own, other], axis=1), jnp.concatenate([other, own], axis=1)
            )
        )
    grad_w_down, grad_w_gate, grad_w_up = ff_sums[0].T, ff_sums[1], ff_sums[2]

    got = scatter(attn_grads)
    attn_sum = lax.dynamic_index_in_dim(got, zl, 0, keepdims=False) + links.z1(
        lax.dynamic_index_in_dim(got, 1 - zl, 0, keepdims=False)
    )
    grad_w_query = attn_sum[:, :head]
    grad_w_out = attn_sum[:, head : 2 * head].T
    kv_own = attn_sum[:, 2 * head :]
    kv_y = links.y(kv_own)
    kv_wide = jnp.where(y == 0, jnp.concatenate([kv_own, kv_y], axis=1), jnp.concatenate([kv_y, kv_own], axis=1))
    kv_c = links.core(kv_wide)
    grad_w_key = jnp.where(c == 0, kv_wide, kv_c)
    grad_w_value = jnp.where(c == 0, kv_c, kv_wide)

    small = jnp.concatenate(
        [
            grad_attn_in.reshape(links.dp_size, -1),
            grad_attn_out.reshape(links.dp_size, -1),
            grad_ffn_in.reshape(links.dp_size, -1),
            (grad_ffn_out * 0.25).reshape(links.dp_size, -1),
            grad_gain_query.reshape(links.dp_size, -1),
            grad_gain_key.reshape(links.dp_size, -1),
        ],
        axis=1,
    )
    small = small + links.core(small)
    small = small + links.y(small)
    small = small.reshape(2, 2, nx, 1, small.shape[1])
    acc = lax.dynamic_index_in_dim(small, x, 2, keepdims=False)
    for step in range(1, nx):
        acc = acc + links.x(lax.dynamic_index_in_dim(small, (x + step) % nx, 2, keepdims=False), step)
    acc = lax.dynamic_index_in_dim(acc, zh, 0, keepdims=False) + links.z2(
        lax.dynamic_index_in_dim(acc, 1 - zh, 0, keepdims=False)
    )
    acc = lax.dynamic_index_in_dim(acc, zl, 0, keepdims=False) + links.z1(
        lax.dynamic_index_in_dim(acc, 1 - zl, 0, keepdims=False)
    )
    acc = acc.reshape(-1)
    hb = head // links.dp_size
    return (
        layer_out,
        input_grad,
        grad_w_query,
        grad_w_key,
        grad_w_value,
        grad_w_out,
        grad_w_gate,
        grad_w_up,
        grad_w_down,
        acc[:blk],
        acc[blk : 2 * blk],
        acc[2 * blk : 3 * blk],
        acc[3 * blk : 4 * blk],
        acc[4 * blk : 4 * blk + hb],
        acc[4 * blk + hb :],
    )


def solution(mesh):
    links = Links(mesh)
    return jax.shard_map(
        functools.partial(body if links.nx == 2 else body_any, links),
        mesh=mesh,
        in_specs=(
            P("dp", None),
            P("dp"),
            P("dp", None),
            P(None, "tensor"),
            P(),
            P(),
            P("tensor", None),
            P(None, "tensor"),
            P(None, "tensor"),
            P("tensor", None),
            P(),
            P(),
            P(),
            P(),
            P(),
            P(),
        ),
        out_specs=(
            P("dp", None),
            P("dp", None),
            P("dp", "tensor"),
            P("dp", None),
            P("dp", None),
            P("tensor", "dp"),
            P("dp", "tensor"),
            P("dp", "tensor"),
            P("tensor", "dp"),
            P("dp"),
            P("dp"),
            P("dp"),
            P("dp"),
            P("dp"),
            P("dp"),
        ),
        check_vma=False,
    )
```

```python
import functools

import jax
import jax.numpy as jnp
from jax import lax
from jax.experimental import pallas as pl
from jax.experimental.pallas import tpu as pltpu
from jax.sharding import PartitionSpec as P

epsilon = 1e-06
score_scale = 0.0625
NZ = 4

f32 = jnp.float32
bf16 = jnp.bfloat16


def rms_norm(values, gain):
    inverse = lax.rsqrt(jnp.mean(values * values, axis=-1, keepdims=True) + epsilon)
    return values * inverse * (1.0 + gain)


def rms_back(values, gain, grad):
    inverse = lax.rsqrt(jnp.mean(values * values, axis=-1, keepdims=True) + epsilon)
    hat = values * inverse
    scaled = grad * (1.0 + gain)
    back = inverse * (scaled - hat * jnp.mean(scaled * hat, axis=-1, keepdims=True))
    return back, jnp.sum(grad * hat, axis=0)


def product(left, right):
    return jnp.dot(left, right, preferred_element_type=f32)


def product_t(left, right):
    return lax.dot_general(left, right, (((1,), (1,)), ((), ())), preferred_element_type=f32)


def t_product(left, right):
    return lax.dot_general(left, right, (((0,), (0,)), ((), ())), preferred_element_type=f32)


def activate(gate, upward):
    return jax.nn.gelu(gate, approximate=True) * upward


class Links:
    def __init__(self, mesh):
        self.dp_size = mesh.shape["dp"]
        self.nx = self.dp_size // NZ
        tensor = mesh.shape["tensor"]
        self.perm_core = [(t, t ^ 1) for t in range(tensor)]
        self.perm_y = [(t, t ^ 2) for t in range(tensor)]
        nx = self.nx
        self.perm_z1 = [(z * nx + x, (z ^ 1) * nx + x) for z in range(NZ) for x in range(nx)]
        self.perm_z2 = [(z * nx + x, (z ^ 2) * nx + x) for z in range(NZ) for x in range(nx)]

    def core(self, a):
        return lax.ppermute(a, "tensor", self.perm_core)

    def y(self, a):
        return lax.ppermute(a, "tensor", self.perm_y)

    def z1(self, a):
        return lax.ppermute(a, "dp", self.perm_z1)

    def z2(self, a):
        return lax.ppermute(a, "dp", self.perm_z2)

    def x(self, a, step):
        nx = self.nx
        return lax.ppermute(a, "dp", [(z * nx + x, z * nx + (x + step) % nx) for z in range(NZ) for x in range(nx)])


def low(a):
    return a.astype(bf16)


MESH = pl.DeviceIdType.MESH
ANY = pl.BlockSpec(memory_space=pl.ANY)
VMEM = pl.BlockSpec(memory_space=pltpu.VMEM)
TILE, HALF, QUARTER = 256, 128, 256
VMEM_LIMIT = 127 << 19


def spots(nx):
    dp, t = lax.axis_index("dp"), lax.axis_index("tensor")
    z, x = dp // nx, dp % nx
    near = {
        "c": {"tensor": t ^ 1},
        "y": {"tensor": t ^ 2},
        "z1": {"dp": (z ^ 1) * nx + x},
        "z2": {"dp": (z ^ 2) * nx + x},
        "x": {"dp": z * nx + (x ^ 1)},
    }
    return z, x, t // 2, t % 2, near


def remote(src, dst, sems, index, to):
    return pltpu.make_async_remote_copy(
        src_ref=src, dst_ref=dst, send_sem=sems[0].at[index], recv_sem=sems[1].at[index], device_id=to, device_id_type=MESH
    )


def greet(others):
    barrier = pltpu.get_barrier_semaphore()
    for other in others:
        pl.semaphore_signal(barrier, inc=1, device_id=other, device_id_type=MESH)
    pl.semaphore_wait(barrier, len(others))


def tile_row(c, y, i, dc):
    dy = 1 - i // 2
    return pl.multiple_of(((c ^ dc) * 2 + (y ^ dy)) * QUARTER + (i % 2) * HALF, HALF)


def gelu_parts(u):
    k = 0.7978845608028654
    square = u * u
    th = jnp.tanh(k * u * (1.0 + 0.044715 * square))
    side = 0.5 * (1.0 + th)
    return u * side, side + 0.5 * u * (1.0 - th * th) * (k * (1.0 + 3.0 * 0.044715 * square))


def gelu_tanh(u):
    return 0.5 * u * (1.0 + jnp.tanh(0.7978845608028654 * u * (1.0 + 0.044715 * (u * u))))


def gain_row(gains, k):
    return gains[k : k + 1, :]


def forward_kernel(
    nx,
    middle_hbm,
    cotangent,
    gains,
    w_gate_hbm,
    w_up_hbm,
    w_down_hbm,
    normed_hbm,
    other_hbm,
    d_out_hbm,
    d_own_hbm,
    d_first,
    layer_hbm,
    pair_own_hbm,
    for_gate_hbm,
    for_up_hbm,
    gain_grad,
    middle,
    w_gate,
    w_up,
    w_down,
    normed,
    other,
    d_out,
    d_own,
    layer_out,
    out,
    dy,
    inner,
    for_gate,
    for_up,
    part,
    from_core,
    from_y,
    z_stage,
    z_land,
    c_land,
    local,
    stores,
    tile_stores,
    c_send,
    c_recv,
    y_send,
    y_recv,
    z_send,
    z_recv,
):
    z, x, y, c, near = spots(nx)
    core, across, pair = near["c"], near["y"], near["z1"]
    cs, ys, zs = (c_send, c_recv), (y_send, y_recv), (z_send, z_recv)
    first = [
        pltpu.make_async_copy(src, dst, local.at[8 + k])
        for k, (src, dst) in enumerate(
            [(middle_hbm, middle), (w_gate_hbm, w_gate), (w_up_hbm, w_up), (w_down_hbm, w_down)]
        )
    ]
    for copy in first:
        copy.start()
    loads = []
    for i in range(4):
        for dc in range(2):
            copy = pltpu.make_async_copy(
                cotangent.at[pl.ds(tile_row(c, y, i, dc), HALF)],
                dy.at[pl.ds(i * TILE + dc * HALF, HALF)],
                local.at[i * 2 + dc],
            )
            copy.start()
            loads.append(copy)
    greet([core, across, pair])
    columns = w_gate.shape[0]
    cut = pl.cdiv(columns, TILE) * HALF
    for ref in (inner, for_gate, for_up):
        for slot in range(2):
            ref[slot, :, columns:] = jnp.zeros((TILE, 2 * cut - columns), bf16)

    def tile_puts(i):
        slot = i % 2
        at = pl.ds(pl.multiple_of(i * TILE, TILE), TILE)
        mine = pl.ds(pl.multiple_of(z % 2 * cut, HALF), cut)
        return [
            pltpu.make_async_copy(inner.at[slot, :, mine], pair_own_hbm.at[at], tile_stores.at[slot, 0]),
            pltpu.make_async_copy(for_gate.at[slot], for_gate_hbm.at[at], tile_stores.at[slot, 1]),
            pltpu.make_async_copy(for_up.at[slot], for_up_hbm.at[at], tile_stores.at[slot, 2]),
        ]

    def core_copy(i):
        return remote(part.at[i, pl.ds(HALF, HALF)], from_core.at[i], cs, i, core)

    def y_copy(h):
        return remote(part.at[h, pl.ds(0, HALF)], from_y.at[h], ys, h, across)

    def z_copy(i):
        return remote(z_stage.at[i], z_land.at[i], zs, i, pair)

    first_copy = remote(d_own.at[2], d_first, zs, 4, pair)

    def z_forward(i):
        return remote(z_land.at[i], c_land.at[i], cs, 8 + i, core)

    def norm_tile(i, carry):
        at = pl.ds(pl.multiple_of(i * TILE, TILE), TILE)
        m = middle[at, :]
        inverse = lax.rsqrt(jnp.mean(m * m, axis=-1, keepdims=True) + epsilon)
        n = (m * inverse * (1.0 + gain_row(gains, 2))).astype(bf16)
        normed[at, :] = n
        z_stage[i] = n[:HALF].astype(f32)
        z_copy(i).start()
        return carry

    first[0].wait()
    lax.fori_loop(0, 4, norm_tile, 0)
    for copy in first[1:]:
        copy.wait()

    def step(i, carry):
        at = pl.ds(pl.multiple_of(i * TILE, TILE), TILE)
        n = normed[at, :]
        slot = i % 2

        @pl.when(i >= 2)
        def _():
            for copy in tile_puts(i - 2):
                copy.wait()

        for lo in range(0, columns, TILE):
            hi = min(lo + TILE, columns)
            g = product_t(n, w_gate[lo:hi, :])
            u = product_t(n, w_up[lo:hi, :])
            act, slope = gelu_parts(g)
            inner[slot, :, lo:hi] = (act * u).astype(bf16)
            for_gate[slot, :, lo:hi] = (u * slope).astype(bf16)
            for_up[slot, :, lo:hi] = act.astype(bf16)
        part[i] = product(inner[slot, :, :columns], w_down[...])
        for copy in tile_puts(i):
            copy.start()
        core_copy(i).start()
        core_copy(i).wait_recv()
        part[i, :HALF] = part[i, :HALF] + from_core[i]

        @pl.when(i < 2)
        def _():
            y_copy(i).start()

        return carry

    lax.fori_loop(0, 4, step, 0)

    def tile_at(i):
        return pl.ds(pl.multiple_of(i * TILE, TILE), TILE)

    put_normed = pltpu.make_async_copy(normed, normed_hbm, stores.at[8])
    put_layer = pltpu.make_async_copy(layer_out, layer_hbm, stores.at[9])

    def put_own(i):
        return pltpu.make_async_copy(d_own.at[i], d_own_hbm.at[i], stores.at[i])

    def put_d(i):
        return pltpu.make_async_copy(d_out.at[tile_at(i)], d_out_hbm.at[tile_at(i)], stores.at[4 + i])

    def put_other(i):
        return pltpu.make_async_copy(other.at[tile_at(i)], other_hbm.at[tile_at(i)], stores.at[10 + i])

    put_normed.start()
    for i in (2, 3):
        for copy in tile_puts(i):
            copy.wait()
    for copy in loads:
        copy.wait()
    gain_grad[...] = jnp.zeros_like(gain_grad)
    gain = 1.0 + gain_row(gains, 3)

    def finish(i, dc):
        at = pl.ds(pl.multiple_of(i * TILE + dc * HALF, HALF), HALF)
        o, g = out[at, :], dy[at, :].astype(f32)
        inverse = lax.rsqrt(jnp.mean(o * o, axis=-1, keepdims=True) + epsilon)
        hat = o * inverse
        scaled = g * gain
        d = (inverse * (scaled - hat * jnp.mean(scaled * hat, axis=-1, keepdims=True))).astype(bf16)
        d_out[at, :] = d
        gain_grad[...] = gain_grad[...] + jnp.sum((g * hat).reshape(HALF // 8, 8, g.shape[1]), axis=0)
        layer_out[pl.ds(tile_row(c, y, i, dc), HALF), :] = (middle[at, :] + hat * gain).astype(bf16)
        return d

    def half_at(i, dc):
        return pl.ds(pl.multiple_of(i * TILE + dc * HALF, HALF), HALF)

    def spread_y(h):
        return remote(out.at[half_at(2 + h, 0)], out.at[half_at(h, 0)], ys, 2 + h, across)

    def spread_core(i):
        return remote(out.at[half_at(i, 0)], out.at[half_at(i, 1)], cs, 4 + i, core)

    def close_tile(n, carry):
        i = (n + 2) % 4

        @pl.when(n < 2)
        def _():
            y_copy(n).wait_recv()
            out[half_at(i, 0), :] = part[i, :HALF] + from_y[n]
            spread_y(n).start()

        @pl.when(n == 2)
        def _():
            for i in range(3):
                z_copy(i).wait_recv()
                z_forward(i).start()
            for i in range(2):
                take(i)

        @pl.when(n >= 2)
        def _():
            spread_y(i).wait_recv()

        spread_core(i).start()
        d_own[i] = finish(i, 0).astype(f32)

        @pl.when(n == 0)
        def _():
            first_copy.start()

        put_own(i).start()
        spread_core(i).wait_recv()
        finish(i, 1)
        put_d(i).start()
        return carry

    def take(i):
        z_forward(i).wait_recv()
        other[i * TILE : i * TILE + HALF, :] = z_land[i].astype(bf16)
        other[i * TILE + HALF : (i + 1) * TILE, :] = c_land[i].astype(bf16)
        put_other(i).start()

    lax.fori_loop(0, 4, close_tile, 0)
    put_layer.start()
    z_copy(3).wait_recv()
    z_forward(3).start()
    for i in range(2, 4):
        take(i)
    for i in range(4):
        core_copy(i).wait_send()
        z_copy(i).wait_send()
        z_forward(i).wait_send()
        spread_core(i).wait_send()
        put_own(i).wait()
        put_d(i).wait()
        put_other(i).wait()
    for h in range(2):
        y_copy(h).wait_send()
        spread_y(h).wait_send()
    put_normed.wait()
    put_layer.wait()
    first_copy.wait()


def dma(*counts):
    return [pltpu.SemaphoreType.DMA((n,)) for n in counts]


def feed_forward(nx, middle, cotangent, gains, w_gate, w_up, w_down):
    length, width = middle.shape
    columns = pl.cdiv(w_gate.shape[0], TILE) * TILE
    rows_low = jax.ShapeDtypeStruct((length, width), bf16)
    return pl.pallas_call(
        functools.partial(forward_kernel, nx),
        out_shape=(
            rows_low,
            rows_low,
            rows_low,
            jax.ShapeDtypeStruct((4, HALF, width), f32),
            jax.ShapeDtypeStruct((HALF, width), f32),
            rows_low,
            jax.ShapeDtypeStruct((length, columns // 2), bf16),
            jax.ShapeDtypeStruct((length, columns), bf16),
            jax.ShapeDtypeStruct((length, columns), bf16),
            jax.ShapeDtypeStruct((8, width), f32),
        ),
        in_specs=[ANY, ANY, VMEM] + [ANY] * 3,
        out_specs=(ANY,) * 4 + (VMEM, ANY, ANY, ANY, ANY, VMEM),
        scratch_shapes=[pltpu.VMEM((length, width), f32)]
        + [pltpu.VMEM(w_gate.shape, bf16)] * 3
        + [pltpu.VMEM((length, width), bf16)] * 3
        + [
            pltpu.VMEM((4, HALF, width), f32),
            pltpu.VMEM((length, width), bf16),
            pltpu.VMEM((length, width), f32),
            pltpu.VMEM((length, width), bf16),
            pltpu.VMEM((2, TILE, columns), bf16),
            pltpu.VMEM((2, TILE, columns), bf16),
            pltpu.VMEM((2, TILE, columns), bf16),
            pltpu.VMEM((4, TILE, width), f32),
            pltpu.VMEM((4, HALF, width), f32),
            pltpu.VMEM((2, HALF, width), f32),
            pltpu.VMEM((4, HALF, width), f32),
            pltpu.VMEM((4, HALF, width), f32),
            pltpu.VMEM((4, HALF, width), f32),
        ]
        + dma(12, 14)
        + [pltpu.SemaphoreType.DMA((2, 3))]
        + dma(12, 12, 4, 4, 5, 5),
        compiler_params=pltpu.CompilerParams(collective_id=0, has_side_effects=True, vmem_limit_bytes=VMEM_LIMIT),
        name="feed_forward",
    )(middle, cotangent, gains, w_gate, w_up, w_down)


def back_kernel(
    nx,
    d_out_hbm,
    d_own_hbm,
    d_first_hbm,
    for_gate_hbm,
    for_up_hbm,
    other_hbm,
    w_gate_hbm,
    w_up_hbm,
    w_down_hbm,
    w_out_hbm,
    middle_hbm,
    branch_hbm,
    dy_hbm,
    gains,
    d_other_hbm,
    pair_in,
    pair_gates,
    heads_hbm,
    d_branch_hbm,
    d_middle_hbm,
    gain_grads,
    d_other,
    heads,
    d_branch_out,
    d_middle_out,
    puts_sem,
    d_out,
    for_gate,
    for_up,
    other,
    w_gate,
    w_up,
    w_down,
    w_out,
    middle,
    branch,
    dy,
    gates,
    ups,
    inner,
    part,
    from_core,
    from_y,
    z_land,
    c_land,
    loads_sem,
    tiles_sem,
    stores_sem,
    c_send,
    c_recv,
    y_send,
    y_recv,
    z_send,
    z_recv,
):
    z, x, y, c, near = spots(nx)
    core, across, pair = near["c"], near["y"], near["z1"]
    cs, ys, zs = (c_send, c_recv), (y_send, y_recv), (z_send, z_recv)
    parity = z % 2
    real, columns = w_gate_hbm.shape[0], w_gate.shape[0]
    half = columns // 2
    head = heads.shape[2]
    own_row = pl.multiple_of((c * 2 + y) * QUARTER, QUARTER)
    sources = [
        (d_out_hbm, d_out),
        (w_gate_hbm, w_gate.at[pl.ds(0, real)]),
        (w_up_hbm, w_up.at[pl.ds(0, real)]),
        (w_down_hbm, w_down.at[pl.ds(0, real)]),
        (other_hbm, other),
        (w_out_hbm, w_out),
        (middle_hbm.at[pl.ds(2 * TILE, HALF)], middle.at[pl.ds(0, HALF)]),
        (middle_hbm.at[pl.ds(3 * TILE, HALF)], middle.at[pl.ds(HALF, HALF)]),
        (branch_hbm, branch),
        (dy_hbm.at[pl.ds(own_row, QUARTER)], dy),
        (d_first_hbm, z_land.at[2]),
    ]
    loads = [pltpu.make_async_copy(src, dst, loads_sem.at[k]) for k, (src, dst) in enumerate(sources)]
    for copy in loads:
        copy.start()
    if real < columns:
        for ref in (w_gate, w_up, w_down):
            ref[real:, :] = jnp.zeros((columns - real, ref.shape[1]), bf16)
    greet([core, across, pair])

    def core_copy(i):
        return remote(part.at[i, pl.ds(HALF, HALF)], from_core.at[i], cs, i, core)

    def y_copy(h):
        return remote(part.at[h, pl.ds(0, HALF)], from_y.at[h], ys, h, across)

    def z_copy(i):
        return remote(d_own_hbm.at[i], z_land.at[i], zs, i, pair)

    def z_forward(i):
        return remote(z_land.at[i], c_land.at[i], cs, 4 + i, core)

    for i in (3, 0, 1):
        z_copy(i).start()
    def tile_loads(i):
        slot = i % 2
        at = pl.ds(pl.multiple_of(i * TILE, TILE), TILE)
        return [
            pltpu.make_async_copy(for_gate_hbm.at[at], for_gate.at[slot], tiles_sem.at[slot, 0]),
            pltpu.make_async_copy(for_up_hbm.at[at], for_up.at[slot], tiles_sem.at[slot, 1]),
        ]

    for i in range(2):
        for copy in tile_loads(i):
            copy.start()
    for copy in loads[:4]:
        copy.wait()

    mine = pl.multiple_of(parity * half, HALF)

    def stores(i, base):
        slot = i % 2
        at = pl.ds(pl.multiple_of(base + i * TILE, TILE), TILE)
        pick = pl.ds(mine, half)
        first = []
        if base:
            first = [
                pltpu.make_async_copy(
                    inner.at[slot], pair_in.at[pl.ds(pl.multiple_of(i * TILE, TILE), TILE)], stores_sem.at[slot, 0]
                )
            ]
        return first + [
            pltpu.make_async_copy(gates.at[slot, :, pick], pair_gates.at[at, pl.ds(0, half)], stores_sem.at[slot, 1]),
            pltpu.make_async_copy(ups.at[slot, :, pick], pair_gates.at[at, pl.ds(half, half)], stores_sem.at[slot, 2]),
        ]

    def piece(n, d, slot, at, own):
        g = product_t(n, w_gate[at, :])
        u = product_t(n, w_up[at, :])
        di = product_t(d, w_down[at, :])
        act, slope = gelu_parts(g)
        inner[slot, :, own] = (act * u).astype(bf16)
        gates[slot, :, at] = (di * u * slope).astype(bf16)
        ups[slot, :, at] = (di * act).astype(bf16)

    def own_tile(i, carry):
        at = pl.ds(pl.multiple_of(i * TILE, TILE), TILE)
        slot = i % 2

        @pl.when(i >= 2)
        def _():
            for copy in stores(i - 2, 0):
                copy.wait()

        for copy in tile_loads(i):
            copy.wait()
        d = d_out[at, :]
        for lo in range(0, columns, TILE):
            cols = pl.ds(lo, TILE)
            di = product_t(d, w_down[cols, :])
            gates[slot, :, cols] = (di * for_gate[slot, :, cols].astype(f32)).astype(bf16)
            ups[slot, :, cols] = (di * for_up[slot, :, cols].astype(f32)).astype(bf16)

        @pl.when(i < 2)
        def _():
            for copy in tile_loads(i + 2):
                copy.start()

        for copy in stores(i, 0):
            copy.start()
        part[i] = product(gates[slot], w_gate[...]) + product(ups[slot], w_up[...])
        core_copy(i).start()

        @pl.when(i >= 1)
        def _():
            both(i - 1)

        return carry

    def both(i):
        core_copy(i).wait_recv()
        part[i, :HALF] = part[i, :HALF] + from_core[i]

        @pl.when(i < 2)
        def _():
            y_copy(i).start()

    lax.fori_loop(0, 4, own_tile, 0)
    for copy in loads[4:]:
        copy.wait()

    def put_other(i):
        at = pl.ds(pl.multiple_of(i * TILE, TILE), TILE)
        return pltpu.make_async_copy(d_other.at[at], d_other_hbm.at[at], puts_sem.at[i])

    puts = [
        pltpu.make_async_copy(src, dst, puts_sem.at[4 + k])
        for k, (src, dst) in enumerate(
            [(heads, heads_hbm), (d_branch_out, d_branch_hbm), (d_middle_out, d_middle_hbm)]
        )
    ]

    def other_tile(n, carry):
        i, slot = (n + 2) % 4, n % 2

        @pl.when(n > 0)
        def _():
            z_copy(i).wait_recv()

        @pl.when(n >= 1)
        def _():
            z_forward(i).start()

        @pl.when(n < 2)
        def _():
            for copy in stores(i, 0):
                copy.wait()

        @pl.when(n >= 2)
        def _():
            for copy in stores(n, d_out.shape[0]):
                copy.wait()

        z_forward(i).wait_recv()
        lo = pl.multiple_of(i * TILE, TILE)
        d_other[pl.ds(lo, HALF), :] = z_land[i].astype(bf16)
        d_other[pl.ds(lo + HALF, HALF), :] = c_land[i].astype(bf16)
        put_other(i).start()
        n, d = other[pl.ds(lo, TILE), :], d_other[pl.ds(lo, TILE), :]
        for off in range(0, half, TILE):
            size = min(TILE, half - off)
            piece(n, d, slot, pl.ds(pl.multiple_of(mine + off, HALF), size), pl.ds(off, size))
        for copy in stores(i, d_out.shape[0]):
            copy.start()
        return carry

    z_forward(2).start()
    both(jnp.int32(3))
    lax.fori_loop(0, 3, other_tile, 0)

    gain_grads[...] = jnp.zeros_like(gain_grads)

    def fold(a):
        return jnp.sum(a.reshape(a.shape[0] // 8, 8, a.shape[1]), axis=0)

    def of_quarter(h, carry):
        y_copy(h).wait_recv()
        at = pl.ds(pl.multiple_of(h * HALF, HALF), HALF)
        grad = part[2 + h, :HALF] + from_y[h]
        m = middle[at, :]
        inverse = lax.rsqrt(jnp.mean(m * m, axis=-1, keepdims=True) + epsilon)
        hat = m * inverse
        scaled = grad * (1.0 + gain_row(gains, 2))
        d_middle = dy[at, :].astype(f32) + inverse * (scaled - hat * jnp.mean(scaled * hat, axis=-1, keepdims=True))
        gain_grads[0] = gain_grads[0] + fold(grad * hat)
        d_middle_out[at, :] = d_middle
        b = branch[at, :]
        inverse = lax.rsqrt(jnp.mean(b * b, axis=-1, keepdims=True) + epsilon)
        hat = b * inverse
        scaled = d_middle * (1.0 + gain_row(gains, 1))
        d_low = (inverse * (scaled - hat * jnp.mean(scaled * hat, axis=-1, keepdims=True))).astype(bf16)
        gain_grads[1] = gain_grads[1] + fold(d_middle * hat)
        d_branch_out[at, :] = d_low.astype(f32)
        for k in range(4):
            heads[k, at, :] = product_t(d_low, w_out[k * head : (k + 1) * head, :]).astype(bf16).astype(f32)
        return carry

    lax.fori_loop(0, 2, of_quarter, 0)
    for copy in puts:
        copy.start()
    lax.fori_loop(3, 4, other_tile, 0)
    for i in (0, 1):
        for copy in stores(i, d_out.shape[0]):
            copy.wait()
    for copy in puts + [put_other(i) for i in range(4)]:
        copy.wait()
    for i in (3, 0, 1):
        z_copy(i).wait_send()
    for i in range(4):
        core_copy(i).wait_send()
        z_forward(i).wait_send()
    for h in range(2):
        y_copy(h).wait_send()


def feed_back(nx, d_out, d_own, d_first, for_gate, for_up, other, w_gate, w_up, w_down, w_out, middle, branch, dy, gains):
    length, width = d_out.shape
    columns = pl.cdiv(w_gate.shape[0], TILE) * TILE
    head = w_out.shape[0] // 4
    return pl.pallas_call(
        functools.partial(back_kernel, nx),
        out_shape=(
            jax.ShapeDtypeStruct((length, width), bf16),
            jax.ShapeDtypeStruct((length, columns // 2), bf16),
            jax.ShapeDtypeStruct((2 * length, columns), bf16),
            jax.ShapeDtypeStruct((4, QUARTER, head), f32),
            jax.ShapeDtypeStruct((QUARTER, width), f32),
            jax.ShapeDtypeStruct((QUARTER, width), f32),
            jax.ShapeDtypeStruct((2, 8, width), f32),
        ),
        in_specs=[ANY] * 13 + [VMEM],
        out_specs=(ANY,) * 6 + (VMEM,),
        scratch_shapes=[
            pltpu.VMEM((length, width), bf16),
            pltpu.VMEM((4, QUARTER, head), f32),
            pltpu.VMEM((QUARTER, width), f32),
            pltpu.VMEM((QUARTER, width), f32),
            pltpu.SemaphoreType.DMA((7,)),
            pltpu.VMEM((length, width), bf16),
            pltpu.VMEM((2, TILE, columns), bf16),
            pltpu.VMEM((2, TILE, columns), bf16),
            pltpu.VMEM((length, width), bf16),
            pltpu.VMEM((columns, width), bf16),
            pltpu.VMEM((columns, width), bf16),
            pltpu.VMEM((columns, width), bf16),
            pltpu.VMEM((4 * head, width), bf16),
            pltpu.VMEM((QUARTER, width), f32),
            pltpu.VMEM((QUARTER, width), f32),
            pltpu.VMEM((QUARTER, width), bf16),
            pltpu.VMEM((2, TILE, columns), bf16),
            pltpu.VMEM((2, TILE, columns), bf16),
            pltpu.VMEM((2, TILE, columns // 2), bf16),
            pltpu.VMEM((4, TILE, width), f32),
            pltpu.VMEM((4, HALF, width), f32),
            pltpu.VMEM((2, HALF, width), f32),
            pltpu.VMEM((4, HALF, width), f32),
            pltpu.VMEM((4, HALF, width), f32),
            pltpu.SemaphoreType.DMA((12,)),
            pltpu.SemaphoreType.DMA((2, 2)),
            pltpu.SemaphoreType.DMA((2, 3)),
        ]
        + dma(8, 8, 2, 2, 4, 4),
        compiler_params=pltpu.CompilerParams(collective_id=1, has_side_effects=True, vmem_limit_bytes=VMEM_LIMIT),
        name="feed_back",
    )(
        d_out,
        d_own,
        d_first,
        for_gate,
        for_up,
        other,
        w_gate,
        w_up,
        w_down,
        w_out,
        middle,
        branch,
        dy,
        gains,
    )


def visible_pairs(shape, i, segments):
    row = lax.broadcasted_iota(jnp.int32, shape, 0) + i * TILE
    col = lax.broadcasted_iota(jnp.int32, shape, 1)
    first = jnp.sum((segments[...] == 0).astype(jnp.int32), axis=1, keepdims=True)
    return (row >= col) & ((row < first) == (col < first))


def attention_kernel(
    nx,
    tokens,
    w_query,
    w_key,
    w_value,
    w_out,
    segments,
    gain_0,
    gain_1,
    gain_2,
    gain_3,
    gain_4,
    gain_5,
    normed_hbm,
    query_hbm,
    keys_hbm,
    values_hbm,
    query_raw_hbm,
    keys_raw_hbm,
    log_total_hbm,
    context_hbm,
    w_out_all_hbm,
    middle_hbm,
    branch,
    gains,
    middle,
    normed,
    query,
    keys,
    values,
    query_raw,
    keys_raw,
    log_total,
    context,
    w_out_all,
    stores,
    out_own,
    out_land,
    context_own,
    context_core,
    context_land,
    context_all,
    c_send,
    c_recv,
    y_send,
    y_recv,
    x_send,
    x_recv,
):
    z, x, y, c, near = spots(nx)
    cs, ys, xs = (c_send, c_recv), (y_send, y_recv), (x_send, x_recv)
    length, width = tokens.shape
    head = w_query.shape[1]
    given = (gain_0, gain_1, gain_2, gain_3, gain_4, gain_5)
    gain_loads = [
        pltpu.make_async_copy(ref, gains.at[k, pl.ds(0, ref.shape[0])], stores.at[k]) for k, ref in enumerate(given)
    ]
    for copy in gain_loads:
        copy.start()
    out_own[...] = w_out[...].astype(f32)
    greet([near[k] for k in ("c", "y", "x")])
    mine = pl.ds(pl.multiple_of(x * (head // 2), 8), head // 2)
    out_y = remote(out_own.at[mine], out_land.at[0, mine], ys, 0, near["y"])
    out_x = remote(out_land.at[0, mine], out_land.at[0, mine], xs, 0, near["x"])
    out_c = remote(out_own, out_land.at[1], cs, 0, near["c"])
    out_yc = remote(out_land.at[0], out_land.at[2], cs, 1, near["c"])
    out_y.start()
    out_c.start()
    w_out_all[:head, :] = w_out[...]

    for copy in gain_loads:
        copy.wait()

    def norm(v, gain):
        return v * lax.rsqrt(jnp.mean(v * v, axis=-1, keepdims=True) + epsilon) * (1.0 + gain)

    def inputs(i, carry):
        at = pl.ds(pl.multiple_of(i * TILE, TILE), TILE)
        n = norm(tokens[at, :].astype(f32), gain_row(gains, 0)).astype(bf16)
        normed[at, :] = n
        raw = product(n, w_query[...])
        query_raw[at, :] = raw
        query[at, :] = norm(raw, gain_row(gains, 4)[:, :head]).astype(bf16)
        raw = product(n, w_key[...])
        keys_raw[at, :] = raw
        keys[at, :] = norm(raw, gain_row(gains, 5)[:, :head]).astype(bf16)
        values[at, :] = product(n, w_value[...]).astype(bf16)
        return carry

    lax.fori_loop(0, length // TILE, inputs, 0)
    for i in range(length // TILE):
        at, seen = slice(i * TILE, (i + 1) * TILE), (i + 1) * TILE
        s = product_t(query[at, :], keys[:seen, :]) * score_scale
        s = jnp.where(visible_pairs(s.shape, i, segments), s, -1e30)
        largest = jnp.max(s, axis=-1, keepdims=True)
        e = jnp.exp(s - largest)
        total = jnp.sum(e, axis=-1, keepdims=True)
        log_total[at, :] = largest + jnp.log(total)
        low_context = product((e / total).astype(bf16), values[:seen, :]).astype(bf16)
        context[at, :] = low_context
        context_own[at, :] = low_context.astype(f32)

    out_copies = []

    def put(src, dst):
        copy = pltpu.make_async_copy(src, dst, stores.at[len(out_copies)])
        copy.start()
        out_copies.append(copy)

    span = length // 2
    to_core = remote(context_own.at[pl.ds(pl.multiple_of((1 - c) * span, span), span)], context_core, cs, 2, near["c"])
    to_core.start()

    def local(i, other):
        dy = 1 - i // 2
        return pl.multiple_of(((y ^ other) ^ dy) * QUARTER + (i % 2) * HALF, HALF)

    def context_copy(i, k):
        if k == 0:
            src = context_own.at[pl.ds(pl.multiple_of(c * span + local(i, 1), HALF), HALF)]
        else:
            src = context_core.at[pl.ds(local(i, 1), HALF)]
        return remote(src, context_land.at[k, i], ys, 1 + 2 * i + k, near["y"])

    context_copy(0, 0).start()
    for src, dst in (
        (normed, normed_hbm),
        (query, query_hbm),
        (keys, keys_hbm),
        (values, values_hbm),
        (query_raw, query_raw_hbm),
        (keys_raw, keys_raw_hbm),
        (log_total, log_total_hbm),
        (context, context_hbm),
    ):
        put(src, dst)
    out_y.wait_recv()
    out_x.start()
    to_core.wait_recv()
    for i in range(4):
        for k in range(2):
            if i + k > 0:
                context_copy(i, k).start()
    out_c.wait_recv()
    w_out_all[2 * head : 3 * head, :] = out_land[1].astype(bf16)
    for i in range(4):
        rows = pl.ds(i * HALF, HALF)
        context_all[rows, :head] = context[pl.ds(pl.multiple_of(c * span + local(i, 0), HALF), HALF), :]
        context_all[rows, 2 * head : 3 * head] = context_core[pl.ds(local(i, 0), HALF), :].astype(bf16)
    out_x.wait_recv()
    out_yc.start()
    w_out_all[head : 2 * head, :] = out_land[0].astype(bf16)
    out_yc.wait_recv()
    w_out_all[3 * head :, :] = out_land[2].astype(bf16)
    put(w_out_all, w_out_all_hbm)

    def middle_copy(i):
        at = pl.multiple_of(i * TILE, TILE)
        return remote(middle.at[pl.ds(at, HALF)], middle.at[pl.ds(at + HALF, HALF)], cs, 3 + i, near["c"])

    def middle_tile(i, carry):
        rows = pl.ds(pl.multiple_of(i * HALF, HALF), HALF)
        context_copy(i, 0).wait_recv()
        context_all[rows, head : 2 * head] = context_land[0, i].astype(bf16)
        context_copy(i, 1).wait_recv()
        context_all[rows, 3 * head :] = context_land[1, i].astype(bf16)
        b = product(context_all[rows, :], w_out_all[...])
        branch[i % 2] = b
        hidden = tokens[pl.ds(pl.multiple_of(c * span + local(i, 0), HALF), HALF), :].astype(f32)
        middle[pl.ds(pl.multiple_of(i * TILE, TILE), HALF), :] = hidden + norm(b, gain_row(gains, 1))
        middle_copy(i).start()
        return carry

    lax.fori_loop(0, 4, middle_tile, 0)
    for i in range(4):
        middle_copy(i).wait()
        put(middle.at[pl.ds(i * TILE, TILE)], middle_hbm.at[pl.ds(i * TILE, TILE)])
        for k in range(2):
            context_copy(i, k).wait_send()
    for copy in (out_y, out_x, out_c, out_yc, to_core):
        copy.wait_send()
    for copy in out_copies:
        copy.wait()


def attend(nx, tokens, w_query, w_key, w_value, w_out, segment_ids, *gains):
    length, width = tokens.shape
    head = w_query.shape[1]
    of_head = jax.ShapeDtypeStruct((length, head), bf16)
    raw = jax.ShapeDtypeStruct((length, head), f32)
    return pl.pallas_call(
        functools.partial(attention_kernel, nx),
        out_shape=(
            jax.ShapeDtypeStruct((length, width), bf16),
            of_head,
            of_head,
            of_head,
            raw,
            raw,
            jax.ShapeDtypeStruct((length, 1), f32),
            of_head,
            jax.ShapeDtypeStruct((4 * head, width), bf16),
            jax.ShapeDtypeStruct((length, width), f32),
            jax.ShapeDtypeStruct((2, HALF, width), f32),
            jax.ShapeDtypeStruct((8, width), f32),
        ),
        in_specs=[VMEM] * 6 + [ANY] * 6,
        out_specs=(ANY,) * 10 + (VMEM,) * 2,
        scratch_shapes=[
            pltpu.VMEM((length, width), f32),
            pltpu.VMEM((length, width), bf16),
            pltpu.VMEM((length, head), bf16),
            pltpu.VMEM((length, head), bf16),
            pltpu.VMEM((length, head), bf16),
            pltpu.VMEM((length, head), f32),
            pltpu.VMEM((length, head), f32),
            pltpu.VMEM((length, 1), f32),
            pltpu.VMEM((length, head), bf16),
            pltpu.VMEM((4 * head, width), bf16),
            pltpu.SemaphoreType.DMA((13,)),
            pltpu.VMEM((head, width), f32),
            pltpu.VMEM((3, head, width), f32),
            pltpu.VMEM((length, head), f32),
            pltpu.VMEM((length // 2, head), f32),
            pltpu.VMEM((2, 4, HALF, head), f32),
            pltpu.VMEM((length // 2, 4 * head), bf16),
        ]
        + dma(7, 7, 9, 9, 1, 1),
        compiler_params=pltpu.CompilerParams(collective_id=3, has_side_effects=True, vmem_limit_bytes=VMEM_LIMIT),
        name="attend",
    )(
        tokens,
        w_query,
        w_key,
        w_value,
        w_out,
        segment_ids.reshape(1, length),
        *gains,
    )


def reduce_kernel(
    nx,
    d_out_hbm,
    d_other_hbm,
    normed_hbm,
    other_hbm,
    pair_own_hbm,
    pair_other_hbm,
    pair_gates_hbm,
    d_branch_hbm,
    d_middle_hbm,
    tokens_hbm,
    normed_in_hbm,
    query_hbm,
    keys_hbm,
    values_hbm,
    query_raw_hbm,
    keys_raw_hbm,
    context_hbm,
    heads_hbm,
    w_query_hbm,
    w_key_hbm,
    w_value_hbm,
    log_total,
    segments,
    gain_rows,
    of_ffn_out,
    of_middle,
    down_out,
    gate_out,
    up_out,
    query_out,
    out_out,
    key_out,
    value_out,
    input_grad,
    gains,
    input_stage,
    ff_stage,
    dw,
    x_land,
    z2_land,
    z1_land,
    from_core,
    from_y,
    branch_land,
    input_own,
    input_land,
    d_qkv,
    attn,
    attn_z1,
    attn_x,
    attn_z2,
    kv_core,
    kv_across,
    kv_own,
    kv_y,
    kv_wide,
    kv_wide_core,
    gains_land,
    heads_mine,
    heads_y,
    got_c,
    got_y,
    loads,
    c_send,
    c_recv,
    y_send,
    y_recv,
    x_send,
    x_recv,
    z2_send,
    z2_recv,
    z1_send,
    z1_recv,
):
    z, x, y, c, near = spots(nx)
    zh, zl = z // 2, z % 2
    cs, ys, xs = (c_send, c_recv), (y_send, y_recv), (x_send, x_recv)
    z2s, z1s = (z2_send, z2_recv), (z1_send, z1_recv)
    length, width = d_out_hbm.shape
    half = pair_own_hbm.shape[1]
    head = query_hbm.shape[1]
    blk = x_land.shape[1]
    own_row = pl.multiple_of((c * 2 + y) * QUARTER, QUARTER)

    def block(a, b):
        return pl.ds(pl.multiple_of(b * blk, 8), blk)

    def quarter_rows(dc, dy):
        return pl.ds(pl.multiple_of(((c ^ dc) * 2 + (y ^ dy)) * QUARTER, QUARTER), QUARTER)

    heads_in = pltpu.make_async_copy(heads_hbm.at[0], heads_mine, loads.at[6])
    heads_in_y = pltpu.make_async_copy(heads_hbm.at[1], heads_y.at[0], loads.at[7])
    heads_c_copy = remote(heads_hbm.at[pl.ds(2, 2)], got_c, cs, 11, near["c"])
    heads_y_copy = remote(heads_y, got_y, ys, 7, near["y"])

    branch_y = remote(d_branch_hbm, branch_land.at[0], ys, 0, near["y"])
    branch_c = remote(d_branch_hbm, branch_land.at[1], cs, 0, near["c"])
    branch_fwd = remote(branch_land.at[0], branch_land.at[2], cs, 1, near["c"])

    def place(n):
        return n // 2 * 2 + (1 - zl if n % 2 == 0 else zl)

    def owner(n):
        return 2 * (1 - zh if n < 2 else zh) + (1 - zl if n % 2 == 0 else zl)

    def x_copy(m, n):
        slot = m * 4 + place(n)
        return remote(dw.at[m, block(dw, owner(n) * 2 + (1 - x))], x_land.at[slot], xs, slot, near["x"])

    def z2_copy(m, n):
        slot = m * 2 + place(n)
        return remote(dw.at[m, block(dw, owner(n) * 2 + x)], z2_land.at[slot], z2s, slot, near["z2"])

    def z1_copy(m):
        return remote(dw.at[m, block(dw, (2 * zh + 1 - zl) * 2 + x)], z1_land.at[m], z1s, m, near["z1"])

    def start_x(*blocks):
        for m, j in blocks:
            x_copy(m, j).start()

    arrived = set()

    def wait_x(m, j):
        if (m, j) not in arrived:
            arrived.add((m, j))
            x_copy(m, j).wait_recv()

    inner = (z == 1) | (z == 2)

    def far(*blocks):
        for m, k in blocks:
            wait_x(m, k)
            rows = block(dw, owner(k) * 2 + x)
            dw[m, rows, :] = dw[m, rows, :] + x_land[m * 4 + place(k)]

            @pl.when(inner)
            def _():
                z2_copy(m, k).start()

    def outer(m, k):
        @pl.when(jnp.logical_not(inner))
        def _():
            z2_copy(m, k).start()

    def close(m):
        for k in range(2):
            wait_x(m, 2 + k)
            z2_copy(m, k).wait_recv()
            rows = block(dw, owner(2 + k) * 2 + x)
            dw[m, rows, :] = dw[m, rows, :] + x_land[m * 4 + place(2 + k)] + z2_land[m * 2 + place(k)]
            if k == 0:
                z1_copy(m).start()

    def finish(m, ref):
        z1_copy(m).wait_recv()
        own, other = dw[m, block(dw, (2 * zh + zl) * 2 + x), :], z1_land[m]
        ff_stage[:, :half] = jnp.where(zl == 0, own, other)
        ff_stage[:, half:] = jnp.where(zl == 0, other, own)[:, : ref.shape[1] - half]
        copy = pltpu.make_async_copy(ff_stage, ref, loads.at[1])
        copy.start()
        copy.wait()

    def copies(pairs):
        started = [pltpu.make_async_copy(src, dst, loads.at[k]) for k, (src, dst) in enumerate(pairs)]
        for copy in started:
            copy.start()
        return started

    def weights(left, right):
        far_size = pl.cdiv(width // 2, HALF) * HALF
        far_at = pl.multiple_of((1 - zh) * (width - far_size), HALF)
        near_at = pl.multiple_of(zh * far_size, HALF)

        def piece(m, lo, at, size):
            rows = pl.ds(pl.multiple_of(at, HALF), size)
            cols = pl.ds(pl.multiple_of(lo, HALF), half)
            dw[m, rows, :] = t_product(left[:, rows], right[:, cols])

        def form(m, lo, at, size):
            def one(r, carry):
                piece(m, lo, at + r * 2 * HALF, 2 * HALF)
                return carry

            lax.fori_loop(0, size // (2 * HALF), one, 0)

        first_at = owner(0) * 2 * blk // HALF * HALF
        second_at = jnp.where(first_at == far_at, far_at + 3 * HALF, far_at)

        def form_first(m, lo):
            piece(m, lo, first_at, 3 * HALF)
            start_x((m, 0))
            piece(m, lo, second_at, far_size - 3 * HALF)

        waits = copies(
            [
                (d_out_hbm, left.at[pl.ds(0, length)]),
                (d_other_hbm, left.at[pl.ds(length, length)]),
                (pair_own_hbm, right.at[pl.ds(0, length), pl.ds(0, half)]),
                (pair_other_hbm, right.at[pl.ds(length, length), pl.ds(0, half)]),
            ]
        )
        heads_in.start()
        heads_in_y.start()
        greet([near[k] for k in ("c", "y", "x", "z2", "z1")])
        heads_c_copy.start()
        for copy in waits:
            copy.wait()
        form_first(0, 0)
        start_x((0, 1))
        heads_c_copy.wait_recv()
        heads_in_y.wait()
        heads_y[1] = got_c[1]
        heads_y_copy.start()
        branch_y.start()
        branch_c.start()
        form(0, 0, near_at, width - far_size)
        for copy in copies(
            [
                (normed_hbm, left.at[pl.ds(0, length)]),
                (other_hbm, left.at[pl.ds(length, length)]),
                (pair_gates_hbm, right),
            ]
        ):
            copy.wait()
        def form_far(m, carry):
            form_first(m, (m - 1) * half)
            start_x((m, 1))
            return carry

        def form_near(m, carry):
            form(m, (m - 1) * half, near_at, width - far_size)
            return carry

        lax.fori_loop(1, 3, form_far, 0)
        far((0, 0))
        outer(0, 0)
        lax.fori_loop(1, 3, form_near, 0)
        start_x((0, 2), (0, 3), (1, 2), (1, 3), (2, 2), (2, 3))

    pl.run_scoped(weights, pltpu.VMEM((2 * length, width), bf16), pltpu.VMEM((2 * length, 2 * half), bf16))

    def total_of(a):
        return jnp.sum(a, axis=0, keepdims=True)

    gains[...] = jnp.zeros_like(gains)
    gains[1:2, :] = total_of(of_middle[1])
    gains[2:3, :] = total_of(of_middle[0])
    gains[3:4, :] = 0.25 * total_of(of_ffn_out[...])

    def back_norm(raw, gain, grad):
        inverse = lax.rsqrt(jnp.mean(raw * raw, axis=-1, keepdims=True) + epsilon)
        hat = raw * inverse
        scaled = grad * (1.0 + gain)
        return inverse * (scaled - hat * jnp.mean(scaled * hat, axis=-1, keepdims=True)), grad * hat

    def attention(query, keys, values, query_raw, keys_raw, grad_context, d_keys, d_values):
        for copy in copies(
            [
                (query_hbm, query),
                (keys_hbm, keys),
                (values_hbm, values),
                (query_raw_hbm, query_raw),
                (keys_raw_hbm, keys_raw),
            ]
        ):
            copy.wait()
        heads_in.wait()
        grad_context[quarter_rows(0, 0), :] = heads_mine[...].astype(bf16)
        grad_context[quarter_rows(1, 0), :] = got_c[0].astype(bf16)
        heads_y_copy.wait_recv()
        grad_context[quarter_rows(0, 1), :] = got_y[0].astype(bf16)
        grad_context[quarter_rows(1, 1), :] = got_y[1].astype(bf16)
        d_keys[...] = jnp.zeros_like(d_keys)
        d_values[...] = jnp.zeros_like(d_values)

        def back_tile(seen, i, carry):
            at = pl.ds(pl.multiple_of(i * TILE, TILE), TILE)
            q, k = query[at, :], keys[:seen, :]
            s = product_t(q, k) * score_scale
            p = jnp.exp(jnp.where(visible_pairs(s.shape, i, segments), s, -1e30) - log_total[at, :])
            g = grad_context[at, :]
            dp = product_t(g, values[:seen, :])
            balance = jnp.sum(dp * p, axis=-1, keepdims=True)
            ds = (p * (dp - balance)).astype(bf16)
            dq, of_gain = back_norm(query_raw[at, :], gain_row(gain_rows, 4)[:, :head], product(ds, k) * score_scale)
            d_qkv[at, :head] = dq.astype(bf16)
            gains[4:5, :head] = gains[4:5, :head] + jnp.sum(of_gain, axis=0, keepdims=True)
            d_keys[:seen, :] = d_keys[:seen, :] + t_product(ds, q)
            d_values[:seen, :] = d_values[:seen, :] + t_product(p.astype(bf16), g)
            return carry

        tiles = length // TILE
        lax.fori_loop(0, tiles // 2, functools.partial(back_tile, length // 2), 0)
        lax.fori_loop(tiles // 2, tiles, functools.partial(back_tile, length), 0)

        def keys_tile(i, carry):
            at = pl.ds(pl.multiple_of(i * TILE, TILE), TILE)
            dk, of_gain = back_norm(keys_raw[at, :], gain_row(gain_rows, 5)[:, :head], d_keys[at, :] * score_scale)
            d_qkv[at, head : 2 * head] = dk.astype(bf16)
            gains[5:6, :head] = gains[5:6, :head] + jnp.sum(of_gain, axis=0, keepdims=True)
            d_qkv[at, 2 * head :] = d_values[at, :].astype(bf16)
            return carry

        lax.fori_loop(0, tiles, keys_tile, 0)

    pl.run_scoped(
        attention,
        pltpu.VMEM((length, head), bf16),
        pltpu.VMEM((length, head), bf16),
        pltpu.VMEM((length, head), bf16),
        pltpu.VMEM((length, head), f32),
        pltpu.VMEM((length, head), f32),
        pltpu.VMEM((length, head), bf16),
        pltpu.VMEM((length, head), f32),
        pltpu.VMEM((length, head), f32),
    )
    far((0, 1))

    def put_input(dc, dy):
        copy = pltpu.make_async_copy(input_stage, input_grad.at[quarter_rows(dc, dy)], loads.at[0])
        copy.start()
        copy.wait()

    def attn_z1_copy(i):
        b = (2 * (i // 2) + 1 - zl) * 2 + i % 2
        return remote(attn.at[block(attn, b)], attn_z1.at[i], z1s, 3 + i, near["z1"])

    def attn_x_copy(j):
        b = (2 * (zh ^ j) + zl) * 2 + 1 - x
        return remote(attn.at[block(attn, b)], attn_x.at[j], xs, 12 + j, near["x"])

    attn_z2_copy = remote(attn.at[block(attn, (2 * (1 - zh) + zl) * 2 + x)], attn_z2, z2s, 6, near["z2"])

    input_y = remote(input_own, input_land.at[0], ys, 4, near["y"])
    input_c = remote(input_own, input_land.at[1], cs, 7, near["c"])
    input_fwd = remote(input_land.at[0], input_land.at[2], cs, 8, near["c"])

    hops = [
        remote(gains, gains_land.at[k], sems, index, near[to])
        for k, (sems, index, to) in enumerate([(cs, 10, "c"), (ys, 6, "y"), (xs, 14, "x"), (z1s, 7, "z1"), (z2s, 7, "z2")])
    ]

    def hop(k):
        hops[k].start()

    def arrive(k):
        hops[k].wait()
        gains[...] = gains[...] + gains_land[k]

    def rest(w_qkv, part, kv_halves):
        def of_inputs(normed_in, kv):
            for copy in copies([(normed_in_hbm, normed_in)]):
                copy.wait()
            for k in range(2):
                kv[k] = t_product(normed_in[...], d_qkv[:, (1 + k) * head : (2 + k) * head])
            to_core = remote(kv.at[1 - c], kv_core, cs, 6, near["c"])
            to_core.start()
            attn[:, :head] = t_product(normed_in[...], d_qkv[:, :head])
            to_core.wait_recv()
            for k in range(2):
                lanes = slice(k * (head // 2), (k + 1) * (head // 2))
                kv_halves[k] = kv[c, :, lanes] + kv_core[:, lanes]
            to_core.wait_send()

        pl.run_scoped(of_inputs, pltpu.VMEM((length, width), bf16), pltpu.VMEM((2, width, head), f32))
        to_y = remote(kv_halves.at[1 - y], kv_across, ys, 3, near["y"])
        to_y.start()
        for copy in copies(
            [
                (w_query_hbm, w_qkv.at[:, pl.ds(0, head)]),
                (w_key_hbm, w_qkv.at[:, pl.ds(head, head)]),
                (w_value_hbm, w_qkv.at[:, pl.ds(2 * head, head)]),
            ]
        ):
            copy.wait()

        def core_copy(i):
            return remote(part.at[i, pl.ds(HALF, HALF)], from_core.at[i], cs, 2 + i, near["c"])

        def y_copy(h):
            return remote(part.at[h, pl.ds(0, HALF)], from_y.at[h], ys, 1 + h, near["y"])

        def tile(i, carry):
            for dc in range(2):
                rows = d_qkv[pl.ds(tile_row(c, y, i, dc), HALF), :]
                part[i, dc * HALF : (dc + 1) * HALF] = product_t(rows, w_qkv[...])
            core_copy(i).start()
            core_copy(i).wait_recv()
            part[i, :HALF] = part[i, :HALF] + from_core[i]

            @pl.when(i < 2)
            def _():
                y_copy(i).start()

            return carry

        lax.fori_loop(0, 4, tile, 0)


        far((1, 0))
        outer(0, 1)

        def of_branch(context, d_branch, d_middle, tokens):
            waits = copies(
                [
                    (context_hbm, context),
                    (d_branch_hbm, d_branch),
                    (d_middle_hbm, d_middle),
                    (tokens_hbm.at[pl.ds(own_row, QUARTER)], tokens),
                ]
            )
            branch_y.wait_recv()
            branch_fwd.start()
            for copy in waits:
                copy.wait()
            acc = t_product(d_branch[...].astype(bf16), context[quarter_rows(0, 0), :])
            branch_c.wait_recv()
            branch_fwd.wait_recv()
            for k, (dc, dy) in enumerate([(0, 1), (1, 0), (1, 1)]):
                acc = acc + t_product(branch_land[k].astype(bf16), context[quarter_rows(dc, dy), :])
            attn[:, head : 2 * head] = acc
            far((1, 1))
            to_y.wait_recv()
            attn[:, 2 * head :] = kv_halves[y] + kv_across[...]
            for i in range(4):
                attn_z1_copy(i).start()
            far((2, 0), (2, 1))
            outer(1, 0)
            for h in range(2):
                y_copy(h).wait_recv()
                at = slice(h * HALF, (h + 1) * HALF)
                grad = part[2 + h, :HALF] + from_y[h]
                d_in, of_gain = back_norm(tokens[at, :].astype(f32), gain_row(gain_rows, 0), grad)
                gains[0:1, :] = gains[0:1, :] + jnp.sum(of_gain, axis=0, keepdims=True)
                d = (d_middle[at, :] + d_in).astype(bf16)
                input_stage[at, :] = d
                input_own[at, :] = d.astype(f32)

        pl.run_scoped(
            of_branch,
            pltpu.VMEM((length, head), bf16),
            pltpu.VMEM((QUARTER, width), f32),
            pltpu.VMEM((QUARTER, width), f32),
            pltpu.VMEM((QUARTER, width), bf16),
        )
        hop(0)
        arrive(0)
        hop(1)
        input_y.start()
        input_c.start()
        outer(1, 1)
        put_input(0, 0)
        for i in range(4):
            core_copy(i).wait_send()
        for h in range(2):
            y_copy(h).wait_send()
        to_y.wait_send()

    pl.run_scoped(
        rest,
        pltpu.VMEM((width, 3 * head), bf16),
        pltpu.VMEM((4, TILE, width), f32),
        pltpu.VMEM((2, width, head // 2), f32),
    )

    arrive(1)
    hop(2)
    close(0)
    outer(2, 0)
    input_y.wait_recv()
    input_fwd.start()
    input_stage[...] = input_land[0].astype(bf16)
    put_input(0, 1)
    input_c.wait_recv()
    input_stage[...] = input_land[1].astype(bf16)
    put_input(1, 0)
    close(1)
    outer(2, 1)
    for i in range(4):
        attn_z1_copy(i).wait_recv()
        rows = block(attn, (2 * (i // 2) + zl) * 2 + i % 2)
        attn[rows, :] = attn[rows, :] + attn_z1[i]
    for j in (1, 0):
        attn_x_copy(j).start()
    input_fwd.wait_recv()
    input_stage[...] = input_land[2].astype(bf16)
    put_input(1, 1)
    arrive(2)
    hop(3)
    for j in (1, 0):
        attn_x_copy(j).wait_recv()
        rows = block(attn, (2 * (zh ^ j) + zl) * 2 + x)
        attn[rows, :] = attn[rows, :] + attn_x[j]
        if j == 1:
            attn_z2_copy.start()
    close(2)
    finish(0, down_out)
    finish(1, gate_out)
    attn_z2_copy.wait_recv()
    total = attn[block(attn, (2 * zh + zl) * 2 + x), :] + attn_z2[...]
    query_out[...] = total[:, :head]
    out_out[...] = total[:, head : 2 * head]
    kv_own[...] = total[:, 2 * head :]
    wide_y = remote(kv_own, kv_y, ys, 5, near["y"])
    wide_y.start()
    arrive(3)
    hop(4)
    wide_y.wait_recv()
    kv_wide[:, : head // 2] = jnp.where(y == 0, kv_own[...], kv_y[...])
    kv_wide[:, head // 2 :] = jnp.where(y == 0, kv_y[...], kv_own[...])
    wide_c = remote(kv_wide, kv_wide_core, cs, 9, near["c"])
    wide_c.start()
    wide_c.wait_recv()
    key_out[...] = jnp.where(c == 0, kv_wide[...], kv_wide_core[...])
    value_out[...] = jnp.where(c == 0, kv_wide_core[...], kv_wide[...])
    arrive(4)
    finish(2, up_out)
    for m in range(3):
        for j in range(4):
            x_copy(m, j).wait_send()
        for k in range(2):
            z2_copy(m, k).wait_send()
        z1_copy(m).wait_send()
    for i in range(4):
        attn_z1_copy(i).wait_send()
    for j in range(2):
        attn_x_copy(j).wait_send()
    for copy in (attn_z2_copy, branch_y, branch_c, branch_fwd, input_y, input_c, input_fwd, wide_y, wide_c, heads_c_copy, heads_y_copy):
        copy.wait_send()


def reduce_all(nx, dp_size, columns, whole, small):
    length, width = whole[0].shape
    half = whole[4].shape[1]
    head = whole[11].shape[1]
    blk = width // dp_size
    return pl.pallas_call(
        functools.partial(reduce_kernel, nx),
        out_shape=(
            *[jax.ShapeDtypeStruct((blk, columns), f32)] * 3,
            *[jax.ShapeDtypeStruct((blk, head), f32)] * 4,
            jax.ShapeDtypeStruct((length, width), bf16),
            jax.ShapeDtypeStruct((8, width), f32),
        ),
        in_specs=[ANY] * len(whole) + [VMEM] * len(small),
        out_specs=(ANY,) * 3 + (VMEM,) * 4 + (ANY, VMEM),
        scratch_shapes=[
            pltpu.VMEM((QUARTER, width), bf16),
            pltpu.VMEM((blk, columns), f32),
            pltpu.VMEM((3, width, half), f32),
            pltpu.VMEM((12, blk, half), f32),
            pltpu.VMEM((6, blk, half), f32),
            pltpu.VMEM((3, blk, half), f32),
            pltpu.VMEM((4, HALF, width), f32),
            pltpu.VMEM((2, HALF, width), f32),
            pltpu.VMEM((3, QUARTER, width), f32),
            pltpu.VMEM((QUARTER, width), f32),
            pltpu.VMEM((3, QUARTER, width), f32),
            pltpu.VMEM((length, 3 * head), bf16),
            pltpu.VMEM((width, 2 * head + head // 2), f32),
            pltpu.VMEM((4, blk, 2 * head + head // 2), f32),
            pltpu.VMEM((2, blk, 2 * head + head // 2), f32),
            pltpu.VMEM((blk, 2 * head + head // 2), f32),
            pltpu.VMEM((width, head), f32),
            pltpu.VMEM((width, head // 2), f32),
            pltpu.VMEM((blk, head // 2), f32),
            pltpu.VMEM((blk, head // 2), f32),
            pltpu.VMEM((blk, head), f32),
            pltpu.VMEM((blk, head), f32),
            pltpu.VMEM((5, 8, width), f32),
            pltpu.VMEM((QUARTER, head), f32),
            pltpu.VMEM((2, QUARTER, head), f32),
            pltpu.VMEM((2, QUARTER, head), f32),
            pltpu.VMEM((2, QUARTER, head), f32),
        ]
        + dma(8, 12, 12, 8, 8, 15, 15, 8, 8, 8, 8),
        compiler_params=pltpu.CompilerParams(collective_id=2, has_side_effects=True, vmem_limit_bytes=VMEM_LIMIT),
        name="reduce_all",
    )(*whole, *small)


def settle_kernel(*refs):
    count = (len(refs) - 1) // 3
    sems = refs[-1]
    loads, puts = [], []
    for k in range(count):
        given, out, held = refs[k], refs[count + k], refs[2 * count + k]
        loads.append(pltpu.make_async_copy(given, held, sems.at[0, k]))
        puts.append(pltpu.make_async_copy(held, out, sems.at[1, k]))
    for copy in loads:
        copy.start()
    for load, put in zip(loads, puts):
        load.wait()
        put.start()
    for copy in puts:
        copy.wait()


def settle(*arrays):
    return pl.pallas_call(
        settle_kernel,
        out_shape=tuple(jax.ShapeDtypeStruct(a.shape, a.dtype) for a in arrays),
        in_specs=[ANY] * len(arrays),
        out_specs=(ANY,) * len(arrays),
        scratch_shapes=[pltpu.VMEM(a.shape, a.dtype) for a in arrays] + [pltpu.SemaphoreType.DMA((2, len(arrays)))],
        compiler_params=pltpu.CompilerParams(vmem_limit_bytes=VMEM_LIMIT),
        name="settle",
    )(*arrays)


def body(
    links,
    tokens,
    segment_ids,
    cotangent,
    w_query,
    w_key,
    w_value,
    w_out,
    w_gate,
    w_up,
    w_down,
    gain_attn_in,
    gain_attn_out,
    gain_ffn_in,
    gain_ffn_out,
    gain_query,
    gain_key,
):
    length, width = tokens.shape
    head = w_query.shape[1]
    columns = w_gate.shape[1]
    nx = links.nx
    blk = width // links.dp_size
    dp = lax.axis_index("dp")
    wg, wu = w_gate.T, w_up.T
    (
        normed_low,
        query_low,
        keys_low,
        values_low,
        query_raw,
        keys_raw,
        log_total,
        context_low,
        w_out_all,
        middle,
        branch,
        gain_rows,
    ) = attend(
        nx,
        tokens,
        w_query,
        w_key,
        w_value,
        w_out,
        segment_ids,
        gain_attn_in,
        gain_attn_out,
        gain_ffn_in,
        gain_ffn_out,
        gain_query,
        gain_key,
    )
    normed_two, normed_other, d_out, d_own, d_first, layer_out, pair_own, for_gate, for_up, of_ffn_out = feed_forward(
        nx, middle, cotangent, gain_rows, wg, wu, w_down
    )
    d_other, pair_other, pair_gates, heads, d_branch_own, d_middle, of_middle = feed_back(
        nx,
        d_out,
        d_own,
        d_first,
        for_gate,
        for_up,
        normed_other,
        wg,
        wu,
        w_down,
        w_out_all,
        middle,
        branch.reshape(QUARTER, width),
        cotangent,
        gain_rows,
    )
    *sums, gains = reduce_all(
        nx,
        links.dp_size,
        columns,
        [
            d_out,
            d_other,
            normed_two,
            normed_other,
            pair_own,
            pair_other,
            pair_gates,
            d_branch_own,
            d_middle,
            tokens,
            normed_low,
            query_low,
            keys_low,
            values_low,
            query_raw,
            keys_raw,
            context_low,
            heads,
            w_query,
            w_key,
            w_value,
        ],
        [log_total, segment_ids.reshape(1, length), gain_rows, of_ffn_out, of_middle],
    )
    layer_out, down_t, gate, up, query, out_t, key, value, input_grad = settle(layer_out, *sums)
    part = lax.dynamic_slice_in_dim(gains, dp * blk, blk, 1)
    hb = head // links.dp_size
    head_part = lax.dynamic_slice_in_dim(gains, dp * hb, hb, 1)
    return (
        layer_out,
        input_grad,
        query,
        key,
        value,
        out_t.T,
        gate,
        up,
        down_t.T,
        part[0],
        part[1],
        part[2],
        part[3],
        head_part[4],
        head_part[5],
    )


def body_any(
    links,
    tokens,
    segment_ids,
    cotangent,
    w_query,
    w_key,
    w_value,
    w_out,
    w_gate,
    w_up,
    w_down,
    gain_attn_in,
    gain_attn_out,
    gain_ffn_in,
    gain_ffn_out,
    gain_query,
    gain_key,
):
    length, width = tokens.shape
    head = w_query.shape[1]
    quarter = length // 4
    half_ff = w_gate.shape[1] // 2
    nx = links.nx
    blk = width // links.dp_size
    dp, t = lax.axis_index("dp"), lax.axis_index("tensor")
    z, x = dp // nx, dp % nx
    y, c = t // 2, t % 2
    parity = z % 2
    one = jnp.where(segment_ids[0] < length, 1.0, 0.5).astype(f32)

    def keep_low(a):
        return (a * one).astype(bf16)

    def place(dc, dy):
        return ((c ^ dc) * 2 + (y ^ dy)) * quarter

    def rows(a, dc, dy):
        return lax.dynamic_slice_in_dim(a, place(dc, dy), quarter, 0)

    def to_absolute(pieces):
        stack = jnp.stack([pieces[0][0], pieces[0][1], pieces[1][0], pieces[1][1]])
        mine = c * 2 + y
        return jnp.concatenate([lax.dynamic_index_in_dim(stack, mine ^ b, 0, keepdims=False) for b in range(4)], axis=0)

    out_own = w_out.astype(f32)
    out_y = links.y(out_own)
    out_c = links.core(out_own)
    out_yc = links.core(out_y)
    w_out_all = jnp.concatenate([w_out, keep_low(out_c), keep_low(out_y), keep_low(out_yc)], axis=0)

    wg_h = jnp.where(parity == 0, w_gate[:, :half_ff], w_gate[:, half_ff:])
    wu_h = jnp.where(parity == 0, w_up[:, :half_ff], w_up[:, half_ff:])
    wd_h = jnp.where(parity == 0, w_down[:half_ff], w_down[half_ff:])

    hidden_in = tokens.astype(f32)
    normed_low = low(rms_norm(hidden_in, gain_attn_in))
    query_raw = product(normed_low, w_query)
    keys_raw = product(normed_low, w_key)
    query_low = low(rms_norm(query_raw, gain_query))
    keys_low = low(rms_norm(keys_raw, gain_key))
    values_low = low(product(normed_low, w_value))
    places = jnp.arange(length)
    allowed = (places[:, None] >= places[None, :]) & (segment_ids[:, None] == segment_ids[None, :])

    def scores_of():
        raw = product_t(query_low, keys_low) * score_scale
        return jnp.where(allowed, raw, -1e30)

    scores = scores_of()
    largest = jnp.max(scores, axis=-1, keepdims=True)
    exponent = jnp.exp(scores - largest)
    total = jnp.sum(exponent, axis=-1, keepdims=True)
    log_total = largest + jnp.log(total)
    context_low = low(product(low(exponent / total), values_low))

    context = context_low.astype(f32)
    mine = jnp.concatenate([rows(context, 0, 1), rows(context, 0, 0)], axis=0)
    of_core = links.core(jnp.concatenate([rows(context, 1, 1), rows(context, 1, 0)], axis=0))
    of_y = links.y(jnp.concatenate([rows(context, 0, 0), rows(context, 0, 1)], axis=0))
    of_yc = links.y(jnp.concatenate([of_core[quarter:], of_core[:quarter]], axis=0))
    context_all = jnp.concatenate([low(mine), keep_low(of_core), keep_low(of_y), keep_low(of_yc)], axis=1)
    branch = product(context_all, w_out_all)
    hidden_rows = jnp.concatenate([rows(tokens, 0, 1), rows(tokens, 0, 0)], axis=0).astype(f32)
    middle_own = hidden_rows + rms_norm(branch, gain_attn_out)
    middle_core = links.core(middle_own)

    middles, normed_two, inners, parts = [], [], [], []
    saved = []
    for k in range(2):
        at = slice(k * quarter, (k + 1) * quarter)
        middle = jnp.concatenate([middle_own[at], middle_core[at]], axis=0)
        normed_k = low(rms_norm(middle, gain_ffn_in))
        gate, upward = product(normed_k, w_gate), product(normed_k, w_up)
        inner = low(activate(gate, upward))
        part = product(inner, w_down)
        middles.append(middle)
        normed_two.append(normed_k)
        saved.append((gate, upward))
        parts.append(part)
    normed_own = low(rms_norm(middle_own, gain_ffn_in)).astype(f32)
    other_own = links.z1(normed_own)
    other_core = links.core(other_own)
    normed_other = jnp.concatenate([keep_low(other_own), keep_low(other_core)], axis=0)

    def gather_quarters(parts):
        sums = [part[:quarter] + links.core(part[quarter:]) for part in parts]
        return sums[1] + links.y(sums[0])

    output_q = gather_quarters(parts)
    output_y = links.y(output_q)
    output_c = links.core(output_q)
    output_yc = links.core(output_y)
    outputs = [jnp.concatenate([output_y, output_yc], axis=0), jnp.concatenate([output_q, output_c], axis=0)]
    grad_out = cotangent.astype(f32)
    d_outputs, layer_pieces, grad_ffn_out = [], [], 0.0
    for k in range(2):
        dy_k = jnp.concatenate([rows(cotangent, 0, 1 - k), rows(cotangent, 1, 1 - k)], axis=0).astype(f32)
        layer_k = low(middles[k] + rms_norm(outputs[k], gain_ffn_out))
        d_k, gain_k = rms_back(outputs[k], gain_ffn_out, dy_k)
        grad_ffn_out = grad_ffn_out + gain_k
        d_outputs.append(low(d_k))
        layer_pieces.append(layer_k)
    layer_out = to_absolute(
        [
            [layer_pieces[1][:quarter], layer_pieces[0][:quarter]],
            [layer_pieces[1][quarter:], layer_pieces[0][quarter:]],
        ]
    )

    d_own_rows = [d[:quarter].astype(f32) for d in d_outputs]
    got_own = [links.z1(d_own_rows[1]), links.z1(d_own_rows[0])]
    got_core = [links.core(g) for g in got_own]
    d_other = jnp.concatenate(
        [keep_low(got_own[1]), keep_low(got_own[0]), keep_low(got_core[1]), keep_low(got_core[0])], axis=0
    )

    back_parts = []
    for k in range(2):
        gate, upward = saved[k]
        d_inner = product_t(d_outputs[k], w_down)
        _, pull = jax.vjp(activate, gate, upward)
        d_gate, d_up = pull(d_inner)
        back_parts.append(product_t(low(d_gate), w_gate) + product_t(low(d_up), w_up))
    d_normed_q = gather_quarters(back_parts)
    middle_q = middle_own[quarter:]
    branch_q = branch[quarter:]
    dy_q = rows(cotangent, 0, 0).astype(f32)
    d_mid, grad_ffn_in = rms_back(middle_q, gain_ffn_in, d_normed_q)
    d_middle = dy_q + d_mid
    d_branch, grad_attn_out = rms_back(branch_q, gain_attn_out, d_middle)
    d_branch_low = low(d_branch)
    d_context = low(product_t(d_branch_low, w_out_all)).astype(f32)
    heads = [d_context[:, i * head : (i + 1) * head] for i in range(4)]
    c_got = links.core(jnp.concatenate([heads[1], heads[3]], axis=1))
    y_got = links.y(jnp.concatenate([heads[2], c_got[:, head:]], axis=1))
    grad_context = keep_low(
        to_absolute([[heads[0], y_got[:, :head]], [c_got[:, :head], y_got[:, head:]]])
    )
    d_branch_own = d_branch_low.astype(f32)
    d_branch_y = links.y(d_branch_own)
    d_branch_c = links.core(d_branch_own)
    d_branch_yc = links.core(d_branch_y)
    d_branch_all = jnp.concatenate(
        [d_branch_low, keep_low(d_branch_y), keep_low(d_branch_c), keep_low(d_branch_yc)], axis=0
    )
    context_rel = jnp.concatenate(
        [rows(context_low, 0, 0), rows(context_low, 0, 1), rows(context_low, 1, 0), rows(context_low, 1, 1)], axis=0
    )
    grad_w_out_t = t_product(d_branch_all, context_rel)

    attn_prob = jnp.exp(scores_of() - log_total)
    prob_low = low(attn_prob)
    grad_prob = product_t(grad_context, values_low)
    grad_values = low(t_product(prob_low, grad_context))
    balance = jnp.sum(grad_prob * attn_prob, axis=-1, keepdims=True)
    grad_scores = low(attn_prob * (grad_prob - balance))
    grad_query_n = product(grad_scores, keys_low) * score_scale
    grad_keys_n = t_product(grad_scores, query_low) * score_scale
    d_query, grad_gain_query = rms_back(query_raw, gain_query, grad_query_n)
    d_keys, grad_gain_key = rms_back(keys_raw, gain_key, grad_keys_n)
    d_query, d_keys = low(d_query), low(d_keys)
    d_qkv = jnp.concatenate([d_query, d_keys, grad_values], axis=1)
    w_qkv = jnp.concatenate([w_query, w_key, w_value], axis=1)
    in_parts = []
    for k in range(2):
        rows_k = jnp.concatenate([rows(d_qkv, 0, 1 - k), rows(d_qkv, 1, 1 - k)], axis=0)
        in_parts.append(product_t(rows_k, w_qkv))
    d_normed_in = gather_quarters(in_parts)
    hidden_q = rows(tokens, 0, 0).astype(f32)
    d_in, grad_attn_in = rms_back(hidden_q, gain_attn_in, d_normed_in)
    input_q = low(d_middle + d_in)
    input_own = input_q.astype(f32)
    input_y = links.y(input_own)
    input_c = links.core(input_own)
    input_yc = links.core(input_y)
    input_grad = keep_low(to_absolute([[input_own, input_y], [input_c, input_yc]]))

    grad_qkv = t_product(normed_low, d_qkv)
    grad_w_query, grad_kv = grad_qkv[:, :head], grad_qkv[:, head:]
    kv_keep = jnp.where(c == 0, grad_kv[:, :head], grad_kv[:, head:])
    kv_send = jnp.where(c == 0, grad_kv[:, head:], grad_kv[:, :head])
    kv = kv_keep + links.core(kv_send)
    kv_half = head // 2
    kv_keep = jnp.where(y == 0, kv[:, :kv_half], kv[:, kv_half:])
    kv_send = jnp.where(y == 0, kv[:, kv_half:], kv[:, :kv_half])
    kv = kv_keep + links.y(kv_send)
    attn_grads = jnp.concatenate([grad_w_query, grad_w_out_t, kv], axis=1)

    normed_all = jnp.concatenate(
        [normed_two[0][:quarter], normed_two[1][:quarter], normed_two[0][quarter:], normed_two[1][quarter:], normed_other],
        axis=0,
    )
    d_all = jnp.concatenate(
        [d_outputs[0][:quarter], d_outputs[1][:quarter], d_outputs[0][quarter:], d_outputs[1][quarter:], d_other], axis=0
    )
    gate, upward = product(normed_all, wg_h), product(normed_all, wu_h)
    inner, pull = jax.vjp(activate, gate, upward)
    inner = low(inner)
    d_inner = product_t(d_all, wd_h)
    d_gate, d_up = pull(d_inner)
    ff_grads = [t_product(d_all, inner), t_product(normed_all, low(d_gate)), t_product(normed_all, low(d_up))]

    zh, zl = z // 2, z % 2

    def sum_x(grads, z_half):
        mine = lax.dynamic_index_in_dim(grads, z_half, 0, keepdims=False)
        acc = lax.dynamic_index_in_dim(mine, x, 1, keepdims=False)
        for step in range(1, nx):
            to = lax.dynamic_index_in_dim(mine, (x + step) % nx, 1, keepdims=False)
            acc = acc + links.x(to, step)
        return acc

    def scatter(grads):
        grads = grads.reshape(2, 2, nx, blk, grads.shape[1])
        far = sum_x(grads, 1 - zh)
        near = sum_x(grads, zh)
        return near + links.z2(far)

    ff_sums = []
    for grads in ff_grads:
        got = scatter(grads)
        own = lax.dynamic_index_in_dim(got, zl, 0, keepdims=False)
        other = links.z1(lax.dynamic_index_in_dim(got, 1 - zl, 0, keepdims=False))
        ff_sums.append(
            jnp.where(
                parity == 0, jnp.concatenate([own, other], axis=1), jnp.concatenate([other, own], axis=1)
            )
        )
    grad_w_down, grad_w_gate, grad_w_up = ff_sums[0].T, ff_sums[1], ff_sums[2]

    got = scatter(attn_grads)
    attn_sum = lax.dynamic_index_in_dim(got, zl, 0, keepdims=False) + links.z1(
        lax.dynamic_index_in_dim(got, 1 - zl, 0, keepdims=False)
    )
    grad_w_query = attn_sum[:, :head]
    grad_w_out = attn_sum[:, head : 2 * head].T
    kv_own = attn_sum[:, 2 * head :]
    kv_y = links.y(kv_own)
    kv_wide = jnp.where(y == 0, jnp.concatenate([kv_own, kv_y], axis=1), jnp.concatenate([kv_y, kv_own], axis=1))
    kv_c = links.core(kv_wide)
    grad_w_key = jnp.where(c == 0, kv_wide, kv_c)
    grad_w_value = jnp.where(c == 0, kv_c, kv_wide)

    small = jnp.concatenate(
        [
            grad_attn_in.reshape(links.dp_size, -1),
            grad_attn_out.reshape(links.dp_size, -1),
            grad_ffn_in.reshape(links.dp_size, -1),
            (grad_ffn_out * 0.25).reshape(links.dp_size, -1),
            grad_gain_query.reshape(links.dp_size, -1),
            grad_gain_key.reshape(links.dp_size, -1),
        ],
        axis=1,
    )
    small = small + links.core(small)
    small = small + links.y(small)
    small = small.reshape(2, 2, nx, 1, small.shape[1])
    acc = lax.dynamic_index_in_dim(small, x, 2, keepdims=False)
    for step in range(1, nx):
        acc = acc + links.x(lax.dynamic_index_in_dim(small, (x + step) % nx, 2, keepdims=False), step)
    acc = lax.dynamic_index_in_dim(acc, zh, 0, keepdims=False) + links.z2(
        lax.dynamic_index_in_dim(acc, 1 - zh, 0, keepdims=False)
    )
    acc = lax.dynamic_index_in_dim(acc, zl, 0, keepdims=False) + links.z1(
        lax.dynamic_index_in_dim(acc, 1 - zl, 0, keepdims=False)
    )
    acc = acc.reshape(-1)
    hb = head // links.dp_size
    return (
        layer_out,
        input_grad,
        grad_w_query,
        grad_w_key,
        grad_w_value,
        grad_w_out,
        grad_w_gate,
        grad_w_up,
        grad_w_down,
        acc[:blk],
        acc[blk : 2 * blk],
        acc[2 * blk : 3 * blk],
        acc[3 * blk : 4 * blk],
        acc[4 * blk : 4 * blk + hb],
        acc[4 * blk + hb :],
    )


def solution(mesh):
    links = Links(mesh)
    return jax.shard_map(
        functools.partial(body if links.nx == 2 else body_any, links),
        mesh=mesh,
        in_specs=(
            P("dp", None),
            P("dp"),
            P("dp", None),
            P(None, "tensor"),
            P(),
            P(),
            P("tensor", None),
            P(None, "tensor"),
            P(None, "tensor"),
            P("tensor", None),
            P(),
            P(),
            P(),
            P(),
            P(),
            P(),
        ),
        out_specs=(
            P("dp", None),
            P("dp", None),
            P("dp", "tensor"),
            P("dp", None),
            P("dp", None),
            P("tensor", "dp"),
            P("dp", "tensor"),
            P("dp", "tensor"),
            P("tensor", "dp"),
            P("dp"),
            P("dp"),
            P("dp"),
            P("dp"),
            P("dp"),
            P("dp"),
        ),
        check_vma=False,
    )
```
